32 devices in a mesh: dp: 8 (over z, x), tensor: 4 (over y, core).
Axes of the slice: x: 2, y: 2, z: 4, core: 2. Of those that a mesh axis runs over, the one named last changes fastest.
Arguments:
- layer_input: bfloat16 [8192, 2048], P(('dp', 'tensor')), may hold values from -6 to 6
- segments: int32 [8192], P('dp'), may hold values from 0 to 8191, as said below
- positions: int32 [8192], P('dp'), may hold values from 0 to 1023, as said below
- first_gain: bfloat16 [2048], P('dp'), may hold values from 0.5 to 1.5
- first_shift: bfloat16 [2048], P('dp'), may hold values from -4 to 4
- query_weight: bfloat16 [2048, 2048], P('dp', 'tensor'), may hold values from -0.125 to 0.125
- key_weight: bfloat16 [2048, 2048], P('dp', 'tensor'), may hold values from -0.125 to 0.125
- value_weight: bfloat16 [2048, 2048], P('dp', 'tensor'), may hold values from -0.125 to 0.125
- query_bias: bfloat16 [32, 64], P('tensor', 'dp'), may hold values from -6 to 6
- key_bias: bfloat16 [32, 16], P('tensor'), may hold values from -6 to 6
- value_bias: bfloat16 [32, 64], P('tensor', 'dp'), may hold values from -6 to 6
- out_weight: bfloat16 [2048, 2048], P('tensor', 'dp'), may hold values from -0.5 to 0.5
- second_gain: bfloat16 [2048], P('dp'), may hold values from 0.5 to 1.5
- second_shift: bfloat16 [2048], P('dp'), may hold values from -4 to 4
- gate_weight: bfloat16 [2048, 5632], P('dp', 'tensor'), may hold values from -0.125 to 0.125
- up_weight: bfloat16 [2048, 5632], P('dp', 'tensor'), may hold values from -0.125 to 0.125
- down_weight: bfloat16 [5632, 2048], P('tensor', 'dp'), may hold values from -0.078125 to 0.078125
- out_grad: bfloat16 [8192, 2048], P(('dp', 'tensor')), may hold values from -6 to 6
Outputs:
- layer_output: bfloat16 [8192, 2048], P(('dp', 'tensor'))
- input_grad: float32 [8192, 2048], P(('dp', 'tensor'))
- first_gain_grad: float32 [2048], P(('dp', 'tensor'))
- first_shift_grad: float32 [2048], P(('dp', 'tensor'))
- query_weight_grad: float32 [2048, 2048], P('dp', 'tensor')
- key_weight_grad: float32 [2048, 2048], P('dp', 'tensor')
- value_weight_grad: float32 [2048, 2048], P('dp', 'tensor')
- query_bias_grad: float32 [32, 64], P('tensor', 'dp')
- key_bias_grad: float32 [32, 16], P('tensor')
- value_bias_grad: float32 [32, 64], P('tensor', 'dp')
- out_weight_grad: float32 [2048, 2048], P('tensor', 'dp')
- second_gain_grad: float32 [2048], P(('dp', 'tensor'))
- second_shift_grad: float32 [2048], P(('dp', 'tensor'))
- gate_weight_grad: float32 [2048, 5632], P('dp', 'tensor')
- up_weight_grad: float32 [2048, 5632], P('dp', 'tensor')
- down_weight_grad: float32 [5632, 2048], P('tensor', 'dp')
The draws below stay inside these ranges and needn't reach their ends.
Inputs may be any that keep to these rules, and one draw needn't show every extreme that they name: `segments`: the tokens form runs of 1024 rows that start at multiples of 1024; the first token of each run starts a new segment. A token's segment number is the row index of the last token of its segment, so numbers never fall along the rows and no two runs share one. `positions`: each token's position counts the earlier tokens of its segment.
All inputs are finite; a program needn't handle non-finite values.
Results may differ from the reference program's by a relative error of at most 0.015.
Values may be sent and summed in bfloat16 or wider, within the bound.
A program may use at most 256 MiB of HBM per device.

```python
import math
import jax
import jax.numpy as jnp
from jax import lax

D = 2048
H = 32
HD = 64
FF = 5632
ROT = 16
SEQ = 1024
TOKENS = 8192


def document_layout(key):
    folded = jax.random.fold_in(key, 11)
    index = jnp.arange(TOKENS, dtype=jnp.int32)
    rolls = jax.random.randint(folded, (TOKENS,), 0, max(SEQ // 4, 2))
    starts = (rolls == 0) & (index >= SEQ) | (index % SEQ == 0)
    closing = jnp.concatenate([starts[1:], jnp.ones((1,), dtype=bool)])
    numbers = lax.cummin(jnp.where(closing, index, TOKENS).astype(jnp.int32), axis=0, reverse=True)
    earliest = lax.cummax(jnp.where(starts, index, 0).astype(jnp.int32), axis=0)
    return (numbers.astype(jnp.int32), (index - earliest).astype(jnp.int32))


def draw_segments(key, part):
    return document_layout(key)[0]


def draw_positions(key, part):
    return document_layout(key)[1]


def strengthened(values, key, source, target, parts, factor):
    owner, partner = [(jnp.arange(values.shape[axis_at]) // (values.shape[axis_at] // parts)).reshape([-1 if axis == axis_at else 1 for axis in range(values.ndim)]) for axis_at in (source, target)]
    chosen = jax.random.permutation(key, parts)[partner]
    strong = (owner == chosen) | (owner == (partner + parts // 2) % parts)
    return jnp.where(strong, factor * values, values)


def steps_of(own_key, dims, shards, least, high):
    level = 1.0
    for axis_at, parts in shards:
        steps = jax.random.uniform(jax.random.fold_in(jax.random.fold_in(own_key, 6), axis_at), (parts,), jnp.float32, least / len(shards), high / len(shards))
        level = level * jnp.repeat(jnp.exp(steps), dims[axis_at] // parts).reshape((-1,) + (1,) * (len(dims) - 1 - axis_at))
    return level


def normal_values(stream_key, extent, width, reach, shards=(), kind=jnp.bfloat16):
    entries = jax.random.normal(stream_key, extent, jnp.float32) * width
    if len(shards) > 0:
        entries = steps_of(stream_key, extent, shards, -0.22, 0.18) * entries
    return jnp.clip(entries, min=-reach, max=reach).astype(kind)


def gaussian_with(key, dims, width, reach, split, heavy, held_as=jnp.bfloat16):
    values = width * jax.random.normal(key, dims, jnp.float32)
    if split:
        values = values * steps_of(key, dims, split, -0.22, 0.18)
    return jnp.clip(strengthened(values, jax.random.fold_in(key, 3), *heavy), -reach, reach).astype(held_as)


def setup_inputs(seed: int = 0) -> dict:
    streams_of = jax.random.split(jax.random.key(seed), 19)
    return {
        "layer_input": normal_values(streams_of[0], (TOKENS, D), 1.0, 6.0, ((0, 32),)),
        "segments": draw_segments(jax.random.fold_in(streams_of[18], 71), 0),
        "positions": draw_positions(jax.random.fold_in(streams_of[18], 71), 0),
        "first_gain": jnp.clip(1.0 + 0.1 * jax.random.normal(streams_of[3], (D,), jnp.float32), 0.5, 1.5).astype(jnp.bfloat16),
        "first_shift": normal_values(streams_of[4], (D,), 0.3, 4.0, ((0, 8),)),
        "query_weight": normal_values(streams_of[5], (D, D), D ** -0.5, 0.125, ((0, 8), (1, 4))),
        "key_weight": normal_values(streams_of[6], (D, D), D ** -0.5, 0.125, ((0, 8), (1, 4))),
        "value_weight": normal_values(streams_of[7], (D, D), D ** -0.5, 0.125, ((0, 8), (1, 4))),
        "query_bias": normal_values(streams_of[8], (H, HD), 0.5, 6.0, ((0, 4), (1, 8))),
        "key_bias": normal_values(streams_of[9], (H, ROT), 0.5, 6.0, ((0, 4),)),
        "value_bias": normal_values(streams_of[10], (H, HD), 0.5, 6.0, ((0, 4), (1, 8))),
        "out_weight": normal_values(streams_of[11], (D, D), (D // 16) ** -0.5, 0.5, ((0, 4), (1, 8))),
        "second_gain": jnp.clip(1.0 + 0.1 * jax.random.normal(streams_of[12], (D,), jnp.float32), 0.5, 1.5).astype(jnp.bfloat16),
        "second_shift": normal_values(streams_of[13], (D,), 0.3, 4.0, ((0, 8),)),
        "gate_weight": normal_values(streams_of[14], (D, FF), D ** -0.5, 0.125, ((0, 8), (1, 4))),
        "up_weight": normal_values(streams_of[15], (D, FF), D ** -0.5, 0.125, ((0, 8), (1, 4))),
        "down_weight": normal_values(streams_of[16], (FF, D), FF ** -0.5, 0.078125, ((0, 4), (1, 8))),
        "out_grad": gaussian_with(streams_of[17], (TOKENS, D), 1.0, 6.0, ((0, 32),), (0, 1, 32, 2.75)),
    }


EPS = 1e-05
NEG = -1e+30
HIGH = lax.Precision.HIGHEST

@jax.custom_vjp
def low(v):
    return lax.optimization_barrier(v.astype(jnp.bfloat16)).astype(jnp.float32)

@jax.custom_vjp
def low_back(v):
    return v

def low_keep(v):
    return (low(v), None)

def low_pass(kept, grad):
    return (grad,)

def back_keep(v):
    return (v, None)

def back_low(kept, grad):
    return (low(grad),)
low.defvjp(low_keep, low_pass)
low_back.defvjp(back_keep, back_low)

def matmul(left, right):
    return jnp.dot(left, right, precision=HIGH, preferred_element_type=jnp.float32)

def layer_norm(rows, gain, shift):
    center = rows - lax.optimization_barrier(jnp.mean(rows, axis=-1, keepdims=True))
    spread = lax.optimization_barrier(jnp.mean(center * center, axis=-1, keepdims=True))
    return center * lax.rsqrt(spread + EPS) * gain + shift

def rope_angles(positions):
    half = ROT // 2
    freqs = jnp.exp(-(2.0 / ROT) * jnp.arange(half).astype(jnp.float32) * math.log(10000.0))
    return positions.astype(jnp.float32)[:, None] * freqs[None, :]

def rotate(heads, angles):
    half = ROT // 2
    cosine = jnp.cos(angles)[:, None, :]
    sine = jnp.sin(angles)[:, None, :]
    first = heads[..., :half]
    second = heads[..., half:ROT]
    return jnp.concatenate([first * cosine - second * sine, second * cosine + first * sine, heads[..., ROT:]], axis=-1)

def layer(rows, seg_ids, pos_ids, params):
    gain_one, shift_one, w_query, w_key, w_value, b_query, b_key, b_value, w_out, gain_two, shift_two, w_gate, w_up, w_down = params
    norm_one = low(layer_norm(rows, gain_one, shift_one))
    q_lin = low_back(matmul(norm_one, w_query)) + b_query.reshape(-1)
    k_lin = low_back(matmul(norm_one, w_key)) + jnp.pad(b_key, ((0, 0), (0, HD - ROT))).reshape(-1)
    v_lin = low_back(matmul(norm_one, w_value)) + b_value.reshape(-1)
    angles = rope_angles(pos_ids)
    q_rot = low(rotate(q_lin.reshape(SEQ, H, HD), angles))
    k_rot = low(rotate(k_lin.reshape(SEQ, H, HD), angles))
    v_heads = low(v_lin.reshape(SEQ, H, HD))
    raw = jnp.einsum('qhd,khd->hqk', q_rot, k_rot, precision=HIGH)
    scores = low_back(raw) * HD ** (-0.5)
    index = jnp.arange(SEQ)
    allowed = (index[None, :] <= index[:, None]) & (seg_ids[None, :] == seg_ids[:, None])
    scores = jnp.where(allowed[None], scores, NEG)
    probs = low(jax.nn.softmax(scores, axis=-1))
    mixed = jnp.einsum('hqk,khd->qhd', probs, v_heads, precision=HIGH)
    mixed = low(low_back(mixed)).reshape(SEQ, D)
    attended = rows + low_back(matmul(mixed, w_out))
    norm_two = low(layer_norm(attended, gain_two, shift_two))
    gate_lin = low_back(matmul(norm_two, w_gate))
    up_lin = low_back(matmul(norm_two, w_up))
    hidden = low(jax.nn.silu(gate_lin) * up_lin)
    return attended + matmul(hidden, w_down)

def reference(layer_input, segments, positions, first_gain, first_shift, query_weight, key_weight, value_weight, query_bias, key_bias, value_bias, out_weight, second_gain, second_shift, gate_weight, up_weight, down_weight, out_grad):
    params = tuple((item.astype(jnp.float32) for item in (first_gain, first_shift, query_weight, key_weight, value_weight, query_bias, key_bias, value_bias, out_weight, second_gain, second_shift, gate_weight, up_weight, down_weight)))
    count = TOKENS // SEQ
    inputs = layer_input.astype(jnp.float32).reshape(count, SEQ, D)
    seg_all = segments.reshape(count, SEQ)
    pos_all = positions.reshape(count, SEQ)
    cotangents = out_grad.astype(jnp.float32).reshape(count, SEQ, D)
    zeros = jax.tree.map(jnp.zeros_like, params)

    def visit(totals, item):
        rows, seg_ids, pos_ids, cotangent = item
        result, pull = jax.vjp(lambda r, p: layer(r, seg_ids, pos_ids, p), rows, params)
        grad_rows, grad_params = pull(cotangent)
        return (jax.tree.map(jnp.add, totals, grad_params), (result, grad_rows))
    totals, (results, grads) = lax.scan(visit, zeros, (inputs, seg_all, pos_all, cotangents))
    g_gain_one, g_shift_one, g_query, g_key, g_value, g_bquery, g_bkey, g_bvalue, g_out, g_gain_two, g_shift_two, g_gate, g_up, g_down = totals
    return (results.reshape(TOKENS, D).astype(jnp.bfloat16), grads.reshape(TOKENS, D), g_gain_one, g_shift_one, g_query, g_key, g_value, g_bquery, g_bkey, g_bvalue, g_out, g_gain_two, g_shift_two, g_gate, g_up, g_down)
```

```python
import math

import jax
import jax.numpy as jnp
from jax import lax
from jax.experimental import pallas as pl
from jax.experimental.pallas import tpu as pltpu
from jax.sharding import PartitionSpec as P

HD = 64
ROT = 16
SEQ = 1024
HALF = ROT // 2
SCALE = HD ** (-0.5)

EPS = 1e-05
NEG = -1e30
QB = 256
f32 = jnp.float32
bf16 = jnp.bfloat16


def barrier(value, after):
    return lax.optimization_barrier((value, after))[0]


class Ring:
    def __init__(self):
        self.n = lax.axis_size("dp")
        self.ring = self.n % 2 == 0 and self.n <= 8
        order = list(range(0, self.n, 2)) + list(range(self.n - 1, 0, -2))
        self.up = [(order[i], order[(i + 1) % self.n]) for i in range(self.n)]
        self.down = [(b, a) for a, b in self.up]
        me = lax.axis_index("dp")
        self.me = me
        self.pos = jnp.where(me % 2 == 0, me // 2, self.n - 1 - (me - 1) // 2)

    def owner(self, offset):
        p = (self.pos + offset + 2 * self.n) % self.n
        return jnp.where(p < self.n // 2, 2 * p, 2 * (self.n - 1 - p) + 1)

    def gather(self, shard, pieces=1, after=None):
        n = self.n
        rows, cols = shard.shape
        if not self.ring:
            return lax.all_gather(shard, "dp", axis=0, tiled=True), [shard] * n
        if after is not None:
            shard = barrier(shard, after)
        full = jnp.zeros((n, rows, cols), shard.dtype)
        full = lax.dynamic_update_slice(full, shard[None], (self.me, 0, 0))
        size = rows // (2 * pieces)
        lanes = []
        for k in range(2 * pieces):
            lanes.append([k % 2, k * size, shard[k * size : (k + 1) * size]])
        marks = []
        for step in range(1, n):
            for lane in lanes:
                way, base, block = lane
                block = lax.ppermute(block, "dp", self.down if way else self.up)
                lane[2] = block
                whose = self.owner(step if way else -step)
                full = lax.dynamic_update_slice(full, block[None], (whose, base, 0))
            marks.append(lanes[-1][2])
        return full.reshape(n * rows, cols), marks

    def scatter(self, partial, pieces=1, after=None):
        n = self.n
        if not self.ring:
            return lax.psum_scatter(partial.astype(bf16), "dp", scatter_dimension=0, tiled=True).astype(f32)
        cols = partial.shape[1]
        rows = partial.shape[0] // n
        partial = partial.reshape(n, rows, cols)
        size = rows // (2 * pieces)
        done = []
        for k in range(2 * pieces):
            way = k % 2

            def block(step):
                whose = self.owner(1 + step if way else -1 - step)
                return lax.dynamic_slice(partial, (whose, k * size, 0), (1, size, cols))[0].astype(f32)

            moving = block(0)
            for step in range(1, n):
                got = lax.ppermute(moving.astype(bf16), "dp", self.down if way else self.up)
                moving = got.astype(f32) + block(step)
            done.append(moving)
        return jnp.concatenate(done, axis=0)


CORE = [(0, 1), (1, 0), (2, 3), (3, 2)]
CHIP = [(0, 2), (2, 0), (1, 3), (3, 1)]


def tensor_gather(rows, after=None):
    if lax.axis_size("tensor") != 4:
        return lax.all_gather(rows, "tensor", axis=0, tiled=True)
    if after is not None:
        rows = barrier(rows, after)
    t = lax.axis_index("tensor")
    far = lax.ppermute(rows, "tensor", CHIP)
    near = lax.ppermute(rows, "tensor", CORE)
    last = lax.ppermute(far, "tensor", CORE)
    full = jnp.zeros((4,) + rows.shape, rows.dtype)
    for flip, block in ((0, rows), (1, near), (2, far), (3, last)):
        full = lax.dynamic_update_slice(full, block[None], (t ^ flip, 0, 0))
    return full.reshape(4 * rows.shape[0], rows.shape[1])


def tensor_scatter(partial):
    if lax.axis_size("tensor") != 4:
        return lax.psum_scatter(partial.astype(bf16), "tensor", scatter_dimension=0, tiled=True).astype(f32)
    t = lax.axis_index("tensor")
    rows = partial.shape[0] // 4
    blocks = partial.reshape(4, rows, partial.shape[1])

    def block(flip):
        return lax.dynamic_slice(blocks, (t ^ flip, 0, 0), (1,) + blocks.shape[1:])[0]

    other = lax.ppermute(block(3).astype(bf16), "tensor", CORE)
    own = lax.ppermute(block(1).astype(bf16), "tensor", CORE)
    far = lax.ppermute((block(2) + other.astype(f32)).astype(bf16), "tensor", CHIP)
    return block(0) + own.astype(f32) + far.astype(f32)


def sum_all(vector, axes):
    for axis in axes:
        n = lax.axis_size(axis)
        if n & (n - 1):
            vector = lax.psum(vector, axis)
            continue
        step = 1
        while step < n:
            vector = vector + lax.ppermute(vector, axis, [(i, i ^ step) for i in range(n)])
            step *= 2
    return vector


def rotate(rows, cosine, sine, direction):
    first, second = rows[:HALF], rows[HALF:ROT]
    return jnp.concatenate(
        [first * cosine - direction * second * sine, second * cosine + direction * first * sine, rows[ROT:]], axis=0
    )


def dot(a, b, dims):
    return lax.dot_general(a, b, ((dims[0], dims[1]), ((), ())), preferred_element_type=f32)


def forward_kernel(q_ref, k_ref, v_ref, cos_ref, sin_ref, bias_ref, mixed_ref, q_out, k_out, v_out, log_ref):
    seq = q_ref.shape[1]
    cosine, sine = cos_ref[...], sin_ref[...]
    v_all = v_ref[...].astype(bf16)
    v_out[...] = v_all
    parts = []
    for head in range(q_ref.shape[0] // HD):
        rows = slice(head * HD, (head + 1) * HD)
        q = rotate(q_ref[rows, :], cosine, sine, 1.0).astype(bf16)
        k = rotate(k_ref[rows, :], cosine, sine, 1.0).astype(bf16)
        q_out[rows, :] = q
        k_out[rows, :] = k
        keys = k.T
        values = v_all[rows, :]
        q = q * jnp.asarray(SCALE, bf16)
        cols = []
        for start in range(0, seq, QB):
            end = start + QB
            scores = dot(keys[:end], q[:, start:end], ((1,), (0,))) + bias_ref[:end, start:end]
            top = jnp.max(scores, axis=0, keepdims=True)
            expo = jnp.exp(scores - top)
            total = jnp.sum(expo, axis=0, keepdims=True)
            probs = (expo * (1.0 / total)).astype(bf16)
            cols.append(dot(values[:, :end], probs, ((1,), (0,))).astype(bf16))
            log_ref[0, head : head + 1, start:end] = top + jnp.log(total)
        parts.append(jnp.concatenate(cols, axis=1))
    mixed_ref[...] = jnp.concatenate(parts, axis=0).T


def attend_forward(lin, cosine, sine, bias):
    width, seq = lin.shape[0] // 3, lin.shape[1]
    pair = 2 * HD
    count = width // pair
    outs = []
    block = lambda base: pl.BlockSpec((pair, seq), lambda i: (base * count + i, 0))
    whole = lambda shape: pl.BlockSpec(shape, lambda i: (0, 0))
    return pl.pallas_call(
        forward_kernel,
        grid=(count,),
        in_specs=[block(0), block(1), block(2), whole(cosine.shape), whole(sine.shape), whole(bias.shape)],
        out_specs=[
            pl.BlockSpec((seq, pair), lambda i: (0, i)),
            pl.BlockSpec((pair, seq), lambda i: (i, 0)),
            pl.BlockSpec((pair, seq), lambda i: (i, 0)),
            pl.BlockSpec((pair, seq), lambda i: (i, 0)),
            pl.BlockSpec((1, 2, seq), lambda i: (i, 0, 0)),
        ],
        out_shape=[
            jax.ShapeDtypeStruct((seq, width), bf16),
            jax.ShapeDtypeStruct((width, seq), bf16),
            jax.ShapeDtypeStruct((width, seq), bf16),
            jax.ShapeDtypeStruct((width, seq), bf16),
            jax.ShapeDtypeStruct((count, 2, seq), f32),
        ],
        compiler_params=pltpu.CompilerParams(vmem_limit_bytes=48 << 20),
        cost_estimate=pl.CostEstimate(
            flops=4 * width * seq * seq, bytes_accessed=30 << 20, transcendentals=width // HD * seq * seq
        ),
        name="attend_forward",
    )(lin, lin, lin, cosine, sine, bias)


def backward_kernel(q_ref, k_ref, v_ref, d_ref, log_ref, cos_ref, sin_ref, bias_ref, dq_out, dk_out, dv_out, sums_ref, dk_acc, dv_acc):
    seq = q_ref.shape[1]
    cosine, sine = cos_ref[...], sin_ref[...]
    for head in range(q_ref.shape[0] // HD):
        rows = slice(head * HD, (head + 1) * HD)
        q, k, v, d = q_ref[rows, :], k_ref[rows, :], v_ref[rows, :], d_ref[rows, :]
        keys, values = k.T, v.T
        q_small = q * jnp.asarray(SCALE, bf16)
        dk_acc[...] = jnp.zeros_like(dk_acc)
        dv_acc[...] = jnp.zeros_like(dv_acc)
        cols = []
        for start in range(0, seq, QB):
            end = start + QB
            here = slice(start, end)
            scores = dot(keys[:end], q_small[:, here], ((1,), (0,))) + bias_ref[:end, here]
            probs = jnp.exp(scores - log_ref[0, head : head + 1, here])
            grad = dot(values[:end], d[:, here], ((1,), (0,)))
            both = probs * grad
            inner = jnp.sum(both, axis=0, keepdims=True)
            grad = ((both - probs * inner) * SCALE).astype(bf16)
            probs = probs.astype(bf16)
            cols.append(dot(k[:, :end], grad, ((1,), (0,))))
            dk_acc[:, :end] += dot(q[:, here], grad, ((1,), (1,)))
            dv_acc[:, :end] += dot(d[:, here], probs, ((1,), (1,)))
        dq = rotate(jnp.concatenate(cols, axis=1), cosine, sine, -1.0)
        dk = rotate(dk_acc[...], cosine, sine, -1.0)
        dv = dv_acc[...]
        for part, (out, value) in enumerate(((dq_out, dq), (dk_out, dk), (dv_out, dv))):
            out[rows, :] = value.astype(bf16)
            sums_ref[0, rows, part : part + 1] = jnp.sum(value, axis=1, keepdims=True)


def attend_backward(q, k, v, d, logs, cosine, sine, bias):
    width, seq = q.shape
    pair = 2 * HD
    count = width // pair
    block = pl.BlockSpec((pair, seq), lambda i: (i, 0))
    whole = lambda shape: pl.BlockSpec(shape, lambda i: (0, 0))
    return pl.pallas_call(
        backward_kernel,
        grid=(count,),
        in_specs=[block] * 4
        + [pl.BlockSpec((1, 2, seq), lambda i: (i, 0, 0)), whole(cosine.shape), whole(sine.shape), whole(bias.shape)],
        out_specs=[block] * 3 + [pl.BlockSpec((1, pair, 128), lambda i: (i, 0, 0))],
        out_shape=[jax.ShapeDtypeStruct((width, seq), bf16)] * 3 + [jax.ShapeDtypeStruct((count, pair, 128), f32)],
        scratch_shapes=[pltpu.VMEM((HD, seq), f32), pltpu.VMEM((HD, seq), f32)],
        compiler_params=pltpu.CompilerParams(vmem_limit_bytes=48 << 20),
        cost_estimate=pl.CostEstimate(
            flops=10 * width * seq * seq, bytes_accessed=30 << 20, transcendentals=width // HD * seq * seq
        ),
        name="attend_backward",
    )(q, k, v, d, logs, cosine, sine, bias)


def norm_forward(rows):
    center = rows - jnp.mean(rows, axis=-1, keepdims=True)
    rstd = lax.rsqrt(jnp.mean(center * center, axis=-1, keepdims=True) + EPS)
    return center * rstd, rstd


def norm_backward(grad_out, normal, rstd, gain):
    scaled = grad_out * gain
    return rstd * (
        scaled
        - jnp.mean(scaled, axis=-1, keepdims=True)
        - normal * jnp.mean(scaled * normal, axis=-1, keepdims=True)
    )


def local(
    layer_input,
    segments,
    positions,
    first_gain,
    first_shift,
    query_weight,
    key_weight,
    value_weight,
    query_bias,
    key_bias,
    value_bias,
    out_weight,
    second_gain,
    second_shift,
    gate_weight,
    up_weight,
    down_weight,
    out_grad,
):
    ring = Ring()
    n = ring.n
    width = query_weight.shape[1]
    heads = width // HD
    model = layer_input.shape[1]

    x_full = tensor_gather(layer_input)
    g_full = tensor_gather(out_grad, after=x_full)

    small = jnp.concatenate(
        [first_gain, first_shift, second_gain, second_shift, query_bias.reshape(-1), value_bias.reshape(-1)]
    )
    small = lax.all_gather(small.reshape(1, -1), "dp", axis=0, tiled=True)
    part = model // n
    gain_one, shift_one, gain_two, shift_two = (
        small[:, i * part : (i + 1) * part].reshape(model).astype(f32) for i in range(4)
    )
    per = HD // n
    biases = small[:, 4 * part :].reshape(n, 2, heads, per).transpose(1, 2, 0, 3).reshape(2, width).astype(f32)
    bias_key = jnp.pad(key_bias.astype(f32), ((0, 0), (0, HD - ROT))).reshape(-1)
    bias_lin = jnp.concatenate([biases[0], bias_key, biases[1]])

    qkv, marks = ring.gather(jnp.concatenate([query_weight, key_weight, value_weight], axis=1), pieces=2)
    out_t, _ = ring.gather(out_weight.T, after=marks[-2])
    gate, marks = ring.gather(gate_weight, after=marks[-2])
    up, marks = ring.gather(up_weight, pieces=2, after=marks[-2])
    down_t, _ = ring.gather(down_weight.T, pieces=2, after=marks[-2])

    hat_full, _ = norm_forward(x_full.astype(f32))
    normed = (hat_full * gain_one + shift_one).astype(bf16)

    lin = dot(qkv, normed, ((0,), (1,))) + bias_lin[:, None]
    freqs = jnp.exp(-(2.0 / ROT) * jnp.arange(HALF).astype(f32) * math.log(10000.0))
    angles = freqs[:, None] * positions.astype(f32)[None, :]
    cosine, sine = jnp.cos(angles), jnp.sin(angles)
    index = jnp.arange(segments.shape[0], dtype=jnp.int32)
    allowed = (index[:, None] <= index[None, :]) & (segments[:, None] == segments[None, :])
    bias = jnp.where(allowed, 0.0, NEG).astype(f32)
    mixed, q_rot, k_rot, v_heads, logs = attend_forward(lin, cosine, sine, bias)
    rows = layer_input.astype(f32)
    attended = rows + tensor_scatter(dot(mixed, out_t, ((1,), (1,))))

    hat_two, rstd_two = norm_forward(attended)
    second = tensor_gather((hat_two * gain_two + shift_two).astype(bf16))
    gate_lin = dot(second, gate, ((1,), (0,)))
    up_lin = dot(second, up, ((1,), (0,)))
    sigma = jax.nn.sigmoid(gate_lin)
    activated = gate_lin * sigma
    hidden = (activated * up_lin).astype(bf16)
    layer_output = (attended + tensor_scatter(dot(hidden, down_t, ((1,), (1,))))).astype(bf16)

    down_grad = dot(g_full, hidden, ((0,), (0,)))
    grad_hidden = dot(g_full, down_t, ((1,), (0,)))
    grad_gate = (grad_hidden * up_lin * sigma * (1.0 + gate_lin * (1.0 - sigma))).astype(bf16)
    grad_up = (grad_hidden * activated).astype(bf16)
    grad_second = tensor_scatter(dot(grad_gate, gate, ((1,), (1,))) + dot(grad_up, up, ((1,), (1,))))
    gate_grad = dot(second, grad_gate, ((0,), (0,)))
    up_grad = dot(second, grad_up, ((0,), (0,)))
    down_sum = ring.scatter(down_grad).T
    gate_sum = ring.scatter(gate_grad)
    up_sum = ring.scatter(up_grad)
    grad_attended = out_grad.astype(f32) + norm_backward(grad_second, hat_two, rstd_two, gain_two)
    residual = tensor_gather(grad_attended.astype(bf16))

    grad_mixed = dot(out_t, residual, ((0,), (1,))).astype(bf16)
    out_grad_t = dot(residual, mixed, ((0,), (0,)))
    out_sum = ring.scatter(out_grad_t).T
    dq, dk, dv, sums = attend_backward(q_rot, k_rot, v_heads, grad_mixed, logs, cosine, sine, bias)
    grad_lin = jnp.concatenate([dq, dk, dv], axis=0)
    qkv_grad = dot(normed, grad_lin, ((0,), (1,)))
    qkv_sum = ring.scatter(qkv_grad, pieces=2)
    grad_first = tensor_scatter(dot(grad_lin, qkv, ((0,), (1,))))
    hat_one, rstd_one = norm_forward(rows)
    input_grad = grad_attended + norm_backward(grad_first, hat_one, rstd_one, gain_one)

    vectors = jnp.stack(
        [
            jnp.sum(grad_first * hat_one, axis=0),
            jnp.sum(grad_first, axis=0),
            jnp.sum(grad_second * hat_two, axis=0),
            jnp.sum(grad_second, axis=0),
        ]
    )
    vectors = sum_all(vectors, ["tensor"])
    sums = sums.reshape(width, 128)[:, :3]
    packed = sum_all(jnp.concatenate([vectors.reshape(-1), sums.reshape(-1)]), ["dp"])
    each = model // (n * lax.axis_size("tensor"))
    at = ring.me * lax.axis_size("tensor") + lax.axis_index("tensor")
    vectors = lax.dynamic_slice(packed[: 4 * model].reshape(4, -1, each), (0, at, 0), (4, 1, each))[:, 0]
    sums = packed[4 * model :].reshape(heads, n, per, 3)
    mine = lax.dynamic_slice(sums, (0, ring.me, 0, 0), (heads, 1, per, 3))[:, 0]
    key_sum = sums[..., 1].reshape(heads, HD)[:, :ROT]

    return (
        layer_output,
        input_grad,
        vectors[0],
        vectors[1],
        qkv_sum[:, :width],
        qkv_sum[:, width : 2 * width],
        qkv_sum[:, 2 * width :],
        mine[..., 0],
        key_sum,
        mine[..., 2],
        out_sum,
        vectors[2],
        vectors[3],
        gate_sum,
        up_sum,
        down_sum,
    )


def solution(mesh):
    both = ("dp", "tensor")
    return jax.shard_map(
        local,
        mesh=mesh,
        in_specs=(
            P(both, None),
            P("dp"),
            P("dp"),
            P("dp"),
            P("dp"),
            P("dp", "tensor"),
            P("dp", "tensor"),
            P("dp", "tensor"),
            P("tensor", "dp"),
            P("tensor", None),
            P("tensor", "dp"),
            P("tensor", "dp"),
            P("dp"),
            P("dp"),
            P("dp", "tensor"),
            P("dp", "tensor"),
            P("tensor", "dp"),
            P(both, None),
        ),
        out_specs=(
            P(both, None),
            P(both, None),
            P(both),
            P(both),
            P("dp", "tensor"),
            P("dp", "tensor"),
            P("dp", "tensor"),
            P("tensor", "dp"),
            P("tensor", None),
            P("tensor", "dp"),
            P("tensor", "dp"),
            P(both),
            P(both),
            P("dp", "tensor"),
            P("dp", "tensor"),
            P("tensor", "dp"),
        ),
        check_vma=False,
    )
```

```python
import math

import jax
import jax.numpy as jnp
from jax import lax
from jax.experimental import pallas as pl
from jax.experimental.pallas import tpu as pltpu
from jax.sharding import PartitionSpec as P

HD = 64
ROT = 16
SEQ = 1024
HALF = ROT // 2
SCALE = HD ** (-0.5)

EPS = 1e-05
NEG = -1e30
QB = 256
f32 = jnp.float32
bf16 = jnp.bfloat16


def barrier(value, after):
    return lax.optimization_barrier((value, after))[0]


class Ring:
    def __init__(self):
        self.n = lax.axis_size("dp")
        self.ring = self.n % 2 == 0 and self.n <= 8
        order = list(range(0, self.n, 2)) + list(range(self.n - 1, 0, -2))
        self.up = [(order[i], order[(i + 1) % self.n]) for i in range(self.n)]
        self.down = [(b, a) for a, b in self.up]
        me = lax.axis_index("dp")
        self.me = me
        self.pos = jnp.where(me % 2 == 0, me // 2, self.n - 1 - (me - 1) // 2)

    def owner(self, offset):
        p = (self.pos + offset + 2 * self.n) % self.n
        return jnp.where(p < self.n // 2, 2 * p, 2 * (self.n - 1 - p) + 1)

    def gather(self, shard, pieces=1, after=None):
        n = self.n
        rows, cols = shard.shape
        if not self.ring:
            return lax.all_gather(shard, "dp", axis=0, tiled=True), [shard] * n
        if after is not None:
            shard = barrier(shard, after)
        full = jnp.zeros((n, rows, cols), shard.dtype)
        full = lax.dynamic_update_slice(full, shard[None], (self.me, 0, 0))
        size = rows // (2 * pieces)
        lanes = []
        for k in range(2 * pieces):
            lanes.append([k % 2, k * size, shard[k * size : (k + 1) * size]])
        marks = []
        for step in range(1, n):
            for lane in lanes:
                way, base, block = lane
                block = lax.ppermute(block, "dp", self.down if way else self.up)
                lane[2] = block
                whose = self.owner(step if way else -step)
                full = lax.dynamic_update_slice(full, block[None], (whose, base, 0))
            marks.append(lanes[-1][2])
        return full.reshape(n * rows, cols), marks

    def scatter(self, partial, pieces=1, after=None):
        n = self.n
        if not self.ring:
            return lax.psum_scatter(partial.astype(bf16), "dp", scatter_dimension=0, tiled=True).astype(f32)
        cols = partial.shape[1]
        rows = partial.shape[0] // n
        partial = partial.reshape(n, rows, cols)
        size = rows // (2 * pieces)
        done = []
        for k in range(2 * pieces):
            way = k % 2

            def block(step):
                whose = self.owner(1 + step if way else -1 - step)
                return lax.dynamic_slice(partial, (whose, k * size, 0), (1, size, cols))[0].astype(f32)

            moving = block(0)
            for step in range(1, n):
                got = lax.ppermute(moving.astype(bf16), "dp", self.down if way else self.up)
                moving = got.astype(f32) + block(step)
            done.append(moving)
        return jnp.concatenate(done, axis=0)


CORE = [(0, 1), (1, 0), (2, 3), (3, 2)]
CHIP = [(0, 2), (2, 0), (1, 3), (3, 1)]


def tensor_gather(rows, after=None):
    if lax.axis_size("tensor") != 4:
        return lax.all_gather(rows, "tensor", axis=0, tiled=True)
    if after is not None:
        rows = barrier(rows, after)
    t = lax.axis_index("tensor")
    far = lax.ppermute(rows, "tensor", CHIP)
    near = lax.ppermute(rows, "tensor", CORE)
    last = lax.ppermute(far, "tensor", CORE)
    full = jnp.zeros((4,) + rows.shape, rows.dtype)
    for flip, block in ((0, rows), (1, near), (2, far), (3, last)):
        full = lax.dynamic_update_slice(full, block[None], (t ^ flip, 0, 0))
    return full.reshape(4 * rows.shape[0], rows.shape[1])


def tensor_scatter(partial):
    if lax.axis_size("tensor") != 4:
        return lax.psum_scatter(partial.astype(bf16), "tensor", scatter_dimension=0, tiled=True).astype(f32)
    t = lax.axis_index("tensor")
    rows = partial.shape[0] // 4
    blocks = partial.reshape(4, rows, partial.shape[1])

    def block(flip):
        return lax.dynamic_slice(blocks, (t ^ flip, 0, 0), (1,) + blocks.shape[1:])[0]

    other = lax.ppermute(block(3).astype(bf16), "tensor", CORE)
    own = lax.ppermute(block(1).astype(bf16), "tensor", CORE)
    far = lax.ppermute((block(2) + other.astype(f32)).astype(bf16), "tensor", CHIP)
    return block(0) + own.astype(f32) + far.astype(f32)


def sum_all(vector, axes):
    for axis in axes:
        n = lax.axis_size(axis)
        if n & (n - 1):
            vector = lax.psum(vector, axis)
            continue
        step = 1
        while step < n:
            vector = vector + lax.ppermute(vector, axis, [(i, i ^ step) for i in range(n)])
            step *= 2
    return vector


def rotate(rows, cosine, sine, direction):
    first, second = rows[:HALF], rows[HALF:ROT]
    return jnp.concatenate(
        [first * cosine - direction * second * sine, second * cosine + direction * first * sine, rows[ROT:]], axis=0
    )


def dot(a, b, dims):
    return lax.dot_general(a, b, ((dims[0], dims[1]), ((), ())), preferred_element_type=f32)


def forward_kernel(q_ref, k_ref, v_ref, cos_ref, sin_ref, bias_ref, mixed_ref, q_out, k_out, v_out, log_ref):
    seq = q_ref.shape[1]
    cosine, sine = cos_ref[...], sin_ref[...]
    v_all = v_ref[...].astype(bf16)
    v_out[...] = v_all
    parts = []
    for head in range(q_ref.shape[0] // HD):
        rows = slice(head * HD, (head + 1) * HD)
        q = rotate(q_ref[rows, :], cosine, sine, 1.0).astype(bf16)
        k = rotate(k_ref[rows, :], cosine, sine, 1.0).astype(bf16)
        q_out[rows, :] = q
        k_out[rows, :] = k
        keys = k.T
        values = v_all[rows, :]
        q = q * jnp.asarray(SCALE, bf16)
        cols = []
        for start in range(0, seq, QB):
            end = start + QB
            scores = dot(keys[:end], q[:, start:end], ((1,), (0,))) + bias_ref[:end, start:end]
            top = jnp.max(scores, axis=0, keepdims=True)
            expo = jnp.exp(scores - top)
            total = jnp.sum(expo, axis=0, keepdims=True)
            probs = (expo * (1.0 / total)).astype(bf16)
            cols.append(dot(values[:, :end], probs, ((1,), (0,))).astype(bf16))
            log_ref[0, head : head + 1, start:end] = top + jnp.log(total)
        parts.append(jnp.concatenate(cols, axis=1))
    mixed_ref[...] = jnp.concatenate(parts, axis=0).T


def attend_forward(lin, cosine, sine, bias):
    width, seq = lin.shape[0] // 3, lin.shape[1]
    pair = 2 * HD
    count = width // pair
    outs = []
    block = lambda base: pl.BlockSpec((pair, seq), lambda i: (base * count + i, 0))
    whole = lambda shape: pl.BlockSpec(shape, lambda i: (0, 0))
    return pl.pallas_call(
        forward_kernel,
        grid=(count,),
        in_specs=[block(0), block(1), block(2), whole(cosine.shape), whole(sine.shape), whole(bias.shape)],
        out_specs=[
            pl.BlockSpec((seq, pair), lambda i: (0, i)),
            pl.BlockSpec((pair, seq), lambda i: (i, 0)),
            pl.BlockSpec((pair, seq), lambda i: (i, 0)),
            pl.BlockSpec((pair, seq), lambda i: (i, 0)),
            pl.BlockSpec((1, 2, seq), lambda i: (i, 0, 0)),
        ],
        out_shape=[
            jax.ShapeDtypeStruct((seq, width), bf16),
            jax.ShapeDtypeStruct((width, seq), bf16),
            jax.ShapeDtypeStruct((width, seq), bf16),
            jax.ShapeDtypeStruct((width, seq), bf16),
            jax.ShapeDtypeStruct((count, 2, seq), f32),
        ],
        compiler_params=pltpu.CompilerParams(vmem_limit_bytes=48 << 20),
        cost_estimate=pl.CostEstimate(
            flops=4 * width * seq * seq, bytes_accessed=30 << 20, transcendentals=width // HD * seq * seq
        ),
        name="attend_forward",
    )(lin, lin, lin, cosine, sine, bias)


def backward_kernel(q_ref, k_ref, v_ref, d_ref, log_ref, cos_ref, sin_ref, bias_ref, dq_out, dk_out, dv_out, sums_ref, dk_acc, dv_acc):
    seq = q_ref.shape[1]
    cosine, sine = cos_ref[...], sin_ref[...]
    for head in range(q_ref.shape[0] // HD):
        rows = slice(head * HD, (head + 1) * HD)
        q, k, v, d = q_ref[rows, :], k_ref[rows, :], v_ref[rows, :], d_ref[rows, :]
        keys, values = k.T, v.T
        q_small = q * jnp.asarray(SCALE, bf16)
        dk_acc[...] = jnp.zeros_like(dk_acc)
        dv_acc[...] = jnp.zeros_like(dv_acc)
        cols = []
        for start in range(0, seq, QB):
            end = start + QB
            here = slice(start, end)
            scores = dot(keys[:end], q_small[:, here], ((1,), (0,))) + bias_ref[:end, here]
            probs = jnp.exp(scores - log_ref[0, head : head + 1, here])
            grad = dot(values[:end], d[:, here], ((1,), (0,)))
            both = probs * grad
            inner = jnp.sum(both, axis=0, keepdims=True)
            grad = ((both - probs * inner) * SCALE).astype(bf16)
            probs = probs.astype(bf16)
            cols.append(dot(k[:, :end], grad, ((1,), (0,))))
            dk_acc[:, :end] += dot(q[:, here], grad, ((1,), (1,)))
            dv_acc[:, :end] += dot(d[:, here], probs, ((1,), (1,)))
        dq = rotate(jnp.concatenate(cols, axis=1), cosine, sine, -1.0)
        dk = rotate(dk_acc[...], cosine, sine, -1.0)
        dv = dv_acc[...]
        for part, (out, value) in enumerate(((dq_out, dq), (dk_out, dk), (dv_out, dv))):
            out[rows, :] = value.astype(bf16)
            sums_ref[0, rows, part : part + 1] = jnp.sum(value, axis=1, keepdims=True)


def attend_backward(q, k, v, d, logs, cosine, sine, bias):
    width, seq = q.shape
    pair = 2 * HD
    count = width // pair
    block = pl.BlockSpec((pair, seq), lambda i: (i, 0))
    whole = lambda shape: pl.BlockSpec(shape, lambda i: (0, 0))
    return pl.pallas_call(
        backward_kernel,
        grid=(count,),
        in_specs=[block] * 4
        + [pl.BlockSpec((1, 2, seq), lambda i: (i, 0, 0)), whole(cosine.shape), whole(sine.shape), whole(bias.shape)],
        out_specs=[block] * 3 + [pl.BlockSpec((1, pair, 128), lambda i: (i, 0, 0))],
        out_shape=[jax.ShapeDtypeStruct((width, seq), bf16)] * 3 + [jax.ShapeDtypeStruct((count, pair, 128), f32)],
        scratch_shapes=[pltpu.VMEM((HD, seq), f32), pltpu.VMEM((HD, seq), f32)],
        compiler_params=pltpu.CompilerParams(vmem_limit_bytes=48 << 20),
        cost_estimate=pl.CostEstimate(
            flops=10 * width * seq * seq, bytes_accessed=30 << 20, transcendentals=width // HD * seq * seq
        ),
        name="attend_backward",
    )(q, k, v, d, logs, cosine, sine, bias)


MESH = pl.DeviceIdType.MESH
HBM = pl.BlockSpec(memory_space=pl.ANY)
VMEM = pl.BlockSpec(memory_space=pltpu.VMEM)
DMA = pltpu.SemaphoreType.DMA


class Place:
    def __init__(self, n):
        self.n = n
        self.me = lax.axis_index("dp")
        self.t = lax.axis_index("tensor")
        odd = lax.rem(self.me, 2)
        half = lax.div(self.me, 2)
        self.pos = jnp.where(odd == 0, half, n - 1 - half)
        self.up = self.owner(1)
        self.down = self.owner(-1)
        self.core = self.t + 1 - 2 * lax.rem(self.t, 2)
        self.chip = lax.rem(self.t + 2, 4)
        self.cross = lax.rem(self.core + 2, 4)

    def owner(self, offset):
        p = lax.rem(self.pos + (offset + 2 * self.n), self.n)
        return jnp.where(p < self.n // 2, 2 * p, 2 * (self.n - 1 - p) + 1)

    def barrier(self, dp, tensor):
        sem = pltpu.get_barrier_semaphore()
        for there in dp:
            pl.semaphore_signal(sem, inc=1, device_id={"dp": there}, device_id_type=MESH)
        for there in tensor:
            pl.semaphore_signal(sem, inc=1, device_id={"tensor": there}, device_id_type=MESH)
        pl.semaphore_wait(sem, len(dp) + len(tensor))


class Lane:
    def __init__(self, place, full, base, size, way, send, recv):
        self.place, self.full, self.base, self.size, self.way = place, full, base, size, way
        self.send, self.recv = send, recv

    def whose(self, step):
        return self.place.owner(step if self.way else -step)

    def copy(self, step, whose):
        piece = self.full.at[whose, pl.ds(self.base, self.size)]
        return pltpu.make_async_remote_copy(
            src_ref=piece,
            dst_ref=piece,
            send_sem=self.send.at[step - 1],
            recv_sem=self.recv.at[step - 1],
            device_id={"dp": self.place.down if self.way else self.place.up},
            device_id_type=MESH,
        )

    def start(self, step):
        self.copy(step, self.whose(step - 1)).start()

    def arrive(self, step):
        self.copy(step, self.whose(step)).wait_recv()

    def finish(self):
        for step in range(1, self.place.n):
            self.copy(step, self.whose(step - 1)).wait_send()


class Exchange:
    def __init__(self, send, recv):
        self.send, self.recv = send, recv

    def copy(self, number, src, dst, there):
        return pltpu.make_async_remote_copy(
            src_ref=src,
            dst_ref=dst,
            send_sem=self.send.at[number],
            recv_sem=self.recv.at[number],
            device_id={"tensor": there},
            device_id_type=MESH,
        )


def row_norm(value, gain, shift):
    center = value - jnp.mean(value, axis=1, keepdims=True)
    rstd = lax.rsqrt(jnp.mean(center * center, axis=1, keepdims=True) + EPS)
    return center * rstd * gain + shift


def lane_vector(full, first, count):
    pieces = [full[d, r : r + 1, :].astype(f32) for d in range(full.shape[0]) for r in range(first, first + count)]
    return jnp.concatenate(pieces, axis=1)


def enter_kernel(
    n,
    x_ref, g_ref, wq, wk, wv, wo, small_ref,
    normed_out, g_out, qkv_out, out_out, lin, small_full,
    x_full, normed, left, right, outs,
    small_send, small_recv, send, recv, x_send, x_recv, local, stored,
):
    place = Place(n)
    rows = x_ref.shape[0]
    size = wq.shape[0]
    width = wq.shape[1]
    half = width // 2
    me, t = place.me, place.t
    loads = [
        pltpu.make_async_copy(wq, left.at[me, :, pl.ds(0, width)], local.at[0]),
        pltpu.make_async_copy(wk.at[:, pl.ds(0, half)], left.at[me, :, pl.ds(width, half)], local.at[1]),
        pltpu.make_async_copy(wk.at[:, pl.ds(half, half)], right.at[me, :, pl.ds(0, half)], local.at[2]),
        pltpu.make_async_copy(wv, right.at[me, :, pl.ds(half, width)], local.at[3]),
        pltpu.make_async_copy(x_ref, x_full.at[t], local.at[4]),
        pltpu.make_async_copy(g_ref, g_out.at[t], local.at[5]),
    ]
    for load in loads:
        load.start()
    outs[me] = wo[...].T
    small_full[me] = small_ref[...]
    place.barrier([place.owner(k) for k in range(1, n)], [place.core, place.chip])

    smalls = []
    for k in range(1, n):
        smalls.append(
            pltpu.make_async_remote_copy(
                src_ref=small_ref,
                dst_ref=small_full.at[me],
                send_sem=small_send.at[k - 1],
                recv_sem=small_recv.at[k - 1],
                device_id={"dp": place.owner(k)},
                device_id_type=MESH,
            )
        )
        smalls[-1].start()

    swap = Exchange(x_send, x_recv)
    to_chip = swap.copy(0, x_ref, x_full.at[t], place.chip)
    to_core = swap.copy(1, x_ref, x_full.at[t], place.core)
    relay = swap.copy(2, x_full.at[place.chip], x_full.at[place.chip], place.core)
    g_chip = swap.copy(3, g_ref, g_out.at[t], place.chip)
    g_core = swap.copy(4, g_ref, g_out.at[t], place.core)
    g_relay = swap.copy(5, g_out.at[place.chip], g_out.at[place.chip], place.core)
    to_chip.start()
    to_core.start()
    for load in loads[:4]:
        load.wait()
    lanes = []
    for number, (full, base, count, way) in enumerate(
        (
            (left, 0, size // 2, 0),
            (right, 0, size // 2, 1),
            (left, size // 2, size // 2, 0),
            (right, size // 2, size // 2, 1),
            (outs, 0, size // 2, 0),
            (outs, size // 2, size // 2, 1),
        )
    ):
        lanes.append(Lane(place, full, base, count, way, send.at[number], recv.at[number]))

    def store(step):
        whose, other = place.owner(-step), place.owner(step)
        if step == n:
            return []
        return [
            pltpu.make_async_copy(left.at[whose], qkv_out.at[whose, :, pl.ds(0, width + half)], stored.at[0, step]),
            pltpu.make_async_copy(right.at[other], qkv_out.at[other, :, pl.ds(width + half, width + half)], stored.at[1, step]),
            pltpu.make_async_copy(outs.at[whose, pl.ds(0, size // 2)], out_out.at[whose, pl.ds(0, size // 2)], stored.at[2, step]),
            pltpu.make_async_copy(
                outs.at[other, pl.ds(size // 2, size // 2)], out_out.at[other, pl.ds(size // 2, size // 2)], stored.at[3, step]
            ),
        ]

    writes = []

    def tick(step):
        for lane in lanes:
            if step > 1:
                lane.arrive(step - 1)
            if step < n:
                lane.start(step)
        for write in store(step - 1):
            write.start()
            writes.append(write)

    gain = shift = None

    def norm(block):
        @pl.loop(0, rows // 16)
        def _(i):
            here = pl.ds(pl.multiple_of(i * 16, 16), 16)
            there = pl.ds(pl.multiple_of(block * rows + i * 16, 16), 16)
            normed[there, :] = row_norm(x_full[block, here, :].astype(f32), gain, shift).astype(bf16)

    def project(step):
        for full, whose, base in ((left, place.owner(-step), 0), (right, place.owner(step), width + half)):
            xs = normed[:, pl.ds(pl.multiple_of(whose * size, size), size)]
            for j in range(0, width + half, 256):
                part = dot(full[whose, :, j : j + 256].T, xs, ((1,), (1,)))
                where = slice(base + j, base + j + 256)
                if step == 0:
                    lin[where, :] = part
                else:
                    lin[where, :] += part

    tick(1)
    loads[4].wait()
    for small in smalls:
        small.wait_recv()
    count = small_ref.shape[1]
    gain = lane_vector(small_full, 0, size // count)
    shift = lane_vector(small_full, size // count, size // count)
    norm(t)
    to_core.wait_recv()
    norm(place.core)
    tick(2)
    tick(3)
    to_chip.wait_recv()
    relay.start()
    g_chip.start()
    g_core.start()
    norm(place.chip)
    tick(4)
    relay.wait_recv()
    norm(place.cross)
    normed_store = pltpu.make_async_copy(normed, normed_out, local.at[6])
    normed_store.start()
    project(0)
    done = 1
    for step in range(5, n):
        tick(step)
        while done < min(step - 1, 2 * (step - 4) + 1):
            project(done)
            done += 1
    g_chip.wait_recv()
    g_relay.start()
    while done < n - 1:
        project(done)
        done += 1
    tick(n)
    project(n - 1)
    for copy in (to_chip, to_core, relay, g_chip, g_core, g_relay):
        copy.wait_send()
    g_core.wait_recv()
    g_relay.wait_recv()
    for small in smalls:
        small.wait_send()
    for lane in lanes:
        lane.finish()
    loads[5].wait()
    for write in writes:
        write.wait()
    normed_store.wait()


def enter(x, g, wq, wk, wv, wo, small, n):
    rows, model = x.shape
    size, width = wq.shape
    big = 3 * width // 2
    kernel = lambda *refs: enter_kernel(n, *refs)
    return pl.pallas_call(
        kernel,
        in_specs=[HBM] * 5 + [VMEM, VMEM],
        out_specs=[HBM, HBM, HBM, HBM, VMEM, VMEM],
        out_shape=[
            jax.ShapeDtypeStruct((4 * rows, model), bf16),
            jax.ShapeDtypeStruct((4, rows, model), bf16),
            jax.ShapeDtypeStruct((n, size, 3 * width), bf16),
            jax.ShapeDtypeStruct((n, size, width), bf16),
            jax.ShapeDtypeStruct((3 * width, 4 * rows), f32),
            jax.ShapeDtypeStruct((n,) + small.shape, bf16),
        ],
        scratch_shapes=[
            pltpu.VMEM((4, rows, model), bf16),
            pltpu.VMEM((4 * rows, model), bf16),
            pltpu.VMEM((n, size, big), bf16),
            pltpu.VMEM((n, size, big), bf16),
            pltpu.VMEM((n, size, width), bf16),
            DMA((n - 1,)),
            DMA((n - 1,)),
            DMA((6, n - 1)),
            DMA((6, n - 1)),
            DMA((6,)),
            DMA((6,)),
            DMA((7,)),
            DMA((4, n)),
        ],
        compiler_params=pltpu.CompilerParams(collective_id=1, has_side_effects=True, vmem_limit_bytes=56 << 20),
        cost_estimate=pl.CostEstimate(flops=6 * width * rows * 4 * model, bytes_accessed=40 << 20, transcendentals=0),
        name="enter",
    )(x, g, wq, wk, wv, wo, small)


def norm_forward(rows):
    center = rows - jnp.mean(rows, axis=-1, keepdims=True)
    rstd = lax.rsqrt(jnp.mean(center * center, axis=-1, keepdims=True) + EPS)
    return center * rstd, rstd


def norm_backward(grad_out, normal, rstd, gain):
    scaled = grad_out * gain
    return rstd * (
        scaled
        - jnp.mean(scaled, axis=-1, keepdims=True)
        - normal * jnp.mean(scaled * normal, axis=-1, keepdims=True)
    )


def local(
    layer_input,
    segments,
    positions,
    first_gain,
    first_shift,
    query_weight,
    key_weight,
    value_weight,
    query_bias,
    key_bias,
    value_bias,
    out_weight,
    second_gain,
    second_shift,
    gate_weight,
    up_weight,
    down_weight,
    out_grad,
):
    ring = Ring()
    n = ring.n
    width = query_weight.shape[1]
    heads = width // HD
    model = layer_input.shape[1]

    bias_key = jnp.pad(key_bias.astype(f32), ((0, 0), (0, HD - ROT))).reshape(-1)
    part = model // n
    per = HD // n
    if ring.ring:
        lanes = 128
        small = jnp.concatenate(
            [first_gain, first_shift, second_gain, second_shift, query_bias.reshape(-1), value_bias.reshape(-1)]
        )
        small = jnp.pad(small.reshape(-1, lanes), ((0, 16 - small.shape[0] // lanes), (0, 0)))
        normed, g_full, qkv, out_t, lin, small = enter(
            layer_input, out_grad, query_weight, key_weight, value_weight, out_weight, small, n
        )
        g_full = g_full.reshape(-1, model)
        qkv = qkv.reshape(model, -1)
        out_t = out_t.reshape(model, -1)
        small = small.reshape(n, -1)[:, : 4 * part + 2 * heads * per]
        gate, marks = ring.gather(gate_weight, after=lin)
        up, marks = ring.gather(up_weight, pieces=2, after=marks[-2])
        down_t, _ = ring.gather(down_weight.T, pieces=2, after=marks[-2])
    else:
        x_full = tensor_gather(layer_input)
        g_full = tensor_gather(out_grad, after=x_full)
        small = jnp.concatenate(
            [first_gain, first_shift, second_gain, second_shift, query_bias.reshape(-1), value_bias.reshape(-1)]
        )
        small = lax.all_gather(small.reshape(1, -1), "dp", axis=0, tiled=True)
        qkv, _ = ring.gather(jnp.concatenate([query_weight, key_weight, value_weight], axis=1))
        out_t, _ = ring.gather(out_weight.T)
        gate, _ = ring.gather(gate_weight)
        up, _ = ring.gather(up_weight)
        down_t, _ = ring.gather(down_weight.T)
    gain_one, shift_one, gain_two, shift_two = (
        small[:, i * part : (i + 1) * part].reshape(model).astype(f32) for i in range(4)
    )
    biases = small[:, 4 * part :].reshape(n, 2, heads, per).transpose(1, 2, 0, 3).reshape(2, width).astype(f32)
    bias_lin = jnp.concatenate([biases[0], bias_key, biases[1]])
    if not ring.ring:
        hat_full, _ = norm_forward(x_full.astype(f32))
        normed = (hat_full * gain_one + shift_one).astype(bf16)
        lin = dot(qkv, normed, ((0,), (1,)))
    lin = lin + bias_lin[:, None]

    freqs = jnp.exp(-(2.0 / ROT) * jnp.arange(HALF).astype(f32) * math.log(10000.0))
    angles = freqs[:, None] * positions.astype(f32)[None, :]
    cosine, sine = jnp.cos(angles), jnp.sin(angles)
    index = jnp.arange(segments.shape[0], dtype=jnp.int32)
    allowed = (index[:, None] <= index[None, :]) & (segments[:, None] == segments[None, :])
    bias = jnp.where(allowed, 0.0, NEG).astype(f32)
    mixed, q_rot, k_rot, v_heads, logs = attend_forward(lin, cosine, sine, bias)
    rows = layer_input.astype(f32)
    attended = rows + tensor_scatter(dot(mixed, out_t, ((1,), (1,))))

    hat_two, rstd_two = norm_forward(attended)
    second = tensor_gather((hat_two * gain_two + shift_two).astype(bf16))
    gate_lin = dot(second, gate, ((1,), (0,)))
    up_lin = dot(second, up, ((1,), (0,)))
    sigma = jax.nn.sigmoid(gate_lin)
    activated = gate_lin * sigma
    hidden = (activated * up_lin).astype(bf16)
    layer_output = (attended + tensor_scatter(dot(hidden, down_t, ((1,), (1,))))).astype(bf16)

    down_grad = dot(g_full, hidden, ((0,), (0,)))
    grad_hidden = dot(g_full, down_t, ((1,), (0,)))
    grad_gate = (grad_hidden * up_lin * sigma * (1.0 + gate_lin * (1.0 - sigma))).astype(bf16)
    grad_up = (grad_hidden * activated).astype(bf16)
    grad_second = tensor_scatter(dot(grad_gate, gate, ((1,), (1,))) + dot(grad_up, up, ((1,), (1,))))
    gate_grad = dot(second, grad_gate, ((0,), (0,)))
    up_grad = dot(second, grad_up, ((0,), (0,)))
    down_sum = ring.scatter(down_grad).T
    gate_sum = ring.scatter(gate_grad)
    up_sum = ring.scatter(up_grad)
    grad_attended = out_grad.astype(f32) + norm_backward(grad_second, hat_two, rstd_two, gain_two)
    residual = tensor_gather(grad_attended.astype(bf16))

    grad_mixed = dot(out_t, residual, ((0,), (1,))).astype(bf16)
    out_grad_t = dot(residual, mixed, ((0,), (0,)))
    out_sum = ring.scatter(out_grad_t).T
    dq, dk, dv, sums = attend_backward(q_rot, k_rot, v_heads, grad_mixed, logs, cosine, sine, bias)
    grad_lin = jnp.concatenate([dq, dk, dv], axis=0)
    qkv_grad = dot(normed, grad_lin, ((0,), (1,)))
    qkv_sum = ring.scatter(qkv_grad, pieces=2)
    grad_first = tensor_scatter(dot(grad_lin, qkv, ((0,), (1,))))
    hat_one, rstd_one = norm_forward(rows)
    input_grad = grad_attended + norm_backward(grad_first, hat_one, rstd_one, gain_one)

    vectors = jnp.stack(
        [
            jnp.sum(grad_first * hat_one, axis=0),
            jnp.sum(grad_first, axis=0),
            jnp.sum(grad_second * hat_two, axis=0),
            jnp.sum(grad_second, axis=0),
        ]
    )
    vectors = sum_all(vectors, ["tensor"])
    sums = sums.reshape(width, 128)[:, :3]
    packed = sum_all(jnp.concatenate([vectors.reshape(-1), sums.reshape(-1)]), ["dp"])
    each = model // (n * lax.axis_size("tensor"))
    at = ring.me * lax.axis_size("tensor") + lax.axis_index("tensor")
    vectors = lax.dynamic_slice(packed[: 4 * model].reshape(4, -1, each), (0, at, 0), (4, 1, each))[:, 0]
    sums = packed[4 * model :].reshape(heads, n, per, 3)
    mine = lax.dynamic_slice(sums, (0, ring.me, 0, 0), (heads, 1, per, 3))[:, 0]
    key_sum = sums[..., 1].reshape(heads, HD)[:, :ROT]

    return (
        layer_output,
        input_grad,
        vectors[0],
        vectors[1],
        qkv_sum[:, :width],
        qkv_sum[:, width : 2 * width],
        qkv_sum[:, 2 * width :],
        mine[..., 0],
        key_sum,
        mine[..., 2],
        out_sum,
        vectors[2],
        vectors[3],
        gate_sum,
        up_sum,
        down_sum,
    )


def solution(mesh):
    both = ("dp", "tensor")
    return jax.shard_map(
        local,
        mesh=mesh,
        in_specs=(
            P(both, None),
            P("dp"),
            P("dp"),
            P("dp"),
            P("dp"),
            P("dp", "tensor"),
            P("dp", "tensor"),
            P("dp", "tensor"),
            P("tensor", "dp"),
            P("tensor", None),
            P("tensor", "dp"),
            P("tensor", "dp"),
            P("dp"),
            P("dp"),
            P("dp", "tensor"),
            P("dp", "tensor"),
            P("tensor", "dp"),
            P(both, None),
        ),
        out_specs=(
            P(both, None),
            P(both, None),
            P(both),
            P(both),
            P("dp", "tensor"),
            P("dp", "tensor"),
            P("dp", "tensor"),
            P("tensor", "dp"),
            P("tensor", None),
            P("tensor", "dp"),
            P("tensor", "dp"),
            P(both),
            P(both),
            P("dp", "tensor"),
            P("dp", "tensor"),
            P("tensor", "dp"),
        ),
        check_vma=False,
    )
```

```python
import math

import jax
import jax.numpy as jnp
from jax import lax
from jax.experimental import pallas as pl
from jax.experimental.pallas import tpu as pltpu
from jax.sharding import PartitionSpec as P

HD = 64
ROT = 16
SEQ = 1024
HALF = ROT // 2
SCALE = HD ** (-0.5)

EPS = 1e-05
NEG = -1e30
QB = 256
f32 = jnp.float32
bf16 = jnp.bfloat16


def barrier(value, after):
    return lax.optimization_barrier((value, after))[0]


class Ring:
    def __init__(self):
        self.n = lax.axis_size("dp")
        self.ring = self.n == 8 and lax.axis_size("tensor") == 4
        order = list(range(0, self.n, 2)) + list(range(self.n - 1, 0, -2))
        self.up = [(order[i], order[(i + 1) % self.n]) for i in range(self.n)]
        self.down = [(b, a) for a, b in self.up]
        me = lax.axis_index("dp")
        self.me = me
        self.pos = jnp.where(me % 2 == 0, me // 2, self.n - 1 - (me - 1) // 2)

    def owner(self, offset):
        p = (self.pos + offset + 2 * self.n) % self.n
        return jnp.where(p < self.n // 2, 2 * p, 2 * (self.n - 1 - p) + 1)

    def gather(self, shard, pieces=1, after=None):
        n = self.n
        rows, cols = shard.shape
        if not self.ring:
            return lax.all_gather(shard, "dp", axis=0, tiled=True), [shard] * n
        if after is not None:
            shard = barrier(shard, after)
        full = jnp.zeros((n, rows, cols), shard.dtype)
        full = lax.dynamic_update_slice(full, shard[None], (self.me, 0, 0))
        size = rows // (2 * pieces)
        lanes = []
        for k in range(2 * pieces):
            lanes.append([k % 2, k * size, shard[k * size : (k + 1) * size]])
        marks = []
        for step in range(1, n):
            for lane in lanes:
                way, base, block = lane
                block = lax.ppermute(block, "dp", self.down if way else self.up)
                lane[2] = block
                whose = self.owner(step if way else -step)
                full = lax.dynamic_update_slice(full, block[None], (whose, base, 0))
            marks.append(lanes[-1][2])
        return full.reshape(n * rows, cols), marks

    def scatter(self, partial, pieces=1, after=None):
        n = self.n
        if not self.ring:
            return lax.psum_scatter(partial.astype(bf16), "dp", scatter_dimension=0, tiled=True).astype(f32)
        cols = partial.shape[1]
        rows = partial.shape[0] // n
        partial = partial.reshape(n, rows, cols)
        size = rows // (2 * pieces)
        done = []
        for k in range(2 * pieces):
            way = k % 2

            def block(step):
                whose = self.owner(1 + step if way else -1 - step)
                return lax.dynamic_slice(partial, (whose, k * size, 0), (1, size, cols))[0].astype(f32)

            moving = block(0)
            for step in range(1, n):
                got = lax.ppermute(moving.astype(bf16), "dp", self.down if way else self.up)
                moving = got.astype(f32) + block(step)
            done.append(moving)
        return jnp.concatenate(done, axis=0)


CORE = [(0, 1), (1, 0), (2, 3), (3, 2)]
CHIP = [(0, 2), (2, 0), (1, 3), (3, 1)]


def tensor_gather(rows, after=None):
    if lax.axis_size("tensor") != 4:
        return lax.all_gather(rows, "tensor", axis=0, tiled=True)
    if after is not None:
        rows = barrier(rows, after)
    t = lax.axis_index("tensor")
    far = lax.ppermute(rows, "tensor", CHIP)
    near = lax.ppermute(rows, "tensor", CORE)
    last = lax.ppermute(far, "tensor", CORE)
    full = jnp.zeros((4,) + rows.shape, rows.dtype)
    for flip, block in ((0, rows), (1, near), (2, far), (3, last)):
        full = lax.dynamic_update_slice(full, block[None], (t ^ flip, 0, 0))
    return full.reshape(4 * rows.shape[0], rows.shape[1])


def tensor_scatter(partial):
    if lax.axis_size("tensor") != 4:
        return lax.psum_scatter(partial.astype(bf16), "tensor", scatter_dimension=0, tiled=True).astype(f32)
    t = lax.axis_index("tensor")
    rows = partial.shape[0] // 4
    blocks = partial.reshape(4, rows, partial.shape[1])

    def block(flip):
        return lax.dynamic_slice(blocks, (t ^ flip, 0, 0), (1,) + blocks.shape[1:])[0]

    other = lax.ppermute(block(3).astype(bf16), "tensor", CORE)
    own = lax.ppermute(block(1).astype(bf16), "tensor", CORE)
    far = lax.ppermute((block(2) + other.astype(f32)).astype(bf16), "tensor", CHIP)
    return block(0) + own.astype(f32) + far.astype(f32)


def sum_all(vector, axes):
    for axis in axes:
        n = lax.axis_size(axis)
        if n & (n - 1):
            vector = lax.psum(vector, axis)
            continue
        step = 1
        while step < n:
            vector = vector + lax.ppermute(vector, axis, [(i, i ^ step) for i in range(n)])
            step *= 2
    return vector


def rotate(rows, cosine, sine, direction):
    first, second = rows[:HALF], rows[HALF:ROT]
    return jnp.concatenate(
        [first * cosine - direction * second * sine, second * cosine + direction * first * sine, rows[ROT:]], axis=0
    )


def dot(a, b, dims):
    return lax.dot_general(a, b, ((dims[0], dims[1]), ((), ())), preferred_element_type=f32)


def forward_kernel(q_ref, k_ref, v_ref, cos_ref, sin_ref, bias_ref, mixed_ref, q_out, k_out, v_out, log_ref):
    seq = q_ref.shape[1]
    cosine, sine = cos_ref[...], sin_ref[...]
    v_all = v_ref[...].astype(bf16)
    v_out[...] = v_all
    parts = []
    for head in range(q_ref.shape[0] // HD):
        rows = slice(head * HD, (head + 1) * HD)
        q = rotate(q_ref[rows, :], cosine, sine, 1.0).astype(bf16)
        k = rotate(k_ref[rows, :], cosine, sine, 1.0).astype(bf16)
        q_out[rows, :] = q
        k_out[rows, :] = k
        keys = k.T
        values = v_all[rows, :]
        q = q * jnp.asarray(SCALE, bf16)
        cols = []
        for start in range(0, seq, QB):
            end = start + QB
            scores = dot(keys[:end], q[:, start:end], ((1,), (0,))) + bias_ref[:end, start:end]
            top = jnp.max(scores, axis=0, keepdims=True)
            expo = jnp.exp(scores - top)
            total = jnp.sum(expo, axis=0, keepdims=True)
            probs = (expo * (1.0 / total)).astype(bf16)
            cols.append(dot(values[:, :end], probs, ((1,), (0,))).astype(bf16))
            log_ref[0, head : head + 1, start:end] = top + jnp.log(total)
        parts.append(jnp.concatenate(cols, axis=1))
    mixed_ref[...] = jnp.concatenate(parts, axis=0).T


def attend_forward(lin, cosine, sine, bias):
    width, seq = lin.shape[0] // 3, lin.shape[1]
    pair = 2 * HD
    count = width // pair
    outs = []
    block = lambda base: pl.BlockSpec((pair, seq), lambda i: (base * count + i, 0))
    whole = lambda shape: pl.BlockSpec(shape, lambda i: (0, 0))
    return pl.pallas_call(
        forward_kernel,
        grid=(count,),
        in_specs=[block(0), block(1), block(2), whole(cosine.shape), whole(sine.shape), whole(bias.shape)],
        out_specs=[
            pl.BlockSpec((seq, pair), lambda i: (0, i)),
            pl.BlockSpec((pair, seq), lambda i: (i, 0)),
            pl.BlockSpec((pair, seq), lambda i: (i, 0)),
            pl.BlockSpec((pair, seq), lambda i: (i, 0)),
            pl.BlockSpec((1, 2, seq), lambda i: (i, 0, 0)),
        ],
        out_shape=[
            jax.ShapeDtypeStruct((seq, width), bf16),
            jax.ShapeDtypeStruct((width, seq), bf16),
            jax.ShapeDtypeStruct((width, seq), bf16),
            jax.ShapeDtypeStruct((width, seq), bf16),
            jax.ShapeDtypeStruct((count, 2, seq), f32),
        ],
        compiler_params=pltpu.CompilerParams(vmem_limit_bytes=48 << 20),
        cost_estimate=pl.CostEstimate(
            flops=4 * width * seq * seq, bytes_accessed=30 << 20, transcendentals=width // HD * seq * seq
        ),
        name="attend_forward",
    )(lin, lin, lin, cosine, sine, bias)


def backward_kernel(q_ref, k_ref, v_ref, d_ref, log_ref, cos_ref, sin_ref, bias_ref, dq_out, dk_out, dv_out, sums_ref, dk_acc, dv_acc):
    seq = q_ref.shape[1]
    cosine, sine = cos_ref[...], sin_ref[...]
    for head in range(q_ref.shape[0] // HD):
        rows = slice(head * HD, (head + 1) * HD)
        q, k, v, d = q_ref[rows, :], k_ref[rows, :], v_ref[rows, :], d_ref[rows, :]
        keys, values = k.T, v.T
        q_small = q * jnp.asarray(SCALE, bf16)
        dk_acc[...] = jnp.zeros_like(dk_acc)
        dv_acc[...] = jnp.zeros_like(dv_acc)
        cols = []
        for start in range(0, seq, QB):
            end = start + QB
            here = slice(start, end)
            scores = dot(keys[:end], q_small[:, here], ((1,), (0,))) + bias_ref[:end, here]
            probs = jnp.exp(scores - log_ref[0, head : head + 1, here])
            grad = dot(values[:end], d[:, here], ((1,), (0,)))
            both = probs * grad
            inner = jnp.sum(both, axis=0, keepdims=True)
            grad = ((both - probs * inner) * SCALE).astype(bf16)
            probs = probs.astype(bf16)
            cols.append(dot(k[:, :end], grad, ((1,), (0,))))
            dk_acc[:, :end] += dot(q[:, here], grad, ((1,), (1,)))
            dv_acc[:, :end] += dot(d[:, here], probs, ((1,), (1,)))
        dq = rotate(jnp.concatenate(cols, axis=1), cosine, sine, -1.0)
        dk = rotate(dk_acc[...], cosine, sine, -1.0)
        dv = dv_acc[...]
        for part, (out, value) in enumerate(((dq_out, dq), (dk_out, dk), (dv_out, dv))):
            out[rows, :] = value.astype(bf16)
            sums_ref[0, rows, part : part + 1] = jnp.sum(value, axis=1, keepdims=True)


def attend_backward(q, k, v, d, logs, cosine, sine, bias):
    width, seq = q.shape
    pair = 2 * HD
    count = width // pair
    block = pl.BlockSpec((pair, seq), lambda i: (i, 0))
    whole = lambda shape: pl.BlockSpec(shape, lambda i: (0, 0))
    return pl.pallas_call(
        backward_kernel,
        grid=(count,),
        in_specs=[block] * 4
        + [pl.BlockSpec((1, 2, seq), lambda i: (i, 0, 0)), whole(cosine.shape), whole(sine.shape), whole(bias.shape)],
        out_specs=[block] * 3 + [pl.BlockSpec((1, pair, 128), lambda i: (i, 0, 0))],
        out_shape=[jax.ShapeDtypeStruct((width, seq), bf16)] * 3 + [jax.ShapeDtypeStruct((count, pair, 128), f32)],
        scratch_shapes=[pltpu.VMEM((HD, seq), f32), pltpu.VMEM((HD, seq), f32)],
        compiler_params=pltpu.CompilerParams(vmem_limit_bytes=48 << 20),
        cost_estimate=pl.CostEstimate(
            flops=10 * width * seq * seq, bytes_accessed=30 << 20, transcendentals=width // HD * seq * seq
        ),
        name="attend_backward",
    )(q, k, v, d, logs, cosine, sine, bias)


MESH = pl.DeviceIdType.MESH
HBM = pl.BlockSpec(memory_space=pl.ANY)
VMEM = pl.BlockSpec(memory_space=pltpu.VMEM)
DMA = pltpu.SemaphoreType.DMA


class Place:
    def __init__(self, n):
        self.n = n
        self.me = lax.axis_index("dp")
        self.t = lax.axis_index("tensor")
        odd = lax.rem(self.me, 2)
        half = lax.div(self.me, 2)
        self.pos = jnp.where(odd == 0, half, n - 1 - half)
        self.up = self.owner(1)
        self.down = self.owner(-1)
        self.core = self.t + 1 - 2 * lax.rem(self.t, 2)
        self.chip = lax.rem(self.t + 2, 4)
        self.cross = lax.rem(self.core + 2, 4)

    def owner(self, offset):
        p = lax.rem(self.pos + (offset + 2 * self.n), self.n)
        return jnp.where(p < self.n // 2, 2 * p, 2 * (self.n - 1 - p) + 1)

    def barrier(self, dp, tensor):
        sem = pltpu.get_barrier_semaphore()
        for there in dp:
            pl.semaphore_signal(sem, inc=1, device_id={"dp": there}, device_id_type=MESH)
        for there in tensor:
            pl.semaphore_signal(sem, inc=1, device_id={"tensor": there}, device_id_type=MESH)
        pl.semaphore_wait(sem, len(dp) + len(tensor))


class Lane:
    def __init__(self, place, full, base, size, way, send, recv):
        self.place, self.full, self.base, self.size, self.way = place, full, base, size, way
        self.send, self.recv = send, recv

    def whose(self, step):
        return self.place.owner(step if self.way else -step)

    def copy(self, step, whose):
        piece = self.full.at[whose, pl.ds(self.base, self.size)]
        return pltpu.make_async_remote_copy(
            src_ref=piece,
            dst_ref=piece,
            send_sem=self.send.at[step - 1],
            recv_sem=self.recv.at[step - 1],
            device_id={"dp": self.place.down if self.way else self.place.up},
            device_id_type=MESH,
        )

    def start(self, step):
        self.copy(step, self.whose(step - 1)).start()

    def arrive(self, step):
        self.copy(step, self.whose(step)).wait_recv()

    def finish(self):
        for step in range(1, self.place.n):
            self.copy(step, self.whose(step - 1)).wait_send()


class Exchange:
    def __init__(self, send, recv):
        self.send, self.recv = send, recv

    def copy(self, number, src, dst, there):
        return pltpu.make_async_remote_copy(
            src_ref=src,
            dst_ref=dst,
            send_sem=self.send.at[number],
            recv_sem=self.recv.at[number],
            device_id={"tensor": there},
            device_id_type=MESH,
        )


def row_norm(value, gain, shift):
    center = value - jnp.mean(value, axis=1, keepdims=True)
    rstd = lax.rsqrt(jnp.mean(center * center, axis=1, keepdims=True) + EPS)
    return center * rstd * gain + shift


def lane_vector(full, first, count):
    pieces = [full[d, r : r + 1, :].astype(f32) for d in range(full.shape[0]) for r in range(first, first + count)]
    return jnp.concatenate(pieces, axis=1)


def enter_kernel(
    n,
    x_ref, g_ref, wq, wk, wv, wo, small_ref,
    normed_out, g_out, qkv_out, out_out, lin, small_full,
    x_full, normed, left, right, outs,
    small_send, small_recv, send, recv, x_send, x_recv, local, stored,
):
    place = Place(n)
    rows = x_ref.shape[0]
    size = wq.shape[0]
    width = wq.shape[1]
    half = width // 2
    me, t = place.me, place.t
    loads = [
        pltpu.make_async_copy(wq, left.at[me, :, pl.ds(0, width)], local.at[0]),
        pltpu.make_async_copy(wk.at[:, pl.ds(0, half)], left.at[me, :, pl.ds(width, half)], local.at[1]),
        pltpu.make_async_copy(wk.at[:, pl.ds(half, half)], right.at[me, :, pl.ds(0, half)], local.at[2]),
        pltpu.make_async_copy(wv, right.at[me, :, pl.ds(half, width)], local.at[3]),
        pltpu.make_async_copy(x_ref, x_full.at[t], local.at[4]),
        pltpu.make_async_copy(g_ref, g_out.at[t], local.at[5]),
    ]
    for load in loads:
        load.start()
    outs[me] = wo[...].T
    small_full[me] = small_ref[...]
    place.barrier([place.owner(k) for k in range(1, n)], [place.core, place.chip])

    smalls = []
    for k in range(1, n):
        smalls.append(
            pltpu.make_async_remote_copy(
                src_ref=small_ref,
                dst_ref=small_full.at[me],
                send_sem=small_send.at[k - 1],
                recv_sem=small_recv.at[k - 1],
                device_id={"dp": place.owner(k)},
                device_id_type=MESH,
            )
        )
        smalls[-1].start()

    swap = Exchange(x_send, x_recv)
    to_chip = swap.copy(0, x_ref, x_full.at[t], place.chip)
    to_core = swap.copy(1, x_ref, x_full.at[t], place.core)
    relay = swap.copy(2, x_full.at[place.chip], x_full.at[place.chip], place.core)
    g_chip = swap.copy(3, g_ref, g_out.at[t], place.chip)
    g_core = swap.copy(4, g_ref, g_out.at[t], place.core)
    g_relay = swap.copy(5, g_out.at[place.chip], g_out.at[place.chip], place.core)
    to_chip.start()
    to_core.start()
    for load in loads[:4]:
        load.wait()
    lanes = []
    for number, (full, base, count, way) in enumerate(
        (
            (left, 0, size // 2, 0),
            (right, 0, size // 2, 1),
            (left, size // 2, size // 2, 0),
            (right, size // 2, size // 2, 1),
            (outs, 0, size // 2, 0),
            (outs, size // 2, size // 2, 1),
        )
    ):
        lanes.append(Lane(place, full, base, count, way, send.at[number], recv.at[number]))

    def store(step):
        whose, other = place.owner(-step), place.owner(step)
        if step == n:
            return []
        return [
            pltpu.make_async_copy(left.at[whose], qkv_out.at[whose, :, pl.ds(0, width + half)], stored.at[0, step]),
            pltpu.make_async_copy(right.at[other], qkv_out.at[other, :, pl.ds(width + half, width + half)], stored.at[1, step]),
            pltpu.make_async_copy(outs.at[whose, pl.ds(0, size // 2)], out_out.at[whose, pl.ds(0, size // 2)], stored.at[2, step]),
            pltpu.make_async_copy(
                outs.at[other, pl.ds(size // 2, size // 2)], out_out.at[other, pl.ds(size // 2, size // 2)], stored.at[3, step]
            ),
        ]

    writes = []

    def tick(step):
        for lane in lanes:
            if step > 1:
                lane.arrive(step - 1)
            if step < n:
                lane.start(step)
        for write in store(step - 1):
            write.start()
            writes.append(write)

    gain = shift = None

    def norm(block):
        @pl.loop(0, rows // 16)
        def _(i):
            here = pl.ds(pl.multiple_of(i * 16, 16), 16)
            there = pl.ds(pl.multiple_of(block * rows + i * 16, 16), 16)
            normed[there, :] = row_norm(x_full[block, here, :].astype(f32), gain, shift).astype(bf16)

    def project(step):
        for full, whose, base in ((left, place.owner(-step), 0), (right, place.owner(step), width + half)):
            xs = normed[:, pl.ds(pl.multiple_of(whose * size, size), size)]
            for j in range(0, width + half, 256):
                part = dot(full[whose, :, j : j + 256].T, xs, ((1,), (1,)))
                where = slice(base + j, base + j + 256)
                if step == 0:
                    lin[where, :] = part
                else:
                    lin[where, :] += part

    tick(1)
    loads[4].wait()
    for small in smalls:
        small.wait_recv()
    count = small_ref.shape[1]
    gain = lane_vector(small_full, 0, size // count)
    shift = lane_vector(small_full, size // count, size // count)
    norm(t)
    to_core.wait_recv()
    norm(place.core)
    tick(2)
    tick(3)
    to_chip.wait_recv()
    relay.start()
    g_chip.start()
    g_core.start()
    norm(place.chip)
    tick(4)
    relay.wait_recv()
    norm(place.cross)
    normed_store = pltpu.make_async_copy(normed, normed_out, local.at[6])
    normed_store.start()
    project(0)
    done = 1
    for step in range(5, n):
        tick(step)
        while done < min(step - 1, 2 * (step - 4) + 1):
            project(done)
            done += 1
    g_chip.wait_recv()
    g_relay.start()
    while done < n - 1:
        project(done)
        done += 1
    tick(n)
    project(n - 1)
    for copy in (to_chip, to_core, relay, g_chip, g_core, g_relay):
        copy.wait_send()
    g_core.wait_recv()
    g_relay.wait_recv()
    for small in smalls:
        small.wait_send()
    for lane in lanes:
        lane.finish()
    loads[5].wait()
    for write in writes:
        write.wait()
    normed_store.wait()


def enter(x, g, wq, wk, wv, wo, small, n):
    rows, model = x.shape
    size, width = wq.shape
    big = 3 * width // 2
    kernel = lambda *refs: enter_kernel(n, *refs)
    return pl.pallas_call(
        kernel,
        in_specs=[HBM] * 5 + [VMEM, VMEM],
        out_specs=[HBM, HBM, HBM, HBM, VMEM, VMEM],
        out_shape=[
            jax.ShapeDtypeStruct((4 * rows, model), bf16),
            jax.ShapeDtypeStruct((4, rows, model), bf16),
            jax.ShapeDtypeStruct((n, size, 3 * width), bf16),
            jax.ShapeDtypeStruct((n, size, width), bf16),
            jax.ShapeDtypeStruct((3 * width, 4 * rows), f32),
            jax.ShapeDtypeStruct((n,) + small.shape, bf16),
        ],
        scratch_shapes=[
            pltpu.VMEM((4, rows, model), bf16),
            pltpu.VMEM((4 * rows, model), bf16),
            pltpu.VMEM((n, size, big), bf16),
            pltpu.VMEM((n, size, big), bf16),
            pltpu.VMEM((n, size, width), bf16),
            DMA((n - 1,)),
            DMA((n - 1,)),
            DMA((6, n - 1)),
            DMA((6, n - 1)),
            DMA((6,)),
            DMA((6,)),
            DMA((7,)),
            DMA((4, n)),
        ],
        compiler_params=pltpu.CompilerParams(collective_id=1, has_side_effects=True, vmem_limit_bytes=56 << 20),
        cost_estimate=pl.CostEstimate(flops=6 * width * rows * 4 * model, bytes_accessed=40 << 20, transcendentals=0),
        name="enter",
    )(x, g, wq, wk, wv, wo, small)

def attend_pair(pair, lin, bias_ref, cosine, sine, mask, q_all, k_all, v_all, logs, flat, mixed):
    width, seq = q_all.shape

    @pl.loop(0, 2)
    def _(j):
        head = pair * 2 + j
        first = pl.multiple_of(head * HD, HD)
        rows = pl.ds(first, HD)

        def load(part):
            at = pl.ds(pl.multiple_of(part * width + first, HD), HD)
            return lin[at, :] + bias_ref[at, :]

        q = rotate(load(0), cosine, sine, 1.0).astype(bf16)
        k = rotate(load(1), cosine, sine, 1.0).astype(bf16)
        values = load(2).astype(bf16)
        q_all[rows, :] = q
        k_all[rows, :] = k
        v_all[rows, :] = values
        keys = k.T
        q = q * jnp.asarray(SCALE, bf16)
        mine = pl.ds(pl.multiple_of(j * HD, HD), HD)
        for start in range(0, seq, QB):
            end = start + QB
            scores = dot(keys[:end], q[:, start:end], ((1,), (0,))) + mask[:end, start:end]
            top = jnp.max(scores, axis=0, keepdims=True)
            expo = jnp.exp(scores - top)
            total = jnp.sum(expo, axis=0, keepdims=True)
            probs = (expo * (1.0 / total)).astype(bf16)
            flat[mine, start:end] = dot(values[:, :end], probs, ((1,), (0,))).astype(bf16)
            logs[pl.ds(head, 1), start:end] = top + jnp.log(total)

    mixed[:, pair * 2 * HD : (pair + 1) * 2 * HD] = flat[...].T


def build_mask(mask, seg_row, seg_col):
    seq = mask.shape[0]

    @pl.loop(0, seq // 32)
    def _(i):
        here = pl.ds(pl.multiple_of(i * 32, 32), 32)
        key = lax.broadcasted_iota(jnp.int32, (32, seq), 0) + i * 32
        query = lax.broadcasted_iota(jnp.int32, (32, seq), 1)
        allowed = (key <= query) & (seg_col[here, :] == seg_row[...])
        mask[here, :] = jnp.where(allowed, 0.0, NEG).astype(f32)


def middle_kernel(
    n,
    lin_ref, bias_ref, cos_ref, sin_ref, seg_row, seg_col, x_ref, out_ref, small, gate_w, up_w, down_w, g_ref,
    q_out, k_out, v_out, logs, mixed_out, att_out, second_out, gate_out, up_out, hidden_out, ffn_out, dgate_out, dup_out,
    gate, up, down, second, near_send, near_recv, far_send, far_recv, attended,
    send, recv, x_send, x_recv, local, stored, staged,
):
    place = Place(n)
    t = place.t
    rows, model = x_ref.shape
    size, cols = gate_w.shape
    seq = 4 * rows
    width = out_ref.shape[1]
    loads = [
        pltpu.make_async_copy(gate_w, gate.at[place.me], local.at[0]),
        pltpu.make_async_copy(up_w, up.at[place.me], local.at[1]),
    ]
    for load in loads:
        load.start()
    down[place.me] = down_w[...].T
    place.barrier([place.up, place.down], [place.core, place.chip])
    for load in loads:
        load.wait()

    half, quarter = size // 2, size // 4
    lanes = [
        [Lane(place, full, half * sub, half, way, send.at[2 * way + sub], recv.at[2 * way + sub]) for way, full in ((0, gate), (1, up))]
        for sub in range(2)
    ]
    downs = [
        [
            Lane(place, down, half * way + quarter * sub, quarter, way, send.at[4 + 2 * way + sub], recv.at[4 + 2 * way + sub])
            for way in range(2)
        ]
        for sub in range(2)
    ]

    def write(step):
        gated, upped = place.owner(-step), place.owner(step)
        return [
            pltpu.make_async_copy(gate.at[gated], gate_out.at[gated], stored.at[0, step]),
            pltpu.make_async_copy(up.at[upped], up_out.at[upped], stored.at[1, step]),
        ]

    def tick(kind, step, sub):
        for lane in (downs if kind else lanes)[sub]:
            if step > 1:
                lane.arrive(step - 1)
            if step < n:
                lane.start(step)
        if sub == 1 and not kind:
            for copy in write(step - 1):
                copy.start()

    plan = [(0, step, sub) for step in range(1, n) for sub in range(2)]
    plan += [(1, 1, 0), (1, 1, 1), (0, n, 0), (0, n, 1)]
    plan += [(1, step, sub) for step in range(2, n + 1) for sub in range(2)]
    plan = iter(plan)

    def advance(count=1):
        for _ in range(count):
            tick(*next(plan))

    swap = Exchange(x_send, x_recv)
    near = [swap.copy(i, near_send.at[i], near_recv.at[i], place.core) for i in range(2)]
    far = swap.copy(2, far_send, far_recv, place.chip)
    to_chip = swap.copy(3, second.at[t], second.at[t], place.chip)
    to_core = swap.copy(4, second.at[t], second.at[t], place.core)
    relay = swap.copy(5, second.at[place.chip], second.at[place.chip], place.core)
    copies = near + [far, to_chip, to_core, relay]

    advance(2)

    def attention(lin, mask, q_all, k_all, v_all, flat, mixed, out_t):
        pairs = width // (2 * HD)
        fetch = []
        for part in range(3):
            for pair in range(pairs):
                at = pl.ds(part * width + pair * 2 * HD, 2 * HD)
                fetch.append(pltpu.make_async_copy(lin_ref.at[at], lin.at[at], local.at[2 + part * pairs + pair]))
        for pair in range(pairs):
            for part in range(3):
                fetch[part * pairs + pair].start()
        weights = pltpu.make_async_copy(out_ref, out_t, local.at[2 + 3 * pairs])
        weights.start()
        build_mask(mask, seg_row, seg_col)
        cosine, sine = cos_ref[...], sin_ref[...]
        for pair in range(pairs):
            for part in range(3):
                fetch[part * pairs + pair].wait()
            attend_pair(pair, lin, bias_ref, cosine, sine, mask, q_all, k_all, v_all, logs, flat, mixed)
            advance()
        keep = [
            pltpu.make_async_copy(src, dst, local.at[3 + 3 * pairs + i])
            for i, (src, dst) in enumerate(((q_all, q_out), (k_all, k_out), (v_all, v_out), (mixed, mixed_out)))
        ]
        for copy in keep:
            copy.start()
        weights.wait()

        def project(block, j):
            at = pl.ds(pl.multiple_of(block * rows, rows), rows)
            return dot(mixed[at, :], out_t[j : j + 512, :], ((1,), (1,)))

        for i, block in enumerate((place.cross, place.core)):
            for j in range(0, model, 512):
                near_send[i, :, j : j + 512] = project(block, j).astype(bf16)
            near[i].start()
        near[0].wait_recv()
        for j in range(0, model, 512):
            tile = slice(j, j + 512)
            far_send[:, tile] = (project(place.chip, j) + near_recv[0, :, tile].astype(f32)).astype(bf16)
        far.start()
        own = pltpu.make_async_copy(x_ref, far_copy, local.at[7 + 3 * pairs])
        own.start()
        advance()
        near[1].wait_recv()
        own.wait()
        for j in range(0, model, 512):
            tile = slice(j, j + 512)
            attended[:, tile] = far_copy[:, tile].astype(f32) + project(t, j) + near_recv[1, :, tile].astype(f32)
        for copy in keep:
            copy.wait()

    far_copy = second.at[t]
    pl.run_scoped(
        attention,
        pltpu.VMEM((3 * width, seq), f32),
        pltpu.VMEM((seq, seq), f32),
        pltpu.VMEM((width, seq), bf16),
        pltpu.VMEM((width, seq), bf16),
        pltpu.VMEM((width, seq), bf16),
        pltpu.VMEM((2 * HD, seq), bf16),
        pltpu.VMEM((seq, width), bf16),
        pltpu.VMEM((model, width), bf16),
    )
    last = 7 + 3 * (width // (2 * HD))

    def feed(gate_lin, up_lin, grad, hidden, g, stage):
        g_load = pltpu.make_async_copy(g_ref, g, local.at[last + 1])
        g_load.start()
        gate_lin[...] = jnp.zeros_like(gate_lin)
        up_lin[...] = jnp.zeros_like(up_lin)
        grad[...] = jnp.zeros_like(grad)
        count = small.shape[2]
        gain = lane_vector(small, 2 * size // count, size // count)
        shift = lane_vector(small, 3 * size // count, size // count)
        advance(2)
        far.wait_recv()

        @pl.loop(0, rows // 16)
        def _(i):
            here = pl.ds(pl.multiple_of(i * 16, 16), 16)
            value = attended[here, :] + far_recv[here, :].astype(f32)
            attended[here, :] = value
            second[t, here, :] = row_norm(value, gain, shift).astype(bf16)

        to_chip.start()
        to_core.start()
        att_store = pltpu.make_async_copy(attended, att_out, local.at[last + 2])
        att_store.start()

        def add(block, low, high):
            @pl.loop(low, high)
            def _(step):
                for full, total, whose in ((gate, gate_lin, place.owner(-step)), (up, up_lin, place.owner(step))):
                    xs = second[block, :, pl.ds(pl.multiple_of(whose * size, size), size)]
                    total[block] += dot(xs, full[whose], ((1,), (0,)))

        advance()
        ready = 5
        add(t, 0, ready)
        to_core.wait_recv()
        advance()
        add(place.core, 0, ready)
        advance()
        to_chip.wait_recv()
        relay.start()
        add(place.chip, 0, ready)
        relay.wait_recv()
        second_store = pltpu.make_async_copy(second, second_out, local.at[last + 3])
        second_store.start()
        advance()
        add(place.cross, 0, ready)
        every = lambda low, high: pl.loop(0, 4)(lambda block: add(block, low, high))
        every(ready, n - 2)
        advance(2)
        advance()
        every(n - 2, n - 1)
        advance(2)
        every(n - 1, n)

        @pl.loop(0, 4 * rows // 16)
        def _(i):
            block = lax.div(i, rows // 16)
            here = pl.ds(pl.multiple_of(lax.rem(i, rows // 16) * 16, 16), 16)
            value = gate_lin[block, here, :]
            hidden[block, here, :] = (value * jax.nn.sigmoid(value) * up_lin[block, here, :]).astype(bf16)

        hidden_store = pltpu.make_async_copy(hidden, hidden_out, local.at[last + 4])
        hidden_store.start()
        g_load.wait()
        stages = []

        def use(whose):
            number = len(stages)
            slot = number % 2
            if number >= 2:
                stages[number - 2].wait()
            at = pl.ds(pl.multiple_of(whose * size, size), size)

            @pl.loop(0, 4)
            def _(block):
                grad[block] += dot(g[block, :, at], down[whose], ((1,), (0,)))
                stage[slot, block] = dot(hidden[block], down[whose], ((1,), (1,))).astype(bf16)

            stages.append(pltpu.make_async_copy(stage.at[slot], ffn_out.at[:, :, at], staged.at[number]))
            stages[-1].start()

        use(place.me)
        for step in range(2, n + 1):
            advance(2)
            if step - 1 == n // 2:
                use(place.owner(n // 2))
            elif step - 1 > n // 2:
                use(place.owner(step - 1))
                use(place.owner(1 - step))
        for lane in lanes[0] + lanes[1] + downs[0] + downs[1]:
            lane.finish()
        for step in range(n):
            for copy in write(step):
                copy.wait()

        @pl.loop(0, 4 * rows // 16)
        def _(i):
            block = lax.div(i, rows // 16)
            here = pl.ds(pl.multiple_of(lax.rem(i, rows // 16) * 16, 16), 16)
            value = gate_lin[block, here, :]
            sigma = jax.nn.sigmoid(value)
            incoming = grad[block, here, :]
            gate[block, here, :] = (incoming * up_lin[block, here, :] * sigma * (1.0 + value * (1.0 - sigma))).astype(bf16)
            gate[4 + block, here, :] = (incoming * (value * sigma)).astype(bf16)

        final = [
            pltpu.make_async_copy(gate.at[pl.ds(0, 4)], dgate_out, local.at[last + 5]),
            pltpu.make_async_copy(gate.at[pl.ds(4, 4)], dup_out, local.at[last + 6]),
        ]
        for copy in final:
            copy.start()
        for copy in final + stages[-2:] + [hidden_store, second_store, att_store]:
            copy.wait()

    pl.run_scoped(
        feed,
        pltpu.VMEM((4, rows, cols), f32),
        pltpu.VMEM((4, rows, cols), f32),
        pltpu.VMEM((4, rows, cols), f32),
        pltpu.VMEM((4, rows, cols), bf16),
        pltpu.VMEM((4, rows, model), bf16),
        pltpu.VMEM((2, 4, rows, size), bf16),
    )
    for copy in copies:
        copy.wait_send()


def middle(lin, bias, cosine, sine, segments, x, out_t, small, gate, up, down, g, n):
    rows, model = x.shape
    size, cols = gate.shape
    seq = 4 * rows
    width = out_t.shape[1]
    heads = width // HD
    shape = jax.ShapeDtypeStruct
    return pl.pallas_call(
        lambda *refs: middle_kernel(n, *refs),
        in_specs=[HBM] + [VMEM] * 5 + [HBM, HBM, VMEM, HBM, HBM, VMEM, HBM],
        out_specs=[HBM, HBM, HBM, VMEM] + [HBM] * 9,
        out_shape=[
            shape((width, seq), bf16),
            shape((width, seq), bf16),
            shape((width, seq), bf16),
            shape((heads, seq), f32),
            shape((seq, width), bf16),
            shape((rows, model), f32),
            shape((4, rows, model), bf16),
            shape((n, size, cols), bf16),
            shape((n, size, cols), bf16),
            shape((4, rows, cols), bf16),
            shape((4, rows, model), bf16),
            shape((4, rows, cols), bf16),
            shape((4, rows, cols), bf16),
        ],
        scratch_shapes=[
            pltpu.VMEM((n, size, cols), bf16),
            pltpu.VMEM((n, size, cols), bf16),
            pltpu.VMEM((n, size, cols), bf16),
            pltpu.VMEM((4, rows, model), bf16),
            pltpu.VMEM((2, rows, model), bf16),
            pltpu.VMEM((2, rows, model), bf16),
            pltpu.VMEM((rows, model), bf16),
            pltpu.VMEM((rows, model), bf16),
            pltpu.VMEM((rows, model), f32),
            DMA((8, n - 1)),
            DMA((8, n - 1)),
            DMA((6,)),
            DMA((6,)),
            DMA((14 + 3 * width // (2 * HD),)),
            DMA((2, n)),
            DMA((n,)),
        ],
        compiler_params=pltpu.CompilerParams(collective_id=2, has_side_effects=True, vmem_limit_bytes=62 << 20),
        cost_estimate=pl.CostEstimate(
            flops=10 * seq * model * cols, bytes_accessed=60 << 20, transcendentals=heads * seq * seq
        ),
        name="middle",
    )(
        lin, bias[:, None], cosine, sine, segments[None, :], segments[:, None],
        x, out_t, small, gate, up, down, g.reshape(4, rows, model),
    )


def norm_forward(rows):
    center = rows - jnp.mean(rows, axis=-1, keepdims=True)
    rstd = lax.rsqrt(jnp.mean(center * center, axis=-1, keepdims=True) + EPS)
    return center * rstd, rstd


def norm_backward(grad_out, normal, rstd, gain):
    scaled = grad_out * gain
    return rstd * (
        scaled
        - jnp.mean(scaled, axis=-1, keepdims=True)
        - normal * jnp.mean(scaled * normal, axis=-1, keepdims=True)
    )


def local(
    layer_input,
    segments,
    positions,
    first_gain,
    first_shift,
    query_weight,
    key_weight,
    value_weight,
    query_bias,
    key_bias,
    value_bias,
    out_weight,
    second_gain,
    second_shift,
    gate_weight,
    up_weight,
    down_weight,
    out_grad,
):
    ring = Ring()
    n = ring.n
    width = query_weight.shape[1]
    heads = width // HD
    model = layer_input.shape[1]

    bias_key = jnp.pad(key_bias.astype(f32), ((0, 0), (0, HD - ROT))).reshape(-1)
    part = model // n
    per = HD // n
    if ring.ring:
        lanes = 128
        small = jnp.concatenate(
            [first_gain, first_shift, second_gain, second_shift, query_bias.reshape(-1), value_bias.reshape(-1)]
        )
        small = jnp.pad(small.reshape(-1, lanes), ((0, 16 - small.shape[0] // lanes), (0, 0)))
        normed, g_full, qkv, out_t, lin, small = enter(
            layer_input, out_grad, query_weight, key_weight, value_weight, out_weight, small, n
        )
        g_full = g_full.reshape(-1, model)
        qkv = qkv.reshape(model, -1)
        out_t = out_t.reshape(model, -1)
        packed_small = small
        small = small.reshape(n, -1)[:, : 4 * part + 2 * heads * per]
    else:
        x_full = tensor_gather(layer_input)
        g_full = tensor_gather(out_grad, after=x_full)
        small = jnp.concatenate(
            [first_gain, first_shift, second_gain, second_shift, query_bias.reshape(-1), value_bias.reshape(-1)]
        )
        small = lax.all_gather(small.reshape(1, -1), "dp", axis=0, tiled=True)
        qkv, _ = ring.gather(jnp.concatenate([query_weight, key_weight, value_weight], axis=1))
        out_t, _ = ring.gather(out_weight.T)
        gate, _ = ring.gather(gate_weight)
        up, _ = ring.gather(up_weight)
        down_t, _ = ring.gather(down_weight.T)
    gain_one, shift_one, gain_two, shift_two = (
        small[:, i * part : (i + 1) * part].reshape(model).astype(f32) for i in range(4)
    )
    biases = small[:, 4 * part :].reshape(n, 2, heads, per).transpose(1, 2, 0, 3).reshape(2, width).astype(f32)
    bias_lin = jnp.concatenate([biases[0], bias_key, biases[1]])
    if not ring.ring:
        hat_full, _ = norm_forward(x_full.astype(f32))
        normed = (hat_full * gain_one + shift_one).astype(bf16)
        lin = dot(qkv, normed, ((0,), (1,)))

    freqs = jnp.exp(-(2.0 / ROT) * jnp.arange(HALF).astype(f32) * math.log(10000.0))
    angles = freqs[:, None] * positions.astype(f32)[None, :]
    cosine, sine = jnp.cos(angles), jnp.sin(angles)
    index = jnp.arange(segments.shape[0], dtype=jnp.int32)
    allowed = (index[:, None] <= index[None, :]) & (segments[:, None] == segments[None, :])
    bias = jnp.where(allowed, 0.0, NEG).astype(f32)
    rows = layer_input.astype(f32)
    if ring.ring:
        q_rot, k_rot, v_heads, logs, mixed, attended, second, gate, up, hidden, ffn, grad_gate, grad_up = middle(
            lin, bias_lin, cosine, sine, segments, layer_input, out_t, packed_small, gate_weight, up_weight, down_weight, g_full, n
        )
        logs = logs.reshape(-1, 2, logs.shape[1])
        second, gate, up = second.reshape(-1, model), gate.reshape(model, -1), up.reshape(model, -1)
        hidden, ffn = hidden.reshape(second.shape[0], -1), ffn.reshape(-1, model)
        grad_gate, grad_up = grad_gate.reshape(hidden.shape), grad_up.reshape(hidden.shape)
        hat_two, rstd_two = norm_forward(attended)
    else:
        mixed, q_rot, k_rot, v_heads, logs = attend_forward(lin + bias_lin[:, None], cosine, sine, bias)
        attended = rows + tensor_scatter(dot(mixed, out_t, ((1,), (1,))))

        hat_two, rstd_two = norm_forward(attended)
        second = tensor_gather((hat_two * gain_two + shift_two).astype(bf16))
        gate_lin = dot(second, gate, ((1,), (0,)))
        up_lin = dot(second, up, ((1,), (0,)))
        sigma = jax.nn.sigmoid(gate_lin)
        activated = gate_lin * sigma
        hidden = (activated * up_lin).astype(bf16)
        ffn = dot(hidden, down_t, ((1,), (1,)))
        grad_hidden = dot(g_full, down_t, ((1,), (0,)))
        grad_gate = (grad_hidden * up_lin * sigma * (1.0 + gate_lin * (1.0 - sigma))).astype(bf16)
        grad_up = (grad_hidden * activated).astype(bf16)
    layer_output = (attended + tensor_scatter(ffn.astype(f32))).astype(bf16)

    down_grad = dot(g_full, hidden, ((0,), (0,)))
    grad_second = tensor_scatter(dot(grad_gate, gate, ((1,), (1,))) + dot(grad_up, up, ((1,), (1,))))
    gate_grad = dot(second, grad_gate, ((0,), (0,)))
    up_grad = dot(second, grad_up, ((0,), (0,)))
    down_sum = ring.scatter(down_grad).T
    gate_sum = ring.scatter(gate_grad)
    up_sum = ring.scatter(up_grad)
    grad_attended = out_grad.astype(f32) + norm_backward(grad_second, hat_two, rstd_two, gain_two)
    residual = tensor_gather(grad_attended.astype(bf16))

    grad_mixed = dot(out_t, residual, ((0,), (1,))).astype(bf16)
    out_grad_t = dot(residual, mixed, ((0,), (0,)))
    out_sum = ring.scatter(out_grad_t).T
    dq, dk, dv, sums = attend_backward(q_rot, k_rot, v_heads, grad_mixed, logs, cosine, sine, bias)
    grad_lin = jnp.concatenate([dq, dk, dv], axis=0)
    qkv_grad = dot(normed, grad_lin, ((0,), (1,)))
    qkv_sum = ring.scatter(qkv_grad, pieces=2)
    grad_first = tensor_scatter(dot(grad_lin, qkv, ((0,), (1,))))
    hat_one, rstd_one = norm_forward(rows)
    input_grad = grad_attended + norm_backward(grad_first, hat_one, rstd_one, gain_one)

    vectors = jnp.stack(
        [
            jnp.sum(grad_first * hat_one, axis=0),
            jnp.sum(grad_first, axis=0),
            jnp.sum(grad_second * hat_two, axis=0),
            jnp.sum(grad_second, axis=0),
        ]
    )
    vectors = sum_all(vectors, ["tensor"])
    sums = sums.reshape(width, 128)[:, :3]
    packed = sum_all(jnp.concatenate([vectors.reshape(-1), sums.reshape(-1)]), ["dp"])
    each = model // (n * lax.axis_size("tensor"))
    at = ring.me * lax.axis_size("tensor") + lax.axis_index("tensor")
    vectors = lax.dynamic_slice(packed[: 4 * model].reshape(4, -1, each), (0, at, 0), (4, 1, each))[:, 0]
    sums = packed[4 * model :].reshape(heads, n, per, 3)
    mine = lax.dynamic_slice(sums, (0, ring.me, 0, 0), (heads, 1, per, 3))[:, 0]
    key_sum = sums[..., 1].reshape(heads, HD)[:, :ROT]

    return (
        layer_output,
        input_grad,
        vectors[0],
        vectors[1],
        qkv_sum[:, :width],
        qkv_sum[:, width : 2 * width],
        qkv_sum[:, 2 * width :],
        mine[..., 0],
        key_sum,
        mine[..., 2],
        out_sum,
        vectors[2],
        vectors[3],
        gate_sum,
        up_sum,
        down_sum,
    )


def solution(mesh):
    both = ("dp", "tensor")
    return jax.shard_map(
        local,
        mesh=mesh,
        in_specs=(
            P(both, None),
            P("dp"),
            P("dp"),
            P("dp"),
            P("dp"),
            P("dp", "tensor"),
            P("dp", "tensor"),
            P("dp", "tensor"),
            P("tensor", "dp"),
            P("tensor", None),
            P("tensor", "dp"),
            P("tensor", "dp"),
            P("dp"),
            P("dp"),
            P("dp", "tensor"),
            P("dp", "tensor"),
            P("tensor", "dp"),
            P(both, None),
        ),
        out_specs=(
            P(both, None),
            P(both, None),
            P(both),
            P(both),
            P("dp", "tensor"),
            P("dp", "tensor"),
            P("dp", "tensor"),
            P("tensor", "dp"),
            P("tensor", None),
            P("tensor", "dp"),
            P("tensor", "dp"),
            P(both),
            P(both),
            P("dp", "tensor"),
            P("dp", "tensor"),
            P("tensor", "dp"),
        ),
        check_vma=False,
    )
```

```python
import math

import jax
import jax.numpy as jnp
from jax import lax
from jax.experimental import pallas as pl
from jax.experimental.pallas import tpu as pltpu
from jax.sharding import PartitionSpec as P

HD = 64
ROT = 16
SEQ = 1024
HALF = ROT // 2
SCALE = HD ** (-0.5)

EPS = 1e-05
NEG = -1e30
QB = 256
f32 = jnp.float32
bf16 = jnp.bfloat16


def barrier(value, after):
    return lax.optimization_barrier((value, after))[0]


class Ring:
    def __init__(self):
        self.n = lax.axis_size("dp")
        self.ring = self.n == 8 and lax.axis_size("tensor") == 4
        order = list(range(0, self.n, 2)) + list(range(self.n - 1, 0, -2))
        self.up = [(order[i], order[(i + 1) % self.n]) for i in range(self.n)]
        self.down = [(b, a) for a, b in self.up]
        me = lax.axis_index("dp")
        self.me = me
        self.pos = jnp.where(me % 2 == 0, me // 2, self.n - 1 - (me - 1) // 2)

    def owner(self, offset):
        p = (self.pos + offset + 2 * self.n) % self.n
        return jnp.where(p < self.n // 2, 2 * p, 2 * (self.n - 1 - p) + 1)

    def gather(self, shard, pieces=1, after=None):
        n = self.n
        rows, cols = shard.shape
        if not self.ring:
            return lax.all_gather(shard, "dp", axis=0, tiled=True), [shard] * n
        if after is not None:
            shard = barrier(shard, after)
        full = jnp.zeros((n, rows, cols), shard.dtype)
        full = lax.dynamic_update_slice(full, shard[None], (self.me, 0, 0))
        size = rows // (2 * pieces)
        lanes = []
        for k in range(2 * pieces):
            lanes.append([k % 2, k * size, shard[k * size : (k + 1) * size]])
        marks = []
        for step in range(1, n):
            for lane in lanes:
                way, base, block = lane
                block = lax.ppermute(block, "dp", self.down if way else self.up)
                lane[2] = block
                whose = self.owner(step if way else -step)
                full = lax.dynamic_update_slice(full, block[None], (whose, base, 0))
            marks.append(lanes[-1][2])
        return full.reshape(n * rows, cols), marks

    def scatter(self, partial, pieces=1, after=None):
        n = self.n
        if not self.ring:
            return lax.psum_scatter(partial.astype(bf16), "dp", scatter_dimension=0, tiled=True).astype(f32)
        cols = partial.shape[1]
        rows = partial.shape[0] // n
        partial = partial.reshape(n, rows, cols)
        size = rows // (2 * pieces)
        done = []
        for k in range(2 * pieces):
            way = k % 2

            def block(step):
                whose = self.owner(1 + step if way else -1 - step)
                return lax.dynamic_slice(partial, (whose, k * size, 0), (1, size, cols))[0].astype(f32)

            moving = block(0)
            for step in range(1, n):
                got = lax.ppermute(moving.astype(bf16), "dp", self.down if way else self.up)
                moving = got.astype(f32) + block(step)
            done.append(moving)
        return jnp.concatenate(done, axis=0)


CORE = [(0, 1), (1, 0), (2, 3), (3, 2)]
CHIP = [(0, 2), (2, 0), (1, 3), (3, 1)]


def tensor_gather(rows, after=None):
    if lax.axis_size("tensor") != 4:
        return lax.all_gather(rows, "tensor", axis=0, tiled=True)
    if after is not None:
        rows = barrier(rows, after)
    t = lax.axis_index("tensor")
    far = lax.ppermute(rows, "tensor", CHIP)
    near = lax.ppermute(rows, "tensor", CORE)
    last = lax.ppermute(far, "tensor", CORE)
    full = jnp.zeros((4,) + rows.shape, rows.dtype)
    for flip, block in ((0, rows), (1, near), (2, far), (3, last)):
        full = lax.dynamic_update_slice(full, block[None], (t ^ flip, 0, 0))
    return full.reshape(4 * rows.shape[0], rows.shape[1])


def tensor_scatter(partial):
    if lax.axis_size("tensor") != 4:
        return lax.psum_scatter(partial.astype(bf16), "tensor", scatter_dimension=0, tiled=True).astype(f32)
    t = lax.axis_index("tensor")
    rows = partial.shape[0] // 4
    blocks = partial.reshape(4, rows, partial.shape[1])

    def block(flip):
        return lax.dynamic_slice(blocks, (t ^ flip, 0, 0), (1,) + blocks.shape[1:])[0]

    other = lax.ppermute(block(3).astype(bf16), "tensor", CORE)
    own = lax.ppermute(block(1).astype(bf16), "tensor", CORE)
    far = lax.ppermute((block(2) + other.astype(f32)).astype(bf16), "tensor", CHIP)
    return block(0) + own.astype(f32) + far.astype(f32)


def sum_all(vector, axes):
    for axis in axes:
        n = lax.axis_size(axis)
        if n & (n - 1):
            vector = lax.psum(vector, axis)
            continue
        step = 1
        while step < n:
            vector = vector + lax.ppermute(vector, axis, [(i, i ^ step) for i in range(n)])
            step *= 2
    return vector


def rotate(rows, cosine, sine, direction):
    first, second = rows[:HALF], rows[HALF:ROT]
    return jnp.concatenate(
        [first * cosine - direction * second * sine, second * cosine + direction * first * sine, rows[ROT:]], axis=0
    )


def dot(a, b, dims):
    return lax.dot_general(a, b, ((dims[0], dims[1]), ((), ())), preferred_element_type=f32)


def forward_kernel(q_ref, k_ref, v_ref, cos_ref, sin_ref, bias_ref, mixed_ref, q_out, k_out, v_out, log_ref):
    seq = q_ref.shape[1]
    cosine, sine = cos_ref[...], sin_ref[...]
    v_all = v_ref[...].astype(bf16)
    v_out[...] = v_all
    parts = []
    for head in range(q_ref.shape[0] // HD):
        rows = slice(head * HD, (head + 1) * HD)
        q = rotate(q_ref[rows, :], cosine, sine, 1.0).astype(bf16)
        k = rotate(k_ref[rows, :], cosine, sine, 1.0).astype(bf16)
        q_out[rows, :] = q
        k_out[rows, :] = k
        keys = k.T
        values = v_all[rows, :]
        q = q * jnp.asarray(SCALE, bf16)
        cols = []
        for start in range(0, seq, QB):
            end = start + QB
            scores = dot(keys[:end], q[:, start:end], ((1,), (0,))) + bias_ref[:end, start:end]
            top = jnp.max(scores, axis=0, keepdims=True)
            expo = jnp.exp(scores - top)
            total = jnp.sum(expo, axis=0, keepdims=True)
            probs = (expo * (1.0 / total)).astype(bf16)
            cols.append(dot(values[:, :end], probs, ((1,), (0,))).astype(bf16))
            log_ref[0, head : head + 1, start:end] = top + jnp.log(total)
        parts.append(jnp.concatenate(cols, axis=1))
    mixed_ref[...] = jnp.concatenate(parts, axis=0).T


def attend_forward(lin, cosine, sine, bias):
    width, seq = lin.shape[0] // 3, lin.shape[1]
    pair = 2 * HD
    count = width // pair
    outs = []
    block = lambda base: pl.BlockSpec((pair, seq), lambda i: (base * count + i, 0))
    whole = lambda shape: pl.BlockSpec(shape, lambda i: (0, 0))
    return pl.pallas_call(
        forward_kernel,
        grid=(count,),
        in_specs=[block(0), block(1), block(2), whole(cosine.shape), whole(sine.shape), whole(bias.shape)],
        out_specs=[
            pl.BlockSpec((seq, pair), lambda i: (0, i)),
            pl.BlockSpec((pair, seq), lambda i: (i, 0)),
            pl.BlockSpec((pair, seq), lambda i: (i, 0)),
            pl.BlockSpec((pair, seq), lambda i: (i, 0)),
            pl.BlockSpec((1, 2, seq), lambda i: (i, 0, 0)),
        ],
        out_shape=[
            jax.ShapeDtypeStruct((seq, width), bf16),
            jax.ShapeDtypeStruct((width, seq), bf16),
            jax.ShapeDtypeStruct((width, seq), bf16),
            jax.ShapeDtypeStruct((width, seq), bf16),
            jax.ShapeDtypeStruct((count, 2, seq), f32),
        ],
        compiler_params=pltpu.CompilerParams(vmem_limit_bytes=48 << 20),
        cost_estimate=pl.CostEstimate(
            flops=4 * width * seq * seq, bytes_accessed=30 << 20, transcendentals=width // HD * seq * seq
        ),
        name="attend_forward",
    )(lin, lin, lin, cosine, sine, bias)


def backward_kernel(q_ref, k_ref, v_ref, d_ref, log_ref, cos_ref, sin_ref, bias_ref, dq_out, dk_out, dv_out, sums_ref, dk_acc, dv_acc):
    seq = q_ref.shape[1]
    cosine, sine = cos_ref[...], sin_ref[...]
    for head in range(q_ref.shape[0] // HD):
        rows = slice(head * HD, (head + 1) * HD)
        q, k, v, d = q_ref[rows, :], k_ref[rows, :], v_ref[rows, :], d_ref[rows, :]
        keys, values = k.T, v.T
        q_small = q * jnp.asarray(SCALE, bf16)
        dk_acc[...] = jnp.zeros_like(dk_acc)
        dv_acc[...] = jnp.zeros_like(dv_acc)
        cols = []
        for start in range(0, seq, QB):
            end = start + QB
            here = slice(start, end)
            scores = dot(keys[:end], q_small[:, here], ((1,), (0,))) + bias_ref[:end, here]
            probs = jnp.exp(scores - log_ref[0, head : head + 1, here])
            grad = dot(values[:end], d[:, here], ((1,), (0,)))
            both = probs * grad
            inner = jnp.sum(both, axis=0, keepdims=True)
            grad = ((both - probs * inner) * SCALE).astype(bf16)
            probs = probs.astype(bf16)
            cols.append(dot(k[:, :end], grad, ((1,), (0,))))
            dk_acc[:, :end] += dot(q[:, here], grad, ((1,), (1,)))
            dv_acc[:, :end] += dot(d[:, here], probs, ((1,), (1,)))
        dq = rotate(jnp.concatenate(cols, axis=1), cosine, sine, -1.0)
        dk = rotate(dk_acc[...], cosine, sine, -1.0)
        dv = dv_acc[...]
        for part, (out, value) in enumerate(((dq_out, dq), (dk_out, dk), (dv_out, dv))):
            out[rows, :] = value.astype(bf16)
            sums_ref[0, rows, part : part + 1] = jnp.sum(value, axis=1, keepdims=True)


def attend_backward(q, k, v, d, logs, cosine, sine, bias):
    width, seq = q.shape
    pair = 2 * HD
    count = width // pair
    block = pl.BlockSpec((pair, seq), lambda i: (i, 0))
    whole = lambda shape: pl.BlockSpec(shape, lambda i: (0, 0))
    return pl.pallas_call(
        backward_kernel,
        grid=(count,),
        in_specs=[block] * 4
        + [pl.BlockSpec((1, 2, seq), lambda i: (i, 0, 0)), whole(cosine.shape), whole(sine.shape), whole(bias.shape)],
        out_specs=[block] * 3 + [pl.BlockSpec((1, pair, 128), lambda i: (i, 0, 0))],
        out_shape=[jax.ShapeDtypeStruct((width, seq), bf16)] * 3 + [jax.ShapeDtypeStruct((count, pair, 128), f32)],
        scratch_shapes=[pltpu.VMEM((HD, seq), f32), pltpu.VMEM((HD, seq), f32)],
        compiler_params=pltpu.CompilerParams(vmem_limit_bytes=48 << 20),
        cost_estimate=pl.CostEstimate(
            flops=10 * width * seq * seq, bytes_accessed=30 << 20, transcendentals=width // HD * seq * seq
        ),
        name="attend_backward",
    )(q, k, v, d, logs, cosine, sine, bias)


MESH = pl.DeviceIdType.MESH
HBM = pl.BlockSpec(memory_space=pl.ANY)
VMEM = pl.BlockSpec(memory_space=pltpu.VMEM)
DMA = pltpu.SemaphoreType.DMA


class Place:
    def __init__(self, n):
        self.n = n
        self.me = lax.axis_index("dp")
        self.t = lax.axis_index("tensor")
        odd = lax.rem(self.me, 2)
        half = lax.div(self.me, 2)
        self.pos = jnp.where(odd == 0, half, n - 1 - half)
        self.up = self.owner(1)
        self.down = self.owner(-1)
        self.core = self.t + 1 - 2 * lax.rem(self.t, 2)
        self.chip = lax.rem(self.t + 2, 4)
        self.cross = lax.rem(self.core + 2, 4)

    def owner(self, offset):
        p = lax.rem(self.pos + (offset + 2 * self.n), self.n)
        return jnp.where(p < self.n // 2, 2 * p, 2 * (self.n - 1 - p) + 1)

    def barrier(self, dp, tensor):
        sem = pltpu.get_barrier_semaphore()
        for there in dp:
            pl.semaphore_signal(sem, inc=1, device_id={"dp": there}, device_id_type=MESH)
        for there in tensor:
            pl.semaphore_signal(sem, inc=1, device_id={"tensor": there}, device_id_type=MESH)
        pl.semaphore_wait(sem, len(dp) + len(tensor))


class Lane:
    def __init__(self, place, full, base, size, way, send, recv):
        self.place, self.full, self.base, self.size, self.way = place, full, base, size, way
        self.send, self.recv = send, recv

    def whose(self, step):
        return self.place.owner(step if self.way else -step)

    def copy(self, step, whose):
        piece = self.full.at[whose, pl.ds(self.base, self.size)]
        return pltpu.make_async_remote_copy(
            src_ref=piece,
            dst_ref=piece,
            send_sem=self.send.at[step - 1],
            recv_sem=self.recv.at[step - 1],
            device_id={"dp": self.place.down if self.way else self.place.up},
            device_id_type=MESH,
        )

    def start(self, step):
        self.copy(step, self.whose(step - 1)).start()

    def arrive(self, step):
        self.copy(step, self.whose(step)).wait_recv()

    def finish(self):
        for step in range(1, self.place.n):
            self.copy(step, self.whose(step - 1)).wait_send()


class Exchange:
    def __init__(self, send, recv):
        self.send, self.recv = send, recv

    def copy(self, number, src, dst, there):
        return pltpu.make_async_remote_copy(
            src_ref=src,
            dst_ref=dst,
            send_sem=self.send.at[number],
            recv_sem=self.recv.at[number],
            device_id={"tensor": there},
            device_id_type=MESH,
        )


def row_norm(value, gain, shift):
    center = value - jnp.mean(value, axis=1, keepdims=True)
    rstd = lax.rsqrt(jnp.mean(center * center, axis=1, keepdims=True) + EPS)
    return center * rstd * gain + shift


def lane_vector(full, first, count):
    pieces = [full[d, r : r + 1, :].astype(f32) for d in range(full.shape[0]) for r in range(first, first + count)]
    return jnp.concatenate(pieces, axis=1)


def enter_kernel(
    n,
    x_ref, g_ref, wq, wk, wv, wo, small_ref,
    normed_out, g_out, qkv_out, out_out, lin, small_full,
    x_full, normed, left, right, outs,
    small_send, small_recv, send, recv, x_send, x_recv, local, stored,
):
    place = Place(n)
    rows = x_ref.shape[0]
    size = wq.shape[0]
    width = wq.shape[1]
    half = width // 2
    me, t = place.me, place.t
    loads = [
        pltpu.make_async_copy(wq, left.at[me, :, pl.ds(0, width)], local.at[0]),
        pltpu.make_async_copy(wk.at[:, pl.ds(0, half)], left.at[me, :, pl.ds(width, half)], local.at[1]),
        pltpu.make_async_copy(wk.at[:, pl.ds(half, half)], right.at[me, :, pl.ds(0, half)], local.at[2]),
        pltpu.make_async_copy(wv, right.at[me, :, pl.ds(half, width)], local.at[3]),
        pltpu.make_async_copy(x_ref, x_full.at[t], local.at[4]),
        pltpu.make_async_copy(g_ref, g_out.at[t], local.at[5]),
    ]
    for load in loads:
        load.start()
    outs[me] = wo[...].T
    small_full[me] = small_ref[...]
    place.barrier([place.owner(k) for k in range(1, n)], [place.core, place.chip])

    smalls = []
    for k in range(1, n):
        smalls.append(
            pltpu.make_async_remote_copy(
                src_ref=small_ref,
                dst_ref=small_full.at[me],
                send_sem=small_send.at[k - 1],
                recv_sem=small_recv.at[k - 1],
                device_id={"dp": place.owner(k)},
                device_id_type=MESH,
            )
        )
        smalls[-1].start()

    swap = Exchange(x_send, x_recv)
    to_chip = swap.copy(0, x_ref, x_full.at[t], place.chip)
    to_core = swap.copy(1, x_ref, x_full.at[t], place.core)
    relay = swap.copy(2, x_full.at[place.chip], x_full.at[place.chip], place.core)
    g_chip = swap.copy(3, g_ref, g_out.at[t], place.chip)
    g_core = swap.copy(4, g_ref, g_out.at[t], place.core)
    g_relay = swap.copy(5, g_out.at[place.chip], g_out.at[place.chip], place.core)
    to_chip.start()
    to_core.start()
    for load in loads[:4]:
        load.wait()
    lanes = []
    for number, (full, base, count, way) in enumerate(
        (
            (left, 0, size // 2, 0),
            (right, 0, size // 2, 1),
            (left, size // 2, size // 2, 0),
            (right, size // 2, size // 2, 1),
            (outs, 0, size // 2, 0),
            (outs, size // 2, size // 2, 1),
        )
    ):
        lanes.append(Lane(place, full, base, count, way, send.at[number], recv.at[number]))

    def store(step):
        whose, other = place.owner(-step), place.owner(step)
        if step == n:
            return []
        return [
            pltpu.make_async_copy(left.at[whose], qkv_out.at[whose, :, pl.ds(0, width + half)], stored.at[0, step]),
            pltpu.make_async_copy(right.at[other], qkv_out.at[other, :, pl.ds(width + half, width + half)], stored.at[1, step]),
            pltpu.make_async_copy(outs.at[whose, pl.ds(0, size // 2)], out_out.at[whose, pl.ds(0, size // 2)], stored.at[2, step]),
            pltpu.make_async_copy(
                outs.at[other, pl.ds(size // 2, size // 2)], out_out.at[other, pl.ds(size // 2, size // 2)], stored.at[3, step]
            ),
        ]

    writes = []

    def tick(step):
        for lane in lanes:
            if step > 1:
                lane.arrive(step - 1)
            if step < n:
                lane.start(step)
        for write in store(step - 1):
            write.start()
            writes.append(write)

    gain = shift = None

    def norm(block):
        @pl.loop(0, rows // 16)
        def _(i):
            here = pl.ds(pl.multiple_of(i * 16, 16), 16)
            there = pl.ds(pl.multiple_of(block * rows + i * 16, 16), 16)
            normed[there, :] = row_norm(x_full[block, here, :].astype(f32), gain, shift).astype(bf16)

    def project(step):
        for full, whose, base in ((left, place.owner(-step), 0), (right, place.owner(step), width + half)):
            xs = normed[:, pl.ds(pl.multiple_of(whose * size, size), size)]
            for j in range(0, width + half, 256):
                part = dot(full[whose, :, j : j + 256].T, xs, ((1,), (1,)))
                where = slice(base + j, base + j + 256)
                if step == 0:
                    lin[where, :] = part
                else:
                    lin[where, :] += part

    tick(1)
    loads[4].wait()
    for small in smalls:
        small.wait_recv()
    count = small_ref.shape[1]
    gain = lane_vector(small_full, 0, size // count)
    shift = lane_vector(small_full, size // count, size // count)
    norm(t)
    to_core.wait_recv()
    norm(place.core)
    tick(2)
    tick(3)
    to_chip.wait_recv()
    relay.start()
    g_chip.start()
    g_core.start()
    norm(place.chip)
    tick(4)
    relay.wait_recv()
    norm(place.cross)
    normed_store = pltpu.make_async_copy(normed, normed_out, local.at[6])
    normed_store.start()
    project(0)
    done = 1
    for step in range(5, n):
        tick(step)
        while done < min(step - 1, 2 * (step - 4) + 1):
            project(done)
            done += 1
    g_chip.wait_recv()
    g_relay.start()
    while done < n - 1:
        project(done)
        done += 1
    tick(n)
    project(n - 1)
    for copy in (to_chip, to_core, relay, g_chip, g_core, g_relay):
        copy.wait_send()
    g_core.wait_recv()
    g_relay.wait_recv()
    for small in smalls:
        small.wait_send()
    for lane in lanes:
        lane.finish()
    loads[5].wait()
    for write in writes:
        write.wait()
    normed_store.wait()


def enter(x, g, wq, wk, wv, wo, small, n):
    rows, model = x.shape
    size, width = wq.shape
    big = 3 * width // 2
    kernel = lambda *refs: enter_kernel(n, *refs)
    return pl.pallas_call(
        kernel,
        in_specs=[HBM] * 5 + [VMEM, VMEM],
        out_specs=[HBM, HBM, HBM, HBM, VMEM, VMEM],
        out_shape=[
            jax.ShapeDtypeStruct((4 * rows, model), bf16),
            jax.ShapeDtypeStruct((4, rows, model), bf16),
            jax.ShapeDtypeStruct((n, size, 3 * width), bf16),
            jax.ShapeDtypeStruct((n, size, width), bf16),
            jax.ShapeDtypeStruct((3 * width, 4 * rows), f32),
            jax.ShapeDtypeStruct((n,) + small.shape, bf16),
        ],
        scratch_shapes=[
            pltpu.VMEM((4, rows, model), bf16),
            pltpu.VMEM((4 * rows, model), bf16),
            pltpu.VMEM((n, size, big), bf16),
            pltpu.VMEM((n, size, big), bf16),
            pltpu.VMEM((n, size, width), bf16),
            DMA((n - 1,)),
            DMA((n - 1,)),
            DMA((6, n - 1)),
            DMA((6, n - 1)),
            DMA((6,)),
            DMA((6,)),
            DMA((7,)),
            DMA((4, n)),
        ],
        compiler_params=pltpu.CompilerParams(collective_id=1, has_side_effects=True, vmem_limit_bytes=56 << 20),
        cost_estimate=pl.CostEstimate(flops=6 * width * rows * 4 * model, bytes_accessed=40 << 20, transcendentals=0),
        name="enter",
    )(x, g, wq, wk, wv, wo, small)

def attend_pair(pair, lin, bias_ref, cosine, sine, mask, q_all, k_all, v_all, logs, flat, mixed):
    width, seq = q_all.shape

    @pl.loop(0, 2)
    def _(j):
        head = pair * 2 + j
        first = pl.multiple_of(head * HD, HD)
        rows = pl.ds(first, HD)

        def load(part):
            at = pl.ds(pl.multiple_of(part * width + first, HD), HD)
            return lin[at, :] + bias_ref[at, :]

        q = rotate(load(0), cosine, sine, 1.0).astype(bf16)
        k = rotate(load(1), cosine, sine, 1.0).astype(bf16)
        values = load(2).astype(bf16)
        q_all[rows, :] = q
        k_all[rows, :] = k
        v_all[rows, :] = values
        keys = k.T
        q = q * jnp.asarray(SCALE, bf16)
        mine = pl.ds(pl.multiple_of(j * HD, HD), HD)
        for start in range(0, seq, QB):
            end = start + QB
            scores = dot(keys[:end], q[:, start:end], ((1,), (0,))) + mask[:end, start:end]
            top = jnp.max(scores, axis=0, keepdims=True)
            expo = jnp.exp(scores - top)
            total = jnp.sum(expo, axis=0, keepdims=True)
            probs = (expo * (1.0 / total)).astype(bf16)
            flat[mine, start:end] = dot(values[:, :end], probs, ((1,), (0,))).astype(bf16)
            logs[pl.ds(head, 1), start:end] = top + jnp.log(total)

    mixed[:, pair * 2 * HD : (pair + 1) * 2 * HD] = flat[...].T


def build_mask(mask, seg_row, seg_col):
    seq = mask.shape[0]

    @pl.loop(0, seq // 32)
    def _(i):
        here = pl.ds(pl.multiple_of(i * 32, 32), 32)
        key = lax.broadcasted_iota(jnp.int32, (32, seq), 0) + i * 32
        query = lax.broadcasted_iota(jnp.int32, (32, seq), 1)
        allowed = (key <= query) & (seg_col[here, :] == seg_row[...])
        mask[here, :] = jnp.where(allowed, 0.0, NEG).astype(f32)


def middle_kernel(
    n,
    lin_ref, bias_ref, cos_ref, sin_ref, seg_row, seg_col, x_ref, out_ref, small, gate_w, up_w, down_w, g_ref,
    q_out, k_out, v_out, logs, mixed_out, att_out, second_out, gate_out, up_out, hidden_out, ffn_out, dgate_out, dup_out,
    gate, up, down, second, near_send, near_recv, far_send, far_recv, attended,
    send, recv, x_send, x_recv, local, stored, staged,
):
    place = Place(n)
    t = place.t
    rows, model = x_ref.shape
    size, cols = gate_w.shape
    seq = 4 * rows
    width = out_ref.shape[1]
    loads = [
        pltpu.make_async_copy(gate_w, gate.at[place.me], local.at[0]),
        pltpu.make_async_copy(up_w, up.at[place.me], local.at[1]),
    ]
    for load in loads:
        load.start()
    down[place.me] = down_w[...].T
    place.barrier([place.up, place.down], [place.core, place.chip])
    for load in loads:
        load.wait()

    half, quarter = size // 2, size // 4
    lanes = [
        [Lane(place, full, half * sub, half, way, send.at[2 * way + sub], recv.at[2 * way + sub]) for way, full in ((0, gate), (1, up))]
        for sub in range(2)
    ]
    downs = [
        [
            Lane(place, down, half * way + quarter * sub, quarter, way, send.at[4 + 2 * way + sub], recv.at[4 + 2 * way + sub])
            for way in range(2)
        ]
        for sub in range(2)
    ]

    def write(step):
        gated, upped = place.owner(-step), place.owner(step)
        return [
            pltpu.make_async_copy(gate.at[gated], gate_out.at[gated], stored.at[0, step]),
            pltpu.make_async_copy(up.at[upped], up_out.at[upped], stored.at[1, step]),
        ]

    def tick(kind, step, sub):
        for lane in (downs if kind else lanes)[sub]:
            if step > 1:
                lane.arrive(step - 1)
            if step < n:
                lane.start(step)
        if sub == 1 and not kind:
            for copy in write(step - 1):
                copy.start()

    plan = [(0, step, sub) for step in range(1, n) for sub in range(2)]
    plan += [(1, 1, 0), (1, 1, 1), (0, n, 0), (0, n, 1)]
    plan += [(1, step, sub) for step in range(2, n + 1) for sub in range(2)]
    plan = iter(plan)

    def advance(count=1):
        for _ in range(count):
            tick(*next(plan))

    swap = Exchange(x_send, x_recv)
    near = [swap.copy(i, near_send.at[i], near_recv.at[i], place.core) for i in range(2)]
    far = swap.copy(2, far_send, far_recv, place.chip)
    to_chip = swap.copy(3, second.at[t], second.at[t], place.chip)
    to_core = swap.copy(4, second.at[t], second.at[t], place.core)
    relay = swap.copy(5, second.at[place.chip], second.at[place.chip], place.core)
    copies = near + [far, to_chip, to_core, relay]

    advance(2)

    def attention(lin, mask, q_all, k_all, v_all, flat, mixed, out_t):
        pairs = width // (2 * HD)
        fetch = []
        for part in range(3):
            for pair in range(pairs):
                at = pl.ds(part * width + pair * 2 * HD, 2 * HD)
                fetch.append(pltpu.make_async_copy(lin_ref.at[at], lin.at[at], local.at[2 + part * pairs + pair]))
        for pair in range(pairs):
            for part in range(3):
                fetch[part * pairs + pair].start()
        weights = pltpu.make_async_copy(out_ref, out_t, local.at[2 + 3 * pairs])
        weights.start()
        build_mask(mask, seg_row, seg_col)
        cosine, sine = cos_ref[...], sin_ref[...]
        for pair in range(pairs):
            for part in range(3):
                fetch[part * pairs + pair].wait()
            attend_pair(pair, lin, bias_ref, cosine, sine, mask, q_all, k_all, v_all, logs, flat, mixed)
            advance()
        keep = [
            pltpu.make_async_copy(src, dst, local.at[3 + 3 * pairs + i])
            for i, (src, dst) in enumerate(((q_all, q_out), (k_all, k_out), (v_all, v_out), (mixed, mixed_out)))
        ]
        for copy in keep:
            copy.start()
        weights.wait()

        def project(block, j):
            at = pl.ds(pl.multiple_of(block * rows, rows), rows)
            return dot(mixed[at, :], out_t[j : j + 512, :], ((1,), (1,)))

        for i, block in enumerate((place.cross, place.core)):
            for j in range(0, model, 512):
                near_send[i, :, j : j + 512] = project(block, j).astype(bf16)
            near[i].start()
        near[0].wait_recv()
        for j in range(0, model, 512):
            tile = slice(j, j + 512)
            far_send[:, tile] = (project(place.chip, j) + near_recv[0, :, tile].astype(f32)).astype(bf16)
        far.start()
        own = pltpu.make_async_copy(x_ref, far_copy, local.at[7 + 3 * pairs])
        own.start()
        advance()
        near[1].wait_recv()
        own.wait()
        for j in range(0, model, 512):
            tile = slice(j, j + 512)
            attended[:, tile] = far_copy[:, tile].astype(f32) + project(t, j) + near_recv[1, :, tile].astype(f32)
        for copy in keep:
            copy.wait()

    far_copy = second.at[t]
    pl.run_scoped(
        attention,
        pltpu.VMEM((3 * width, seq), f32),
        pltpu.VMEM((seq, seq), f32),
        pltpu.VMEM((width, seq), bf16),
        pltpu.VMEM((width, seq), bf16),
        pltpu.VMEM((width, seq), bf16),
        pltpu.VMEM((2 * HD, seq), bf16),
        pltpu.VMEM((seq, width), bf16),
        pltpu.VMEM((model, width), bf16),
    )
    last = 7 + 3 * (width // (2 * HD))

    def feed(gate_lin, up_lin, grad, hidden, g, stage):
        g_load = pltpu.make_async_copy(g_ref, g, local.at[last + 1])
        g_load.start()
        gate_lin[...] = jnp.zeros_like(gate_lin)
        up_lin[...] = jnp.zeros_like(up_lin)
        grad[...] = jnp.zeros_like(grad)
        count = small.shape[2]
        gain = lane_vector(small, 2 * size // count, size // count)
        shift = lane_vector(small, 3 * size // count, size // count)
        advance(2)
        far.wait_recv()

        @pl.loop(0, rows // 16)
        def _(i):
            here = pl.ds(pl.multiple_of(i * 16, 16), 16)
            value = attended[here, :] + far_recv[here, :].astype(f32)
            attended[here, :] = value
            second[t, here, :] = row_norm(value, gain, shift).astype(bf16)

        to_chip.start()
        to_core.start()
        att_store = pltpu.make_async_copy(attended, att_out, local.at[last + 2])
        att_store.start()

        def add(block, low, high):
            @pl.loop(low, high)
            def _(step):
                for full, total, whose in ((gate, gate_lin, place.owner(-step)), (up, up_lin, place.owner(step))):
                    xs = second[block, :, pl.ds(pl.multiple_of(whose * size, size), size)]
                    total[block] += dot(xs, full[whose], ((1,), (0,)))

        advance()
        ready = 5
        add(t, 0, ready)
        to_core.wait_recv()
        advance()
        add(place.core, 0, ready)
        advance()
        to_chip.wait_recv()
        relay.start()
        add(place.chip, 0, ready)
        relay.wait_recv()
        second_store = pltpu.make_async_copy(second, second_out, local.at[last + 3])
        second_store.start()
        advance()
        add(place.cross, 0, ready)
        every = lambda low, high: pl.loop(0, 4)(lambda block: add(block, low, high))
        every(ready, n - 2)
        advance(2)
        advance()
        every(n - 2, n - 1)
        advance(2)
        every(n - 1, n)

        @pl.loop(0, 4 * rows // 16)
        def _(i):
            block = lax.div(i, rows // 16)
            here = pl.ds(pl.multiple_of(lax.rem(i, rows // 16) * 16, 16), 16)
            value = gate_lin[block, here, :]
            hidden[block, here, :] = (value * jax.nn.sigmoid(value) * up_lin[block, here, :]).astype(bf16)

        hidden_store = pltpu.make_async_copy(hidden, hidden_out, local.at[last + 4])
        hidden_store.start()
        g_load.wait()
        stages = []

        def use(whose):
            number = len(stages)
            slot = number % 2
            if number >= 2:
                stages[number - 2].wait()
            at = pl.ds(pl.multiple_of(whose * size, size), size)

            @pl.loop(0, 4)
            def _(block):
                grad[block] += dot(g[block, :, at], down[whose], ((1,), (0,)))
                stage[slot, block] = dot(hidden[block], down[whose], ((1,), (1,))).astype(bf16)

            stages.append(pltpu.make_async_copy(stage.at[slot], ffn_out.at[:, :, at], staged.at[number]))
            stages[-1].start()

        use(place.me)
        for step in range(2, n + 1):
            advance(2)
            if step - 1 == n // 2:
                use(place.owner(n // 2))
            elif step - 1 > n // 2:
                use(place.owner(step - 1))
                use(place.owner(1 - step))
        for lane in lanes[0] + lanes[1] + downs[0] + downs[1]:
            lane.finish()
        for step in range(n):
            for copy in write(step):
                copy.wait()

        @pl.loop(0, 4 * rows // 16)
        def _(i):
            block = lax.div(i, rows // 16)
            here = pl.ds(pl.multiple_of(lax.rem(i, rows // 16) * 16, 16), 16)
            value = gate_lin[block, here, :]
            sigma = jax.nn.sigmoid(value)
            incoming = grad[block, here, :]
            gate[block, here, :] = (incoming * up_lin[block, here, :] * sigma * (1.0 + value * (1.0 - sigma))).astype(bf16)
            gate[4 + block, here, :] = (incoming * (value * sigma)).astype(bf16)

        final = [
            pltpu.make_async_copy(gate.at[pl.ds(0, 4)], dgate_out, local.at[last + 5]),
            pltpu.make_async_copy(gate.at[pl.ds(4, 4)], dup_out, local.at[last + 6]),
        ]
        for copy in final:
            copy.start()
        for copy in final + stages[-2:] + [hidden_store, second_store, att_store]:
            copy.wait()

    pl.run_scoped(
        feed,
        pltpu.VMEM((4, rows, cols), f32),
        pltpu.VMEM((4, rows, cols), f32),
        pltpu.VMEM((4, rows, cols), f32),
        pltpu.VMEM((4, rows, cols), bf16),
        pltpu.VMEM((4, rows, model), bf16),
        pltpu.VMEM((2, 4, rows, size), bf16),
    )
    for copy in copies:
        copy.wait_send()


def middle(lin, bias, cosine, sine, segments, x, out_t, small, gate, up, down, g, n):
    rows, model = x.shape
    size, cols = gate.shape
    seq = 4 * rows
    width = out_t.shape[1]
    heads = width // HD
    shape = jax.ShapeDtypeStruct
    return pl.pallas_call(
        lambda *refs: middle_kernel(n, *refs),
        in_specs=[HBM] + [VMEM] * 5 + [HBM, HBM, VMEM, HBM, HBM, VMEM, HBM],
        out_specs=[HBM, HBM, HBM, VMEM] + [HBM] * 9,
        out_shape=[
            shape((width, seq), bf16),
            shape((width, seq), bf16),
            shape((width, seq), bf16),
            shape((heads, seq), f32),
            shape((seq, width), bf16),
            shape((rows, model), f32),
            shape((4, rows, model), bf16),
            shape((n, size, cols), bf16),
            shape((n, size, cols), bf16),
            shape((4, rows, cols), bf16),
            shape((4, rows, model), bf16),
            shape((4, rows, cols), bf16),
            shape((4, rows, cols), bf16),
        ],
        scratch_shapes=[
            pltpu.VMEM((n, size, cols), bf16),
            pltpu.VMEM((n, size, cols), bf16),
            pltpu.VMEM((n, size, cols), bf16),
            pltpu.VMEM((4, rows, model), bf16),
            pltpu.VMEM((2, rows, model), bf16),
            pltpu.VMEM((2, rows, model), bf16),
            pltpu.VMEM((rows, model), bf16),
            pltpu.VMEM((rows, model), bf16),
            pltpu.VMEM((rows, model), f32),
            DMA((8, n - 1)),
            DMA((8, n - 1)),
            DMA((6,)),
            DMA((6,)),
            DMA((14 + 3 * width // (2 * HD),)),
            DMA((2, n)),
            DMA((n,)),
        ],
        compiler_params=pltpu.CompilerParams(collective_id=2, has_side_effects=True, vmem_limit_bytes=62 << 20),
        cost_estimate=pl.CostEstimate(
            flops=10 * seq * model * cols, bytes_accessed=60 << 20, transcendentals=heads * seq * seq
        ),
        name="middle",
    )(
        lin, bias[:, None], cosine, sine, segments[None, :], segments[:, None],
        x, out_t, small, gate, up, down, g.reshape(4, rows, model),
    )

class Sum:
    def __init__(self, place, slots, way, send, recv):
        self.place, self.slots, self.way, self.send, self.recv = place, slots, way, send, recv

    def whose(self, step):
        return self.place.owner(1 + step if self.way else -1 - step)

    def copy(self, step):
        return pltpu.make_async_remote_copy(
            src_ref=self.slots.at[step - 1],
            dst_ref=self.slots.at[step],
            send_sem=self.send.at[step - 1],
            recv_sem=self.recv.at[step - 1],
            device_id={"dp": self.place.down if self.way else self.place.up},
            device_id_type=MESH,
        )

    def tick(self, step, left, right, final):
        if step > 0:
            self.copy(step).wait_recv()
        cols = self.slots.shape[2]
        for low in range(0, cols, 512):
            tile = slice(low, min(low + 512, cols))
            part = dot(left, right(tile), ((1,), (0,)))
            if step > 0:
                part = part + self.slots[step, :, tile].astype(f32)
            if step == self.place.n - 1:
                final(tile, part)
            else:
                self.slots[step, :, tile] = part.astype(bf16)
        if step < self.place.n - 1:
            self.copy(step + 1).start()

    def finish(self):
        for step in range(1, self.place.n):
            self.copy(step).wait_send()


def columns_of(left, whose, size, way):
    half = size // 2
    return left[:, pl.ds(pl.multiple_of(whose * size + way * half, half), half)].T


def retreat_pair(pair, q_all, k_all, v_all, d_all, logs, cosine, sine, mask, dk_acc, dv_acc, tmp, vec):
    width, seq = q_all.shape

    @pl.loop(0, 2)
    def _(j):
        head = pair * 2 + j
        rows = pl.ds(pl.multiple_of(head * HD, HD), HD)
        q, k, v, d = q_all[rows, :], k_all[rows, :], v_all[rows, :], d_all[rows, :]
        keys, values = k.T, v.T
        q_small = q * jnp.asarray(SCALE, bf16)
        dk_acc[...] = jnp.zeros_like(dk_acc)
        dv_acc[...] = jnp.zeros_like(dv_acc)
        cols = []
        for start in range(0, seq, QB):
            end = start + QB
            here = slice(start, end)
            scores = dot(keys[:end], q_small[:, here], ((1,), (0,))) + mask[:end, here]
            probs = jnp.exp(scores - logs[pl.ds(head, 1), here])
            grad = dot(values[:end], d[:, here], ((1,), (0,)))
            both = probs * grad
            inner = jnp.sum(both, axis=0, keepdims=True)
            grad = ((both - probs * inner) * SCALE).astype(bf16)
            probs = probs.astype(bf16)
            cols.append(dot(k[:, :end], grad, ((1,), (0,))))
            dk_acc[:, :end] += dot(q[:, here], grad, ((1,), (1,)))
            dv_acc[:, :end] += dot(d[:, here], probs, ((1,), (1,)))
        dq = rotate(jnp.concatenate(cols, axis=1), cosine, sine, -1.0)
        dk = rotate(dk_acc[...], cosine, sine, -1.0)
        dv = dv_acc[...]
        mine = pl.ds(pl.multiple_of(j * HD, HD), HD)
        for part, (out, value) in enumerate(((q_all, dq), (k_all, dk), (v_all, dv))):
            out[rows, :] = value.astype(bf16)
            lanes = value[:, :128]
            for i in range(128, seq, 128):
                lanes = lanes + value[:, i : i + 128]
            tmp[part, mine, :] = lanes

    for part in range(3):
        at = part * width + pair * 2 * HD
        vec[4:5, at : at + 2 * HD] = jnp.sum(tmp[part].T, axis=0, keepdims=True)


def back_kernel(
    n,
    dgate_ref, dup_ref, hidden_ref, second_ref, g_ref, gate_ref, up_ref, att_ref, small, out_ref,
    q_ref, k_ref, v_ref, logs, cos_ref, sin_ref, seg_row, seg_col,
    down_sum, gate_sum, up_sum, datt_out, resid_out, dlin_out, vec,
    slots, g, second, hidden, dgate, dup, near_send, near_recv, far_send, far_recv, datt, acc,
    send, recv, x_send, x_recv, local,
):
    place = Place(n)
    t = place.t
    rows, model = att_ref.shape
    size, cols = gate_ref.shape[1:]
    seq, width = 4 * rows, out_ref.shape[1]
    loads = [
        pltpu.make_async_copy(src, dst, local.at[i])
        for i, (src, dst) in enumerate(
            ((g_ref, g), (hidden_ref, hidden), (second_ref, second), (dgate_ref, dgate), (dup_ref, dup))
        )
    ]
    for load in loads:
        load.start()
    place.barrier([place.up, place.down], [place.core, place.chip])

    lanes = [[Sum(place, slots.at[2 * i + way], way, send.at[2 * i + way], recv.at[2 * i + way]) for way in range(2)] for i in range(3)]
    sources = ((g, hidden), (second, dgate), (second, dup))
    sums = (down_sum, gate_sum, up_sum)

    def stored(i):
        return pltpu.make_async_copy(datt.at[:, pl.ds(0, cols)], sums[i], local.at[6 + i])

    def tick(step, i):
        left, right = sources[i]
        if step == n - 1:
            (stored(i - 1) if i else datt_copy()).wait()
        for lane in lanes[i]:

            def final(tile, total):
                datt[lane.way * size // 2 : (lane.way + 1) * size // 2, tile] = total

            lane.tick(step, columns_of(left, lane.whose(step), size, lane.way), lambda tile: right[:, tile], final)
        if step == n - 1:
            stored(i).start()

    plan = iter([(step, i) for step in range(n) for i in range(3)])

    def advance(count=1):
        for _ in range(count):
            tick(*next(plan))

    def datt_copy():
        return pltpu.make_async_copy(datt, datt_out, local.at[9])

    swap = Exchange(x_send, x_recv)
    near = [swap.copy(i, near_send.at[i], near_recv.at[i], place.core) for i in range(2)]
    far = swap.copy(2, far_send, far_recv, place.chip)
    to_chip = swap.copy(3, far_send, resid_out.at[t], place.chip)
    to_core = swap.copy(4, far_send, resid_out.at[t], place.core)
    relay = swap.copy(5, resid_out.at[place.chip], resid_out.at[place.chip], place.core)
    keep = pltpu.make_async_copy(far_send, resid_out.at[t], local.at[10])
    own = pl.ds(pl.multiple_of(t * rows, rows), rows)

    def feed(gate, up):
        weights = [
            pltpu.make_async_copy(gate_ref, gate, local.at[11]),
            pltpu.make_async_copy(up_ref, up, local.at[12]),
        ]
        for copy in weights:
            copy.start()
        loads[0].wait()
        loads[1].wait()
        advance()
        loads[2].wait()
        loads[3].wait()
        advance()
        loads[4].wait()
        advance()
        for copy in weights:
            copy.wait()

        def product(block, j):
            at = pl.ds(pl.multiple_of(block * rows, rows), rows)
            return dot(dgate[at, :], gate[j], ((1,), (1,))) + dot(dup[at, :], up[j], ((1,), (1,)))

        for i, block in enumerate((place.cross, place.core)):
            for j in range(n):
                near_send[i, :, j * size : (j + 1) * size] = product(block, j).astype(bf16)
            near[i].start()
            advance()
        near[0].wait_recv()
        for j in range(n):
            tile = slice(j * size, (j + 1) * size)
            far_send[:, tile] = (product(place.chip, j) + near_recv[0, :, tile].astype(f32)).astype(bf16)
        far.start()
        advance()
        near[1].wait_recv()
        for j in range(n):
            tile = slice(j * size, (j + 1) * size)
            datt[:, tile] = product(t, j) + near_recv[1, :, tile].astype(f32)
        advance()

    pl.run_scoped(feed, pltpu.VMEM((n, size, cols), bf16), pltpu.VMEM((n, size, cols), bf16))

    def attention(attended, mask, q_all, k_all, v_all, d_all, out_t, dk_acc, dv_acc, tmp):
        load_attended = pltpu.make_async_copy(att_ref, attended, local.at[5])
        load_attended.start()
        fetch = [
            pltpu.make_async_copy(src, dst, local.at[13 + i])
            for i, (src, dst) in enumerate(((out_ref, out_t), (q_ref, q_all), (k_ref, k_all), (v_ref, v_all)))
        ]
        for copy in fetch:
            copy.start()
        build_mask(mask, seg_row, seg_col)
        count = small.shape[2]
        gain = lane_vector(small, 2 * size // count, size // count)
        acc[...] = jnp.zeros_like(acc)
        advance(1)
        far.wait_recv()
        far.wait_send()
        load_attended.wait()

        @pl.loop(0, rows // 16)
        def _(i):
            here = pl.ds(pl.multiple_of(i * 16, 16), 16)
            value = attended[here, :]
            center = value - jnp.mean(value, axis=1, keepdims=True)
            rstd = lax.rsqrt(jnp.mean(center * center, axis=1, keepdims=True) + EPS)
            hat = center * rstd
            incoming = datt[here, :] + far_recv[here, :].astype(f32)
            acc[0] += incoming * hat
            acc[1] += incoming
            scaled = incoming * gain
            back = rstd * (
                scaled - jnp.mean(scaled, axis=1, keepdims=True) - hat * jnp.mean(scaled * hat, axis=1, keepdims=True)
            )
            whole = g[pl.ds(pl.multiple_of(t * rows + i * 16, 16), 16), :].astype(f32) + back
            datt[here, :] = whole
            far_send[here, :] = whole.astype(bf16)

        to_chip.start()
        to_core.start()
        keep.start()
        datt_copy().start()
        vec[...] = jnp.zeros_like(vec)
        vec[2:3, :] = jnp.sum(acc[0], axis=0, keepdims=True)
        vec[3:4, :] = jnp.sum(acc[1], axis=0, keepdims=True)
        for copy in near:
            copy.wait_send()
        fetch[0].wait()

        def mix(block, source):
            value = dot(source[...], out_t[...], ((1,), (0,))).astype(bf16)
            d_all[:, pl.ds(pl.multiple_of(block * rows, rows), rows)] = value.T

        def bring(block, slot, number):
            return pltpu.make_async_copy(resid_out.at[block], near_send.at[slot], local.at[number])

        mix(t, far_send)
        advance()
        to_core.wait_recv()
        first = bring(place.core, 0, 17)
        first.start()
        first.wait()
        mix(place.core, near_send.at[0])
        advance(2)
        to_chip.wait_recv()
        relay.start()
        second_block = bring(place.chip, 1, 18)
        second_block.start()
        second_block.wait()
        mix(place.chip, near_send.at[1])
        relay.wait_recv()
        third = bring(place.cross, 0, 19)
        third.start()
        third.wait()
        mix(place.cross, near_send.at[0])
        for copy in fetch[1:]:
            copy.wait()
        cosine, sine = cos_ref[...], sin_ref[...]
        for pair in range(width // (2 * HD)):
            advance()
            retreat_pair(pair, q_all, k_all, v_all, d_all, logs, cosine, sine, mask, dk_acc, dv_acc, tmp, vec)
        final = [
            pltpu.make_async_copy(src, dlin_out.at[pl.ds(i * width, width)], local.at[20 + i])
            for i, src in enumerate((q_all, k_all, v_all))
        ]
        for copy in final:
            copy.start()
        advance(2)
        for copy in final:
            copy.wait()

    pl.run_scoped(
        attention,
        pltpu.VMEM((rows, model), f32),
        pltpu.VMEM((seq, seq), f32),
        pltpu.VMEM((width, seq), bf16),
        pltpu.VMEM((width, seq), bf16),
        pltpu.VMEM((width, seq), bf16),
        pltpu.VMEM((width, seq), bf16),
        pltpu.VMEM((model, width), bf16),
        pltpu.VMEM((HD, seq), f32),
        pltpu.VMEM((HD, seq), f32),
        pltpu.VMEM((3, 2 * HD, 128), f32),
    )
    for step in plan:
        tick(*step)
    for pair in lanes:
        for lane in pair:
            lane.finish()
    for copy in (to_chip, to_core, relay):
        copy.wait_send()
    keep.wait()
    stored(2).wait()


def back(dgate, dup, hidden, second, g, gate, up, attended, small, out_t, q, k, v, logs, cosine, sine, segments, n):
    rows, model = attended.shape
    size, cols = model // n, hidden.shape[1]
    seq, width = 4 * rows, out_t.shape[1]
    shape = jax.ShapeDtypeStruct
    return pl.pallas_call(
        lambda *refs: back_kernel(n, *refs),
        in_specs=[HBM] * 8 + [VMEM] + [HBM] * 4 + [VMEM] * 5,
        out_specs=[HBM] * 6 + [VMEM],
        out_shape=[
            shape((size, cols), f32),
            shape((size, cols), f32),
            shape((size, cols), f32),
            shape((rows, model), f32),
            shape((4, rows, model), bf16),
            shape((3 * width, seq), bf16),
            shape((8, model), f32),
        ],
        scratch_shapes=[
            pltpu.VMEM((6, n, size // 2, cols), bf16),
            pltpu.VMEM((seq, model), bf16),
            pltpu.VMEM((seq, model), bf16),
            pltpu.VMEM((seq, cols), bf16),
            pltpu.VMEM((seq, cols), bf16),
            pltpu.VMEM((seq, cols), bf16),
            pltpu.VMEM((2, rows, model), bf16),
            pltpu.VMEM((2, rows, model), bf16),
            pltpu.VMEM((rows, model), bf16),
            pltpu.VMEM((rows, model), bf16),
            pltpu.VMEM((rows, model), f32),
            pltpu.VMEM((2, 16, model), f32),
            DMA((6, n - 1)),
            DMA((6, n - 1)),
            DMA((6,)),
            DMA((6,)),
            DMA((23,)),
        ],
        compiler_params=pltpu.CompilerParams(collective_id=3, has_side_effects=True, vmem_limit_bytes=62 << 20),
        cost_estimate=pl.CostEstimate(
            flops=14 * seq * model * cols, bytes_accessed=60 << 20, transcendentals=width // HD * seq * seq
        ),
        name="back",
    )(
        dgate, dup, hidden, second, g, gate.reshape(n, size, cols), up.reshape(n, size, cols), attended, small, out_t,
        q, k, v, logs, cosine, sine, segments[None, :], segments[:, None],
    )


def norm_forward(rows):
    center = rows - jnp.mean(rows, axis=-1, keepdims=True)
    rstd = lax.rsqrt(jnp.mean(center * center, axis=-1, keepdims=True) + EPS)
    return center * rstd, rstd


def norm_backward(grad_out, normal, rstd, gain):
    scaled = grad_out * gain
    return rstd * (
        scaled
        - jnp.mean(scaled, axis=-1, keepdims=True)
        - normal * jnp.mean(scaled * normal, axis=-1, keepdims=True)
    )


def local(
    layer_input,
    segments,
    positions,
    first_gain,
    first_shift,
    query_weight,
    key_weight,
    value_weight,
    query_bias,
    key_bias,
    value_bias,
    out_weight,
    second_gain,
    second_shift,
    gate_weight,
    up_weight,
    down_weight,
    out_grad,
):
    ring = Ring()
    n = ring.n
    width = query_weight.shape[1]
    heads = width // HD
    model = layer_input.shape[1]

    bias_key = jnp.pad(key_bias.astype(f32), ((0, 0), (0, HD - ROT))).reshape(-1)
    part = model // n
    per = HD // n
    if ring.ring:
        lanes = 128
        small = jnp.concatenate(
            [first_gain, first_shift, second_gain, second_shift, query_bias.reshape(-1), value_bias.reshape(-1)]
        )
        small = jnp.pad(small.reshape(-1, lanes), ((0, 16 - small.shape[0] // lanes), (0, 0)))
        normed, g_full, qkv, out_t, lin, small = enter(
            layer_input, out_grad, query_weight, key_weight, value_weight, out_weight, small, n
        )
        g_full = g_full.reshape(-1, model)
        qkv = qkv.reshape(model, -1)
        out_t = out_t.reshape(model, -1)
        packed_small = small
        small = small.reshape(n, -1)[:, : 4 * part + 2 * heads * per]
    else:
        x_full = tensor_gather(layer_input)
        g_full = tensor_gather(out_grad, after=x_full)
        small = jnp.concatenate(
            [first_gain, first_shift, second_gain, second_shift, query_bias.reshape(-1), value_bias.reshape(-1)]
        )
        small = lax.all_gather(small.reshape(1, -1), "dp", axis=0, tiled=True)
        qkv, _ = ring.gather(jnp.concatenate([query_weight, key_weight, value_weight], axis=1))
        out_t, _ = ring.gather(out_weight.T)
        gate, _ = ring.gather(gate_weight)
        up, _ = ring.gather(up_weight)
        down_t, _ = ring.gather(down_weight.T)
    gain_one, shift_one, gain_two, shift_two = (
        small[:, i * part : (i + 1) * part].reshape(model).astype(f32) for i in range(4)
    )
    biases = small[:, 4 * part :].reshape(n, 2, heads, per).transpose(1, 2, 0, 3).reshape(2, width).astype(f32)
    bias_lin = jnp.concatenate([biases[0], bias_key, biases[1]])
    if not ring.ring:
        hat_full, _ = norm_forward(x_full.astype(f32))
        normed = (hat_full * gain_one + shift_one).astype(bf16)
        lin = dot(qkv, normed, ((0,), (1,)))

    freqs = jnp.exp(-(2.0 / ROT) * jnp.arange(HALF).astype(f32) * math.log(10000.0))
    angles = freqs[:, None] * positions.astype(f32)[None, :]
    cosine, sine = jnp.cos(angles), jnp.sin(angles)
    index = jnp.arange(segments.shape[0], dtype=jnp.int32)
    allowed = (index[:, None] <= index[None, :]) & (segments[:, None] == segments[None, :])
    bias = jnp.where(allowed, 0.0, NEG).astype(f32)
    rows = layer_input.astype(f32)
    if ring.ring:
        q_rot, k_rot, v_heads, logs, mixed, attended, second, gate, up, hidden, ffn, grad_gate, grad_up = middle(
            lin, bias_lin, cosine, sine, segments, layer_input, out_t, packed_small, gate_weight, up_weight, down_weight, g_full, n
        )
        second, gate, up = second.reshape(-1, model), gate.reshape(model, -1), up.reshape(model, -1)
        hidden, ffn = hidden.reshape(second.shape[0], -1), ffn.reshape(-1, model)
        grad_gate, grad_up = grad_gate.reshape(hidden.shape), grad_up.reshape(hidden.shape)
    else:
        mixed, q_rot, k_rot, v_heads, logs = attend_forward(lin + bias_lin[:, None], cosine, sine, bias)
        attended = rows + tensor_scatter(dot(mixed, out_t, ((1,), (1,))))

        hat_two, rstd_two = norm_forward(attended)
        second = tensor_gather((hat_two * gain_two + shift_two).astype(bf16))
        gate_lin = dot(second, gate, ((1,), (0,)))
        up_lin = dot(second, up, ((1,), (0,)))
        sigma = jax.nn.sigmoid(gate_lin)
        activated = gate_lin * sigma
        hidden = (activated * up_lin).astype(bf16)
        ffn = dot(hidden, down_t, ((1,), (1,)))
        grad_hidden = dot(g_full, down_t, ((1,), (0,)))
        grad_gate = (grad_hidden * up_lin * sigma * (1.0 + gate_lin * (1.0 - sigma))).astype(bf16)
        grad_up = (grad_hidden * activated).astype(bf16)
    layer_output = (attended + tensor_scatter(ffn.astype(f32))).astype(bf16)

    if ring.ring:
        down_sum, gate_sum, up_sum, grad_attended, residual, grad_lin, vec = back(
            grad_gate, grad_up, hidden, second, g_full, gate, up, attended, packed_small, out_t,
            q_rot, k_rot, v_heads, logs, cosine, sine, segments, n
        )
        down_sum, residual = down_sum.T, residual.reshape(-1, model)
        sums = vec[4, : 3 * width].reshape(3, width).T
        second_vectors = vec[2:4]
    else:
        down_grad = dot(g_full, hidden, ((0,), (0,)))
        grad_second = tensor_scatter(dot(grad_gate, gate, ((1,), (1,))) + dot(grad_up, up, ((1,), (1,))))
        gate_grad = dot(second, grad_gate, ((0,), (0,)))
        up_grad = dot(second, grad_up, ((0,), (0,)))
        down_sum = ring.scatter(down_grad).T
        gate_sum = ring.scatter(gate_grad)
        up_sum = ring.scatter(up_grad)
        grad_attended = out_grad.astype(f32) + norm_backward(grad_second, hat_two, rstd_two, gain_two)
        residual = tensor_gather(grad_attended.astype(bf16))
        grad_mixed = dot(out_t, residual, ((0,), (1,))).astype(bf16)
        dq, dk, dv, sums = attend_backward(q_rot, k_rot, v_heads, grad_mixed, logs, cosine, sine, bias)
        grad_lin = jnp.concatenate([dq, dk, dv], axis=0)
        sums = sums.reshape(width, 128)[:, :3]
        second_vectors = jnp.stack([jnp.sum(grad_second * hat_two, axis=0), jnp.sum(grad_second, axis=0)])

    out_grad_t = dot(residual, mixed, ((0,), (0,)))
    out_sum = ring.scatter(out_grad_t).T
    qkv_grad = dot(normed, grad_lin, ((0,), (1,)))
    qkv_sum = ring.scatter(qkv_grad, pieces=2)
    grad_first = tensor_scatter(dot(grad_lin, qkv, ((0,), (1,))))
    hat_one, rstd_one = norm_forward(rows)
    input_grad = grad_attended + norm_backward(grad_first, hat_one, rstd_one, gain_one)

    vectors = jnp.stack([jnp.sum(grad_first * hat_one, axis=0), jnp.sum(grad_first, axis=0)])
    vectors = jnp.concatenate([vectors, second_vectors])
    vectors = sum_all(vectors, ["tensor"])
    packed = sum_all(jnp.concatenate([vectors.reshape(-1), sums.reshape(-1)]), ["dp"])
    each = model // (n * lax.axis_size("tensor"))
    at = ring.me * lax.axis_size("tensor") + lax.axis_index("tensor")
    vectors = lax.dynamic_slice(packed[: 4 * model].reshape(4, -1, each), (0, at, 0), (4, 1, each))[:, 0]
    sums = packed[4 * model :].reshape(heads, n, per, 3)
    mine = lax.dynamic_slice(sums, (0, ring.me, 0, 0), (heads, 1, per, 3))[:, 0]
    key_sum = sums[..., 1].reshape(heads, HD)[:, :ROT]

    return (
        layer_output,
        input_grad,
        vectors[0],
        vectors[1],
        qkv_sum[:, :width],
        qkv_sum[:, width : 2 * width],
        qkv_sum[:, 2 * width :],
        mine[..., 0],
        key_sum,
        mine[..., 2],
        out_sum,
        vectors[2],
        vectors[3],
        gate_sum,
        up_sum,
        down_sum,
    )


def solution(mesh):
    both = ("dp", "tensor")
    return jax.shard_map(
        local,
        mesh=mesh,
        in_specs=(
            P(both, None),
            P("dp"),
            P("dp"),
            P("dp"),
            P("dp"),
            P("dp", "tensor"),
            P("dp", "tensor"),
            P("dp", "tensor"),
            P("tensor", "dp"),
            P("tensor", None),
            P("tensor", "dp"),
            P("tensor", "dp"),
            P("dp"),
            P("dp"),
            P("dp", "tensor"),
            P("dp", "tensor"),
            P("tensor", "dp"),
            P(both, None),
        ),
        out_specs=(
            P(both, None),
            P(both, None),
            P(both),
            P(both),
            P("dp", "tensor"),
            P("dp", "tensor"),
            P("dp", "tensor"),
            P("tensor", "dp"),
            P("tensor", None),
            P("tensor", "dp"),
            P("tensor", "dp"),
            P(both),
            P(both),
            P("dp", "tensor"),
            P("dp", "tensor"),
            P("tensor", "dp"),
        ),
        check_vma=False,
    )
```

```python
import math

import jax
import jax.numpy as jnp
from jax import lax
from jax.experimental import pallas as pl
from jax.experimental.pallas import tpu as pltpu
from jax.sharding import PartitionSpec as P

HD = 64
ROT = 16
SEQ = 1024
HALF = ROT // 2
SCALE = HD ** (-0.5)

EPS = 1e-05
NEG = -1e30
QB = 256
f32 = jnp.float32
bf16 = jnp.bfloat16


def barrier(value, after):
    return lax.optimization_barrier((value, after))[0]


class Ring:
    def __init__(self):
        self.n = lax.axis_size("dp")
        self.ring = self.n == 8 and lax.axis_size("tensor") == 4
        order = list(range(0, self.n, 2)) + list(range(self.n - 1, 0, -2))
        self.up = [(order[i], order[(i + 1) % self.n]) for i in range(self.n)]
        self.down = [(b, a) for a, b in self.up]
        me = lax.axis_index("dp")
        self.me = me
        self.pos = jnp.where(me % 2 == 0, me // 2, self.n - 1 - (me - 1) // 2)

    def owner(self, offset):
        p = (self.pos + offset + 2 * self.n) % self.n
        return jnp.where(p < self.n // 2, 2 * p, 2 * (self.n - 1 - p) + 1)

    def gather(self, shard, pieces=1, after=None):
        n = self.n
        rows, cols = shard.shape
        if not self.ring:
            return lax.all_gather(shard, "dp", axis=0, tiled=True), [shard] * n
        if after is not None:
            shard = barrier(shard, after)
        full = jnp.zeros((n, rows, cols), shard.dtype)
        full = lax.dynamic_update_slice(full, shard[None], (self.me, 0, 0))
        size = rows // (2 * pieces)
        lanes = []
        for k in range(2 * pieces):
            lanes.append([k % 2, k * size, shard[k * size : (k + 1) * size]])
        marks = []
        for step in range(1, n):
            for lane in lanes:
                way, base, block = lane
                block = lax.ppermute(block, "dp", self.down if way else self.up)
                lane[2] = block
                whose = self.owner(step if way else -step)
                full = lax.dynamic_update_slice(full, block[None], (whose, base, 0))
            marks.append(lanes[-1][2])
        return full.reshape(n * rows, cols), marks

    def scatter(self, partial, pieces=1, after=None):
        n = self.n
        if not self.ring:
            return lax.psum_scatter(partial.astype(bf16), "dp", scatter_dimension=0, tiled=True).astype(f32)
        cols = partial.shape[1]
        rows = partial.shape[0] // n
        partial = partial.reshape(n, rows, cols)
        size = rows // (2 * pieces)
        done = []
        for k in range(2 * pieces):
            way = k % 2

            def block(step):
                whose = self.owner(1 + step if way else -1 - step)
                return lax.dynamic_slice(partial, (whose, k * size, 0), (1, size, cols))[0].astype(f32)

            moving = block(0)
            for step in range(1, n):
                got = lax.ppermute(moving.astype(bf16), "dp", self.down if way else self.up)
                moving = got.astype(f32) + block(step)
            done.append(moving)
        return jnp.concatenate(done, axis=0)


CORE = [(0, 1), (1, 0), (2, 3), (3, 2)]
CHIP = [(0, 2), (2, 0), (1, 3), (3, 1)]


def tensor_gather(rows, after=None):
    if lax.axis_size("tensor") != 4:
        return lax.all_gather(rows, "tensor", axis=0, tiled=True)
    if after is not None:
        rows = barrier(rows, after)
    t = lax.axis_index("tensor")
    far = lax.ppermute(rows, "tensor", CHIP)
    near = lax.ppermute(rows, "tensor", CORE)
    last = lax.ppermute(far, "tensor", CORE)
    full = jnp.zeros((4,) + rows.shape, rows.dtype)
    for flip, block in ((0, rows), (1, near), (2, far), (3, last)):
        full = lax.dynamic_update_slice(full, block[None], (t ^ flip, 0, 0))
    return full.reshape(4 * rows.shape[0], rows.shape[1])


def tensor_scatter(partial):
    if lax.axis_size("tensor") != 4:
        return lax.psum_scatter(partial.astype(bf16), "tensor", scatter_dimension=0, tiled=True).astype(f32)
    t = lax.axis_index("tensor")
    rows = partial.shape[0] // 4
    blocks = partial.reshape(4, rows, partial.shape[1])

    def block(flip):
        return lax.dynamic_slice(blocks, (t ^ flip, 0, 0), (1,) + blocks.shape[1:])[0]

    other = lax.ppermute(block(3).astype(bf16), "tensor", CORE)
    own = lax.ppermute(block(1).astype(bf16), "tensor", CORE)
    far = lax.ppermute((block(2) + other.astype(f32)).astype(bf16), "tensor", CHIP)
    return block(0) + own.astype(f32) + far.astype(f32)


def sum_all(vector, axes):
    for axis in axes:
        n = lax.axis_size(axis)
        if n & (n - 1):
            vector = lax.psum(vector, axis)
            continue
        step = 1
        while step < n:
            vector = vector + lax.ppermute(vector, axis, [(i, i ^ step) for i in range(n)])
            step *= 2
    return vector


def rotate(rows, cosine, sine, direction):
    first, second = rows[:HALF], rows[HALF:ROT]
    return jnp.concatenate(
        [first * cosine - direction * second * sine, second * cosine + direction * first * sine, rows[ROT:]], axis=0
    )


def dot(a, b, dims):
    return lax.dot_general(a, b, ((dims[0], dims[1]), ((), ())), preferred_element_type=f32)


def forward_kernel(q_ref, k_ref, v_ref, cos_ref, sin_ref, bias_ref, mixed_ref, q_out, k_out, v_out, log_ref):
    seq = q_ref.shape[1]
    cosine, sine = cos_ref[...], sin_ref[...]
    v_all = v_ref[...].astype(bf16)
    v_out[...] = v_all
    parts = []
    for head in range(q_ref.shape[0] // HD):
        rows = slice(head * HD, (head + 1) * HD)
        q = rotate(q_ref[rows, :], cosine, sine, 1.0).astype(bf16)
        k = rotate(k_ref[rows, :], cosine, sine, 1.0).astype(bf16)
        q_out[rows, :] = q
        k_out[rows, :] = k
        keys = k.T
        values = v_all[rows, :]
        q = q * jnp.asarray(SCALE, bf16)
        cols = []
        for start in range(0, seq, QB):
            end = start + QB
            scores = dot(keys[:end], q[:, start:end], ((1,), (0,))) + bias_ref[:end, start:end]
            top = jnp.max(scores, axis=0, keepdims=True)
            expo = jnp.exp(scores - top)
            total = jnp.sum(expo, axis=0, keepdims=True)
            probs = (expo * (1.0 / total)).astype(bf16)
            cols.append(dot(values[:, :end], probs, ((1,), (0,))).astype(bf16))
            log_ref[0, head : head + 1, start:end] = top + jnp.log(total)
        parts.append(jnp.concatenate(cols, axis=1))
    mixed_ref[...] = jnp.concatenate(parts, axis=0).T


def attend_forward(lin, cosine, sine, bias):
    width, seq = lin.shape[0] // 3, lin.shape[1]
    pair = 2 * HD
    count = width // pair
    outs = []
    block = lambda base: pl.BlockSpec((pair, seq), lambda i: (base * count + i, 0))
    whole = lambda shape: pl.BlockSpec(shape, lambda i: (0, 0))
    return pl.pallas_call(
        forward_kernel,
        grid=(count,),
        in_specs=[block(0), block(1), block(2), whole(cosine.shape), whole(sine.shape), whole(bias.shape)],
        out_specs=[
            pl.BlockSpec((seq, pair), lambda i: (0, i)),
            pl.BlockSpec((pair, seq), lambda i: (i, 0)),
            pl.BlockSpec((pair, seq), lambda i: (i, 0)),
            pl.BlockSpec((pair, seq), lambda i: (i, 0)),
            pl.BlockSpec((1, 2, seq), lambda i: (i, 0, 0)),
        ],
        out_shape=[
            jax.ShapeDtypeStruct((seq, width), bf16),
            jax.ShapeDtypeStruct((width, seq), bf16),
            jax.ShapeDtypeStruct((width, seq), bf16),
            jax.ShapeDtypeStruct((width, seq), bf16),
            jax.ShapeDtypeStruct((count, 2, seq), f32),
        ],
        compiler_params=pltpu.CompilerParams(vmem_limit_bytes=48 << 20),
        cost_estimate=pl.CostEstimate(
            flops=4 * width * seq * seq, bytes_accessed=30 << 20, transcendentals=width // HD * seq * seq
        ),
        name="attend_forward",
    )(lin, lin, lin, cosine, sine, bias)


def backward_kernel(q_ref, k_ref, v_ref, d_ref, log_ref, cos_ref, sin_ref, bias_ref, dq_out, dk_out, dv_out, sums_ref, dk_acc, dv_acc):
    seq = q_ref.shape[1]
    cosine, sine = cos_ref[...], sin_ref[...]
    for head in range(q_ref.shape[0] // HD):
        rows = slice(head * HD, (head + 1) * HD)
        q, k, v, d = q_ref[rows, :], k_ref[rows, :], v_ref[rows, :], d_ref[rows, :]
        keys, values = k.T, v.T
        q_small = q * jnp.asarray(SCALE, bf16)
        dk_acc[...] = jnp.zeros_like(dk_acc)
        dv_acc[...] = jnp.zeros_like(dv_acc)
        cols = []
        for start in range(0, seq, QB):
            end = start + QB
            here = slice(start, end)
            scores = dot(keys[:end], q_small[:, here], ((1,), (0,))) + bias_ref[:end, here]
            probs = jnp.exp(scores - log_ref[0, head : head + 1, here])
            grad = dot(values[:end], d[:, here], ((1,), (0,)))
            both = probs * grad
            inner = jnp.sum(both, axis=0, keepdims=True)
            grad = ((both - probs * inner) * SCALE).astype(bf16)
            probs = probs.astype(bf16)
            cols.append(dot(k[:, :end], grad, ((1,), (0,))))
            dk_acc[:, :end] += dot(q[:, here], grad, ((1,), (1,)))
            dv_acc[:, :end] += dot(d[:, here], probs, ((1,), (1,)))
        dq = rotate(jnp.concatenate(cols, axis=1), cosine, sine, -1.0)
        dk = rotate(dk_acc[...], cosine, sine, -1.0)
        dv = dv_acc[...]
        for part, (out, value) in enumerate(((dq_out, dq), (dk_out, dk), (dv_out, dv))):
            out[rows, :] = value.astype(bf16)
            sums_ref[0, rows, part : part + 1] = jnp.sum(value, axis=1, keepdims=True)


def attend_backward(q, k, v, d, logs, cosine, sine, bias):
    width, seq = q.shape
    pair = 2 * HD
    count = width // pair
    block = pl.BlockSpec((pair, seq), lambda i: (i, 0))
    whole = lambda shape: pl.BlockSpec(shape, lambda i: (0, 0))
    return pl.pallas_call(
        backward_kernel,
        grid=(count,),
        in_specs=[block] * 4
        + [pl.BlockSpec((1, 2, seq), lambda i: (i, 0, 0)), whole(cosine.shape), whole(sine.shape), whole(bias.shape)],
        out_specs=[block] * 3 + [pl.BlockSpec((1, pair, 128), lambda i: (i, 0, 0))],
        out_shape=[jax.ShapeDtypeStruct((width, seq), bf16)] * 3 + [jax.ShapeDtypeStruct((count, pair, 128), f32)],
        scratch_shapes=[pltpu.VMEM((HD, seq), f32), pltpu.VMEM((HD, seq), f32)],
        compiler_params=pltpu.CompilerParams(vmem_limit_bytes=48 << 20),
        cost_estimate=pl.CostEstimate(
            flops=10 * width * seq * seq, bytes_accessed=30 << 20, transcendentals=width // HD * seq * seq
        ),
        name="attend_backward",
    )(q, k, v, d, logs, cosine, sine, bias)


MESH = pl.DeviceIdType.MESH
HBM = pl.BlockSpec(memory_space=pl.ANY)
VMEM = pl.BlockSpec(memory_space=pltpu.VMEM)
DMA = pltpu.SemaphoreType.DMA


class Place:
    def __init__(self, n):
        self.n = n
        self.me = lax.axis_index("dp")
        self.t = lax.axis_index("tensor")
        odd = lax.rem(self.me, 2)
        half = lax.div(self.me, 2)
        self.pos = jnp.where(odd == 0, half, n - 1 - half)
        self.up = self.owner(1)
        self.down = self.owner(-1)
        self.core = self.t + 1 - 2 * lax.rem(self.t, 2)
        self.chip = lax.rem(self.t + 2, 4)
        self.cross = lax.rem(self.core + 2, 4)

    def owner(self, offset):
        p = lax.rem(self.pos + (offset + 2 * self.n), self.n)
        return jnp.where(p < self.n // 2, 2 * p, 2 * (self.n - 1 - p) + 1)

    def barrier(self, dp, tensor):
        sem = pltpu.get_barrier_semaphore()
        for there in dp:
            pl.semaphore_signal(sem, inc=1, device_id={"dp": there}, device_id_type=MESH)
        for there in tensor:
            pl.semaphore_signal(sem, inc=1, device_id={"tensor": there}, device_id_type=MESH)
        pl.semaphore_wait(sem, len(dp) + len(tensor))


class Lane:
    def __init__(self, place, full, base, size, way, send, recv):
        self.place, self.full, self.base, self.size, self.way = place, full, base, size, way
        self.send, self.recv = send, recv

    def whose(self, step):
        return self.place.owner(step if self.way else -step)

    def copy(self, step, whose):
        piece = self.full.at[whose, pl.ds(self.base, self.size)]
        return pltpu.make_async_remote_copy(
            src_ref=piece,
            dst_ref=piece,
            send_sem=self.send.at[step - 1],
            recv_sem=self.recv.at[step - 1],
            device_id={"dp": self.place.down if self.way else self.place.up},
            device_id_type=MESH,
        )

    def start(self, step):
        self.copy(step, self.whose(step - 1)).start()

    def arrive(self, step):
        self.copy(step, self.whose(step)).wait_recv()

    def finish(self):
        for step in range(1, self.place.n):
            self.copy(step, self.whose(step - 1)).wait_send()


class Exchange:
    def __init__(self, send, recv):
        self.send, self.recv = send, recv

    def copy(self, number, src, dst, there):
        return pltpu.make_async_remote_copy(
            src_ref=src,
            dst_ref=dst,
            send_sem=self.send.at[number],
            recv_sem=self.recv.at[number],
            device_id={"tensor": there},
            device_id_type=MESH,
        )


def row_norm(value, gain, shift):
    center = value - jnp.mean(value, axis=1, keepdims=True)
    rstd = lax.rsqrt(jnp.mean(center * center, axis=1, keepdims=True) + EPS)
    return center * rstd * gain + shift


def lane_vector(full, first, count):
    pieces = [full[d, r : r + 1, :].astype(f32) for d in range(full.shape[0]) for r in range(first, first + count)]
    return jnp.concatenate(pieces, axis=1)


def enter_kernel(
    n,
    x_ref, g_ref, wq, wk, wv, wo, small_ref,
    normed_out, g_out, qkv_out, out_out, lin, small_full,
    x_full, normed, left, right, outs,
    small_send, small_recv, send, recv, x_send, x_recv, local, stored,
):
    place = Place(n)
    rows = x_ref.shape[0]
    size = wq.shape[0]
    width = wq.shape[1]
    half = width // 2
    me, t = place.me, place.t
    loads = [
        pltpu.make_async_copy(wq, left.at[me, :, pl.ds(0, width)], local.at[0]),
        pltpu.make_async_copy(wk.at[:, pl.ds(0, half)], left.at[me, :, pl.ds(width, half)], local.at[1]),
        pltpu.make_async_copy(wk.at[:, pl.ds(half, half)], right.at[me, :, pl.ds(0, half)], local.at[2]),
        pltpu.make_async_copy(wv, right.at[me, :, pl.ds(half, width)], local.at[3]),
        pltpu.make_async_copy(x_ref, x_full.at[t], local.at[4]),
        pltpu.make_async_copy(g_ref, g_out.at[t], local.at[5]),
    ]
    for load in loads:
        load.start()
    outs[me] = wo[...].T
    small_full[me] = small_ref[...]
    place.barrier([place.owner(k) for k in range(1, n)], [place.core, place.chip])

    smalls = []
    for k in range(1, n):
        smalls.append(
            pltpu.make_async_remote_copy(
                src_ref=small_ref,
                dst_ref=small_full.at[me],
                send_sem=small_send.at[k - 1],
                recv_sem=small_recv.at[k - 1],
                device_id={"dp": place.owner(k)},
                device_id_type=MESH,
            )
        )
        smalls[-1].start()

    swap = Exchange(x_send, x_recv)
    to_chip = swap.copy(0, x_ref, x_full.at[t], place.chip)
    to_core = swap.copy(1, x_ref, x_full.at[t], place.core)
    relay = swap.copy(2, x_full.at[place.chip], x_full.at[place.chip], place.core)
    g_chip = swap.copy(3, g_ref, g_out.at[t], place.chip)
    g_core = swap.copy(4, g_ref, g_out.at[t], place.core)
    g_relay = swap.copy(5, g_out.at[place.chip], g_out.at[place.chip], place.core)
    to_chip.start()
    to_core.start()
    for load in loads[:4]:
        load.wait()
    lanes = []
    for number, (full, base, count, way) in enumerate(
        (
            (left, 0, size // 2, 0),
            (right, 0, size // 2, 1),
            (left, size // 2, size // 2, 0),
            (right, size // 2, size // 2, 1),
            (outs, 0, size // 2, 0),
            (outs, size // 2, size // 2, 1),
        )
    ):
        lanes.append(Lane(place, full, base, count, way, send.at[number], recv.at[number]))

    def store(step):
        whose, other = place.owner(-step), place.owner(step)
        if step == n:
            return []
        return [
            pltpu.make_async_copy(left.at[whose], qkv_out.at[whose, :, pl.ds(0, width + half)], stored.at[0, step]),
            pltpu.make_async_copy(right.at[other], qkv_out.at[other, :, pl.ds(width + half, width + half)], stored.at[1, step]),
            pltpu.make_async_copy(outs.at[whose, pl.ds(0, size // 2)], out_out.at[whose, pl.ds(0, size // 2)], stored.at[2, step]),
            pltpu.make_async_copy(
                outs.at[other, pl.ds(size // 2, size // 2)], out_out.at[other, pl.ds(size // 2, size // 2)], stored.at[3, step]
            ),
        ]

    writes = []

    def tick(step):
        for lane in lanes:
            if step > 1:
                lane.arrive(step - 1)
            if step < n:
                lane.start(step)
        for write in store(step - 1):
            write.start()
            writes.append(write)

    gain = shift = None

    def norm(block):
        @pl.loop(0, rows // 16)
        def _(i):
            here = pl.ds(pl.multiple_of(i * 16, 16), 16)
            there = pl.ds(pl.multiple_of(block * rows + i * 16, 16), 16)
            normed[there, :] = row_norm(x_full[block, here, :].astype(f32), gain, shift).astype(bf16)

    def project(step):
        for full, whose, base in ((left, place.owner(-step), 0), (right, place.owner(step), width + half)):
            xs = normed[:, pl.ds(pl.multiple_of(whose * size, size), size)]
            for j in range(0, width + half, 256):
                part = dot(full[whose, :, j : j + 256].T, xs, ((1,), (1,)))
                where = slice(base + j, base + j + 256)
                if step == 0:
                    lin[where, :] = part
                else:
                    lin[where, :] += part

    tick(1)
    loads[4].wait()
    for small in smalls:
        small.wait_recv()
    count = small_ref.shape[1]
    gain = lane_vector(small_full, 0, size // count)
    shift = lane_vector(small_full, size // count, size // count)
    norm(t)
    to_core.wait_recv()
    norm(place.core)
    tick(2)
    tick(3)
    to_chip.wait_recv()
    relay.start()
    g_chip.start()
    g_core.start()
    norm(place.chip)
    tick(4)
    relay.wait_recv()
    norm(place.cross)
    normed_store = pltpu.make_async_copy(normed, normed_out, local.at[6])
    normed_store.start()
    project(0)
    done = 1
    for step in range(5, n):
        tick(step)
        while done < min(step - 1, 2 * (step - 4) + 1):
            project(done)
            done += 1
    g_chip.wait_recv()
    g_relay.start()
    while done < n - 1:
        project(done)
        done += 1
    tick(n)
    project(n - 1)
    for copy in (to_chip, to_core, relay, g_chip, g_core, g_relay):
        copy.wait_send()
    g_core.wait_recv()
    g_relay.wait_recv()
    for small in smalls:
        small.wait_send()
    for lane in lanes:
        lane.finish()
    loads[5].wait()
    for write in writes:
        write.wait()
    normed_store.wait()


def enter(x, g, wq, wk, wv, wo, small, n):
    rows, model = x.shape
    size, width = wq.shape
    big = 3 * width // 2
    kernel = lambda *refs: enter_kernel(n, *refs)
    return pl.pallas_call(
        kernel,
        in_specs=[HBM] * 5 + [VMEM, VMEM],
        out_specs=[HBM, HBM, HBM, HBM, VMEM, VMEM],
        out_shape=[
            jax.ShapeDtypeStruct((4 * rows, model), bf16),
            jax.ShapeDtypeStruct((4, rows, model), bf16),
            jax.ShapeDtypeStruct((n, size, 3 * width), bf16),
            jax.ShapeDtypeStruct((n, size, width), bf16),
            jax.ShapeDtypeStruct((3 * width, 4 * rows), f32),
            jax.ShapeDtypeStruct((n,) + small.shape, bf16),
        ],
        scratch_shapes=[
            pltpu.VMEM((4, rows, model), bf16),
            pltpu.VMEM((4 * rows, model), bf16),
            pltpu.VMEM((n, size, big), bf16),
            pltpu.VMEM((n, size, big), bf16),
            pltpu.VMEM((n, size, width), bf16),
            DMA((n - 1,)),
            DMA((n - 1,)),
            DMA((6, n - 1)),
            DMA((6, n - 1)),
            DMA((6,)),
            DMA((6,)),
            DMA((7,)),
            DMA((4, n)),
        ],
        compiler_params=pltpu.CompilerParams(collective_id=1, has_side_effects=True, vmem_limit_bytes=56 << 20),
        cost_estimate=pl.CostEstimate(flops=6 * width * rows * 4 * model, bytes_accessed=40 << 20, transcendentals=0),
        name="enter",
    )(x, g, wq, wk, wv, wo, small)

def attend_pair(pair, lin, bias_ref, cosine, sine, mask, q_all, k_all, v_all, logs, flat, mixed):
    width, seq = q_all.shape

    @pl.loop(0, 2)
    def _(j):
        head = pair * 2 + j
        first = pl.multiple_of(head * HD, HD)
        rows = pl.ds(first, HD)

        def load(part):
            at = pl.ds(pl.multiple_of(part * width + first, HD), HD)
            return lin[at, :] + bias_ref[at, :]

        q = rotate(load(0), cosine, sine, 1.0).astype(bf16)
        k = rotate(load(1), cosine, sine, 1.0).astype(bf16)
        values = load(2).astype(bf16)
        q_all[rows, :] = q
        k_all[rows, :] = k
        v_all[rows, :] = values
        keys = k.T
        q = q * jnp.asarray(SCALE, bf16)
        mine = pl.ds(pl.multiple_of(j * HD, HD), HD)
        for start in range(0, seq, QB):
            end = start + QB
            scores = dot(keys[:end], q[:, start:end], ((1,), (0,))) + mask[:end, start:end]
            top = jnp.max(scores, axis=0, keepdims=True)
            expo = jnp.exp(scores - top)
            total = jnp.sum(expo, axis=0, keepdims=True)
            probs = (expo * (1.0 / total)).astype(bf16)
            flat[mine, start:end] = dot(values[:, :end], probs, ((1,), (0,))).astype(bf16)
            logs[pl.ds(head, 1), start:end] = top + jnp.log(total)

    mixed[:, pair * 2 * HD : (pair + 1) * 2 * HD] = flat[...].T


def build_mask(mask, seg_row, seg_col):
    seq = mask.shape[0]

    @pl.loop(0, seq // 32)
    def _(i):
        here = pl.ds(pl.multiple_of(i * 32, 32), 32)
        key = lax.broadcasted_iota(jnp.int32, (32, seq), 0) + i * 32
        query = lax.broadcasted_iota(jnp.int32, (32, seq), 1)
        allowed = (key <= query) & (seg_col[here, :] == seg_row[...])
        mask[here, :] = jnp.where(allowed, 0.0, NEG).astype(f32)


def middle_kernel(
    n,
    lin_ref, bias_ref, cos_ref, sin_ref, seg_row, seg_col, x_ref, out_ref, small, gate_w, up_w, down_w, g_ref,
    q_out, k_out, v_out, logs, mixed_out, att_out, second_out, gate_out, up_out, hidden_out, ffn_out, dgate_out, dup_out,
    gate, up, down, second, near_send, near_recv, far_send, far_recv, attended,
    send, recv, x_send, x_recv, local, stored, staged,
):
    place = Place(n)
    t = place.t
    rows, model = x_ref.shape
    size, cols = gate_w.shape
    seq = 4 * rows
    width = out_ref.shape[1]
    loads = [
        pltpu.make_async_copy(gate_w, gate.at[place.me], local.at[0]),
        pltpu.make_async_copy(up_w, up.at[place.me], local.at[1]),
    ]
    for load in loads:
        load.start()
    down[place.me] = down_w[...].T
    place.barrier([place.up, place.down], [place.core, place.chip])
    for load in loads:
        load.wait()

    half, quarter = size // 2, size // 4
    lanes = [
        [Lane(place, full, half * sub, half, way, send.at[2 * way + sub], recv.at[2 * way + sub]) for way, full in ((0, gate), (1, up))]
        for sub in range(2)
    ]
    downs = [
        [
            Lane(place, down, half * way + quarter * sub, quarter, way, send.at[4 + 2 * way + sub], recv.at[4 + 2 * way + sub])
            for way in range(2)
        ]
        for sub in range(2)
    ]

    def write(step):
        gated, upped = place.owner(-step), place.owner(step)
        return [
            pltpu.make_async_copy(gate.at[gated], gate_out.at[gated], stored.at[0, step]),
            pltpu.make_async_copy(up.at[upped], up_out.at[upped], stored.at[1, step]),
        ]

    def tick(kind, step, sub):
        for lane in (downs if kind else lanes)[sub]:
            if step > 1:
                lane.arrive(step - 1)
            if step < n:
                lane.start(step)
        if sub == 1 and not kind:
            for copy in write(step - 1):
                copy.start()

    plan = [(0, step, sub) for step in range(1, n) for sub in range(2)]
    plan += [(1, 1, 0), (1, 1, 1), (0, n, 0), (0, n, 1)]
    plan += [(1, step, sub) for step in range(2, n + 1) for sub in range(2)]
    plan = iter(plan)

    def advance(count=1):
        for _ in range(count):
            tick(*next(plan))

    swap = Exchange(x_send, x_recv)
    near = [swap.copy(i, near_send.at[i], near_recv.at[i], place.core) for i in range(2)]
    far = swap.copy(2, far_send, far_recv, place.chip)
    to_chip = swap.copy(3, second.at[t], second.at[t], place.chip)
    to_core = swap.copy(4, second.at[t], second.at[t], place.core)
    relay = swap.copy(5, second.at[place.chip], second.at[place.chip], place.core)
    copies = near + [far, to_chip, to_core, relay]

    advance(2)

    def attention(lin, mask, q_all, k_all, v_all, flat, mixed, out_t):
        pairs = width // (2 * HD)
        fetch = []
        for part in range(3):
            for pair in range(pairs):
                at = pl.ds(part * width + pair * 2 * HD, 2 * HD)
                fetch.append(pltpu.make_async_copy(lin_ref.at[at], lin.at[at], local.at[2 + part * pairs + pair]))
        for pair in range(pairs):
            for part in range(3):
                fetch[part * pairs + pair].start()
        weights = pltpu.make_async_copy(out_ref, out_t, local.at[2 + 3 * pairs])
        weights.start()
        build_mask(mask, seg_row, seg_col)
        cosine, sine = cos_ref[...], sin_ref[...]
        for pair in range(pairs):
            for part in range(3):
                fetch[part * pairs + pair].wait()
            attend_pair(pair, lin, bias_ref, cosine, sine, mask, q_all, k_all, v_all, logs, flat, mixed)
            advance()
        keep = [
            pltpu.make_async_copy(src, dst, local.at[3 + 3 * pairs + i])
            for i, (src, dst) in enumerate(((q_all, q_out), (k_all, k_out), (v_all, v_out), (mixed, mixed_out)))
        ]
        for copy in keep:
            copy.start()
        weights.wait()

        def project(block, j):
            at = pl.ds(pl.multiple_of(block * rows, rows), rows)
            return dot(mixed[at, :], out_t[j : j + 512, :], ((1,), (1,)))

        for i, block in enumerate((place.cross, place.core)):
            for j in range(0, model, 512):
                near_send[i, :, j : j + 512] = project(block, j).astype(bf16)
            near[i].start()
        near[0].wait_recv()
        for j in range(0, model, 512):
            tile = slice(j, j + 512)
            far_send[:, tile] = (project(place.chip, j) + near_recv[0, :, tile].astype(f32)).astype(bf16)
        far.start()
        own = pltpu.make_async_copy(x_ref, far_copy, local.at[7 + 3 * pairs])
        own.start()
        advance()
        near[1].wait_recv()
        own.wait()
        for j in range(0, model, 512):
            tile = slice(j, j + 512)
            attended[:, tile] = far_copy[:, tile].astype(f32) + project(t, j) + near_recv[1, :, tile].astype(f32)
        for copy in keep:
            copy.wait()

    far_copy = second.at[t]
    pl.run_scoped(
        attention,
        pltpu.VMEM((3 * width, seq), f32),
        pltpu.VMEM((seq, seq), f32),
        pltpu.VMEM((width, seq), bf16),
        pltpu.VMEM((width, seq), bf16),
        pltpu.VMEM((width, seq), bf16),
        pltpu.VMEM((2 * HD, seq), bf16),
        pltpu.VMEM((seq, width), bf16),
        pltpu.VMEM((model, width), bf16),
    )
    last = 7 + 3 * (width // (2 * HD))

    def feed(gate_lin, up_lin, grad, hidden, g, stage):
        g_load = pltpu.make_async_copy(g_ref, g, local.at[last + 1])
        g_load.start()
        gate_lin[...] = jnp.zeros_like(gate_lin)
        up_lin[...] = jnp.zeros_like(up_lin)
        grad[...] = jnp.zeros_like(grad)
        count = small.shape[2]
        gain = lane_vector(small, 2 * size // count, size // count)
        shift = lane_vector(small, 3 * size // count, size // count)
        advance(2)
        far.wait_recv()

        @pl.loop(0, rows // 16)
        def _(i):
            here = pl.ds(pl.multiple_of(i * 16, 16), 16)
            value = attended[here, :] + far_recv[here, :].astype(f32)
            attended[here, :] = value
            second[t, here, :] = row_norm(value, gain, shift).astype(bf16)

        to_chip.start()
        to_core.start()
        att_store = pltpu.make_async_copy(attended, att_out, local.at[last + 2])
        att_store.start()

        def add(block, low, high):
            @pl.loop(low, high)
            def _(step):
                for full, total, whose in ((gate, gate_lin, place.owner(-step)), (up, up_lin, place.owner(step))):
                    xs = second[block, :, pl.ds(pl.multiple_of(whose * size, size), size)]
                    total[block] += dot(xs, full[whose], ((1,), (0,)))

        advance()
        ready = 5
        add(t, 0, ready)
        to_core.wait_recv()
        advance()
        add(place.core, 0, ready)
        advance()
        to_chip.wait_recv()
        relay.start()
        add(place.chip, 0, ready)
        relay.wait_recv()
        second_store = pltpu.make_async_copy(second, second_out, local.at[last + 3])
        second_store.start()
        advance()
        add(place.cross, 0, ready)
        every = lambda low, high: pl.loop(0, 4)(lambda block: add(block, low, high))
        every(ready, n - 2)
        advance(2)
        advance()
        every(n - 2, n - 1)
        advance(2)
        every(n - 1, n)

        @pl.loop(0, 4 * rows // 16)
        def _(i):
            block = lax.div(i, rows // 16)
            here = pl.ds(pl.multiple_of(lax.rem(i, rows // 16) * 16, 16), 16)
            value = gate_lin[block, here, :]
            hidden[block, here, :] = (value * jax.nn.sigmoid(value) * up_lin[block, here, :]).astype(bf16)

        hidden_store = pltpu.make_async_copy(hidden, hidden_out, local.at[last + 4])
        hidden_store.start()
        g_load.wait()
        stages = []

        def use(whose):
            number = len(stages)
            slot = number % 2
            if number >= 2:
                stages[number - 2].wait()
            at = pl.ds(pl.multiple_of(whose * size, size), size)

            @pl.loop(0, 4)
            def _(block):
                grad[block] += dot(g[block, :, at], down[whose], ((1,), (0,)))
                stage[slot, block] = dot(hidden[block], down[whose], ((1,), (1,))).astype(bf16)

            stages.append(pltpu.make_async_copy(stage.at[slot], ffn_out.at[:, :, at], staged.at[number]))
            stages[-1].start()

        use(place.me)
        for step in range(2, n + 1):
            advance(2)
            if step - 1 == n // 2:
                use(place.owner(n // 2))
            elif step - 1 > n // 2:
                use(place.owner(step - 1))
                use(place.owner(1 - step))
        for lane in lanes[0] + lanes[1] + downs[0] + downs[1]:
            lane.finish()
        for step in range(n):
            for copy in write(step):
                copy.wait()

        @pl.loop(0, 4 * rows // 16)
        def _(i):
            block = lax.div(i, rows // 16)
            here = pl.ds(pl.multiple_of(lax.rem(i, rows // 16) * 16, 16), 16)
            value = gate_lin[block, here, :]
            sigma = jax.nn.sigmoid(value)
            incoming = grad[block, here, :]
            gate[block, here, :] = (incoming * up_lin[block, here, :] * sigma * (1.0 + value * (1.0 - sigma))).astype(bf16)
            gate[4 + block, here, :] = (incoming * (value * sigma)).astype(bf16)

        final = [
            pltpu.make_async_copy(gate.at[pl.ds(0, 4)], dgate_out, local.at[last + 5]),
            pltpu.make_async_copy(gate.at[pl.ds(4, 4)], dup_out, local.at[last + 6]),
        ]
        for copy in final:
            copy.start()
        for copy in final + stages[-2:] + [hidden_store, second_store, att_store]:
            copy.wait()

    pl.run_scoped(
        feed,
        pltpu.VMEM((4, rows, cols), f32),
        pltpu.VMEM((4, rows, cols), f32),
        pltpu.VMEM((4, rows, cols), f32),
        pltpu.VMEM((4, rows, cols), bf16),
        pltpu.VMEM((4, rows, model), bf16),
        pltpu.VMEM((2, 4, rows, size), bf16),
    )
    for copy in copies:
        copy.wait_send()


def middle(lin, bias, cosine, sine, segments, x, out_t, small, gate, up, down, g, n):
    rows, model = x.shape
    size, cols = gate.shape
    seq = 4 * rows
    width = out_t.shape[1]
    heads = width // HD
    shape = jax.ShapeDtypeStruct
    return pl.pallas_call(
        lambda *refs: middle_kernel(n, *refs),
        in_specs=[HBM] + [VMEM] * 5 + [HBM, HBM, VMEM, HBM, HBM, VMEM, HBM],
        out_specs=[HBM, HBM, HBM, VMEM] + [HBM] * 9,
        out_shape=[
            shape((width, seq), bf16),
            shape((width, seq), bf16),
            shape((width, seq), bf16),
            shape((heads, seq), f32),
            shape((seq, width), bf16),
            shape((rows, model), f32),
            shape((4, rows, model), bf16),
            shape((n, size, cols), bf16),
            shape((n, size, cols), bf16),
            shape((4, rows, cols), bf16),
            shape((4, rows, model), bf16),
            shape((4, rows, cols), bf16),
            shape((4, rows, cols), bf16),
        ],
        scratch_shapes=[
            pltpu.VMEM((n, size, cols), bf16),
            pltpu.VMEM((n, size, cols), bf16),
            pltpu.VMEM((n, size, cols), bf16),
            pltpu.VMEM((4, rows, model), bf16),
            pltpu.VMEM((2, rows, model), bf16),
            pltpu.VMEM((2, rows, model), bf16),
            pltpu.VMEM((rows, model), bf16),
            pltpu.VMEM((rows, model), bf16),
            pltpu.VMEM((rows, model), f32),
            DMA((8, n - 1)),
            DMA((8, n - 1)),
            DMA((6,)),
            DMA((6,)),
            DMA((14 + 3 * width // (2 * HD),)),
            DMA((2, n)),
            DMA((n,)),
        ],
        compiler_params=pltpu.CompilerParams(collective_id=2, has_side_effects=True, vmem_limit_bytes=62 << 20),
        cost_estimate=pl.CostEstimate(
            flops=10 * seq * model * cols, bytes_accessed=60 << 20, transcendentals=heads * seq * seq
        ),
        name="middle",
    )(
        lin, bias[:, None], cosine, sine, segments[None, :], segments[:, None],
        x, out_t, small, gate, up, down, g.reshape(4, rows, model),
    )

class Sum:
    def __init__(self, place, slots, way, send, recv):
        self.place, self.slots, self.way, self.send, self.recv = place, slots, way, send, recv

    def whose(self, step):
        return self.place.owner(1 + step if self.way else -1 - step)

    def copy(self, step):
        return pltpu.make_async_remote_copy(
            src_ref=self.slots.at[step - 1],
            dst_ref=self.slots.at[step],
            send_sem=self.send.at[step - 1],
            recv_sem=self.recv.at[step - 1],
            device_id={"dp": self.place.down if self.way else self.place.up},
            device_id_type=MESH,
        )

    def tick(self, step, product, final):
        if step > 0:
            self.copy(step).wait_recv()
        cols = self.slots.shape[2]
        for low in range(0, cols, 512):
            tile = slice(low, min(low + 512, cols))
            part = product(tile)
            if step > 0:
                part = part + self.slots[step, :, tile].astype(f32)
            if step == self.place.n - 1:
                final(tile, part)
            else:
                self.slots[step, :, tile] = part.astype(bf16)
        if step < self.place.n - 1:
            self.copy(step + 1).start()

    def finish(self):
        for step in range(1, self.place.n):
            self.copy(step).wait_send()


def columns_of(left, whose, size, way):
    half = size // 2
    return left[:, pl.ds(pl.multiple_of(whose * size + way * half, half), half)].T


def retreat_pair(pair, q_all, k_all, v_all, d_all, logs, cosine, sine, mask, dk_acc, dv_acc, tmp, vec):
    width, seq = q_all.shape

    @pl.loop(0, 2)
    def _(j):
        head = pair * 2 + j
        rows = pl.ds(pl.multiple_of(head * HD, HD), HD)
        q, k, v, d = q_all[rows, :], k_all[rows, :], v_all[rows, :], d_all[rows, :]
        keys, values = k.T, v.T
        q_small = q * jnp.asarray(SCALE, bf16)
        dk_acc[...] = jnp.zeros_like(dk_acc)
        dv_acc[...] = jnp.zeros_like(dv_acc)
        cols = []
        for start in range(0, seq, QB):
            end = start + QB
            here = slice(start, end)
            scores = dot(keys[:end], q_small[:, here], ((1,), (0,))) + mask[:end, here]
            probs = jnp.exp(scores - logs[pl.ds(head, 1), here])
            grad = dot(values[:end], d[:, here], ((1,), (0,)))
            both = probs * grad
            inner = jnp.sum(both, axis=0, keepdims=True)
            grad = ((both - probs * inner) * SCALE).astype(bf16)
            probs = probs.astype(bf16)
            cols.append(dot(k[:, :end], grad, ((1,), (0,))))
            dk_acc[:, :end] += dot(q[:, here], grad, ((1,), (1,)))
            dv_acc[:, :end] += dot(d[:, here], probs, ((1,), (1,)))
        dq = rotate(jnp.concatenate(cols, axis=1), cosine, sine, -1.0)
        dk = rotate(dk_acc[...], cosine, sine, -1.0)
        dv = dv_acc[...]
        mine = pl.ds(pl.multiple_of(j * HD, HD), HD)
        for part, (out, value) in enumerate(((q_all, dq), (k_all, dk), (v_all, dv))):
            out[rows, :] = value.astype(bf16)
            lanes = value[:, :128]
            for i in range(128, seq, 128):
                lanes = lanes + value[:, i : i + 128]
            tmp[part, mine, :] = lanes

    for part in range(3):
        at = part * width + pair * 2 * HD
        vec[4:5, at : at + 2 * HD] = jnp.sum(tmp[part].T, axis=0, keepdims=True)


def back_kernel(
    n,
    dgate_ref, dup_ref, hidden_ref, second_ref, g_ref, gate_ref, up_ref, att_ref, small, out_ref,
    q_ref, k_ref, v_ref, logs, cos_ref, sin_ref, seg_row, seg_col,
    down_sum, gate_sum, up_sum, datt_out, resid_out, dlin_out, vec,
    slots, g, second, hidden, dgate, dup, near_send, near_recv, far_send, far_recv, datt, acc,
    send, recv, x_send, x_recv, local,
):
    place = Place(n)
    t = place.t
    rows, model = att_ref.shape
    size, cols = gate_ref.shape[1:]
    seq, width = 4 * rows, out_ref.shape[1]
    loads = [
        pltpu.make_async_copy(src, dst, local.at[i])
        for i, (src, dst) in enumerate(
            ((g_ref, g), (hidden_ref, hidden), (second_ref, second), (dgate_ref, dgate), (dup_ref, dup))
        )
    ]
    for load in loads:
        load.start()
    place.barrier([place.up, place.down], [place.core, place.chip])

    lanes = [[Sum(place, slots.at[2 * i + way], way, send.at[2 * i + way], recv.at[2 * i + way]) for way in range(2)] for i in range(3)]
    sources = ((g, hidden), (second, dgate), (second, dup))
    sums = (down_sum, gate_sum, up_sum)

    def stored(i):
        return pltpu.make_async_copy(datt.at[:, pl.ds(0, cols)], sums[i], local.at[6 + i])

    def tick(step, i):
        left, right = sources[i]
        if step == n - 1:
            (stored(i - 1) if i else datt_copy()).wait()
        for lane in lanes[i]:

            def final(tile, total):
                datt[lane.way * size // 2 : (lane.way + 1) * size // 2, tile] = total

            block = columns_of(left, lane.whose(step), size, lane.way)
            lane.tick(step, lambda tile: dot(block, right[:, tile], ((1,), (0,))), final)
        if step == n - 1:
            stored(i).start()

    plan = iter([(step, i) for step in range(n) for i in range(3)])

    def advance(count=1):
        for _ in range(count):
            tick(*next(plan))

    def datt_copy():
        return pltpu.make_async_copy(datt, datt_out, local.at[9])

    swap = Exchange(x_send, x_recv)
    near = [swap.copy(i, near_send.at[i], near_recv.at[i], place.core) for i in range(2)]
    far = swap.copy(2, far_send, far_recv, place.chip)
    to_chip = swap.copy(3, far_send, resid_out.at[t], place.chip)
    to_core = swap.copy(4, far_send, resid_out.at[t], place.core)
    relay = swap.copy(5, resid_out.at[place.chip], resid_out.at[place.chip], place.core)
    keep = pltpu.make_async_copy(far_send, resid_out.at[t], local.at[10])
    own = pl.ds(pl.multiple_of(t * rows, rows), rows)

    def feed(gate, up):
        weights = [
            pltpu.make_async_copy(gate_ref, gate, local.at[11]),
            pltpu.make_async_copy(up_ref, up, local.at[12]),
        ]
        for copy in weights:
            copy.start()
        loads[0].wait()
        loads[1].wait()
        advance()
        loads[2].wait()
        loads[3].wait()
        advance()
        loads[4].wait()
        advance()
        for copy in weights:
            copy.wait()

        def product(block, j):
            at = pl.ds(pl.multiple_of(block * rows, rows), rows)
            return dot(dgate[at, :], gate[j], ((1,), (1,))) + dot(dup[at, :], up[j], ((1,), (1,)))

        for i, block in enumerate((place.cross, place.core)):
            for j in range(n):
                near_send[i, :, j * size : (j + 1) * size] = product(block, j).astype(bf16)
            near[i].start()
            advance()
        near[0].wait_recv()
        for j in range(n):
            tile = slice(j * size, (j + 1) * size)
            far_send[:, tile] = (product(place.chip, j) + near_recv[0, :, tile].astype(f32)).astype(bf16)
        far.start()
        advance()
        near[1].wait_recv()
        for j in range(n):
            tile = slice(j * size, (j + 1) * size)
            datt[:, tile] = product(t, j) + near_recv[1, :, tile].astype(f32)
        advance()

    pl.run_scoped(feed, pltpu.VMEM((n, size, cols), bf16), pltpu.VMEM((n, size, cols), bf16))

    def attention(attended, mask, q_all, k_all, v_all, d_all, out_t, dk_acc, dv_acc, tmp):
        load_attended = pltpu.make_async_copy(att_ref, attended, local.at[5])
        load_attended.start()
        fetch = [
            pltpu.make_async_copy(src, dst, local.at[13 + i])
            for i, (src, dst) in enumerate(((out_ref, out_t), (q_ref, q_all), (k_ref, k_all), (v_ref, v_all)))
        ]
        for copy in fetch:
            copy.start()
        build_mask(mask, seg_row, seg_col)
        count = small.shape[2]
        gain = lane_vector(small, 2 * size // count, size // count)
        acc[...] = jnp.zeros_like(acc)
        advance(1)
        far.wait_recv()
        far.wait_send()
        load_attended.wait()

        @pl.loop(0, rows // 16)
        def _(i):
            here = pl.ds(pl.multiple_of(i * 16, 16), 16)
            value = attended[here, :]
            center = value - jnp.mean(value, axis=1, keepdims=True)
            rstd = lax.rsqrt(jnp.mean(center * center, axis=1, keepdims=True) + EPS)
            hat = center * rstd
            incoming = datt[here, :] + far_recv[here, :].astype(f32)
            acc[0] += incoming * hat
            acc[1] += incoming
            scaled = incoming * gain
            back = rstd * (
                scaled - jnp.mean(scaled, axis=1, keepdims=True) - hat * jnp.mean(scaled * hat, axis=1, keepdims=True)
            )
            whole = g[pl.ds(pl.multiple_of(t * rows + i * 16, 16), 16), :].astype(f32) + back
            datt[here, :] = whole
            far_send[here, :] = whole.astype(bf16)

        to_chip.start()
        to_core.start()
        keep.start()
        datt_copy().start()
        vec[...] = jnp.zeros_like(vec)
        vec[2:3, :] = jnp.sum(acc[0], axis=0, keepdims=True)
        vec[3:4, :] = jnp.sum(acc[1], axis=0, keepdims=True)
        for copy in near:
            copy.wait_send()
        fetch[0].wait()

        def mix(block, source):
            value = dot(source[...], out_t[...], ((1,), (0,))).astype(bf16)
            d_all[:, pl.ds(pl.multiple_of(block * rows, rows), rows)] = value.T

        def bring(block, slot, number):
            return pltpu.make_async_copy(resid_out.at[block], near_send.at[slot], local.at[number])

        mix(t, far_send)
        advance()
        to_core.wait_recv()
        first = bring(place.core, 0, 17)
        first.start()
        first.wait()
        mix(place.core, near_send.at[0])
        advance(2)
        to_chip.wait_recv()
        relay.start()
        second_block = bring(place.chip, 1, 18)
        second_block.start()
        second_block.wait()
        mix(place.chip, near_send.at[1])
        relay.wait_recv()
        third = bring(place.cross, 0, 19)
        third.start()
        third.wait()
        mix(place.cross, near_send.at[0])
        for copy in fetch[1:]:
            copy.wait()
        cosine, sine = cos_ref[...], sin_ref[...]
        for pair in range(width // (2 * HD)):
            advance()
            retreat_pair(pair, q_all, k_all, v_all, d_all, logs, cosine, sine, mask, dk_acc, dv_acc, tmp, vec)
        final = [
            pltpu.make_async_copy(src, dlin_out.at[pl.ds(i * width, width)], local.at[20 + i])
            for i, src in enumerate((q_all, k_all, v_all))
        ]
        for copy in final:
            copy.start()
        advance(2)
        for copy in final:
            copy.wait()

    pl.run_scoped(
        attention,
        pltpu.VMEM((rows, model), f32),
        pltpu.VMEM((seq, seq), f32),
        pltpu.VMEM((width, seq), bf16),
        pltpu.VMEM((width, seq), bf16),
        pltpu.VMEM((width, seq), bf16),
        pltpu.VMEM((width, seq), bf16),
        pltpu.VMEM((model, width), bf16),
        pltpu.VMEM((HD, seq), f32),
        pltpu.VMEM((HD, seq), f32),
        pltpu.VMEM((3, 2 * HD, 128), f32),
    )
    for step in plan:
        tick(*step)
    for pair in lanes:
        for lane in pair:
            lane.finish()
    for copy in (to_chip, to_core, relay):
        copy.wait_send()
    keep.wait()
    stored(2).wait()


def back(dgate, dup, hidden, second, g, gate, up, attended, small, out_t, q, k, v, logs, cosine, sine, segments, n):
    rows, model = attended.shape
    size, cols = model // n, hidden.shape[1]
    seq, width = 4 * rows, out_t.shape[1]
    shape = jax.ShapeDtypeStruct
    return pl.pallas_call(
        lambda *refs: back_kernel(n, *refs),
        in_specs=[HBM] * 8 + [VMEM] + [HBM] * 4 + [VMEM] * 5,
        out_specs=[HBM] * 6 + [VMEM],
        out_shape=[
            shape((size, cols), f32),
            shape((size, cols), f32),
            shape((size, cols), f32),
            shape((rows, model), f32),
            shape((4, rows, model), bf16),
            shape((3 * width, seq), bf16),
            shape((8, model), f32),
        ],
        scratch_shapes=[
            pltpu.VMEM((6, n, size // 2, cols), bf16),
            pltpu.VMEM((seq, model), bf16),
            pltpu.VMEM((seq, model), bf16),
            pltpu.VMEM((seq, cols), bf16),
            pltpu.VMEM((seq, cols), bf16),
            pltpu.VMEM((seq, cols), bf16),
            pltpu.VMEM((2, rows, model), bf16),
            pltpu.VMEM((2, rows, model), bf16),
            pltpu.VMEM((rows, model), bf16),
            pltpu.VMEM((rows, model), bf16),
            pltpu.VMEM((rows, model), f32),
            pltpu.VMEM((2, 16, model), f32),
            DMA((6, n - 1)),
            DMA((6, n - 1)),
            DMA((6,)),
            DMA((6,)),
            DMA((23,)),
        ],
        compiler_params=pltpu.CompilerParams(collective_id=3, has_side_effects=True, vmem_limit_bytes=62 << 20),
        cost_estimate=pl.CostEstimate(
            flops=14 * seq * model * cols, bytes_accessed=60 << 20, transcendentals=width // HD * seq * seq
        ),
        name="back",
    )(
        dgate, dup, hidden, second, g, gate.reshape(n, size, cols), up.reshape(n, size, cols), attended, small, out_t,
        q, k, v, logs, cosine, sine, segments[None, :], segments[:, None],
    )

def leave_kernel(
    n,
    normed_ref, dlin_ref, qkv_ref, mixed_ref, resid_ref, datt_ref, x_ref, att_ref, ffn_ref, small, vec_ref,
    layer_out, input_out, query_sum, key_sum, value_sum, out_sum, vec_out,
    wide, narrow, normed, dlin, qkv, mixed, resid, datt, attended, x, first, near_send, near_recv, far_send, far_recv,
    ffn_own, ffn_recv, ffn_send, ffn_far, layer, acc, totals, wsum, osum, vecs, vec_recv,
    send, recv, x_send, x_recv, v_send, v_recv, local,
):
    place = Place(n)
    t, me = place.t, place.me
    rows, model = att_ref.shape
    size = model // n
    total_cols = dlin_ref.shape[0]
    width = total_cols // 3
    part = total_cols // 2
    loads = [
        pltpu.make_async_copy(src, dst, local.at[i])
        for i, (src, dst) in enumerate(
            (
                (normed_ref, normed),
                (dlin_ref, dlin),
                (resid_ref, resid),
                (mixed_ref, mixed),
                (qkv_ref, qkv),
                (ffn_ref.at[place.chip], ffn_own.at[0]),
                (ffn_ref.at[t], ffn_own.at[1]),
                (att_ref, attended),
                (x_ref, x),
                (datt_ref, datt),
            )
        )
    ]
    for load in loads:
        load.start()
    hops = [1, 2, 4]
    partners = [me + hop - 2 * hop * lax.rem(lax.div(me, hop), 2) for hop in hops]
    place.barrier([place.up, place.down] + partners, [place.core, place.chip])

    lanes = [
        [Sum(place, wide.at[2 * i + way], way, send.at[2 * i + way], recv.at[2 * i + way]) for way in range(2)] for i in range(2)
    ] + [[Sum(place, narrow.at[way], way, send.at[4 + way], recv.at[4 + way]) for way in range(2)]]

    swap = Exchange(x_send, x_recv)
    near = [swap.copy(i, near_send.at[i], near_recv.at[i], place.core) for i in range(2)]
    far = swap.copy(2, far_send, far_recv, place.chip)
    outs = [swap.copy(3 + i, ffn_ref.at[block], ffn_recv.at[i], place.core) for i, block in enumerate((place.cross, place.core))]
    outs_far = swap.copy(5, ffn_send, ffn_far, place.chip)
    for copy in outs:
        copy.start()

    def tick(step, i):
        for lane in lanes[i]:
            half = slice(lane.way * size // 2, (lane.way + 1) * size // 2)
            if i == 2:

                def product(left, tile):
                    return dot(left, mixed[:, tile], ((1,), (0,)))

                def final(tile, total):
                    osum[half, tile] = total

            else:

                def product(left, tile):
                    return dot(left, dlin[part * i + tile.start : part * i + tile.stop, :], ((1,), (1,)))

                def final(tile, total):
                    wsum[half, part * i + tile.start : part * i + tile.stop] = total

            left = columns_of(resid if i == 2 else normed, lane.whose(step), size, lane.way)
            lane.tick(step, lambda tile: product(left, tile), final)

    plan = iter([(step, i) for step in range(n) for i in range(3)])

    def advance(count=1):
        for _ in range(count):
            tick(*next(plan))

    loads[0].wait()
    loads[1].wait()
    advance(2)
    loads[2].wait()
    loads[3].wait()
    advance()
    outs[0].wait_recv()
    loads[5].wait()
    for j in range(0, rows, 64):
        tile = slice(j, j + 64)
        ffn_send[tile, :] = (ffn_own[0, tile, :].astype(f32) + ffn_recv[0, tile, :].astype(f32)).astype(bf16)
    outs_far.start()
    loads[4].wait()

    def product(block, use):
        left = dlin[:, pl.ds(pl.multiple_of(block * rows, rows), rows)].T
        for j in range(n):
            use(slice(j * size, (j + 1) * size), dot(left, qkv[j], ((1,), (1,))))

    for i, block in enumerate((place.cross, place.core)):

        def use_near(tile, value):
            near_send[i, :, tile] = value.astype(bf16)

        product(block, use_near)
        near[i].start()
        advance()
    near[0].wait_recv()

    def use_far(tile, value):
        far_send[:, tile] = (value + near_recv[0, :, tile].astype(f32)).astype(bf16)

    product(place.chip, use_far)
    far.start()
    advance()
    near[1].wait_recv()

    def use_own(tile, value):
        first[:, tile] = value + near_recv[1, :, tile].astype(f32)

    product(t, use_own)
    advance()

    outs[1].wait_recv()
    outs_far.wait_recv()
    loads[6].wait()
    loads[7].wait()
    for j in range(0, rows, 64):
        tile = slice(j, j + 64)
        layer[tile, :] = (
            attended[tile, :]
            + ffn_own[1, tile, :].astype(f32)
            + ffn_recv[1, tile, :].astype(f32)
            + ffn_far[tile, :].astype(f32)
        ).astype(bf16)
    layer_store = pltpu.make_async_copy(layer, layer_out, local.at[10])
    layer_store.start()
    advance()

    count = small.shape[2]
    gain = lane_vector(small, 0, size // count)
    acc[...] = jnp.zeros_like(acc)
    loads[8].wait()
    loads[9].wait()
    advance(2)
    far.wait_recv()

    @pl.loop(0, rows // 16)
    def _(i):
        here = pl.ds(pl.multiple_of(i * 16, 16), 16)
        value = x[here, :].astype(f32)
        center = value - jnp.mean(value, axis=1, keepdims=True)
        rstd = lax.rsqrt(jnp.mean(center * center, axis=1, keepdims=True) + EPS)
        hat = center * rstd
        incoming = first[here, :] + far_recv[here, :].astype(f32)
        acc[0] += incoming * hat
        acc[1] += incoming
        scaled = incoming * gain
        back_rows = rstd * (
            scaled - jnp.mean(scaled, axis=1, keepdims=True) - hat * jnp.mean(scaled * hat, axis=1, keepdims=True)
        )
        totals[here, :] = datt[here, :] + back_rows

    input_store = pltpu.make_async_copy(totals, input_out, local.at[11])
    input_store.start()
    vecs[0] = vec_ref[...]
    vecs[0, 0:1, :] = jnp.sum(acc[0], axis=0, keepdims=True)
    vecs[0, 1:2, :] = jnp.sum(acc[1], axis=0, keepdims=True)

    def hop(number):
        there = {"tensor": (place.core, place.chip)[number]} if number < 2 else {"dp": partners[number - 2]}
        return pltpu.make_async_remote_copy(
            src_ref=vecs.at[number],
            dst_ref=vec_recv.at[number],
            send_sem=v_send.at[number],
            recv_sem=v_recv.at[number],
            device_id=there,
            device_id_type=MESH,
        )

    for number in range(5):
        hop(number).start()
        advance(2)
        hop(number).wait_recv()
        summed = vecs[number] + vec_recv[number]
        if number < 2:
            row = lax.broadcasted_iota(jnp.int32, summed.shape, 0)
            summed = jnp.where(row < 4, summed, vecs[number])
        vecs[number + 1] = summed
    vec_out[...] = vecs[5]
    for item in plan:
        tick(*item)
    results = [
        pltpu.make_async_copy(wsum.at[:, pl.ds(i * width, width)], out, local.at[12 + i])
        for i, out in enumerate((query_sum, key_sum, value_sum))
    ] + [pltpu.make_async_copy(osum, out_sum, local.at[15])]
    for copy in results:
        copy.start()
    for group in lanes:
        for lane in group:
            lane.finish()
    for copy in near + [far] + outs + [outs_far]:
        copy.wait_send()
    for number in range(5):
        hop(number).wait_send()
    for copy in results + [layer_store, input_store]:
        copy.wait()


def leave(normed, dlin, qkv, mixed, resid, datt, x, attended, ffn, small, vec, n):
    rows, model = x.shape
    size = model // n
    seq, width = mixed.shape
    shape = jax.ShapeDtypeStruct
    own = lambda kind: pltpu.VMEM((rows, model), kind)
    return pl.pallas_call(
        lambda *refs: leave_kernel(n, *refs),
        in_specs=[HBM] * 9 + [VMEM] * 2,
        out_specs=[HBM] * 6 + [VMEM],
        out_shape=[shape((rows, model), bf16), shape((rows, model), f32)]
        + [shape((size, width), f32)] * 4
        + [shape((8, model), f32)],
        scratch_shapes=[
            pltpu.VMEM((4, n, size // 2, 3 * width // 2), bf16),
            pltpu.VMEM((2, n, size // 2, width), bf16),
            pltpu.VMEM((seq, model), bf16),
            pltpu.VMEM((3 * width, seq), bf16),
            pltpu.VMEM((n, size, 3 * width), bf16),
            pltpu.VMEM((seq, width), bf16),
            pltpu.VMEM((seq, model), bf16),
            own(f32),
            own(f32),
            own(bf16),
            own(f32),
            pltpu.VMEM((2, rows, model), bf16),
            pltpu.VMEM((2, rows, model), bf16),
            own(bf16),
            own(bf16),
            pltpu.VMEM((2, rows, model), bf16),
            pltpu.VMEM((2, rows, model), bf16),
            own(bf16),
            own(bf16),
            own(bf16),
            pltpu.VMEM((2, 16, model), f32),
            own(f32),
            pltpu.VMEM((size, 3 * width), f32),
            pltpu.VMEM((size, width), f32),
            pltpu.VMEM((6, 8, model), f32),
            pltpu.VMEM((5, 8, model), f32),
            DMA((6, n - 1)),
            DMA((6, n - 1)),
            DMA((6,)),
            DMA((6,)),
            DMA((5,)),
            DMA((5,)),
            DMA((16,)),
        ],
        compiler_params=pltpu.CompilerParams(collective_id=4, has_side_effects=True, vmem_limit_bytes=62 << 20),
        cost_estimate=pl.CostEstimate(flops=14 * seq * model * width, bytes_accessed=40 << 20, transcendentals=0),
        name="leave",
    )(normed, dlin, qkv.reshape(n, size, 3 * width), mixed, resid, datt, x, attended, ffn.reshape(4, rows, model), small, vec)


def norm_forward(rows):
    center = rows - jnp.mean(rows, axis=-1, keepdims=True)
    rstd = lax.rsqrt(jnp.mean(center * center, axis=-1, keepdims=True) + EPS)
    return center * rstd, rstd


def norm_backward(grad_out, normal, rstd, gain):
    scaled = grad_out * gain
    return rstd * (
        scaled
        - jnp.mean(scaled, axis=-1, keepdims=True)
        - normal * jnp.mean(scaled * normal, axis=-1, keepdims=True)
    )


def local(
    layer_input,
    segments,
    positions,
    first_gain,
    first_shift,
    query_weight,
    key_weight,
    value_weight,
    query_bias,
    key_bias,
    value_bias,
    out_weight,
    second_gain,
    second_shift,
    gate_weight,
    up_weight,
    down_weight,
    out_grad,
):
    ring = Ring()
    n = ring.n
    width = query_weight.shape[1]
    heads = width // HD
    model = layer_input.shape[1]

    bias_key = jnp.pad(key_bias.astype(f32), ((0, 0), (0, HD - ROT))).reshape(-1)
    part = model // n
    per = HD // n
    if ring.ring:
        lanes = 128
        small = jnp.concatenate(
            [first_gain, first_shift, second_gain, second_shift, query_bias.reshape(-1), value_bias.reshape(-1)]
        )
        small = jnp.pad(small.reshape(-1, lanes), ((0, 16 - small.shape[0] // lanes), (0, 0)))
        normed, g_full, qkv, out_t, lin, small = enter(
            layer_input, out_grad, query_weight, key_weight, value_weight, out_weight, small, n
        )
        g_full = g_full.reshape(-1, model)
        qkv = qkv.reshape(model, -1)
        out_t = out_t.reshape(model, -1)
        packed_small = small
        small = small.reshape(n, -1)[:, : 4 * part + 2 * heads * per]
    else:
        x_full = tensor_gather(layer_input)
        g_full = tensor_gather(out_grad, after=x_full)
        small = jnp.concatenate(
            [first_gain, first_shift, second_gain, second_shift, query_bias.reshape(-1), value_bias.reshape(-1)]
        )
        small = lax.all_gather(small.reshape(1, -1), "dp", axis=0, tiled=True)
        qkv, _ = ring.gather(jnp.concatenate([query_weight, key_weight, value_weight], axis=1))
        out_t, _ = ring.gather(out_weight.T)
        gate, _ = ring.gather(gate_weight)
        up, _ = ring.gather(up_weight)
        down_t, _ = ring.gather(down_weight.T)
    gain_one, shift_one, gain_two, shift_two = (
        small[:, i * part : (i + 1) * part].reshape(model).astype(f32) for i in range(4)
    )
    biases = small[:, 4 * part :].reshape(n, 2, heads, per).transpose(1, 2, 0, 3).reshape(2, width).astype(f32)
    bias_lin = jnp.concatenate([biases[0], bias_key, biases[1]])
    if not ring.ring:
        hat_full, _ = norm_forward(x_full.astype(f32))
        normed = (hat_full * gain_one + shift_one).astype(bf16)
        lin = dot(qkv, normed, ((0,), (1,)))

    freqs = jnp.exp(-(2.0 / ROT) * jnp.arange(HALF).astype(f32) * math.log(10000.0))
    angles = freqs[:, None] * positions.astype(f32)[None, :]
    cosine, sine = jnp.cos(angles), jnp.sin(angles)
    index = jnp.arange(segments.shape[0], dtype=jnp.int32)
    allowed = (index[:, None] <= index[None, :]) & (segments[:, None] == segments[None, :])
    bias = jnp.where(allowed, 0.0, NEG).astype(f32)
    rows = layer_input.astype(f32)
    if ring.ring:
        q_rot, k_rot, v_heads, logs, mixed, attended, second, gate, up, hidden, ffn, grad_gate, grad_up = middle(
            lin, bias_lin, cosine, sine, segments, layer_input, out_t, packed_small, gate_weight, up_weight, down_weight, g_full, n
        )
        second, gate, up = second.reshape(-1, model), gate.reshape(model, -1), up.reshape(model, -1)
        hidden, ffn = hidden.reshape(second.shape[0], -1), ffn.reshape(-1, model)
        grad_gate, grad_up = grad_gate.reshape(hidden.shape), grad_up.reshape(hidden.shape)
    else:
        mixed, q_rot, k_rot, v_heads, logs = attend_forward(lin + bias_lin[:, None], cosine, sine, bias)
        attended = rows + tensor_scatter(dot(mixed, out_t, ((1,), (1,))))

        hat_two, rstd_two = norm_forward(attended)
        second = tensor_gather((hat_two * gain_two + shift_two).astype(bf16))
        gate_lin = dot(second, gate, ((1,), (0,)))
        up_lin = dot(second, up, ((1,), (0,)))
        sigma = jax.nn.sigmoid(gate_lin)
        activated = gate_lin * sigma
        hidden = (activated * up_lin).astype(bf16)
        ffn = dot(hidden, down_t, ((1,), (1,)))
        grad_hidden = dot(g_full, down_t, ((1,), (0,)))
        grad_gate = (grad_hidden * up_lin * sigma * (1.0 + gate_lin * (1.0 - sigma))).astype(bf16)
        grad_up = (grad_hidden * activated).astype(bf16)
    if ring.ring:
        down_sum, gate_sum, up_sum, grad_attended, residual, grad_lin, vec = back(
            grad_gate, grad_up, hidden, second, g_full, gate, up, attended, packed_small, out_t,
            q_rot, k_rot, v_heads, logs, cosine, sine, segments, n
        )
        layer_output, input_grad, query_sum, key_sum, value_sum, out_sum, vec = leave(
            normed, grad_lin, qkv, mixed, residual.reshape(-1, model), grad_attended, layer_input, attended, ffn, packed_small, vec, n
        )
        down_sum, out_sum = down_sum.T, out_sum.T
        vectors = vec[:4]
        sums = vec[4, : 3 * width].reshape(3, width)
    else:
        down_grad = dot(g_full, hidden, ((0,), (0,)))
        grad_second = tensor_scatter(dot(grad_gate, gate, ((1,), (1,))) + dot(grad_up, up, ((1,), (1,))))
        gate_grad = dot(second, grad_gate, ((0,), (0,)))
        up_grad = dot(second, grad_up, ((0,), (0,)))
        down_sum = ring.scatter(down_grad).T
        gate_sum = ring.scatter(gate_grad)
        up_sum = ring.scatter(up_grad)
        grad_attended = out_grad.astype(f32) + norm_backward(grad_second, hat_two, rstd_two, gain_two)
        residual = tensor_gather(grad_attended.astype(bf16))
        grad_mixed = dot(out_t, residual, ((0,), (1,))).astype(bf16)
        dq, dk, dv, sums = attend_backward(q_rot, k_rot, v_heads, grad_mixed, logs, cosine, sine, bias)
        grad_lin = jnp.concatenate([dq, dk, dv], axis=0)
        sums = sums.reshape(width, 128)[:, :3]
        out_sum = ring.scatter(dot(residual, mixed, ((0,), (0,)))).T
        qkv_sum = ring.scatter(dot(normed, grad_lin, ((0,), (1,))))
        query_sum, key_sum, value_sum = (qkv_sum[:, i * width : (i + 1) * width] for i in range(3))
        grad_first = tensor_scatter(dot(grad_lin, qkv, ((0,), (1,))))
        hat_one, rstd_one = norm_forward(rows)
        input_grad = grad_attended + norm_backward(grad_first, hat_one, rstd_one, gain_one)
        layer_output = (attended + tensor_scatter(ffn.astype(f32))).astype(bf16)
        vectors = jnp.stack(
            [
                jnp.sum(grad_first * hat_one, axis=0),
                jnp.sum(grad_first, axis=0),
                jnp.sum(grad_second * hat_two, axis=0),
                jnp.sum(grad_second, axis=0),
            ]
        )
        packed = sum_all(jnp.concatenate([sum_all(vectors, ["tensor"]).reshape(-1), sums.T.reshape(-1)]), ["dp"])
        vectors, sums = packed[: 4 * model].reshape(4, model), packed[4 * model :].reshape(3, width)

    each = model // (n * lax.axis_size("tensor"))
    at = ring.me * lax.axis_size("tensor") + lax.axis_index("tensor")
    vectors = lax.dynamic_slice(vectors.reshape(4, -1, each), (0, at, 0), (4, 1, each))[:, 0]
    sums = sums.reshape(3, heads, n, per)
    mine = lax.dynamic_slice(sums, (0, 0, ring.me, 0), (3, heads, 1, per))[:, :, 0]
    key_bias_sum = sums[1].reshape(heads, HD)[:, :ROT]

    return (
        layer_output,
        input_grad,
        vectors[0],
        vectors[1],
        query_sum,
        key_sum,
        value_sum,
        mine[0],
        key_bias_sum,
        mine[2],
        out_sum,
        vectors[2],
        vectors[3],
        gate_sum,
        up_sum,
        down_sum,
    )


def solution(mesh):
    both = ("dp", "tensor")
    return jax.shard_map(
        local,
        mesh=mesh,
        in_specs=(
            P(both, None),
            P("dp"),
            P("dp"),
            P("dp"),
            P("dp"),
            P("dp", "tensor"),
            P("dp", "tensor"),
            P("dp", "tensor"),
            P("tensor", "dp"),
            P("tensor", None),
            P("tensor", "dp"),
            P("tensor", "dp"),
            P("dp"),
            P("dp"),
            P("dp", "tensor"),
            P("dp", "tensor"),
            P("tensor", "dp"),
            P(both, None),
        ),
        out_specs=(
            P(both, None),
            P(both, None),
            P(both),
            P(both),
            P("dp", "tensor"),
            P("dp", "tensor"),
            P("dp", "tensor"),
            P("tensor", "dp"),
            P("tensor", None),
            P("tensor", "dp"),
            P("tensor", "dp"),
            P(both),
            P(both),
            P("dp", "tensor"),
            P("dp", "tensor"),
            P("tensor", "dp"),
        ),
        check_vma=False,
    )
```

```python
import math

import jax
import jax.numpy as jnp
from jax import lax
from jax.experimental import pallas as pl
from jax.experimental.pallas import tpu as pltpu
from jax.sharding import PartitionSpec as P

HD = 64
ROT = 16
SEQ = 1024
HALF = ROT // 2
SCALE = HD ** (-0.5)

EPS = 1e-05
NEG = -1e30
QB = 256
f32 = jnp.float32
bf16 = jnp.bfloat16


def barrier(value, after):
    return lax.optimization_barrier((value, after))[0]


class Ring:
    def __init__(self):
        self.n = lax.axis_size("dp")
        self.ring = self.n == 8 and lax.axis_size("tensor") == 4
        order = list(range(0, self.n, 2)) + list(range(self.n - 1, 0, -2))
        self.up = [(order[i], order[(i + 1) % self.n]) for i in range(self.n)]
        self.down = [(b, a) for a, b in self.up]
        me = lax.axis_index("dp")
        self.me = me
        self.pos = jnp.where(me % 2 == 0, me // 2, self.n - 1 - (me - 1) // 2)

    def owner(self, offset):
        p = (self.pos + offset + 2 * self.n) % self.n
        return jnp.where(p < self.n // 2, 2 * p, 2 * (self.n - 1 - p) + 1)

    def gather(self, shard, pieces=1, after=None):
        n = self.n
        rows, cols = shard.shape
        if not self.ring:
            return lax.all_gather(shard, "dp", axis=0, tiled=True), [shard] * n
        if after is not None:
            shard = barrier(shard, after)
        full = jnp.zeros((n, rows, cols), shard.dtype)
        full = lax.dynamic_update_slice(full, shard[None], (self.me, 0, 0))
        size = rows // (2 * pieces)
        lanes = []
        for k in range(2 * pieces):
            lanes.append([k % 2, k * size, shard[k * size : (k + 1) * size]])
        marks = []
        for step in range(1, n):
            for lane in lanes:
                way, base, block = lane
                block = lax.ppermute(block, "dp", self.down if way else self.up)
                lane[2] = block
                whose = self.owner(step if way else -step)
                full = lax.dynamic_update_slice(full, block[None], (whose, base, 0))
            marks.append(lanes[-1][2])
        return full.reshape(n * rows, cols), marks

    def scatter(self, partial, pieces=1, after=None):
        n = self.n
        if not self.ring:
            return lax.psum_scatter(partial.astype(bf16), "dp", scatter_dimension=0, tiled=True).astype(f32)
        cols = partial.shape[1]
        rows = partial.shape[0] // n
        partial = partial.reshape(n, rows, cols)
        size = rows // (2 * pieces)
        done = []
        for k in range(2 * pieces):
            way = k % 2

            def block(step):
                whose = self.owner(1 + step if way else -1 - step)
                return lax.dynamic_slice(partial, (whose, k * size, 0), (1, size, cols))[0].astype(f32)

            moving = block(0)
            for step in range(1, n):
                got = lax.ppermute(moving.astype(bf16), "dp", self.down if way else self.up)
                moving = got.astype(f32) + block(step)
            done.append(moving)
        return jnp.concatenate(done, axis=0)


CORE = [(0, 1), (1, 0), (2, 3), (3, 2)]
CHIP = [(0, 2), (2, 0), (1, 3), (3, 1)]


def tensor_gather(rows, after=None):
    if lax.axis_size("tensor") != 4:
        return lax.all_gather(rows, "tensor", axis=0, tiled=True)
    if after is not None:
        rows = barrier(rows, after)
    t = lax.axis_index("tensor")
    far = lax.ppermute(rows, "tensor", CHIP)
    near = lax.ppermute(rows, "tensor", CORE)
    last = lax.ppermute(far, "tensor", CORE)
    full = jnp.zeros((4,) + rows.shape, rows.dtype)
    for flip, block in ((0, rows), (1, near), (2, far), (3, last)):
        full = lax.dynamic_update_slice(full, block[None], (t ^ flip, 0, 0))
    return full.reshape(4 * rows.shape[0], rows.shape[1])


def tensor_scatter(partial):
    if lax.axis_size("tensor") != 4:
        return lax.psum_scatter(partial.astype(bf16), "tensor", scatter_dimension=0, tiled=True).astype(f32)
    t = lax.axis_index("tensor")
    rows = partial.shape[0] // 4
    blocks = partial.reshape(4, rows, partial.shape[1])

    def block(flip):
        return lax.dynamic_slice(blocks, (t ^ flip, 0, 0), (1,) + blocks.shape[1:])[0]

    other = lax.ppermute(block(3).astype(bf16), "tensor", CORE)
    own = lax.ppermute(block(1).astype(bf16), "tensor", CORE)
    far = lax.ppermute((block(2) + other.astype(f32)).astype(bf16), "tensor", CHIP)
    return block(0) + own.astype(f32) + far.astype(f32)


def sum_all(vector, axes):
    for axis in axes:
        n = lax.axis_size(axis)
        if n & (n - 1):
            vector = lax.psum(vector, axis)
            continue
        step = 1
        while step < n:
            vector = vector + lax.ppermute(vector, axis, [(i, i ^ step) for i in range(n)])
            step *= 2
    return vector


def rotate(rows, cosine, sine, direction):
    first, second = rows[:HALF], rows[HALF:ROT]
    return jnp.concatenate(
        [first * cosine - direction * second * sine, second * cosine + direction * first * sine, rows[ROT:]], axis=0
    )


def dot(a, b, dims):
    return lax.dot_general(a, b, ((dims[0], dims[1]), ((), ())), preferred_element_type=f32)


def forward_kernel(q_ref, k_ref, v_ref, cos_ref, sin_ref, bias_ref, mixed_ref, q_out, k_out, v_out, log_ref):
    seq = q_ref.shape[1]
    cosine, sine = cos_ref[...], sin_ref[...]
    v_all = v_ref[...].astype(bf16)
    v_out[...] = v_all
    parts = []
    for head in range(q_ref.shape[0] // HD):
        rows = slice(head * HD, (head + 1) * HD)
        q = rotate(q_ref[rows, :], cosine, sine, 1.0).astype(bf16)
        k = rotate(k_ref[rows, :], cosine, sine, 1.0).astype(bf16)
        q_out[rows, :] = q
        k_out[rows, :] = k
        keys = k.T
        values = v_all[rows, :]
        q = q * jnp.asarray(SCALE, bf16)
        cols = []
        for start in range(0, seq, QB):
            end = start + QB
            scores = dot(keys[:end], q[:, start:end], ((1,), (0,))) + bias_ref[:end, start:end]
            top = jnp.max(scores, axis=0, keepdims=True)
            expo = jnp.exp(scores - top)
            total = jnp.sum(expo, axis=0, keepdims=True)
            probs = (expo * (1.0 / total)).astype(bf16)
            cols.append(dot(values[:, :end], probs, ((1,), (0,))).astype(bf16))
            log_ref[0, head : head + 1, start:end] = top + jnp.log(total)
        parts.append(jnp.concatenate(cols, axis=1))
    mixed_ref[...] = jnp.concatenate(parts, axis=0).T


def attend_forward(lin, cosine, sine, bias):
    width, seq = lin.shape[0] // 3, lin.shape[1]
    pair = 2 * HD
    count = width // pair
    outs = []
    block = lambda base: pl.BlockSpec((pair, seq), lambda i: (base * count + i, 0))
    whole = lambda shape: pl.BlockSpec(shape, lambda i: (0, 0))
    return pl.pallas_call(
        forward_kernel,
        grid=(count,),
        in_specs=[block(0), block(1), block(2), whole(cosine.shape), whole(sine.shape), whole(bias.shape)],
        out_specs=[
            pl.BlockSpec((seq, pair), lambda i: (0, i)),
            pl.BlockSpec((pair, seq), lambda i: (i, 0)),
            pl.BlockSpec((pair, seq), lambda i: (i, 0)),
            pl.BlockSpec((pair, seq), lambda i: (i, 0)),
            pl.BlockSpec((1, 2, seq), lambda i: (i, 0, 0)),
        ],
        out_shape=[
            jax.ShapeDtypeStruct((seq, width), bf16),
            jax.ShapeDtypeStruct((width, seq), bf16),
            jax.ShapeDtypeStruct((width, seq), bf16),
            jax.ShapeDtypeStruct((width, seq), bf16),
            jax.ShapeDtypeStruct((count, 2, seq), f32),
        ],
        compiler_params=pltpu.CompilerParams(vmem_limit_bytes=48 << 20),
        cost_estimate=pl.CostEstimate(
            flops=4 * width * seq * seq, bytes_accessed=30 << 20, transcendentals=width // HD * seq * seq
        ),
        name="attend_forward",
    )(lin, lin, lin, cosine, sine, bias)


def backward_kernel(q_ref, k_ref, v_ref, d_ref, log_ref, cos_ref, sin_ref, bias_ref, dq_out, dk_out, dv_out, sums_ref, dk_acc, dv_acc):
    seq = q_ref.shape[1]
    cosine, sine = cos_ref[...], sin_ref[...]
    for head in range(q_ref.shape[0] // HD):
        rows = slice(head * HD, (head + 1) * HD)
        q, k, v, d = q_ref[rows, :], k_ref[rows, :], v_ref[rows, :], d_ref[rows, :]
        keys, values = k.T, v.T
        q_small = q * jnp.asarray(SCALE, bf16)
        dk_acc[...] = jnp.zeros_like(dk_acc)
        dv_acc[...] = jnp.zeros_like(dv_acc)
        cols = []
        for start in range(0, seq, QB):
            end = start + QB
            here = slice(start, end)
            scores = dot(keys[:end], q_small[:, here], ((1,), (0,))) + bias_ref[:end, here]
            probs = jnp.exp(scores - log_ref[0, head : head + 1, here])
            grad = dot(values[:end], d[:, here], ((1,), (0,)))
            both = probs * grad
            inner = jnp.sum(both, axis=0, keepdims=True)
            grad = ((both - probs * inner) * SCALE).astype(bf16)
            probs = probs.astype(bf16)
            cols.append(dot(k[:, :end], grad, ((1,), (0,))))
            dk_acc[:, :end] += dot(q[:, here], grad, ((1,), (1,)))
            dv_acc[:, :end] += dot(d[:, here], probs, ((1,), (1,)))
        dq = rotate(jnp.concatenate(cols, axis=1), cosine, sine, -1.0)
        dk = rotate(dk_acc[...], cosine, sine, -1.0)
        dv = dv_acc[...]
        for part, (out, value) in enumerate(((dq_out, dq), (dk_out, dk), (dv_out, dv))):
            out[rows, :] = value.astype(bf16)
            sums_ref[0, rows, part : part + 1] = jnp.sum(value, axis=1, keepdims=True)


def attend_backward(q, k, v, d, logs, cosine, sine, bias):
    width, seq = q.shape
    pair = 2 * HD
    count = width // pair
    block = pl.BlockSpec((pair, seq), lambda i: (i, 0))
    whole = lambda shape: pl.BlockSpec(shape, lambda i: (0, 0))
    return pl.pallas_call(
        backward_kernel,
        grid=(count,),
        in_specs=[block] * 4
        + [pl.BlockSpec((1, 2, seq), lambda i: (i, 0, 0)), whole(cosine.shape), whole(sine.shape), whole(bias.shape)],
        out_specs=[block] * 3 + [pl.BlockSpec((1, pair, 128), lambda i: (i, 0, 0))],
        out_shape=[jax.ShapeDtypeStruct((width, seq), bf16)] * 3 + [jax.ShapeDtypeStruct((count, pair, 128), f32)],
        scratch_shapes=[pltpu.VMEM((HD, seq), f32), pltpu.VMEM((HD, seq), f32)],
        compiler_params=pltpu.CompilerParams(vmem_limit_bytes=48 << 20),
        cost_estimate=pl.CostEstimate(
            flops=10 * width * seq * seq, bytes_accessed=30 << 20, transcendentals=width // HD * seq * seq
        ),
        name="attend_backward",
    )(q, k, v, d, logs, cosine, sine, bias)


MESH = pl.DeviceIdType.MESH
HBM = pl.BlockSpec(memory_space=pl.ANY)
VMEM = pl.BlockSpec(memory_space=pltpu.VMEM)
DMA = pltpu.SemaphoreType.DMA


class Place:
    def __init__(self, n):
        self.n = n
        self.me = lax.axis_index("dp")
        self.t = lax.axis_index("tensor")
        odd = lax.rem(self.me, 2)
        half = lax.div(self.me, 2)
        self.pos = jnp.where(odd == 0, half, n - 1 - half)
        self.up = self.owner(1)
        self.down = self.owner(-1)
        self.core = self.t + 1 - 2 * lax.rem(self.t, 2)
        self.chip = lax.rem(self.t + 2, 4)
        self.cross = lax.rem(self.core + 2, 4)

    def owner(self, offset):
        p = lax.rem(self.pos + (offset + 2 * self.n), self.n)
        return jnp.where(p < self.n // 2, 2 * p, 2 * (self.n - 1 - p) + 1)

    def barrier(self, dp, tensor):
        sem = pltpu.get_barrier_semaphore()
        for there in dp:
            pl.semaphore_signal(sem, inc=1, device_id={"dp": there}, device_id_type=MESH)
        for there in tensor:
            pl.semaphore_signal(sem, inc=1, device_id={"tensor": there}, device_id_type=MESH)
        pl.semaphore_wait(sem, len(dp) + len(tensor))


class Lane:
    def __init__(self, place, full, base, size, way, send, recv):
        self.place, self.full, self.base, self.size, self.way = place, full, base, size, way
        self.send, self.recv = send, recv

    def whose(self, step):
        return self.place.owner(step if self.way else -step)

    def copy(self, step, whose):
        piece = self.full.at[whose, pl.ds(self.base, self.size)]
        return pltpu.make_async_remote_copy(
            src_ref=piece,
            dst_ref=piece,
            send_sem=self.send.at[step - 1],
            recv_sem=self.recv.at[step - 1],
            device_id={"dp": self.place.down if self.way else self.place.up},
            device_id_type=MESH,
        )

    def start(self, step):
        self.copy(step, self.whose(step - 1)).start()

    def arrive(self, step):
        self.copy(step, self.whose(step)).wait_recv()

    def finish(self):
        for step in range(1, self.place.n):
            self.copy(step, self.whose(step - 1)).wait_send()


class Exchange:
    def __init__(self, send, recv):
        self.send, self.recv = send, recv

    def copy(self, number, src, dst, there):
        return pltpu.make_async_remote_copy(
            src_ref=src,
            dst_ref=dst,
            send_sem=self.send.at[number],
            recv_sem=self.recv.at[number],
            device_id={"tensor": there},
            device_id_type=MESH,
        )


def row_norm(value, gain, shift):
    center = value - jnp.mean(value, axis=1, keepdims=True)
    rstd = lax.rsqrt(jnp.mean(center * center, axis=1, keepdims=True) + EPS)
    return center * rstd * gain + shift


def lane_vector(full, first, count):
    pieces = [full[d, r : r + 1, :] for d in range(full.shape[0]) for r in range(first, first + count)]
    return jnp.concatenate(pieces, axis=1)


def enter_kernel(
    n,
    x_ref, g_ref, wq, wk, wv, wo, gain_one, shift_one, gain_two, shift_two, bias_q, bias_v,
    normed_out, g_out, qkv_out, out_out, lin_out, small_full,
    x_full, normed, left, right, outs, lin, small_ref,
    small_send, small_recv, send, recv, x_send, x_recv, local, stored, lin_stored,
):
    place = Place(n)
    rows = x_ref.shape[0]
    size = wq.shape[0]
    width = wq.shape[1]
    half = width // 2
    me, t = place.me, place.t
    loads = [
        pltpu.make_async_copy(wq, left.at[me, :, pl.ds(0, width)], local.at[0]),
        pltpu.make_async_copy(wk.at[:, pl.ds(0, half)], left.at[me, :, pl.ds(width, half)], local.at[1]),
        pltpu.make_async_copy(wk.at[:, pl.ds(half, half)], right.at[me, :, pl.ds(0, half)], local.at[2]),
        pltpu.make_async_copy(wv, right.at[me, :, pl.ds(half, width)], local.at[3]),
        pltpu.make_async_copy(x_ref, x_full.at[t], local.at[4]),
        pltpu.make_async_copy(g_ref, g_out.at[t], local.at[5]),
    ]
    for load in loads:
        load.start()
    outs[me] = wo[...].T
    count = small_ref.shape[1]
    each = size // count
    small_ref[...] = jnp.zeros_like(small_ref)
    for i, vector in enumerate((gain_one, shift_one, gain_two, shift_two)):
        for r in range(each):
            small_ref[i * each + r, :] = vector[r * count : (r + 1) * count].astype(f32)
    heads, per = bias_q.shape
    small_ref[4 * each : 4 * each + heads, 0:per] = bias_q[...].astype(f32)
    small_ref[4 * each : 4 * each + heads, per : 2 * per] = bias_v[...].astype(f32)
    small_full[me] = small_ref[...]
    place.barrier([place.owner(k) for k in range(1, n)], [place.core, place.chip])

    smalls = []
    for k in range(1, n):
        smalls.append(
            pltpu.make_async_remote_copy(
                src_ref=small_ref,
                dst_ref=small_full.at[me],
                send_sem=small_send.at[k - 1],
                recv_sem=small_recv.at[k - 1],
                device_id={"dp": place.owner(k)},
                device_id_type=MESH,
            )
        )
        smalls[-1].start()

    swap = Exchange(x_send, x_recv)
    to_chip = swap.copy(0, x_ref, x_full.at[t], place.chip)
    to_core = swap.copy(1, x_ref, x_full.at[t], place.core)
    relay = swap.copy(2, x_full.at[place.chip], x_full.at[place.chip], place.core)
    g_chip = swap.copy(3, g_ref, g_out.at[t], place.chip)
    g_core = swap.copy(4, g_ref, g_out.at[t], place.core)
    g_relay = swap.copy(5, g_out.at[place.chip], g_out.at[place.chip], place.core)
    to_chip.start()
    to_core.start()
    for load in loads[:4]:
        load.wait()
    lanes = []
    for number, (full, base, count, way) in enumerate(
        (
            (left, 0, size // 2, 0),
            (right, 0, size // 2, 1),
            (left, size // 2, size // 2, 0),
            (right, size // 2, size // 2, 1),
            (outs, 0, size // 2, 0),
            (outs, size // 2, size // 2, 1),
        )
    ):
        lanes.append(Lane(place, full, base, count, way, send.at[number], recv.at[number]))

    def store(step):
        whose, other = place.owner(-step), place.owner(step)
        if step == n:
            return []
        return [
            pltpu.make_async_copy(left.at[whose], qkv_out.at[whose, :, pl.ds(0, width + half)], stored.at[0, step]),
            pltpu.make_async_copy(right.at[other], qkv_out.at[other, :, pl.ds(width + half, width + half)], stored.at[1, step]),
            pltpu.make_async_copy(outs.at[whose, pl.ds(0, size // 2)], out_out.at[whose, pl.ds(0, size // 2)], stored.at[2, step]),
            pltpu.make_async_copy(
                outs.at[other, pl.ds(size // 2, size // 2)], out_out.at[other, pl.ds(size // 2, size // 2)], stored.at[3, step]
            ),
        ]

    writes = []

    def tick(step):
        for lane in lanes:
            if step > 1:
                lane.arrive(step - 1)
            if step < n:
                lane.start(step)
        for write in store(step - 1):
            write.start()
            writes.append(write)

    gain = shift = None

    def norm(block):
        @pl.loop(0, rows // 16)
        def _(i):
            here = pl.ds(pl.multiple_of(i * 16, 16), 16)
            there = pl.ds(pl.multiple_of(block * rows + i * 16, 16), 16)
            normed[there, :] = row_norm(x_full[block, here, :].astype(f32), gain, shift).astype(bf16)

    def project(step):
        for full, whose, base in ((left, place.owner(-step), 0), (right, place.owner(step), width + half)):
            xs = normed[:, pl.ds(pl.multiple_of(whose * size, size), size)]
            for j in range(0, width + half, 256):
                part = dot(full[whose, :, j : j + 256].T, xs, ((1,), (1,)))
                where = slice(base + j, base + j + 256)
                if step == 0:
                    lin[where, :] = part
                else:
                    lin[where, :] += part
                if step == n - 1:
                    lin_store(base + j).start()

    def lin_store(first):
        at = pl.ds(first, 256)
        return pltpu.make_async_copy(lin.at[at], lin_out.at[at], lin_stored.at[first // 256])

    tick(1)
    loads[4].wait()
    for small in smalls:
        small.wait_recv()
    gain = lane_vector(small_full, 0, each)
    shift = lane_vector(small_full, each, each)
    norm(t)
    to_core.wait_recv()
    norm(place.core)
    tick(2)
    tick(3)
    to_chip.wait_recv()
    relay.start()
    g_chip.start()
    g_core.start()
    norm(place.chip)
    tick(4)
    relay.wait_recv()
    norm(place.cross)
    normed_store = pltpu.make_async_copy(normed, normed_out, local.at[6])
    normed_store.start()
    project(0)
    done = 1
    for step in range(5, n):
        tick(step)
        while done < min(step - 1, 2 * (step - 4) + 1):
            project(done)
            done += 1
    g_chip.wait_recv()
    g_relay.start()
    while done < n - 1:
        project(done)
        done += 1
    tick(n)
    project(n - 1)
    for copy in (to_chip, to_core, relay, g_chip, g_core, g_relay):
        copy.wait_send()
    g_core.wait_recv()
    g_relay.wait_recv()
    for small in smalls:
        small.wait_send()
    for lane in lanes:
        lane.finish()
    loads[5].wait()
    for write in writes:
        write.wait()
    normed_store.wait()
    for first in range(0, 3 * width, 256):
        lin_store(first).wait()


def enter(x, g, wq, wk, wv, wo, vectors, biases, n):
    rows, model = x.shape
    size, width = wq.shape
    big = 3 * width // 2
    kernel = lambda *refs: enter_kernel(n, *refs)
    return pl.pallas_call(
        kernel,
        in_specs=[HBM] * 5 + [VMEM] * 7,
        out_specs=[HBM, HBM, HBM, HBM, HBM, VMEM],
        out_shape=[
            jax.ShapeDtypeStruct((4 * rows, model), bf16),
            jax.ShapeDtypeStruct((4, rows, model), bf16),
            jax.ShapeDtypeStruct((n, size, 3 * width), bf16),
            jax.ShapeDtypeStruct((n, size, width), bf16),
            jax.ShapeDtypeStruct((3 * width, 4 * rows), f32),
            jax.ShapeDtypeStruct((n, 16, 128), f32),
        ],
        scratch_shapes=[
            pltpu.VMEM((4, rows, model), bf16),
            pltpu.VMEM((4 * rows, model), bf16),
            pltpu.VMEM((n, size, big), bf16),
            pltpu.VMEM((n, size, big), bf16),
            pltpu.VMEM((n, size, width), bf16),
            pltpu.VMEM((3 * width, 4 * rows), f32),
            pltpu.VMEM((16, 128), f32),
            DMA((n - 1,)),
            DMA((n - 1,)),
            DMA((6, n - 1)),
            DMA((6, n - 1)),
            DMA((6,)),
            DMA((6,)),
            DMA((7,)),
            DMA((4, n)),
            DMA((3 * width // 256,)),
        ],
        compiler_params=pltpu.CompilerParams(collective_id=1, has_side_effects=True, vmem_limit_bytes=56 << 20),
        cost_estimate=pl.CostEstimate(flops=6 * width * rows * 4 * model, bytes_accessed=40 << 20, transcendentals=0),
        name="enter",
    )(x, g, wq, wk, wv, wo, *vectors, *biases)

def attend_pair(pair, lin, bias_ref, cosine, sine, mask, q_all, k_all, v_all, logs, flat, mixed):
    width, seq = q_all.shape

    @pl.loop(0, 2)
    def _(j):
        head = pair * 2 + j
        first = pl.multiple_of(head * HD, HD)
        rows = pl.ds(first, HD)

        def load(part):
            at = pl.ds(pl.multiple_of(part * width + first, HD), HD)
            return lin[at, :] + bias_ref[at, :]

        q = rotate(load(0), cosine, sine, 1.0).astype(bf16)
        k = rotate(load(1), cosine, sine, 1.0).astype(bf16)
        values = load(2).astype(bf16)
        q_all[rows, :] = q
        k_all[rows, :] = k
        v_all[rows, :] = values
        keys = k.T
        q = q * jnp.asarray(SCALE, bf16)
        mine = pl.ds(pl.multiple_of(j * HD, HD), HD)
        for start in range(0, seq, QB):
            end = start + QB
            scores = dot(keys[:end], q[:, start:end], ((1,), (0,))) + mask[:end, start:end]
            top = jnp.max(scores, axis=0, keepdims=True)
            expo = jnp.exp(scores - top)
            total = jnp.sum(expo, axis=0, keepdims=True)
            probs = (expo * (1.0 / total)).astype(bf16)
            flat[mine, start:end] = dot(values[:, :end], probs, ((1,), (0,))).astype(bf16)
            logs[pl.ds(head, 1), start:end] = top + jnp.log(total)

    mixed[:, pair * 2 * HD : (pair + 1) * 2 * HD] = flat[...].T


def build_mask(mask, column, seg_row):
    seq = mask.shape[0]
    segments = seg_row[...].astype(f32)
    column[...] = jnp.broadcast_to(segments, (128, seq)).T

    @pl.loop(0, seq // 32)
    def _(i):
        here = pl.ds(pl.multiple_of(i * 32, 32), 32)
        key = lax.broadcasted_iota(jnp.int32, (32, seq), 0) + i * 32
        query = lax.broadcasted_iota(jnp.int32, (32, seq), 1)
        allowed = (key <= query) & (column[here, 0:1] == segments)
        mask[here, :] = jnp.where(allowed, 0.0, NEG).astype(f32)


def middle_kernel(
    n,
    lin_ref, key_bias, cos_ref, sin_ref, seg_row, x_ref, out_ref, small, gate_w, up_w, down_w, g_ref,
    q_out, k_out, v_out, logs, mixed_out, att_out, second_out, gate_out, up_out, hidden_out, ffn_out, dgate_out, dup_out,
    gate, up, down, second, near_send, near_recv, far_send, far_recv, attended,
    send, recv, x_send, x_recv, local, stored, staged,
):
    place = Place(n)
    t = place.t
    rows, model = x_ref.shape
    size, cols = gate_w.shape
    seq = 4 * rows
    width = out_ref.shape[1]
    loads = [
        pltpu.make_async_copy(gate_w, gate.at[place.me], local.at[0]),
        pltpu.make_async_copy(up_w, up.at[place.me], local.at[1]),
    ]
    for load in loads:
        load.start()
    down[place.me] = down_w[...].T
    place.barrier([place.up, place.down], [place.core, place.chip])
    for load in loads:
        load.wait()

    half, quarter = size // 2, size // 4
    lanes = [
        [Lane(place, full, half * sub, half, way, send.at[2 * way + sub], recv.at[2 * way + sub]) for way, full in ((0, gate), (1, up))]
        for sub in range(2)
    ]
    downs = [
        [
            Lane(place, down, half * way + quarter * sub, quarter, way, send.at[4 + 2 * way + sub], recv.at[4 + 2 * way + sub])
            for way in range(2)
        ]
        for sub in range(2)
    ]

    def write(step):
        gated, upped = place.owner(-step), place.owner(step)
        return [
            pltpu.make_async_copy(gate.at[gated], gate_out.at[gated], stored.at[0, step]),
            pltpu.make_async_copy(up.at[upped], up_out.at[upped], stored.at[1, step]),
        ]

    def tick(kind, step, sub):
        for lane in (downs if kind else lanes)[sub]:
            if step > 1:
                lane.arrive(step - 1)
            if step < n:
                lane.start(step)
        if sub == 1 and not kind:
            for copy in write(step - 1):
                copy.start()

    plan = [(0, step, sub) for step in range(1, n) for sub in range(2)]
    plan += [(1, 1, 0), (1, 1, 1), (0, n, 0), (0, n, 1)]
    plan += [(1, step, sub) for step in range(2, n + 1) for sub in range(2)]
    plan = iter(plan)

    def advance(count=1):
        for _ in range(count):
            tick(*next(plan))

    swap = Exchange(x_send, x_recv)
    near = [swap.copy(i, near_send.at[i], near_recv.at[i], place.core) for i in range(2)]
    far = swap.copy(2, far_send, far_recv, place.chip)
    to_chip = swap.copy(3, second.at[t], second.at[t], place.chip)
    to_core = swap.copy(4, second.at[t], second.at[t], place.core)
    relay = swap.copy(5, second.at[place.chip], second.at[place.chip], place.core)
    copies = near + [far, to_chip, to_core, relay]

    advance(2)

    def attention(lin, mask, q_all, k_all, v_all, flat, mixed, out_t, bias_ref, column):
        pairs = width // (2 * HD)
        fetch = []
        for part in range(3):
            for pair in range(pairs):
                at = pl.ds(part * width + pair * 2 * HD, 2 * HD)
                fetch.append(pltpu.make_async_copy(lin_ref.at[at], lin.at[at], local.at[2 + part * pairs + pair]))
        for pair in range(pairs):
            for part in range(3):
                fetch[part * pairs + pair].start()
        weights = pltpu.make_async_copy(out_ref, out_t, local.at[2 + 3 * pairs])
        weights.start()
        build_mask(mask, column, seg_row)
        heads, per = width // HD, HD // n
        first = small.shape[1] - heads
        turned = [small[d, first:, :].T for d in range(n)]
        keys = key_bias[...].astype(f32).T
        for head in range(heads):
            for part in range(3):
                if part == 1:
                    rest = jnp.zeros((HD - ROT, 1), f32)
                    piece = jnp.concatenate([keys[:, head : head + 1], rest], axis=0)
                else:
                    at = part // 2 * per
                    piece = jnp.concatenate([turned[d][at : at + per, head : head + 1] for d in range(n)], axis=0)
                where = part * width + head * HD
                bias_ref[where : where + HD, :] = piece
        cosine, sine = cos_ref[...], sin_ref[...]
        for pair in range(pairs):
            for part in range(3):
                fetch[part * pairs + pair].wait()
            attend_pair(pair, lin, bias_ref, cosine, sine, mask, q_all, k_all, v_all, logs, flat, mixed)
            advance()
        keep = [
            pltpu.make_async_copy(src, dst, local.at[3 + 3 * pairs + i])
            for i, (src, dst) in enumerate(((q_all, q_out), (k_all, k_out), (v_all, v_out), (mixed, mixed_out)))
        ]
        for copy in keep:
            copy.start()
        weights.wait()

        def project(block, j):
            at = pl.ds(pl.multiple_of(block * rows, rows), rows)
            return dot(mixed[at, :], out_t[j : j + 512, :], ((1,), (1,)))

        for i, block in enumerate((place.cross, place.core)):
            for j in range(0, model, 512):
                near_send[i, :, j : j + 512] = project(block, j).astype(bf16)
            near[i].start()
        near[0].wait_recv()
        for j in range(0, model, 512):
            tile = slice(j, j + 512)
            far_send[:, tile] = (project(place.chip, j) + near_recv[0, :, tile].astype(f32)).astype(bf16)
        far.start()
        own = pltpu.make_async_copy(x_ref, far_copy, local.at[7 + 3 * pairs])
        own.start()
        advance()
        near[1].wait_recv()
        own.wait()
        for j in range(0, model, 512):
            tile = slice(j, j + 512)
            attended[:, tile] = far_copy[:, tile].astype(f32) + project(t, j) + near_recv[1, :, tile].astype(f32)
        for copy in keep:
            copy.wait()

    far_copy = second.at[t]
    pl.run_scoped(
        attention,
        pltpu.VMEM((3 * width, seq), f32),
        pltpu.VMEM((seq, seq), f32),
        pltpu.VMEM((width, seq), bf16),
        pltpu.VMEM((width, seq), bf16),
        pltpu.VMEM((width, seq), bf16),
        pltpu.VMEM((2 * HD, seq), bf16),
        pltpu.VMEM((seq, width), bf16),
        pltpu.VMEM((model, width), bf16),
        pltpu.VMEM((3 * width, 1), f32),
        pltpu.VMEM((seq, 128), f32),
    )
    last = 7 + 3 * (width // (2 * HD))

    def feed(gate_lin, up_lin, grad, hidden, g, stage):
        g_load = pltpu.make_async_copy(g_ref, g, local.at[last + 1])
        g_load.start()
        gate_lin[...] = jnp.zeros_like(gate_lin)
        up_lin[...] = jnp.zeros_like(up_lin)
        grad[...] = jnp.zeros_like(grad)
        count = small.shape[2]
        gain = lane_vector(small, 2 * size // count, size // count)
        shift = lane_vector(small, 3 * size // count, size // count)
        advance(2)
        far.wait_recv()

        @pl.loop(0, rows // 16)
        def _(i):
            here = pl.ds(pl.multiple_of(i * 16, 16), 16)
            value = attended[here, :] + far_recv[here, :].astype(f32)
            attended[here, :] = value
            second[t, here, :] = row_norm(value, gain, shift).astype(bf16)

        to_chip.start()
        to_core.start()
        att_store = pltpu.make_async_copy(attended, att_out, local.at[last + 2])
        att_store.start()

        def add(block, low, high):
            @pl.loop(low, high)
            def _(step):
                for full, total, whose in ((gate, gate_lin, place.owner(-step)), (up, up_lin, place.owner(step))):
                    xs = second[block, :, pl.ds(pl.multiple_of(whose * size, size), size)]
                    total[block] += dot(xs, full[whose], ((1,), (0,)))

        advance()
        ready = 5
        add(t, 0, ready)
        to_core.wait_recv()
        advance()
        add(place.core, 0, ready)
        advance()
        to_chip.wait_recv()
        relay.start()
        add(place.chip, 0, ready)
        relay.wait_recv()
        second_store = pltpu.make_async_copy(second, second_out, local.at[last + 3])
        second_store.start()
        advance()
        add(place.cross, 0, ready)
        every = lambda low, high: pl.loop(0, 4)(lambda block: add(block, low, high))
        every(ready, n - 2)
        advance(2)
        advance()
        every(n - 2, n - 1)
        advance(2)
        every(n - 1, n)

        @pl.loop(0, 4 * rows // 16)
        def _(i):
            block = lax.div(i, rows // 16)
            here = pl.ds(pl.multiple_of(lax.rem(i, rows // 16) * 16, 16), 16)
            value = gate_lin[block, here, :]
            hidden[block, here, :] = (value * jax.nn.sigmoid(value) * up_lin[block, here, :]).astype(bf16)

        hidden_store = pltpu.make_async_copy(hidden, hidden_out, local.at[last + 4])
        hidden_store.start()
        g_load.wait()
        stages = []

        def use(whose):
            number = len(stages)
            slot = number % 2
            if number >= 2:
                stages[number - 2].wait()
            at = pl.ds(pl.multiple_of(whose * size, size), size)

            @pl.loop(0, 4)
            def _(block):
                grad[block] += dot(g[block, :, at], down[whose], ((1,), (0,)))
                stage[slot, block] = dot(hidden[block], down[whose], ((1,), (1,))).astype(bf16)

            stages.append(pltpu.make_async_copy(stage.at[slot], ffn_out.at[:, :, at], staged.at[number]))
            stages[-1].start()

        use(place.me)
        for step in range(2, n + 1):
            advance(2)
            if step - 1 == n // 2:
                use(place.owner(n // 2))
            elif step - 1 > n // 2:
                use(place.owner(step - 1))
                use(place.owner(1 - step))
        for lane in lanes[0] + lanes[1] + downs[0] + downs[1]:
            lane.finish()
        for step in range(n):
            for copy in write(step):
                copy.wait()

        @pl.loop(0, 4 * rows // 16)
        def _(i):
            block = lax.div(i, rows // 16)
            here = pl.ds(pl.multiple_of(lax.rem(i, rows // 16) * 16, 16), 16)
            value = gate_lin[block, here, :]
            sigma = jax.nn.sigmoid(value)
            incoming = grad[block, here, :]
            gate[block, here, :] = (incoming * up_lin[block, here, :] * sigma * (1.0 + value * (1.0 - sigma))).astype(bf16)
            gate[4 + block, here, :] = (incoming * (value * sigma)).astype(bf16)

        final = [
            pltpu.make_async_copy(gate.at[pl.ds(0, 4)], dgate_out, local.at[last + 5]),
            pltpu.make_async_copy(gate.at[pl.ds(4, 4)], dup_out, local.at[last + 6]),
        ]
        for copy in final:
            copy.start()
        for copy in final + stages[-2:] + [hidden_store, second_store, att_store]:
            copy.wait()

    pl.run_scoped(
        feed,
        pltpu.VMEM((4, rows, cols), f32),
        pltpu.VMEM((4, rows, cols), f32),
        pltpu.VMEM((4, rows, cols), f32),
        pltpu.VMEM((4, rows, cols), bf16),
        pltpu.VMEM((4, rows, model), bf16),
        pltpu.VMEM((2, 4, rows, size), bf16),
    )
    for copy in copies:
        copy.wait_send()


def middle(lin, key_bias, cosine, sine, segments, x, out_t, small, gate, up, down, g, n):
    rows, model = x.shape
    size, cols = gate.shape
    seq = 4 * rows
    width = out_t.shape[1]
    heads = width // HD
    shape = jax.ShapeDtypeStruct
    return pl.pallas_call(
        lambda *refs: middle_kernel(n, *refs),
        in_specs=[HBM] + [VMEM] * 4 + [HBM, HBM, VMEM, HBM, HBM, VMEM, HBM],
        out_specs=[HBM, HBM, HBM, VMEM] + [HBM] * 9,
        out_shape=[
            shape((width, seq), bf16),
            shape((width, seq), bf16),
            shape((width, seq), bf16),
            shape((heads, seq), f32),
            shape((seq, width), bf16),
            shape((rows, model), f32),
            shape((4, rows, model), bf16),
            shape((n, size, cols), bf16),
            shape((n, size, cols), bf16),
            shape((4, rows, cols), bf16),
            shape((4, rows, model), bf16),
            shape((4, rows, cols), bf16),
            shape((4, rows, cols), bf16),
        ],
        scratch_shapes=[
            pltpu.VMEM((n, size, cols), bf16),
            pltpu.VMEM((n, size, cols), bf16),
            pltpu.VMEM((n, size, cols), bf16),
            pltpu.VMEM((4, rows, model), bf16),
            pltpu.VMEM((2, rows, model), bf16),
            pltpu.VMEM((2, rows, model), bf16),
            pltpu.VMEM((rows, model), bf16),
            pltpu.VMEM((rows, model), bf16),
            pltpu.VMEM((rows, model), f32),
            DMA((8, n - 1)),
            DMA((8, n - 1)),
            DMA((6,)),
            DMA((6,)),
            DMA((14 + 3 * width // (2 * HD),)),
            DMA((2, n)),
            DMA((n,)),
        ],
        compiler_params=pltpu.CompilerParams(collective_id=2, has_side_effects=True, vmem_limit_bytes=62 << 20),
        cost_estimate=pl.CostEstimate(
            flops=10 * seq * model * cols, bytes_accessed=60 << 20, transcendentals=heads * seq * seq
        ),
        name="middle",
    )(
        lin, key_bias, cosine, sine, segments[None, :],
        x, out_t, small, gate, up, down, g.reshape(4, rows, model),
    )

class Sum:
    def __init__(self, place, slots, way, send, recv):
        self.place, self.slots, self.way, self.send, self.recv = place, slots, way, send, recv

    def whose(self, step):
        return self.place.owner(1 + step if self.way else -1 - step)

    def copy(self, step):
        return pltpu.make_async_remote_copy(
            src_ref=self.slots.at[step - 1],
            dst_ref=self.slots.at[step],
            send_sem=self.send.at[step - 1],
            recv_sem=self.recv.at[step - 1],
            device_id={"dp": self.place.down if self.way else self.place.up},
            device_id_type=MESH,
        )

    def tick(self, step, product, final):
        if step > 0:
            self.copy(step).wait_recv()
        cols = self.slots.shape[2]
        for low in range(0, cols, 512):
            tile = slice(low, min(low + 512, cols))
            part = product(tile)
            if step > 0:
                part = part + self.slots[step, :, tile].astype(f32)
            if step == self.place.n - 1:
                final(tile, part)
            else:
                self.slots[step, :, tile] = part.astype(bf16)
        if step < self.place.n - 1:
            self.copy(step + 1).start()

    def finish(self):
        for step in range(1, self.place.n):
            self.copy(step).wait_send()


def columns_of(left, whose, size, way):
    half = size // 2
    return left[:, pl.ds(pl.multiple_of(whose * size + way * half, half), half)].T


def retreat_pair(pair, q_all, k_all, v_all, d_all, logs, cosine, sine, mask, dk_acc, dv_acc, tmp, vec):
    width, seq = q_all.shape

    @pl.loop(0, 2)
    def _(j):
        head = pair * 2 + j
        rows = pl.ds(pl.multiple_of(head * HD, HD), HD)
        q, k, v, d = q_all[rows, :], k_all[rows, :], v_all[rows, :], d_all[rows, :]
        keys, values = k.T, v.T
        q_small = q * jnp.asarray(SCALE, bf16)
        dk_acc[...] = jnp.zeros_like(dk_acc)
        dv_acc[...] = jnp.zeros_like(dv_acc)
        cols = []
        for start in range(0, seq, QB):
            end = start + QB
            here = slice(start, end)
            scores = dot(keys[:end], q_small[:, here], ((1,), (0,))) + mask[:end, here]
            probs = jnp.exp(scores - logs[pl.ds(head, 1), here])
            grad = dot(values[:end], d[:, here], ((1,), (0,)))
            both = probs * grad
            inner = jnp.sum(both, axis=0, keepdims=True)
            grad = ((both - probs * inner) * SCALE).astype(bf16)
            probs = probs.astype(bf16)
            cols.append(dot(k[:, :end], grad, ((1,), (0,))))
            dk_acc[:, :end] += dot(q[:, here], grad, ((1,), (1,)))
            dv_acc[:, :end] += dot(d[:, here], probs, ((1,), (1,)))
        dq = rotate(jnp.concatenate(cols, axis=1), cosine, sine, -1.0)
        dk = rotate(dk_acc[...], cosine, sine, -1.0)
        dv = dv_acc[...]
        mine = pl.ds(pl.multiple_of(j * HD, HD), HD)
        for part, (out, value) in enumerate(((q_all, dq), (k_all, dk), (v_all, dv))):
            out[rows, :] = value.astype(bf16)
            lanes = value[:, :128]
            for i in range(128, seq, 128):
                lanes = lanes + value[:, i : i + 128]
            tmp[part, mine, :] = lanes

    for part in range(3):
        at = part * width + pair * 2 * HD
        vec[4:5, at : at + 2 * HD] = jnp.sum(tmp[part].T, axis=0, keepdims=True)


def back_kernel(
    n,
    dgate_ref, dup_ref, hidden_ref, second_ref, g_ref, gate_ref, up_ref, att_ref, small, out_ref,
    q_ref, k_ref, v_ref, logs, cos_ref, sin_ref, seg_row,
    down_sum, gate_sum, up_sum, datt_out, resid_out, dlin_out, vec,
    slots, g, second, hidden, dgate, dup, near_send, near_recv, far_send, far_recv, datt, acc,
    send, recv, x_send, x_recv, local,
):
    place = Place(n)
    t = place.t
    rows, model = att_ref.shape
    size, cols = gate_ref.shape[1:]
    seq, width = 4 * rows, out_ref.shape[1]
    loads = [
        pltpu.make_async_copy(src, dst, local.at[i])
        for i, (src, dst) in enumerate(
            ((g_ref, g), (hidden_ref, hidden), (second_ref, second), (dgate_ref, dgate), (dup_ref, dup))
        )
    ]
    for load in loads[:2]:
        load.start()
    place.barrier([place.up, place.down], [place.core, place.chip])

    lanes = [[Sum(place, slots.at[2 * i + way], way, send.at[2 * i + way], recv.at[2 * i + way]) for way in range(2)] for i in range(3)]
    sources = ((g, hidden), (second, dgate), (second, dup))
    sums = (down_sum, gate_sum, up_sum)

    def stored(i):
        return pltpu.make_async_copy(datt.at[:, pl.ds(0, cols)], sums[i], local.at[6 + i])

    def tick(step, i):
        left, right = sources[i]
        if step == n - 1:
            (stored(i - 1) if i else datt_copy()).wait()
        for lane in lanes[i]:

            def final(tile, total):
                datt[lane.way * size // 2 : (lane.way + 1) * size // 2, tile] = total

            block = columns_of(left, lane.whose(step), size, lane.way)
            lane.tick(step, lambda tile: dot(block, right[:, tile], ((1,), (0,))), final)
        if step == n - 1:
            stored(i).start()

    plan = iter([(step, i) for step in range(n) for i in range(3)])

    def advance(count=1):
        for _ in range(count):
            tick(*next(plan))

    def datt_copy():
        return pltpu.make_async_copy(datt, datt_out, local.at[9])

    swap = Exchange(x_send, x_recv)
    near = [swap.copy(i, near_send.at[i], near_recv.at[i], place.core) for i in range(2)]
    far = swap.copy(2, far_send, far_recv, place.chip)
    to_chip = swap.copy(3, far_send, resid_out.at[t], place.chip)
    to_core = swap.copy(4, far_send, resid_out.at[t], place.core)
    relay = swap.copy(5, resid_out.at[place.chip], resid_out.at[place.chip], place.core)
    keep = pltpu.make_async_copy(far_send, resid_out.at[t], local.at[10])
    own = pl.ds(pl.multiple_of(t * rows, rows), rows)

    def feed(gate, up):
        weights = [
            pltpu.make_async_copy(gate_ref, gate, local.at[11]),
            pltpu.make_async_copy(up_ref, up, local.at[12]),
        ]
        loads[0].wait()
        loads[1].wait()
        for load in loads[2:]:
            load.start()
        advance()
        loads[2].wait()
        loads[3].wait()
        for copy in weights:
            copy.start()
        advance()
        loads[4].wait()
        advance()
        for copy in weights:
            copy.wait()

        def product(block, j):
            at = pl.ds(pl.multiple_of(block * rows, rows), rows)
            return dot(dgate[at, :], gate[j], ((1,), (1,))) + dot(dup[at, :], up[j], ((1,), (1,)))

        for i, block in enumerate((place.cross, place.core)):
            for j in range(n):
                near_send[i, :, j * size : (j + 1) * size] = product(block, j).astype(bf16)
            near[i].start()
            advance()
        near[0].wait_recv()
        for j in range(n):
            tile = slice(j * size, (j + 1) * size)
            far_send[:, tile] = (product(place.chip, j) + near_recv[0, :, tile].astype(f32)).astype(bf16)
        far.start()
        advance()
        near[1].wait_recv()
        for j in range(n):
            tile = slice(j * size, (j + 1) * size)
            datt[:, tile] = product(t, j) + near_recv[1, :, tile].astype(f32)
        advance()

    pl.run_scoped(feed, pltpu.VMEM((n, size, cols), bf16), pltpu.VMEM((n, size, cols), bf16))

    def attention(attended, mask, q_all, k_all, v_all, d_all, out_t, dk_acc, dv_acc, tmp, column):
        load_attended = pltpu.make_async_copy(att_ref, attended, local.at[5])
        load_attended.start()
        fetch = [
            pltpu.make_async_copy(src, dst, local.at[13 + i])
            for i, (src, dst) in enumerate(((out_ref, out_t), (q_ref, q_all), (k_ref, k_all), (v_ref, v_all)))
        ]
        for copy in fetch:
            copy.start()
        build_mask(mask, column, seg_row)
        count = small.shape[2]
        gain = lane_vector(small, 2 * size // count, size // count)
        acc[...] = jnp.zeros_like(acc)
        advance(1)
        far.wait_recv()
        far.wait_send()
        load_attended.wait()

        @pl.loop(0, rows // 16)
        def _(i):
            here = pl.ds(pl.multiple_of(i * 16, 16), 16)
            value = attended[here, :]
            center = value - jnp.mean(value, axis=1, keepdims=True)
            rstd = lax.rsqrt(jnp.mean(center * center, axis=1, keepdims=True) + EPS)
            hat = center * rstd
            incoming = datt[here, :] + far_recv[here, :].astype(f32)
            acc[0] += incoming * hat
            acc[1] += incoming
            scaled = incoming * gain
            back = rstd * (
                scaled - jnp.mean(scaled, axis=1, keepdims=True) - hat * jnp.mean(scaled * hat, axis=1, keepdims=True)
            )
            whole = g[pl.ds(pl.multiple_of(t * rows + i * 16, 16), 16), :].astype(f32) + back
            datt[here, :] = whole
            far_send[here, :] = whole.astype(bf16)

        to_chip.start()
        to_core.start()
        keep.start()
        datt_copy().start()
        vec[...] = jnp.zeros_like(vec)
        vec[2:3, :] = jnp.sum(acc[0], axis=0, keepdims=True)
        vec[3:4, :] = jnp.sum(acc[1], axis=0, keepdims=True)
        for copy in near:
            copy.wait_send()
        fetch[0].wait()

        def mix(block, source):
            value = dot(source[...], out_t[...], ((1,), (0,))).astype(bf16)
            d_all[:, pl.ds(pl.multiple_of(block * rows, rows), rows)] = value.T

        def bring(block, slot, number):
            return pltpu.make_async_copy(resid_out.at[block], near_send.at[slot], local.at[number])

        mix(t, far_send)
        advance()
        to_core.wait_recv()
        first = bring(place.core, 0, 17)
        first.start()
        first.wait()
        mix(place.core, near_send.at[0])
        advance(2)
        to_chip.wait_recv()
        relay.start()
        second_block = bring(place.chip, 1, 18)
        second_block.start()
        second_block.wait()
        mix(place.chip, near_send.at[1])
        relay.wait_recv()
        third = bring(place.cross, 0, 19)
        third.start()
        third.wait()
        mix(place.cross, near_send.at[0])
        for copy in fetch[1:]:
            copy.wait()
        cosine, sine = cos_ref[...], sin_ref[...]
        for pair in range(width // (2 * HD)):
            advance()
            retreat_pair(pair, q_all, k_all, v_all, d_all, logs, cosine, sine, mask, dk_acc, dv_acc, tmp, vec)
        final = [
            pltpu.make_async_copy(src, dlin_out.at[pl.ds(i * width, width)], local.at[20 + i])
            for i, src in enumerate((q_all, k_all, v_all))
        ]
        for copy in final:
            copy.start()
        advance(2)
        for copy in final:
            copy.wait()

    pl.run_scoped(
        attention,
        pltpu.VMEM((rows, model), f32),
        pltpu.VMEM((seq, seq), f32),
        pltpu.VMEM((width, seq), bf16),
        pltpu.VMEM((width, seq), bf16),
        pltpu.VMEM((width, seq), bf16),
        pltpu.VMEM((width, seq), bf16),
        pltpu.VMEM((model, width), bf16),
        pltpu.VMEM((HD, seq), f32),
        pltpu.VMEM((HD, seq), f32),
        pltpu.VMEM((3, 2 * HD, 128), f32),
        pltpu.VMEM((seq, 128), f32),
    )
    for step in plan:
        tick(*step)
    for pair in lanes:
        for lane in pair:
            lane.finish()
    for copy in (to_chip, to_core, relay):
        copy.wait_send()
    keep.wait()
    stored(2).wait()


def back(dgate, dup, hidden, second, g, gate, up, attended, small, out_t, q, k, v, logs, cosine, sine, segments, n):
    rows, model = attended.shape
    size, cols = model // n, hidden.shape[1]
    seq, width = 4 * rows, out_t.shape[1]
    shape = jax.ShapeDtypeStruct
    return pl.pallas_call(
        lambda *refs: back_kernel(n, *refs),
        in_specs=[HBM] * 8 + [VMEM] + [HBM] * 4 + [VMEM] * 4,
        out_specs=[HBM] * 6 + [VMEM],
        out_shape=[
            shape((size, cols), f32),
            shape((size, cols), f32),
            shape((size, cols), f32),
            shape((rows, model), f32),
            shape((4, rows, model), bf16),
            shape((3 * width, seq), bf16),
            shape((8, model), f32),
        ],
        scratch_shapes=[
            pltpu.VMEM((6, n, size // 2, cols), bf16),
            pltpu.VMEM((seq, model), bf16),
            pltpu.VMEM((seq, model), bf16),
            pltpu.VMEM((seq, cols), bf16),
            pltpu.VMEM((seq, cols), bf16),
            pltpu.VMEM((seq, cols), bf16),
            pltpu.VMEM((2, rows, model), bf16),
            pltpu.VMEM((2, rows, model), bf16),
            pltpu.VMEM((rows, model), bf16),
            pltpu.VMEM((rows, model), bf16),
            pltpu.VMEM((rows, model), f32),
            pltpu.VMEM((2, 16, model), f32),
            DMA((6, n - 1)),
            DMA((6, n - 1)),
            DMA((6,)),
            DMA((6,)),
            DMA((23,)),
        ],
        compiler_params=pltpu.CompilerParams(collective_id=3, has_side_effects=True, vmem_limit_bytes=62 << 20),
        cost_estimate=pl.CostEstimate(
            flops=14 * seq * model * cols, bytes_accessed=60 << 20, transcendentals=width // HD * seq * seq
        ),
        name="back",
    )(
        dgate, dup, hidden, second, g, gate.reshape(n, size, cols), up.reshape(n, size, cols), attended, small, out_t,
        q, k, v, logs, cosine, sine, segments[None, :],
    )

def leave_kernel(
    n,
    normed_ref, dlin_ref, qkv_ref, mixed_ref, resid_ref, datt_ref, x_ref, att_ref, ffn_ref, small, vec_ref,
    layer_out, input_out, query_sum, key_sum, value_sum, out_sum, vec_out,
    wide, narrow, normed, dlin, qkv, mixed, resid, datt, attended, x, first, near_send, near_recv, far_send, far_recv,
    ffn_own, ffn_recv, ffn_send, ffn_far, layer, acc, totals, wsum, osum, vecs, vec_recv,
    send, recv, x_send, x_recv, v_send, v_recv, local,
):
    place = Place(n)
    t, me = place.t, place.me
    rows, model = att_ref.shape
    size = model // n
    total_cols = dlin_ref.shape[0]
    width = total_cols // 3
    part = total_cols // 2
    loads = [
        pltpu.make_async_copy(src, dst, local.at[i])
        for i, (src, dst) in enumerate(
            (
                (normed_ref, normed),
                (dlin_ref, dlin),
                (resid_ref, resid),
                (mixed_ref, mixed),
                (qkv_ref, qkv),
                (ffn_ref.at[place.chip], ffn_own.at[0]),
                (ffn_ref.at[t], ffn_own.at[1]),
                (att_ref, attended),
                (x_ref, x),
                (datt_ref, datt),
            )
        )
    ]
    for load in loads[:2]:
        load.start()
    hops = [1, 2, 4]
    partners = [me + hop - 2 * hop * lax.rem(lax.div(me, hop), 2) for hop in hops]
    place.barrier([place.up, place.down] + partners, [place.core, place.chip])

    lanes = [
        [Sum(place, wide.at[2 * i + way], way, send.at[2 * i + way], recv.at[2 * i + way]) for way in range(2)] for i in range(2)
    ] + [[Sum(place, narrow.at[way], way, send.at[4 + way], recv.at[4 + way]) for way in range(2)]]

    swap = Exchange(x_send, x_recv)
    near = [swap.copy(i, near_send.at[i], near_recv.at[i], place.core) for i in range(2)]
    far = swap.copy(2, far_send, far_recv, place.chip)
    outs = [swap.copy(3 + i, ffn_ref.at[block], ffn_recv.at[i], place.core) for i, block in enumerate((place.cross, place.core))]
    outs_far = swap.copy(5, ffn_send, ffn_far, place.chip)

    def tick(step, i):
        for lane in lanes[i]:
            half = slice(lane.way * size // 2, (lane.way + 1) * size // 2)
            if i == 2:

                def product(left, tile):
                    return dot(left, mixed[:, tile], ((1,), (0,)))

                def final(tile, total):
                    osum[half, tile] = total

            else:

                def product(left, tile):
                    return dot(left, dlin[part * i + tile.start : part * i + tile.stop, :], ((1,), (1,)))

                def final(tile, total):
                    wsum[half, part * i + tile.start : part * i + tile.stop] = total

            left = columns_of(resid if i == 2 else normed, lane.whose(step), size, lane.way)
            lane.tick(step, lambda tile: product(left, tile), final)

    plan = iter([(step, i) for step in range(n) for i in range(3)])

    def advance(count=1):
        for _ in range(count):
            tick(*next(plan))

    loads[0].wait()
    loads[1].wait()
    for load in loads[2:5]:
        load.start()
    advance(2)
    for load in loads[5:]:
        load.start()
    loads[2].wait()
    loads[3].wait()
    advance()
    loads[4].wait()

    def product(block, use):
        left = dlin[:, pl.ds(pl.multiple_of(block * rows, rows), rows)].T
        for j in range(n):
            use(slice(j * size, (j + 1) * size), dot(left, qkv[j], ((1,), (1,))))

    for i, block in enumerate((place.cross, place.core)):

        def use_near(tile, value):
            near_send[i, :, tile] = value.astype(bf16)

        product(block, use_near)
        near[i].start()
        advance()
    near[0].wait_recv()

    def use_far(tile, value):
        far_send[:, tile] = (value + near_recv[0, :, tile].astype(f32)).astype(bf16)

    product(place.chip, use_far)
    far.start()
    advance()
    near[1].wait_recv()

    def use_own(tile, value):
        first[:, tile] = value + near_recv[1, :, tile].astype(f32)

    product(t, use_own)
    advance()
    for copy in outs:
        copy.start()
    advance()
    outs[0].wait_recv()
    loads[5].wait()
    for j in range(0, rows, 64):
        tile = slice(j, j + 64)
        ffn_send[tile, :] = (ffn_own[0, tile, :].astype(f32) + ffn_recv[0, tile, :].astype(f32)).astype(bf16)
    outs_far.start()

    count = small.shape[2]
    gain = lane_vector(small, 0, size // count)
    acc[...] = jnp.zeros_like(acc)
    loads[8].wait()
    loads[9].wait()
    advance(4)
    far.wait_recv()

    @pl.loop(0, rows // 16)
    def _(i):
        here = pl.ds(pl.multiple_of(i * 16, 16), 16)
        value = x[here, :].astype(f32)
        center = value - jnp.mean(value, axis=1, keepdims=True)
        rstd = lax.rsqrt(jnp.mean(center * center, axis=1, keepdims=True) + EPS)
        hat = center * rstd
        incoming = first[here, :] + far_recv[here, :].astype(f32)
        acc[0] += incoming * hat
        acc[1] += incoming
        scaled = incoming * gain
        back_rows = rstd * (
            scaled - jnp.mean(scaled, axis=1, keepdims=True) - hat * jnp.mean(scaled * hat, axis=1, keepdims=True)
        )
        totals[here, :] = datt[here, :] + back_rows

    input_store = pltpu.make_async_copy(totals, input_out, local.at[11])
    input_store.start()
    vecs[0] = vec_ref[...]
    vecs[0, 0:1, :] = jnp.sum(acc[0], axis=0, keepdims=True)
    vecs[0, 1:2, :] = jnp.sum(acc[1], axis=0, keepdims=True)

    def hop(number):
        there = {"tensor": (place.core, place.chip)[number]} if number < 2 else {"dp": partners[number - 2]}
        return pltpu.make_async_remote_copy(
            src_ref=vecs.at[number],
            dst_ref=vec_recv.at[number],
            send_sem=v_send.at[number],
            recv_sem=v_recv.at[number],
            device_id=there,
            device_id_type=MESH,
        )

    for number in range(5):
        hop(number).start()
        advance(1 if number < 2 else 2)
        hop(number).wait_recv()
        summed = vecs[number] + vec_recv[number]
        if number < 2:
            row = lax.broadcasted_iota(jnp.int32, summed.shape, 0)
            summed = jnp.where(row < 4, summed, vecs[number])
        vecs[number + 1] = summed
    vec_out[...] = vecs[5]
    advance(2)
    outs[1].wait_recv()
    outs_far.wait_recv()
    loads[6].wait()
    loads[7].wait()
    for j in range(0, rows, 64):
        tile = slice(j, j + 64)
        layer[tile, :] = (
            attended[tile, :]
            + ffn_own[1, tile, :].astype(f32)
            + ffn_recv[1, tile, :].astype(f32)
            + ffn_far[tile, :].astype(f32)
        ).astype(bf16)
    layer_store = pltpu.make_async_copy(layer, layer_out, local.at[10])
    layer_store.start()
    for item in plan:
        tick(*item)
    results = [
        pltpu.make_async_copy(wsum.at[:, pl.ds(i * width, width)], out, local.at[12 + i])
        for i, out in enumerate((query_sum, key_sum, value_sum))
    ] + [pltpu.make_async_copy(osum, out_sum, local.at[15])]
    for copy in results:
        copy.start()
    for group in lanes:
        for lane in group:
            lane.finish()
    for copy in near + [far] + outs + [outs_far]:
        copy.wait_send()
    for number in range(5):
        hop(number).wait_send()
    for copy in results + [layer_store, input_store]:
        copy.wait()


def leave(normed, dlin, qkv, mixed, resid, datt, x, attended, ffn, small, vec, n):
    rows, model = x.shape
    size = model // n
    seq, width = mixed.shape
    shape = jax.ShapeDtypeStruct
    own = lambda kind: pltpu.VMEM((rows, model), kind)
    return pl.pallas_call(
        lambda *refs: leave_kernel(n, *refs),
        in_specs=[HBM] * 9 + [VMEM] * 2,
        out_specs=[HBM] * 6 + [VMEM],
        out_shape=[shape((rows, model), bf16), shape((rows, model), f32)]
        + [shape((size, width), f32)] * 4
        + [shape((8, model), f32)],
        scratch_shapes=[
            pltpu.VMEM((4, n, size // 2, 3 * width // 2), bf16),
            pltpu.VMEM((2, n, size // 2, width), bf16),
            pltpu.VMEM((seq, model), bf16),
            pltpu.VMEM((3 * width, seq), bf16),
            pltpu.VMEM((n, size, 3 * width), bf16),
            pltpu.VMEM((seq, width), bf16),
            pltpu.VMEM((seq, model), bf16),
            own(f32),
            own(f32),
            own(bf16),
            own(f32),
            pltpu.VMEM((2, rows, model), bf16),
            pltpu.VMEM((2, rows, model), bf16),
            own(bf16),
            own(bf16),
            pltpu.VMEM((2, rows, model), bf16),
            pltpu.VMEM((2, rows, model), bf16),
            own(bf16),
            own(bf16),
            own(bf16),
            pltpu.VMEM((2, 16, model), f32),
            own(f32),
            pltpu.VMEM((size, 3 * width), f32),
            pltpu.VMEM((size, width), f32),
            pltpu.VMEM((6, 8, model), f32),
            pltpu.VMEM((5, 8, model), f32),
            DMA((6, n - 1)),
            DMA((6, n - 1)),
            DMA((6,)),
            DMA((6,)),
            DMA((5,)),
            DMA((5,)),
            DMA((16,)),
        ],
        compiler_params=pltpu.CompilerParams(collective_id=4, has_side_effects=True, vmem_limit_bytes=62 << 20),
        cost_estimate=pl.CostEstimate(flops=14 * seq * model * width, bytes_accessed=40 << 20, transcendentals=0),
        name="leave",
    )(normed, dlin, qkv.reshape(n, size, 3 * width), mixed, resid, datt, x, attended, ffn.reshape(4, rows, model), small, vec)

def finish_kernel(
    n,
    layer, input_grad, query_sum, key_sum, value_sum, out_sum, gate_sum, up_sum, down_sum, vec,
    layer_out, input_out, gain_one, shift_one, query_out, key_out, value_out, bias_q, bias_k, bias_v, out_out, gain_two, shift_two,
    gate_out, up_out, down_out,
    out_in, out_turned, down_in, down_turned, held_input, held_layer, held, small_held, sems,
):
    loads = [
        pltpu.make_async_copy(src, dst, sems.at[i])
        for i, (src, dst) in enumerate(
            (
                (down_sum, down_in),
                (out_sum, out_in),
                (input_grad, held_input),
                (layer, held_layer),
                (gate_sum, held.at[0]),
                (up_sum, held.at[1]),
                (query_sum, small_held.at[0]),
                (key_sum, small_held.at[1]),
                (value_sum, small_held.at[2]),
            )
        )
    ]
    for load in loads:
        load.start()
    me, t = lax.axis_index("dp"), lax.axis_index("tensor")
    each = gain_one.shape[1]
    at = me * 4 + t
    fit = 128 // each
    for r, out in enumerate((gain_one, shift_one, gain_two, shift_two)):
        wide = vec[r : r + 1, pl.ds(pl.multiple_of(lax.div(at, fit) * 128, 128), 128)]
        value = wide[:, 0:each]
        for i in range(1, fit):
            value = jnp.where(lax.rem(at, fit) == i, wide[:, i * each : (i + 1) * each], value)
        out[...] = value
    heads, per = bias_q.shape
    row = vec[4:5, :]
    for part, out in ((0, bias_q), (2, bias_v)):
        base = part * heads * HD
        own = jnp.concatenate([row[:, base + h * HD : base + (h + 1) * HD] for h in range(heads)], axis=0)
        value = own[:, 0:per]
        for d in range(1, n):
            value = jnp.where(me == d, own[:, d * per : (d + 1) * per], value)
        out[...] = value
    base = heads * HD
    bias_k[...] = jnp.concatenate([row[:, base + h * HD : base + h * HD + ROT] for h in range(heads)], axis=0)
    stores = []

    def store(src, dst):
        stores.append(pltpu.make_async_copy(src, dst, sems.at[9 + len(stores)]))
        stores[-1].start()

    loads[0].wait()
    down_turned[...] = down_in[...].T
    store(down_turned, down_out)
    loads[1].wait()
    out_turned[...] = out_in[...].T
    store(out_turned, out_out)
    for load, src, dst in zip(
        loads[2:],
        (held_input, held_layer, held.at[0], held.at[1], small_held.at[0], small_held.at[1], small_held.at[2]),
        (input_out, layer_out, gate_out, up_out, query_out, key_out, value_out),
    ):
        load.wait()
        store(src, dst)
    for copy in stores:
        copy.wait()


def finish(layer, input_grad, query_sum, key_sum, value_sum, out_sum, gate_sum, up_sum, down_sum, vec, n):
    shape = jax.ShapeDtypeStruct
    size, width = query_sum.shape
    heads, model = width // HD, vec.shape[1]
    each = shape((1, model // (4 * n)), f32)
    bias = shape((heads, HD // n), f32)
    like = lambda value: shape(value.shape, value.dtype)
    results = pl.pallas_call(
        lambda *refs: finish_kernel(n, *refs),
        in_specs=[HBM] * 9 + [VMEM],
        out_specs=[HBM, HBM, VMEM, VMEM, HBM, HBM, HBM, VMEM, VMEM, VMEM, HBM, VMEM, VMEM, HBM, HBM, HBM],
        out_shape=[
            like(layer), like(input_grad), each, each, like(query_sum), like(key_sum), like(value_sum),
            bias, shape((heads, ROT), f32), bias, shape((width, size), f32), each, each,
            like(gate_sum), like(up_sum), shape(down_sum.shape[::-1], f32),
        ],
        scratch_shapes=[
            pltpu.VMEM(out_sum.shape, f32),
            pltpu.VMEM(out_sum.shape[::-1], f32),
            pltpu.VMEM(down_sum.shape, f32),
            pltpu.VMEM(down_sum.shape[::-1], f32),
            pltpu.VMEM(input_grad.shape, f32),
            pltpu.VMEM(layer.shape, bf16),
            pltpu.VMEM((2,) + gate_sum.shape, f32),
            pltpu.VMEM((3,) + query_sum.shape, f32),
            DMA((18,)),
        ],
        compiler_params=pltpu.CompilerParams(vmem_limit_bytes=62 << 20),
        name="finish",
    )(layer, input_grad, query_sum, key_sum, value_sum, out_sum, gate_sum, up_sum, down_sum, vec)
    return tuple(r.reshape(-1) if r.shape[0] == 1 else r for r in results)


def norm_forward(rows):
    center = rows - jnp.mean(rows, axis=-1, keepdims=True)
    rstd = lax.rsqrt(jnp.mean(center * center, axis=-1, keepdims=True) + EPS)
    return center * rstd, rstd


def norm_backward(grad_out, normal, rstd, gain):
    scaled = grad_out * gain
    return rstd * (
        scaled
        - jnp.mean(scaled, axis=-1, keepdims=True)
        - normal * jnp.mean(scaled * normal, axis=-1, keepdims=True)
    )


def local(
    layer_input,
    segments,
    positions,
    first_gain,
    first_shift,
    query_weight,
    key_weight,
    value_weight,
    query_bias,
    key_bias,
    value_bias,
    out_weight,
    second_gain,
    second_shift,
    gate_weight,
    up_weight,
    down_weight,
    out_grad,
):
    ring = Ring()
    n = ring.n
    width = query_weight.shape[1]
    heads = width // HD
    model = layer_input.shape[1]

    per = HD // n
    if ring.ring:
        normed, g_full, qkv, out_t, lin, small = enter(
            layer_input, out_grad, query_weight, key_weight, value_weight, out_weight,
            (first_gain, first_shift, second_gain, second_shift), (query_bias, value_bias), n
        )
        g_full = g_full.reshape(-1, model)
        qkv = qkv.reshape(model, -1)
        out_t = out_t.reshape(model, -1)
    else:
        gather = lambda vector: lax.all_gather(vector, "dp", axis=0, tiled=True).astype(f32)
        gain_one, shift_one, gain_two, shift_two = map(gather, (first_gain, first_shift, second_gain, second_shift))
        bias_query, bias_value = (gather(b.T).T.reshape(-1) for b in (query_bias, value_bias))
        bias_key = jnp.pad(key_bias.astype(f32), ((0, 0), (0, HD - ROT))).reshape(-1)
        bias_lin = jnp.concatenate([bias_query, bias_key, bias_value])
        x_full = tensor_gather(layer_input)
        g_full = tensor_gather(out_grad, after=x_full)
        qkv, _ = ring.gather(jnp.concatenate([query_weight, key_weight, value_weight], axis=1))
        out_t, _ = ring.gather(out_weight.T)
        gate, _ = ring.gather(gate_weight)
        up, _ = ring.gather(up_weight)
        down_t, _ = ring.gather(down_weight.T)
        hat_full, _ = norm_forward(x_full.astype(f32))
        normed = (hat_full * gain_one + shift_one).astype(bf16)
        lin = dot(qkv, normed, ((0,), (1,)))

    freqs = jnp.exp(-(2.0 / ROT) * jnp.arange(HALF).astype(f32) * math.log(10000.0))
    angles = freqs[:, None] * positions.astype(f32)[None, :]
    cosine, sine = jnp.cos(angles), jnp.sin(angles)
    rows = layer_input.astype(f32)
    if ring.ring:
        q_rot, k_rot, v_heads, logs, mixed, attended, second, gate, up, hidden, ffn, grad_gate, grad_up = middle(
            lin, key_bias, cosine, sine, segments, layer_input, out_t, small, gate_weight, up_weight, down_weight, g_full, n
        )
        second, gate, up = second.reshape(-1, model), gate.reshape(model, -1), up.reshape(model, -1)
        hidden, ffn = hidden.reshape(second.shape[0], -1), ffn.reshape(-1, model)
        grad_gate, grad_up = grad_gate.reshape(hidden.shape), grad_up.reshape(hidden.shape)
    else:
        index = jnp.arange(segments.shape[0], dtype=jnp.int32)
        allowed = (index[:, None] <= index[None, :]) & (segments[:, None] == segments[None, :])
        bias = jnp.where(allowed, 0.0, NEG).astype(f32)
        mixed, q_rot, k_rot, v_heads, logs = attend_forward(lin + bias_lin[:, None], cosine, sine, bias)
        attended = rows + tensor_scatter(dot(mixed, out_t, ((1,), (1,))))

        hat_two, rstd_two = norm_forward(attended)
        second = tensor_gather((hat_two * gain_two + shift_two).astype(bf16))
        gate_lin = dot(second, gate, ((1,), (0,)))
        up_lin = dot(second, up, ((1,), (0,)))
        sigma = jax.nn.sigmoid(gate_lin)
        activated = gate_lin * sigma
        hidden = (activated * up_lin).astype(bf16)
        ffn = dot(hidden, down_t, ((1,), (1,)))
        grad_hidden = dot(g_full, down_t, ((1,), (0,)))
        grad_gate = (grad_hidden * up_lin * sigma * (1.0 + gate_lin * (1.0 - sigma))).astype(bf16)
        grad_up = (grad_hidden * activated).astype(bf16)
    if ring.ring:
        down_sum, gate_sum, up_sum, grad_attended, residual, grad_lin, vec = back(
            grad_gate, grad_up, hidden, second, g_full, gate, up, attended, small, out_t,
            q_rot, k_rot, v_heads, logs, cosine, sine, segments, n
        )
        layer_output, input_grad, query_sum, key_sum, value_sum, out_sum, vec = leave(
            normed, grad_lin, qkv, mixed, residual.reshape(-1, model), grad_attended, layer_input, attended, ffn, small, vec, n
        )
        return finish(
            layer_output, input_grad, query_sum, key_sum, value_sum, out_sum, gate_sum, up_sum, down_sum, vec, n
        )
    else:
        down_grad = dot(g_full, hidden, ((0,), (0,)))
        grad_second = tensor_scatter(dot(grad_gate, gate, ((1,), (1,))) + dot(grad_up, up, ((1,), (1,))))
        gate_grad = dot(second, grad_gate, ((0,), (0,)))
        up_grad = dot(second, grad_up, ((0,), (0,)))
        down_sum = ring.scatter(down_grad).T
        gate_sum = ring.scatter(gate_grad)
        up_sum = ring.scatter(up_grad)
        grad_attended = out_grad.astype(f32) + norm_backward(grad_second, hat_two, rstd_two, gain_two)
        residual = tensor_gather(grad_attended.astype(bf16))
        grad_mixed = dot(out_t, residual, ((0,), (1,))).astype(bf16)
        dq, dk, dv, sums = attend_backward(q_rot, k_rot, v_heads, grad_mixed, logs, cosine, sine, bias)
        grad_lin = jnp.concatenate([dq, dk, dv], axis=0)
        sums = sums.reshape(width, 128)[:, :3]
        out_sum = ring.scatter(dot(residual, mixed, ((0,), (0,)))).T
        qkv_sum = ring.scatter(dot(normed, grad_lin, ((0,), (1,))))
        query_sum, key_sum, value_sum = (qkv_sum[:, i * width : (i + 1) * width] for i in range(3))
        grad_first = tensor_scatter(dot(grad_lin, qkv, ((0,), (1,))))
        hat_one, rstd_one = norm_forward(rows)
        input_grad = grad_attended + norm_backward(grad_first, hat_one, rstd_one, gain_one)
        layer_output = (attended + tensor_scatter(ffn.astype(f32))).astype(bf16)
        vectors = jnp.stack(
            [
                jnp.sum(grad_first * hat_one, axis=0),
                jnp.sum(grad_first, axis=0),
                jnp.sum(grad_second * hat_two, axis=0),
                jnp.sum(grad_second, axis=0),
            ]
        )
        packed = sum_all(jnp.concatenate([sum_all(vectors, ["tensor"]).reshape(-1), sums.T.reshape(-1)]), ["dp"])
        vectors, sums = packed[: 4 * model].reshape(4, model), packed[4 * model :].reshape(3, width)

    each = model // (n * lax.axis_size("tensor"))
    at = ring.me * lax.axis_size("tensor") + lax.axis_index("tensor")
    vectors = lax.dynamic_slice(vectors.reshape(4, -1, each), (0, at, 0), (4, 1, each))[:, 0]
    sums = sums.reshape(3, heads, n, per)
    mine = lax.dynamic_slice(sums, (0, 0, ring.me, 0), (3, heads, 1, per))[:, :, 0]
    key_bias_sum = sums[1].reshape(heads, HD)[:, :ROT]

    return (
        layer_output,
        input_grad,
        vectors[0],
        vectors[1],
        query_sum,
        key_sum,
        value_sum,
        mine[0],
        key_bias_sum,
        mine[2],
        out_sum,
        vectors[2],
        vectors[3],
        gate_sum,
        up_sum,
        down_sum,
    )


def solution(mesh):
    both = ("dp", "tensor")
    return jax.shard_map(
        local,
        mesh=mesh,
        in_specs=(
            P(both, None),
            P("dp"),
            P("dp"),
            P("dp"),
            P("dp"),
            P("dp", "tensor"),
            P("dp", "tensor"),
            P("dp", "tensor"),
            P("tensor", "dp"),
            P("tensor", None),
            P("tensor", "dp"),
            P("tensor", "dp"),
            P("dp"),
            P("dp"),
            P("dp", "tensor"),
            P("dp", "tensor"),
            P("tensor", "dp"),
            P(both, None),
        ),
        out_specs=(
            P(both, None),
            P(both, None),
            P(both),
            P(both),
            P("dp", "tensor"),
            P("dp", "tensor"),
            P("dp", "tensor"),
            P("tensor", "dp"),
            P("tensor", None),
            P("tensor", "dp"),
            P("tensor", "dp"),
            P(both),
            P(both),
            P("dp", "tensor"),
            P("dp", "tensor"),
            P("tensor", "dp"),
        ),
        check_vma=False,
    )
```

```python
import math

import jax
import jax.numpy as jnp
from jax import lax
from jax.experimental import pallas as pl
from jax.experimental.pallas import tpu as pltpu
from jax.sharding import PartitionSpec as P

HD = 64
ROT = 16
SEQ = 1024
HALF = ROT // 2
SCALE = HD ** (-0.5)

EPS = 1e-05
NEG = -1e30
QB = 256
f32 = jnp.float32
bf16 = jnp.bfloat16


def barrier(value, after):
    return lax.optimization_barrier((value, after))[0]


class Ring:
    def __init__(self):
        self.n = lax.axis_size("dp")
        self.ring = self.n == 8 and lax.axis_size("tensor") == 4
        order = list(range(0, self.n, 2)) + list(range(self.n - 1, 0, -2))
        self.up = [(order[i], order[(i + 1) % self.n]) for i in range(self.n)]
        self.down = [(b, a) for a, b in self.up]
        me = lax.axis_index("dp")
        self.me = me
        self.pos = jnp.where(me % 2 == 0, me // 2, self.n - 1 - (me - 1) // 2)

    def owner(self, offset):
        p = (self.pos + offset + 2 * self.n) % self.n
        return jnp.where(p < self.n // 2, 2 * p, 2 * (self.n - 1 - p) + 1)

    def gather(self, shard, pieces=1, after=None):
        n = self.n
        rows, cols = shard.shape
        if not self.ring:
            return lax.all_gather(shard, "dp", axis=0, tiled=True), [shard] * n
        if after is not None:
            shard = barrier(shard, after)
        full = jnp.zeros((n, rows, cols), shard.dtype)
        full = lax.dynamic_update_slice(full, shard[None], (self.me, 0, 0))
        size = rows // (2 * pieces)
        lanes = []
        for k in range(2 * pieces):
            lanes.append([k % 2, k * size, shard[k * size : (k + 1) * size]])
        marks = []
        for step in range(1, n):
            for lane in lanes:
                way, base, block = lane
                block = lax.ppermute(block, "dp", self.down if way else self.up)
                lane[2] = block
                whose = self.owner(step if way else -step)
                full = lax.dynamic_update_slice(full, block[None], (whose, base, 0))
            marks.append(lanes[-1][2])
        return full.reshape(n * rows, cols), marks

    def scatter(self, partial, pieces=1, after=None):
        n = self.n
        if not self.ring:
            return lax.psum_scatter(partial.astype(bf16), "dp", scatter_dimension=0, tiled=True).astype(f32)
        cols = partial.shape[1]
        rows = partial.shape[0] // n
        partial = partial.reshape(n, rows, cols)
        size = rows // (2 * pieces)
        done = []
        for k in range(2 * pieces):
            way = k % 2

            def block(step):
                whose = self.owner(1 + step if way else -1 - step)
                return lax.dynamic_slice(partial, (whose, k * size, 0), (1, size, cols))[0].astype(f32)

            moving = block(0)
            for step in range(1, n):
                got = lax.ppermute(moving.astype(bf16), "dp", self.down if way else self.up)
                moving = got.astype(f32) + block(step)
            done.append(moving)
        return jnp.concatenate(done, axis=0)


CORE = [(0, 1), (1, 0), (2, 3), (3, 2)]
CHIP = [(0, 2), (2, 0), (1, 3), (3, 1)]


def tensor_gather(rows, after=None):
    if lax.axis_size("tensor") != 4:
        return lax.all_gather(rows, "tensor", axis=0, tiled=True)
    if after is not None:
        rows = barrier(rows, after)
    t = lax.axis_index("tensor")
    far = lax.ppermute(rows, "tensor", CHIP)
    near = lax.ppermute(rows, "tensor", CORE)
    last = lax.ppermute(far, "tensor", CORE)
    full = jnp.zeros((4,) + rows.shape, rows.dtype)
    for flip, block in ((0, rows), (1, near), (2, far), (3, last)):
        full = lax.dynamic_update_slice(full, block[None], (t ^ flip, 0, 0))
    return full.reshape(4 * rows.shape[0], rows.shape[1])


def tensor_scatter(partial):
    if lax.axis_size("tensor") != 4:
        return lax.psum_scatter(partial.astype(bf16), "tensor", scatter_dimension=0, tiled=True).astype(f32)
    t = lax.axis_index("tensor")
    rows = partial.shape[0] // 4
    blocks = partial.reshape(4, rows, partial.shape[1])

    def block(flip):
        return lax.dynamic_slice(blocks, (t ^ flip, 0, 0), (1,) + blocks.shape[1:])[0]

    other = lax.ppermute(block(3).astype(bf16), "tensor", CORE)
    own = lax.ppermute(block(1).astype(bf16), "tensor", CORE)
    far = lax.ppermute((block(2) + other.astype(f32)).astype(bf16), "tensor", CHIP)
    return block(0) + own.astype(f32) + far.astype(f32)


def sum_all(vector, axes):
    for axis in axes:
        n = lax.axis_size(axis)
        if n & (n - 1):
            vector = lax.psum(vector, axis)
            continue
        step = 1
        while step < n:
            vector = vector + lax.ppermute(vector, axis, [(i, i ^ step) for i in range(n)])
            step *= 2
    return vector


def rotate(rows, cosine, sine, direction):
    first, second = rows[:HALF], rows[HALF:ROT]
    return jnp.concatenate(
        [first * cosine - direction * second * sine, second * cosine + direction * first * sine, rows[ROT:]], axis=0
    )


def dot(a, b, dims):
    return lax.dot_general(a, b, ((dims[0], dims[1]), ((), ())), preferred_element_type=f32)


def forward_kernel(q_ref, k_ref, v_ref, cos_ref, sin_ref, bias_ref, mixed_ref, q_out, k_out, v_out, log_ref):
    seq = q_ref.shape[1]
    cosine, sine = cos_ref[...], sin_ref[...]
    v_all = v_ref[...].astype(bf16)
    v_out[...] = v_all
    parts = []
    for head in range(q_ref.shape[0] // HD):
        rows = slice(head * HD, (head + 1) * HD)
        q = rotate(q_ref[rows, :], cosine, sine, 1.0).astype(bf16)
        k = rotate(k_ref[rows, :], cosine, sine, 1.0).astype(bf16)
        q_out[rows, :] = q
        k_out[rows, :] = k
        keys = k.T
        values = v_all[rows, :]
        q = q * jnp.asarray(SCALE, bf16)
        cols = []
        for start in range(0, seq, QB):
            end = start + QB
            scores = dot(keys[:end], q[:, start:end], ((1,), (0,))) + bias_ref[:end, start:end]
            top = jnp.max(scores, axis=0, keepdims=True)
            expo = jnp.exp(scores - top)
            total = jnp.sum(expo, axis=0, keepdims=True)
            probs = (expo * (1.0 / total)).astype(bf16)
            cols.append(dot(values[:, :end], probs, ((1,), (0,))).astype(bf16))
            log_ref[0, head : head + 1, start:end] = top + jnp.log(total)
        parts.append(jnp.concatenate(cols, axis=1))
    mixed_ref[...] = jnp.concatenate(parts, axis=0).T


def attend_forward(lin, cosine, sine, bias):
    width, seq = lin.shape[0] // 3, lin.shape[1]
    pair = 2 * HD
    count = width // pair
    outs = []
    block = lambda base: pl.BlockSpec((pair, seq), lambda i: (base * count + i, 0))
    whole = lambda shape: pl.BlockSpec(shape, lambda i: (0, 0))
    return pl.pallas_call(
        forward_kernel,
        grid=(count,),
        in_specs=[block(0), block(1), block(2), whole(cosine.shape), whole(sine.shape), whole(bias.shape)],
        out_specs=[
            pl.BlockSpec((seq, pair), lambda i: (0, i)),
            pl.BlockSpec((pair, seq), lambda i: (i, 0)),
            pl.BlockSpec((pair, seq), lambda i: (i, 0)),
            pl.BlockSpec((pair, seq), lambda i: (i, 0)),
            pl.BlockSpec((1, 2, seq), lambda i: (i, 0, 0)),
        ],
        out_shape=[
            jax.ShapeDtypeStruct((seq, width), bf16),
            jax.ShapeDtypeStruct((width, seq), bf16),
            jax.ShapeDtypeStruct((width, seq), bf16),
            jax.ShapeDtypeStruct((width, seq), bf16),
            jax.ShapeDtypeStruct((count, 2, seq), f32),
        ],
        compiler_params=pltpu.CompilerParams(vmem_limit_bytes=48 << 20),
        cost_estimate=pl.CostEstimate(
            flops=4 * width * seq * seq, bytes_accessed=30 << 20, transcendentals=width // HD * seq * seq
        ),
        name="attend_forward",
    )(lin, lin, lin, cosine, sine, bias)


def backward_kernel(q_ref, k_ref, v_ref, d_ref, log_ref, cos_ref, sin_ref, bias_ref, dq_out, dk_out, dv_out, sums_ref, dk_acc, dv_acc):
    seq = q_ref.shape[1]
    cosine, sine = cos_ref[...], sin_ref[...]
    for head in range(q_ref.shape[0] // HD):
        rows = slice(head * HD, (head + 1) * HD)
        q, k, v, d = q_ref[rows, :], k_ref[rows, :], v_ref[rows, :], d_ref[rows, :]
        keys, values = k.T, v.T
        q_small = q * jnp.asarray(SCALE, bf16)
        dk_acc[...] = jnp.zeros_like(dk_acc)
        dv_acc[...] = jnp.zeros_like(dv_acc)
        cols = []
        for start in range(0, seq, QB):
            end = start + QB
            here = slice(start, end)
            scores = dot(keys[:end], q_small[:, here], ((1,), (0,))) + bias_ref[:end, here]
            probs = jnp.exp(scores - log_ref[0, head : head + 1, here])
            grad = dot(values[:end], d[:, here], ((1,), (0,)))
            both = probs * grad
            inner = jnp.sum(both, axis=0, keepdims=True)
            grad = ((both - probs * inner) * SCALE).astype(bf16)
            probs = probs.astype(bf16)
            cols.append(dot(k[:, :end], grad, ((1,), (0,))))
            dk_acc[:, :end] += dot(q[:, here], grad, ((1,), (1,)))
            dv_acc[:, :end] += dot(d[:, here], probs, ((1,), (1,)))
        dq = rotate(jnp.concatenate(cols, axis=1), cosine, sine, -1.0)
        dk = rotate(dk_acc[...], cosine, sine, -1.0)
        dv = dv_acc[...]
        for part, (out, value) in enumerate(((dq_out, dq), (dk_out, dk), (dv_out, dv))):
            out[rows, :] = value.astype(bf16)
            sums_ref[0, rows, part : part + 1] = jnp.sum(value, axis=1, keepdims=True)


def attend_backward(q, k, v, d, logs, cosine, sine, bias):
    width, seq = q.shape
    pair = 2 * HD
    count = width // pair
    block = pl.BlockSpec((pair, seq), lambda i: (i, 0))
    whole = lambda shape: pl.BlockSpec(shape, lambda i: (0, 0))
    return pl.pallas_call(
        backward_kernel,
        grid=(count,),
        in_specs=[block] * 4
        + [pl.BlockSpec((1, 2, seq), lambda i: (i, 0, 0)), whole(cosine.shape), whole(sine.shape), whole(bias.shape)],
        out_specs=[block] * 3 + [pl.BlockSpec((1, pair, 128), lambda i: (i, 0, 0))],
        out_shape=[jax.ShapeDtypeStruct((width, seq), bf16)] * 3 + [jax.ShapeDtypeStruct((count, pair, 128), f32)],
        scratch_shapes=[pltpu.VMEM((HD, seq), f32), pltpu.VMEM((HD, seq), f32)],
        compiler_params=pltpu.CompilerParams(vmem_limit_bytes=48 << 20),
        cost_estimate=pl.CostEstimate(
            flops=10 * width * seq * seq, bytes_accessed=30 << 20, transcendentals=width // HD * seq * seq
        ),
        name="attend_backward",
    )(q, k, v, d, logs, cosine, sine, bias)


MESH = pl.DeviceIdType.MESH
HBM = pl.BlockSpec(memory_space=pl.ANY)
VMEM = pl.BlockSpec(memory_space=pltpu.VMEM)
DMA = pltpu.SemaphoreType.DMA


class Place:
    def __init__(self, n):
        self.n = n
        self.me = lax.axis_index("dp")
        self.t = lax.axis_index("tensor")
        odd = lax.rem(self.me, 2)
        half = lax.div(self.me, 2)
        self.pos = jnp.where(odd == 0, half, n - 1 - half)
        self.up = self.owner(1)
        self.down = self.owner(-1)
        self.core = self.t + 1 - 2 * lax.rem(self.t, 2)
        self.chip = lax.rem(self.t + 2, 4)
        self.cross = lax.rem(self.core + 2, 4)

    def owner(self, offset):
        p = lax.rem(self.pos + (offset + 2 * self.n), self.n)
        return jnp.where(p < self.n // 2, 2 * p, 2 * (self.n - 1 - p) + 1)

    def barrier(self, dp, tensor):
        sem = pltpu.get_barrier_semaphore()
        for there in dp:
            pl.semaphore_signal(sem, inc=1, device_id={"dp": there}, device_id_type=MESH)
        for there in tensor:
            pl.semaphore_signal(sem, inc=1, device_id={"tensor": there}, device_id_type=MESH)
        pl.semaphore_wait(sem, len(dp) + len(tensor))


class Lane:
    def __init__(self, place, full, base, size, way, send, recv):
        self.place, self.full, self.base, self.size, self.way = place, full, base, size, way
        self.send, self.recv = send, recv

    def whose(self, step):
        return self.place.owner(step if self.way else -step)

    def copy(self, step, whose):
        piece = self.full.at[whose, pl.ds(self.base, self.size)]
        return pltpu.make_async_remote_copy(
            src_ref=piece,
            dst_ref=piece,
            send_sem=self.send.at[step - 1],
            recv_sem=self.recv.at[step - 1],
            device_id={"dp": self.place.down if self.way else self.place.up},
            device_id_type=MESH,
        )

    def start(self, step):
        self.copy(step, self.whose(step - 1)).start()

    def arrive(self, step):
        self.copy(step, self.whose(step)).wait_recv()

    def finish(self):
        for step in range(1, self.place.n):
            self.copy(step, self.whose(step - 1)).wait_send()


class Exchange:
    def __init__(self, send, recv):
        self.send, self.recv = send, recv

    def copy(self, number, src, dst, there):
        return pltpu.make_async_remote_copy(
            src_ref=src,
            dst_ref=dst,
            send_sem=self.send.at[number],
            recv_sem=self.recv.at[number],
            device_id={"tensor": there},
            device_id_type=MESH,
        )


def row_norm(value, gain, shift):
    center = value - jnp.mean(value, axis=1, keepdims=True)
    rstd = lax.rsqrt(jnp.mean(center * center, axis=1, keepdims=True) + EPS)
    return center * rstd * gain + shift


def lane_vector(full, first, count):
    pieces = [full[d, r : r + 1, :] for d in range(full.shape[0]) for r in range(first, first + count)]
    return jnp.concatenate(pieces, axis=1)


def enter_kernel(
    n,
    x_ref, g_ref, wq, wk, wv, wo, gain_one, shift_one, gain_two, shift_two, bias_q, bias_v,
    normed_out, g_out, qkv_out, out_out, lin_out, small_full,
    x_full, normed, left, right, outs, lin, small_ref,
    small_send, small_recv, send, recv, x_send, x_recv, local, stored, lin_stored,
):
    place = Place(n)
    rows = x_ref.shape[0]
    size = wq.shape[0]
    width = wq.shape[1]
    half = width // 2
    me, t = place.me, place.t
    loads = [
        pltpu.make_async_copy(wq, left.at[me, :, pl.ds(0, width)], local.at[0]),
        pltpu.make_async_copy(wk.at[:, pl.ds(0, half)], left.at[me, :, pl.ds(width, half)], local.at[1]),
        pltpu.make_async_copy(wk.at[:, pl.ds(half, half)], right.at[me, :, pl.ds(0, half)], local.at[2]),
        pltpu.make_async_copy(wv, right.at[me, :, pl.ds(half, width)], local.at[3]),
        pltpu.make_async_copy(x_ref, x_full.at[t], local.at[4]),
        pltpu.make_async_copy(g_ref, g_out.at[t], local.at[5]),
    ]
    for load in loads:
        load.start()
    outs[me] = wo[...].T
    count = small_ref.shape[1]
    each = size // count
    small_ref[...] = jnp.zeros_like(small_ref)
    for i, vector in enumerate((gain_one, shift_one, gain_two, shift_two)):
        for r in range(each):
            small_ref[i * each + r, :] = vector[r * count : (r + 1) * count].astype(f32)
    heads, per = bias_q.shape
    small_ref[4 * each : 4 * each + heads, 0:per] = bias_q[...].astype(f32)
    small_ref[4 * each : 4 * each + heads, per : 2 * per] = bias_v[...].astype(f32)
    small_full[me] = small_ref[...]
    place.barrier([place.owner(k) for k in range(1, n)], [place.core, place.chip])

    smalls = []
    for k in range(1, n):
        smalls.append(
            pltpu.make_async_remote_copy(
                src_ref=small_ref,
                dst_ref=small_full.at[me],
                send_sem=small_send.at[k - 1],
                recv_sem=small_recv.at[k - 1],
                device_id={"dp": place.owner(k)},
                device_id_type=MESH,
            )
        )
        smalls[-1].start()

    swap = Exchange(x_send, x_recv)
    to_chip = swap.copy(0, x_ref, x_full.at[t], place.chip)
    to_core = swap.copy(1, x_ref, x_full.at[t], place.core)
    relay = swap.copy(2, x_full.at[place.chip], x_full.at[place.chip], place.core)
    g_chip = swap.copy(3, g_ref, g_out.at[t], place.chip)
    g_core = swap.copy(4, g_ref, g_out.at[t], place.core)
    g_relay = swap.copy(5, g_out.at[place.chip], g_out.at[place.chip], place.core)
    to_chip.start()
    to_core.start()
    for load in loads[:4]:
        load.wait()
    lanes = []
    for number, (full, base, count, way) in enumerate(
        (
            (left, 0, size // 2, 0),
            (right, 0, size // 2, 1),
            (left, size // 2, size // 2, 0),
            (right, size // 2, size // 2, 1),
            (outs, 0, size // 2, 0),
            (outs, size // 2, size // 2, 1),
        )
    ):
        lanes.append(Lane(place, full, base, count, way, send.at[number], recv.at[number]))

    def store(step):
        whose, other = place.owner(-step), place.owner(step)
        if step == n:
            return []
        return [
            pltpu.make_async_copy(left.at[whose], qkv_out.at[whose, :, pl.ds(0, width + half)], stored.at[0, step]),
            pltpu.make_async_copy(right.at[other], qkv_out.at[other, :, pl.ds(width + half, width + half)], stored.at[1, step]),
            pltpu.make_async_copy(outs.at[whose, pl.ds(0, size // 2)], out_out.at[whose, pl.ds(0, size // 2)], stored.at[2, step]),
            pltpu.make_async_copy(
                outs.at[other, pl.ds(size // 2, size // 2)], out_out.at[other, pl.ds(size // 2, size // 2)], stored.at[3, step]
            ),
        ]

    writes = []

    def tick(step):
        for lane in lanes:
            if step > 1:
                lane.arrive(step - 1)
            if step < n:
                lane.start(step)
        for write in store(step - 1):
            write.start()
            writes.append(write)

    gain = shift = None

    def norm(block):
        @pl.loop(0, rows // 16)
        def _(i):
            here = pl.ds(pl.multiple_of(i * 16, 16), 16)
            there = pl.ds(pl.multiple_of(block * rows + i * 16, 16), 16)
            normed[there, :] = row_norm(x_full[block, here, :].astype(f32), gain, shift).astype(bf16)

    def project(step):
        for full, whose, base in ((left, place.owner(-step), 0), (right, place.owner(step), width + half)):
            xs = normed[:, pl.ds(pl.multiple_of(whose * size, size), size)]
            for j in range(0, width + half, 256):
                part = dot(full[whose, :, j : j + 256].T, xs, ((1,), (1,)))
                where = slice(base + j, base + j + 256)
                if step == 0:
                    lin[where, :] = part
                else:
                    lin[where, :] += part
                if step == n - 1:
                    lin_store(base + j).start()

    def lin_store(first):
        at = pl.ds(first, 256)
        return pltpu.make_async_copy(lin.at[at], lin_out.at[at], lin_stored.at[first // 256])

    tick(1)
    loads[4].wait()
    for small in smalls:
        small.wait_recv()
    gain = lane_vector(small_full, 0, each)
    shift = lane_vector(small_full, each, each)
    norm(t)
    to_core.wait_recv()
    norm(place.core)
    tick(2)
    tick(3)
    to_chip.wait_recv()
    relay.start()
    g_chip.start()
    g_core.start()
    norm(place.chip)
    tick(4)
    relay.wait_recv()
    norm(place.cross)
    normed_store = pltpu.make_async_copy(normed, normed_out, local.at[6])
    normed_store.start()
    project(0)
    done = 1
    for step in range(5, n):
        tick(step)
        while done < min(step - 1, 2 * (step - 4) + 1):
            project(done)
            done += 1
    g_chip.wait_recv()
    g_relay.start()
    while done < n - 1:
        project(done)
        done += 1
    tick(n)
    project(n - 1)
    for copy in (to_chip, to_core, relay, g_chip, g_core, g_relay):
        copy.wait_send()
    g_core.wait_recv()
    g_relay.wait_recv()
    for small in smalls:
        small.wait_send()
    for lane in lanes:
        lane.finish()
    loads[5].wait()
    for write in writes:
        write.wait()
    normed_store.wait()
    for first in range(0, 3 * width, 256):
        lin_store(first).wait()


def enter(x, g, wq, wk, wv, wo, vectors, biases, n):
    rows, model = x.shape
    size, width = wq.shape
    big = 3 * width // 2
    kernel = lambda *refs: enter_kernel(n, *refs)
    return pl.pallas_call(
        kernel,
        in_specs=[HBM] * 5 + [VMEM] * 7,
        out_specs=[HBM, HBM, HBM, HBM, HBM, VMEM],
        out_shape=[
            jax.ShapeDtypeStruct((4 * rows, model), bf16),
            jax.ShapeDtypeStruct((4, rows, model), bf16),
            jax.ShapeDtypeStruct((n, size, 3 * width), bf16),
            jax.ShapeDtypeStruct((n, size, width), bf16),
            jax.ShapeDtypeStruct((3 * width, 4 * rows), f32),
            jax.ShapeDtypeStruct((n, 16, 128), f32),
        ],
        scratch_shapes=[
            pltpu.VMEM((4, rows, model), bf16),
            pltpu.VMEM((4 * rows, model), bf16),
            pltpu.VMEM((n, size, big), bf16),
            pltpu.VMEM((n, size, big), bf16),
            pltpu.VMEM((n, size, width), bf16),
            pltpu.VMEM((3 * width, 4 * rows), f32),
            pltpu.VMEM((16, 128), f32),
            DMA((n - 1,)),
            DMA((n - 1,)),
            DMA((6, n - 1)),
            DMA((6, n - 1)),
            DMA((6,)),
            DMA((6,)),
            DMA((7,)),
            DMA((4, n)),
            DMA((3 * width // 256,)),
        ],
        compiler_params=pltpu.CompilerParams(collective_id=1, has_side_effects=True, vmem_limit_bytes=56 << 20),
        cost_estimate=pl.CostEstimate(flops=6 * width * rows * 4 * model, bytes_accessed=40 << 20, transcendentals=0),
        name="enter",
    )(x, g, wq, wk, wv, wo, *vectors, *biases)

def attend_pair(pair, lin, bias_ref, cosine, sine, mask, q_all, k_all, v_all, logs, flat, mixed):
    width, seq = q_all.shape

    @pl.loop(0, 2)
    def _(j):
        head = pair * 2 + j
        first = pl.multiple_of(head * HD, HD)
        rows = pl.ds(first, HD)

        def load(part):
            at = pl.ds(pl.multiple_of(part * width + first, HD), HD)
            return lin[at, :] + bias_ref[at, :]

        q = rotate(load(0), cosine, sine, 1.0).astype(bf16)
        k = rotate(load(1), cosine, sine, 1.0).astype(bf16)
        values = load(2).astype(bf16)
        q_all[rows, :] = q
        k_all[rows, :] = k
        v_all[rows, :] = values
        keys = k.T
        q = q * jnp.asarray(SCALE, bf16)
        mine = pl.ds(pl.multiple_of(j * HD, HD), HD)
        for start in range(0, seq, QB):
            end = start + QB
            scores = dot(keys[:end], q[:, start:end], ((1,), (0,))) + mask[:end, start:end]
            top = jnp.max(scores, axis=0, keepdims=True)
            expo = jnp.exp(scores - top)
            total = jnp.sum(expo, axis=0, keepdims=True)
            probs = (expo * (1.0 / total)).astype(bf16)
            flat[mine, start:end] = dot(values[:, :end], probs, ((1,), (0,))).astype(bf16)
            logs[pl.ds(head, 1), start:end] = top + jnp.log(total)

    mixed[:, pair * 2 * HD : (pair + 1) * 2 * HD] = flat[...].T


def build_mask(mask, column, seg_row):
    seq = mask.shape[0]
    segments = seg_row[...].astype(f32)
    column[...] = jnp.broadcast_to(segments, (128, seq)).T

    @pl.loop(0, seq // 32)
    def _(i):
        here = pl.ds(pl.multiple_of(i * 32, 32), 32)
        key = lax.broadcasted_iota(jnp.int32, (32, seq), 0) + i * 32
        query = lax.broadcasted_iota(jnp.int32, (32, seq), 1)
        allowed = (key <= query) & (column[here, 0:1] == segments)
        mask[here, :] = jnp.where(allowed, 0.0, NEG).astype(f32)


def middle_kernel(
    n,
    lin_ref, key_bias, cos_ref, sin_ref, seg_row, x_ref, out_ref, small, gate_w, up_w, down_w, g_ref,
    q_out, k_out, v_out, logs, mixed_out, att_out, second_out, gate_out, up_out, hidden_out, ffn_out, dgate_out, dup_out,
    gate, up, down, second, near_send, near_recv, far_send, far_recv, attended,
    send, recv, x_send, x_recv, local, stored, staged,
):
    place = Place(n)
    t = place.t
    rows, model = x_ref.shape
    size, cols = gate_w.shape
    seq = 4 * rows
    width = out_ref.shape[1]
    loads = [
        pltpu.make_async_copy(gate_w, gate.at[place.me], local.at[0]),
        pltpu.make_async_copy(up_w, up.at[place.me], local.at[1]),
    ]
    for load in loads:
        load.start()
    down[place.me] = down_w[...].T
    place.barrier([place.up, place.down], [place.core, place.chip])
    for load in loads:
        load.wait()

    half, quarter = size // 2, size // 4
    lanes = [
        [Lane(place, full, half * sub, half, way, send.at[2 * way + sub], recv.at[2 * way + sub]) for way, full in ((0, gate), (1, up))]
        for sub in range(2)
    ]
    downs = [
        [
            Lane(place, down, half * way + quarter * sub, quarter, way, send.at[4 + 2 * way + sub], recv.at[4 + 2 * way + sub])
            for way in range(2)
        ]
        for sub in range(2)
    ]

    def write(step):
        gated, upped = place.owner(-step), place.owner(step)
        return [
            pltpu.make_async_copy(gate.at[gated], gate_out.at[gated], stored.at[0, step]),
            pltpu.make_async_copy(up.at[upped], up_out.at[upped], stored.at[1, step]),
        ]

    def tick(kind, step, sub):
        for lane in (downs if kind else lanes)[sub]:
            if step > 1:
                lane.arrive(step - 1)
            if step < n:
                lane.start(step)
        if sub == 1 and not kind:
            for copy in write(step - 1):
                copy.start()

    plan = [(0, step, sub) for step in range(1, n) for sub in range(2)]
    plan += [(1, 1, 0), (1, 1, 1), (0, n, 0), (0, n, 1)]
    plan += [(1, step, sub) for step in range(2, n + 1) for sub in range(2)]
    plan = iter(plan)

    def advance(count=1):
        for _ in range(count):
            tick(*next(plan))

    swap = Exchange(x_send, x_recv)
    near = [swap.copy(i, near_send.at[i], near_recv.at[i], place.core) for i in range(2)]
    far = swap.copy(2, far_send, far_recv, place.chip)
    to_chip = swap.copy(3, second.at[t], second.at[t], place.chip)
    to_core = swap.copy(4, second.at[t], second.at[t], place.core)
    relay = swap.copy(5, second.at[place.chip], second.at[place.chip], place.core)
    copies = near + [far, to_chip, to_core, relay]

    advance(2)

    def attention(lin, mask, q_all, k_all, v_all, flat, mixed, out_t, bias_ref, column):
        pairs = width // (2 * HD)
        fetch = []
        for part in range(3):
            for pair in range(pairs):
                at = pl.ds(part * width + pair * 2 * HD, 2 * HD)
                fetch.append(pltpu.make_async_copy(lin_ref.at[at], lin.at[at], local.at[2 + part * pairs + pair]))
        for pair in range(pairs):
            for part in range(3):
                fetch[part * pairs + pair].start()
        weights = pltpu.make_async_copy(out_ref, out_t, local.at[2 + 3 * pairs])
        weights.start()
        build_mask(mask, column, seg_row)
        heads, per = width // HD, HD // n
        first = small.shape[1] - heads
        turned = [small[d, first:, :].T for d in range(n)]
        keys = key_bias[...].astype(f32).T
        for head in range(heads):
            for part in range(3):
                if part == 1:
                    rest = jnp.zeros((HD - ROT, 1), f32)
                    piece = jnp.concatenate([keys[:, head : head + 1], rest], axis=0)
                else:
                    at = part // 2 * per
                    piece = jnp.concatenate([turned[d][at : at + per, head : head + 1] for d in range(n)], axis=0)
                where = part * width + head * HD
                bias_ref[where : where + HD, :] = piece
        cosine, sine = cos_ref[...], sin_ref[...]
        for pair in range(pairs):
            for part in range(3):
                fetch[part * pairs + pair].wait()
            attend_pair(pair, lin, bias_ref, cosine, sine, mask, q_all, k_all, v_all, logs, flat, mixed)
            advance()
        keep = [
            pltpu.make_async_copy(src, dst, local.at[3 + 3 * pairs + i])
            for i, (src, dst) in enumerate(((q_all, q_out), (k_all, k_out), (v_all, v_out), (mixed, mixed_out)))
        ]
        for copy in keep:
            copy.start()
        weights.wait()

        def project(block, j):
            at = pl.ds(pl.multiple_of(block * rows, rows), rows)
            return dot(mixed[at, :], out_t[j : j + 512, :], ((1,), (1,)))

        for i, block in enumerate((place.cross, place.core)):
            for j in range(0, model, 512):
                near_send[i, :, j : j + 512] = project(block, j).astype(bf16)
            near[i].start()
        near[0].wait_recv()
        for j in range(0, model, 512):
            tile = slice(j, j + 512)
            far_send[:, tile] = (project(place.chip, j) + near_recv[0, :, tile].astype(f32)).astype(bf16)
        far.start()
        own = pltpu.make_async_copy(x_ref, far_copy, local.at[7 + 3 * pairs])
        own.start()
        advance()
        near[1].wait_recv()
        own.wait()
        for j in range(0, model, 512):
            tile = slice(j, j + 512)
            attended[:, tile] = far_copy[:, tile].astype(f32) + project(t, j) + near_recv[1, :, tile].astype(f32)
        for copy in keep:
            copy.wait()

    far_copy = second.at[t]
    pl.run_scoped(
        attention,
        pltpu.VMEM((3 * width, seq), f32),
        pltpu.VMEM((seq, seq), f32),
        pltpu.VMEM((width, seq), bf16),
        pltpu.VMEM((width, seq), bf16),
        pltpu.VMEM((width, seq), bf16),
        pltpu.VMEM((2 * HD, seq), bf16),
        pltpu.VMEM((seq, width), bf16),
        pltpu.VMEM((model, width), bf16),
        pltpu.VMEM((3 * width, 1), f32),
        pltpu.VMEM((seq, 128), f32),
    )
    last = 7 + 3 * (width // (2 * HD))

    def feed(gate_lin, up_lin, grad, hidden, g, stage):
        g_load = pltpu.make_async_copy(g_ref, g, local.at[last + 1])
        g_load.start()
        gate_lin[...] = jnp.zeros_like(gate_lin)
        up_lin[...] = jnp.zeros_like(up_lin)
        grad[...] = jnp.zeros_like(grad)
        count = small.shape[2]
        gain = lane_vector(small, 2 * size // count, size // count)
        shift = lane_vector(small, 3 * size // count, size // count)
        advance(2)
        far.wait_recv()

        @pl.loop(0, rows // 16)
        def _(i):
            here = pl.ds(pl.multiple_of(i * 16, 16), 16)
            value = attended[here, :] + far_recv[here, :].astype(f32)
            attended[here, :] = value
            second[t, here, :] = row_norm(value, gain, shift).astype(bf16)

        to_chip.start()
        to_core.start()
        att_store = pltpu.make_async_copy(attended, att_out, local.at[last + 2])
        att_store.start()

        def add(block, low, high):
            @pl.loop(low, high)
            def _(step):
                for full, total, whose in ((gate, gate_lin, place.owner(-step)), (up, up_lin, place.owner(step))):
                    xs = second[block, :, pl.ds(pl.multiple_of(whose * size, size), size)]
                    total[block] += dot(xs, full[whose], ((1,), (0,)))

        advance()
        ready = 5
        add(t, 0, ready)
        to_core.wait_recv()
        advance()
        add(place.core, 0, ready)
        advance()
        to_chip.wait_recv()
        relay.start()
        add(place.chip, 0, ready)
        relay.wait_recv()
        second_store = pltpu.make_async_copy(second, second_out, local.at[last + 3])
        second_store.start()
        advance()
        add(place.cross, 0, ready)
        every = lambda low, high: pl.loop(0, 4)(lambda block: add(block, low, high))
        every(ready, n - 2)
        advance(2)
        advance()
        every(n - 2, n - 1)
        advance(2)
        every(n - 1, n)

        @pl.loop(0, 4 * rows // 16)
        def _(i):
            block = lax.div(i, rows // 16)
            here = pl.ds(pl.multiple_of(lax.rem(i, rows // 16) * 16, 16), 16)
            value = gate_lin[block, here, :]
            sigma = jax.nn.sigmoid(value)
            activated = value * sigma
            upward = up_lin[block, here, :]
            hidden[block, here, :] = (activated * upward).astype(bf16)
            gate_lin[block, here, :] = activated
            up_lin[block, here, :] = upward * sigma * (1.0 + value * (1.0 - sigma))

        hidden_store = pltpu.make_async_copy(hidden, hidden_out, local.at[last + 4])
        hidden_store.start()
        g_load.wait()
        stages = []

        def output(whose, base, count):
            number = len(stages)
            slot = number % 2
            if number >= 2:
                stages[number - 2].wait()

            right = down[whose, base : base + count].T
            for block in range(4):
                tile = dot(hidden[block], right, ((1,), (0,)))
                stage[slot, block, :, 0:count] = tile.astype(bf16)

            at = pl.ds(pl.multiple_of(whose * size + base, count), count)
            stages.append(pltpu.make_async_copy(stage.at[slot, :, :, pl.ds(0, count)], ffn_out.at[:, :, at], staged.at[number]))
            stages[-1].start()

        def collect(whose, base, count):
            at = pl.ds(pl.multiple_of(whose * size + base, count), count)

            @pl.loop(0, 4)
            def _(block):
                grad[block] += dot(g[block, :, at], down[whose, base : base + count], ((1,), (0,)))

        def use(whose, base=0, count=size):
            collect(whose, base, count)
            output(whose, base, count)

        after, before = place.owner(n - 1), place.owner(1 - n)
        use(place.me)
        for step in range(2, n):
            advance(2)
            if step - 1 == n // 2:
                use(place.owner(n // 2))
                use(after, 0, half)
                use(before, half, half)
            elif step - 1 > n // 2:
                use(place.owner(step - 1))
                use(place.owner(1 - step))
        for lane in lanes[0] + lanes[1]:
            lane.finish()
        for step in range(n):
            for copy in write(step):
                copy.wait()
        advance(2)
        collect(before, 0, half)
        collect(after, half, half)
        final = []
        for block in range(4):

            @pl.loop(0, rows // 16)
            def _(i):
                here = pl.ds(pl.multiple_of(i * 16, 16), 16)
                incoming = grad[block, here, :]
                gate[block, here, :] = (incoming * up_lin[block, here, :]).astype(bf16)
                gate[4 + block, here, :] = (incoming * gate_lin[block, here, :]).astype(bf16)

            for first, out in ((0, dgate_out), (4, dup_out)):
                final.append(pltpu.make_async_copy(gate.at[first + block], out.at[block], local.at[last + 5 + len(final)]))
                final[-1].start()
        output(before, 0, half)
        output(after, half, half)
        for lane in downs[0] + downs[1]:
            lane.finish()
        for copy in final + stages[-2:] + [hidden_store, second_store, att_store]:
            copy.wait()

    pl.run_scoped(
        feed,
        pltpu.VMEM((4, rows, cols), f32),
        pltpu.VMEM((4, rows, cols), f32),
        pltpu.VMEM((4, rows, cols), f32),
        pltpu.VMEM((4, rows, cols), bf16),
        pltpu.VMEM((4, rows, model), bf16),
        pltpu.VMEM((2, 4, rows, size), bf16),
    )
    for copy in copies:
        copy.wait_send()


def middle(lin, key_bias, cosine, sine, segments, x, out_t, small, gate, up, down, g, n):
    rows, model = x.shape
    size, cols = gate.shape
    seq = 4 * rows
    width = out_t.shape[1]
    heads = width // HD
    shape = jax.ShapeDtypeStruct
    return pl.pallas_call(
        lambda *refs: middle_kernel(n, *refs),
        in_specs=[HBM] + [VMEM] * 4 + [HBM, HBM, VMEM, HBM, HBM, VMEM, HBM],
        out_specs=[HBM, HBM, HBM, VMEM] + [HBM] * 9,
        out_shape=[
            shape((width, seq), bf16),
            shape((width, seq), bf16),
            shape((width, seq), bf16),
            shape((heads, seq), f32),
            shape((seq, width), bf16),
            shape((rows, model), f32),
            shape((4, rows, model), bf16),
            shape((n, size, cols), bf16),
            shape((n, size, cols), bf16),
            shape((4, rows, cols), bf16),
            shape((4, rows, model), bf16),
            shape((4, rows, cols), bf16),
            shape((4, rows, cols), bf16),
        ],
        scratch_shapes=[
            pltpu.VMEM((n, size, cols), bf16),
            pltpu.VMEM((n, size, cols), bf16),
            pltpu.VMEM((n, size, cols), bf16),
            pltpu.VMEM((4, rows, model), bf16),
            pltpu.VMEM((2, rows, model), bf16),
            pltpu.VMEM((2, rows, model), bf16),
            pltpu.VMEM((rows, model), bf16),
            pltpu.VMEM((rows, model), bf16),
            pltpu.VMEM((rows, model), f32),
            DMA((8, n - 1)),
            DMA((8, n - 1)),
            DMA((6,)),
            DMA((6,)),
            DMA((20 + 3 * width // (2 * HD),)),
            DMA((2, n)),
            DMA((2 * n,)),
        ],
        compiler_params=pltpu.CompilerParams(collective_id=2, has_side_effects=True, vmem_limit_bytes=62 << 20),
        cost_estimate=pl.CostEstimate(
            flops=10 * seq * model * cols, bytes_accessed=60 << 20, transcendentals=heads * seq * seq
        ),
        name="middle",
    )(
        lin, key_bias, cosine, sine, segments[None, :],
        x, out_t, small, gate, up, down, g.reshape(4, rows, model),
    )

class Sum:
    def __init__(self, place, slots, way, send, recv):
        self.place, self.slots, self.way, self.send, self.recv = place, slots, way, send, recv

    def whose(self, step):
        return self.place.owner(1 + step if self.way else -1 - step)

    def copy(self, step):
        return pltpu.make_async_remote_copy(
            src_ref=self.slots.at[step - 1],
            dst_ref=self.slots.at[step],
            send_sem=self.send.at[step - 1],
            recv_sem=self.recv.at[step - 1],
            device_id={"dp": self.place.down if self.way else self.place.up},
            device_id_type=MESH,
        )

    def tick(self, step, product, final):
        if step > 0:
            self.copy(step).wait_recv()
        cols = self.slots.shape[2]
        for low in range(0, cols, 512):
            tile = slice(low, min(low + 512, cols))
            part = product(tile)
            if step > 0:
                part = part + self.slots[step, :, tile].astype(f32)
            if step == self.place.n - 1:
                final(tile, part)
            else:
                self.slots[step, :, tile] = part.astype(bf16)
        if step < self.place.n - 1:
            self.copy(step + 1).start()

    def finish(self):
        for step in range(1, self.place.n):
            self.copy(step).wait_send()


def columns_of(left, whose, size, way):
    half = size // 2
    return left[:, pl.ds(pl.multiple_of(whose * size + way * half, half), half)].T


def retreat_pair(pair, q_all, k_all, v_all, d_all, logs, cosine, sine, mask, dk_acc, dv_acc, tmp, vec):
    width, seq = q_all.shape

    @pl.loop(0, 2)
    def _(j):
        head = pair * 2 + j
        rows = pl.ds(pl.multiple_of(head * HD, HD), HD)
        q, k, v, d = q_all[rows, :], k_all[rows, :], v_all[rows, :], d_all[rows, :]
        keys, values = k.T, v.T
        q_small = q * jnp.asarray(SCALE, bf16)
        dk_acc[...] = jnp.zeros_like(dk_acc)
        dv_acc[...] = jnp.zeros_like(dv_acc)
        cols = []
        for start in range(0, seq, QB):
            end = start + QB
            here = slice(start, end)
            scores = dot(keys[:end], q_small[:, here], ((1,), (0,))) + mask[:end, here]
            probs = jnp.exp(scores - logs[pl.ds(head, 1), here])
            grad = dot(values[:end], d[:, here], ((1,), (0,)))
            both = probs * grad
            inner = jnp.sum(both, axis=0, keepdims=True)
            grad = ((both - probs * inner) * SCALE).astype(bf16)
            probs = probs.astype(bf16)
            cols.append(dot(k[:, :end], grad, ((1,), (0,))))
            dk_acc[:, :end] += dot(q[:, here], grad, ((1,), (1,)))
            dv_acc[:, :end] += dot(d[:, here], probs, ((1,), (1,)))
        dq = rotate(jnp.concatenate(cols, axis=1), cosine, sine, -1.0)
        dk = rotate(dk_acc[...], cosine, sine, -1.0)
        dv = dv_acc[...]
        mine = pl.ds(pl.multiple_of(j * HD, HD), HD)
        for part, (out, value) in enumerate(((q_all, dq), (k_all, dk), (v_all, dv))):
            out[rows, :] = value.astype(bf16)
            lanes = value[:, :128]
            for i in range(128, seq, 128):
                lanes = lanes + value[:, i : i + 128]
            tmp[part, mine, :] = lanes

    for part in range(3):
        at = part * width + pair * 2 * HD
        vec[4:5, at : at + 2 * HD] = jnp.sum(tmp[part].T, axis=0, keepdims=True)


def back_kernel(
    n,
    dgate_ref, dup_ref, hidden_ref, second_ref, g_ref, gate_ref, up_ref, att_ref, small, out_ref,
    q_ref, k_ref, v_ref, logs, cos_ref, sin_ref, seg_row,
    down_sum, gate_sum, up_sum, datt_out, resid_out, dlin_out, vec,
    slots, g, second, hidden, dgate, dup, near_send, near_recv, far_send, far_recv, datt, acc,
    send, recv, x_send, x_recv, local,
):
    place = Place(n)
    t = place.t
    rows, model = att_ref.shape
    size, cols = gate_ref.shape[1:]
    seq, width = 4 * rows, out_ref.shape[1]
    loads = [
        pltpu.make_async_copy(src, dst, local.at[i])
        for i, (src, dst) in enumerate(
            ((g_ref, g), (hidden_ref, hidden), (second_ref, second), (dgate_ref, dgate), (dup_ref, dup))
        )
    ]
    for load in loads[:2]:
        load.start()
    place.barrier([place.up, place.down], [place.core, place.chip])

    lanes = [[Sum(place, slots.at[2 * i + way], way, send.at[2 * i + way], recv.at[2 * i + way]) for way in range(2)] for i in range(3)]
    sources = ((g, hidden), (second, dgate), (second, dup))
    sums = (down_sum, gate_sum, up_sum)

    def stored(i):
        return pltpu.make_async_copy(datt.at[:, pl.ds(0, cols)], sums[i], local.at[6 + i])

    def tick(step, i):
        left, right = sources[i]
        if step == n - 1:
            (stored(i - 1) if i else datt_copy()).wait()
        for lane in lanes[i]:

            def final(tile, total):
                datt[lane.way * size // 2 : (lane.way + 1) * size // 2, tile] = total

            block = columns_of(left, lane.whose(step), size, lane.way)
            lane.tick(step, lambda tile: dot(block, right[:, tile], ((1,), (0,))), final)
        if step == n - 1:
            stored(i).start()

    plan = iter([(step, i) for step in range(n) for i in range(3)])

    def advance(count=1):
        for _ in range(count):
            tick(*next(plan))

    def datt_copy():
        return pltpu.make_async_copy(datt, datt_out, local.at[9])

    swap = Exchange(x_send, x_recv)
    near = [swap.copy(i, near_send.at[i], near_recv.at[i], place.core) for i in range(2)]
    far = swap.copy(2, far_send, far_recv, place.chip)
    to_chip = swap.copy(3, far_send, resid_out.at[t], place.chip)
    to_core = swap.copy(4, far_send, resid_out.at[t], place.core)
    relay = swap.copy(5, resid_out.at[place.chip], resid_out.at[place.chip], place.core)
    keep = pltpu.make_async_copy(far_send, resid_out.at[t], local.at[10])
    own = pl.ds(pl.multiple_of(t * rows, rows), rows)

    def feed(gate, up):
        weights = [
            pltpu.make_async_copy(gate_ref, gate, local.at[11]),
            pltpu.make_async_copy(up_ref, up, local.at[12]),
        ]
        loads[0].wait()
        loads[1].wait()
        for load in loads[2:]:
            load.start()
        advance()
        loads[2].wait()
        loads[3].wait()
        for copy in weights:
            copy.start()
        advance()
        loads[4].wait()
        advance()
        for copy in weights:
            copy.wait()

        def product(block, j):
            at = pl.ds(pl.multiple_of(block * rows, rows), rows)
            return dot(dgate[at, :], gate[j], ((1,), (1,))) + dot(dup[at, :], up[j], ((1,), (1,)))

        for i, block in enumerate((place.cross, place.core)):
            for j in range(n):
                near_send[i, :, j * size : (j + 1) * size] = product(block, j).astype(bf16)
            near[i].start()
            advance()
        near[0].wait_recv()
        for j in range(n):
            tile = slice(j * size, (j + 1) * size)
            far_send[:, tile] = (product(place.chip, j) + near_recv[0, :, tile].astype(f32)).astype(bf16)
        far.start()
        advance()
        near[1].wait_recv()
        for j in range(n):
            tile = slice(j * size, (j + 1) * size)
            datt[:, tile] = product(t, j) + near_recv[1, :, tile].astype(f32)
        advance()

    pl.run_scoped(feed, pltpu.VMEM((n, size, cols), bf16), pltpu.VMEM((n, size, cols), bf16))

    def attention(attended, mask, q_all, k_all, v_all, d_all, out_t, dk_acc, dv_acc, tmp, column):
        load_attended = pltpu.make_async_copy(att_ref, attended, local.at[5])
        load_attended.start()
        fetch = [
            pltpu.make_async_copy(src, dst, local.at[13 + i])
            for i, (src, dst) in enumerate(((out_ref, out_t), (q_ref, q_all), (k_ref, k_all), (v_ref, v_all)))
        ]
        for copy in fetch:
            copy.start()
        build_mask(mask, column, seg_row)
        count = small.shape[2]
        gain = lane_vector(small, 2 * size // count, size // count)
        acc[...] = jnp.zeros_like(acc)
        advance(1)
        far.wait_recv()
        far.wait_send()
        load_attended.wait()

        @pl.loop(0, rows // 16)
        def _(i):
            here = pl.ds(pl.multiple_of(i * 16, 16), 16)
            value = attended[here, :]
            center = value - jnp.mean(value, axis=1, keepdims=True)
            rstd = lax.rsqrt(jnp.mean(center * center, axis=1, keepdims=True) + EPS)
            hat = center * rstd
            incoming = datt[here, :] + far_recv[here, :].astype(f32)
            acc[0] += incoming * hat
            acc[1] += incoming
            scaled = incoming * gain
            back = rstd * (
                scaled - jnp.mean(scaled, axis=1, keepdims=True) - hat * jnp.mean(scaled * hat, axis=1, keepdims=True)
            )
            whole = g[pl.ds(pl.multiple_of(t * rows + i * 16, 16), 16), :].astype(f32) + back
            datt[here, :] = whole
            far_send[here, :] = whole.astype(bf16)

        to_chip.start()
        to_core.start()
        keep.start()
        datt_copy().start()
        vec[...] = jnp.zeros_like(vec)
        vec[2:3, :] = jnp.sum(acc[0], axis=0, keepdims=True)
        vec[3:4, :] = jnp.sum(acc[1], axis=0, keepdims=True)
        for copy in near:
            copy.wait_send()
        fetch[0].wait()

        def mix(block, source):
            value = dot(source[...], out_t[...], ((1,), (0,))).astype(bf16)
            d_all[:, pl.ds(pl.multiple_of(block * rows, rows), rows)] = value.T

        def bring(block, slot, number):
            return pltpu.make_async_copy(resid_out.at[block], near_send.at[slot], local.at[number])

        mix(t, far_send)
        advance()
        to_core.wait_recv()
        first = bring(place.core, 0, 17)
        first.start()
        first.wait()
        mix(place.core, near_send.at[0])
        advance(2)
        to_chip.wait_recv()
        relay.start()
        second_block = bring(place.chip, 1, 18)
        second_block.start()
        second_block.wait()
        mix(place.chip, near_send.at[1])
        relay.wait_recv()
        third = bring(place.cross, 0, 19)
        third.start()
        third.wait()
        mix(place.cross, near_send.at[0])
        for copy in fetch[1:]:
            copy.wait()
        cosine, sine = cos_ref[...], sin_ref[...]
        for pair in range(width // (2 * HD)):
            advance()
            retreat_pair(pair, q_all, k_all, v_all, d_all, logs, cosine, sine, mask, dk_acc, dv_acc, tmp, vec)
            here = slice(pair * 2 * HD, (pair + 1) * 2 * HD)
            out_t[0:seq, here] = q_all[here, :].T
            out_t[seq : 2 * seq, here] = k_all[here, :].T
            turned = v_all[here, :].T
            for block in range(4):
                at = block * width + pair * 2 * HD
                near_recv[0, :, at : at + 2 * HD] = turned[block * rows : (block + 1) * rows]
        final = [
            pltpu.make_async_copy(out_t.at[pl.ds(i * seq, seq)], dlin_out.at[:, pl.ds(i * width, width)], local.at[20 + i])
            for i in range(2)
        ] + [
            pltpu.make_async_copy(
                near_recv.at[0, :, pl.ds(block * width, width)],
                dlin_out.at[pl.ds(block * rows, rows), pl.ds(2 * width, width)],
                local.at[22 + block],
            )
            for block in range(4)
        ]
        for copy in final:
            copy.start()
        advance(2)
        for copy in final:
            copy.wait()

    pl.run_scoped(
        attention,
        pltpu.VMEM((rows, model), f32),
        pltpu.VMEM((seq, seq), f32),
        pltpu.VMEM((width, seq), bf16),
        pltpu.VMEM((width, seq), bf16),
        pltpu.VMEM((width, seq), bf16),
        pltpu.VMEM((width, seq), bf16),
        pltpu.VMEM((model, width), bf16),
        pltpu.VMEM((HD, seq), f32),
        pltpu.VMEM((HD, seq), f32),
        pltpu.VMEM((3, 2 * HD, 128), f32),
        pltpu.VMEM((seq, 128), f32),
    )
    for step in plan:
        tick(*step)
    for pair in lanes:
        for lane in pair:
            lane.finish()
    for copy in (to_chip, to_core, relay):
        copy.wait_send()
    keep.wait()
    stored(2).wait()


def back(dgate, dup, hidden, second, g, gate, up, attended, small, out_t, q, k, v, logs, cosine, sine, segments, n):
    rows, model = attended.shape
    size, cols = model // n, hidden.shape[1]
    seq, width = 4 * rows, out_t.shape[1]
    shape = jax.ShapeDtypeStruct
    return pl.pallas_call(
        lambda *refs: back_kernel(n, *refs),
        in_specs=[HBM] * 8 + [VMEM] + [HBM] * 4 + [VMEM] * 4,
        out_specs=[HBM] * 6 + [VMEM],
        out_shape=[
            shape((size, cols), f32),
            shape((size, cols), f32),
            shape((size, cols), f32),
            shape((rows, model), f32),
            shape((4, rows, model), bf16),
            shape((seq, 3 * width), bf16),
            shape((8, model), f32),
        ],
        scratch_shapes=[
            pltpu.VMEM((6, n, size // 2, cols), bf16),
            pltpu.VMEM((seq, model), bf16),
            pltpu.VMEM((seq, model), bf16),
            pltpu.VMEM((seq, cols), bf16),
            pltpu.VMEM((seq, cols), bf16),
            pltpu.VMEM((seq, cols), bf16),
            pltpu.VMEM((2, rows, model), bf16),
            pltpu.VMEM((2, rows, model), bf16),
            pltpu.VMEM((rows, model), bf16),
            pltpu.VMEM((rows, model), bf16),
            pltpu.VMEM((rows, model), f32),
            pltpu.VMEM((2, 16, model), f32),
            DMA((6, n - 1)),
            DMA((6, n - 1)),
            DMA((6,)),
            DMA((6,)),
            DMA((26,)),
        ],
        compiler_params=pltpu.CompilerParams(collective_id=3, has_side_effects=True, vmem_limit_bytes=62 << 20),
        cost_estimate=pl.CostEstimate(
            flops=14 * seq * model * cols, bytes_accessed=60 << 20, transcendentals=width // HD * seq * seq
        ),
        name="back",
    )(
        dgate, dup, hidden, second, g, gate.reshape(n, size, cols), up.reshape(n, size, cols), attended, small, out_t,
        q, k, v, logs, cosine, sine, segments[None, :],
    )

def leave_kernel(
    n,
    normed_ref, dlin_ref, qkv_ref, mixed_ref, resid_ref, datt_ref, x_ref, att_ref, ffn_ref, small, vec_ref,
    layer_out, input_out, query_sum, key_sum, value_sum, out_sum, vec_out,
    wide, narrow, normed, dlin, qkv, turned, mixed, resid, datt, attended, x, first, near_send, near_recv, far_send, far_recv,
    ffn_own, ffn_recv, ffn_send, ffn_far, layer, acc, totals, wsum, osum, vecs, vec_recv,
    send, recv, x_send, x_recv, v_send, v_recv, local,
):
    place = Place(n)
    t, me = place.t, place.me
    rows, model = att_ref.shape
    size = model // n
    total_cols = dlin_ref.shape[1]
    width = total_cols // 3
    part = total_cols // 2
    loads = [
        pltpu.make_async_copy(src, dst, local.at[i])
        for i, (src, dst) in enumerate(
            (
                (normed_ref, normed),
                (dlin_ref, dlin),
                (resid_ref, resid),
                (mixed_ref, mixed),
                (qkv_ref, qkv),
                (ffn_ref.at[place.chip], ffn_own.at[0]),
                (ffn_ref.at[t], ffn_own.at[1]),
                (att_ref, attended),
                (x_ref, x),
                (datt_ref, datt),
            )
        )
    ]
    for load in loads[:2]:
        load.start()
    hops = [1, 2, 4]
    partners = [me + hop - 2 * hop * lax.rem(lax.div(me, hop), 2) for hop in hops]
    place.barrier([place.up, place.down] + partners, [place.core, place.chip])

    lanes = [
        [Sum(place, wide.at[2 * i + way], way, send.at[2 * i + way], recv.at[2 * i + way]) for way in range(2)] for i in range(2)
    ] + [[Sum(place, narrow.at[way], way, send.at[4 + way], recv.at[4 + way]) for way in range(2)]]

    swap = Exchange(x_send, x_recv)
    near = [swap.copy(i, near_send.at[i], near_recv.at[i], place.core) for i in range(2)]
    far = swap.copy(2, far_send, far_recv, place.chip)
    outs = [swap.copy(3 + i, ffn_ref.at[block], ffn_recv.at[i], place.core) for i, block in enumerate((place.cross, place.core))]
    outs_far = swap.copy(5, ffn_send, ffn_far, place.chip)

    def tick(step, i):
        for lane in lanes[i]:
            half = slice(lane.way * size // 2, (lane.way + 1) * size // 2)
            if i == 2:

                def product(left, tile):
                    return dot(left, mixed[:, tile], ((1,), (0,)))

                def final(tile, total):
                    osum[tile, half] = total.T

            else:

                def product(left, tile):
                    return dot(left, dlin[:, part * i + tile.start : part * i + tile.stop], ((1,), (0,)))

                def final(tile, total):
                    wsum[half, part * i + tile.start : part * i + tile.stop] = total

            left = columns_of(resid if i == 2 else normed, lane.whose(step), size, lane.way)
            lane.tick(step, lambda tile: product(left, tile), final)

    plan = iter([(step, i) for step in range(n) for i in range(3)])

    def advance(count=1):
        for _ in range(count):
            tick(*next(plan))

    loads[0].wait()
    loads[1].wait()
    for load in loads[2:5]:
        load.start()
    advance(2)
    for load in loads[5:]:
        load.start()
    loads[2].wait()
    loads[3].wait()
    advance()
    loads[4].wait()

    def lines(block):
        return dlin[pl.ds(pl.multiple_of(block * rows, rows), rows), :]

    def product(block, use):
        for j in range(n):
            use(slice(j * size, (j + 1) * size), dot(lines(block), turned[j], ((1,), (0,))))

    for j in range(n):
        turned[j] = qkv[j].T
    for i, block in enumerate((place.cross, place.core)):

        def use_near(tile, value):
            near_send[i, :, tile] = value.astype(bf16)

        product(block, use_near)
        near[i].start()
        advance()
    near[0].wait_recv()

    def use_far(tile, value):
        far_send[:, tile] = (value + near_recv[0, :, tile].astype(f32)).astype(bf16)

    product(place.chip, use_far)
    far.start()
    advance()

    def use_own(tile, value):
        first[:, tile] = value

    product(t, use_own)
    near[1].wait_recv()
    advance()
    for copy in outs:
        copy.start()
    advance()
    outs[0].wait_recv()
    loads[5].wait()
    for j in range(0, rows, 64):
        tile = slice(j, j + 64)
        ffn_send[tile, :] = (ffn_own[0, tile, :].astype(f32) + ffn_recv[0, tile, :].astype(f32)).astype(bf16)
    outs_far.start()

    count = small.shape[2]
    gain = lane_vector(small, 0, size // count)
    acc[...] = jnp.zeros_like(acc)
    loads[8].wait()
    loads[9].wait()
    advance(4)
    far.wait_recv()

    @pl.loop(0, rows // 16)
    def _(i):
        here = pl.ds(pl.multiple_of(i * 16, 16), 16)
        value = x[here, :].astype(f32)
        center = value - jnp.mean(value, axis=1, keepdims=True)
        rstd = lax.rsqrt(jnp.mean(center * center, axis=1, keepdims=True) + EPS)
        hat = center * rstd
        incoming = first[here, :] + near_recv[1, here, :].astype(f32) + far_recv[here, :].astype(f32)
        acc[0] += incoming * hat
        acc[1] += incoming
        scaled = incoming * gain
        back_rows = rstd * (
            scaled - jnp.mean(scaled, axis=1, keepdims=True) - hat * jnp.mean(scaled * hat, axis=1, keepdims=True)
        )
        totals[here, :] = datt[here, :] + back_rows

    input_store = pltpu.make_async_copy(totals, input_out, local.at[11])
    input_store.start()
    vecs[0] = vec_ref[...]
    vecs[0, 0:1, :] = jnp.sum(acc[0], axis=0, keepdims=True)
    vecs[0, 1:2, :] = jnp.sum(acc[1], axis=0, keepdims=True)

    def hop(number):
        there = {"tensor": (place.core, place.chip)[number]} if number < 2 else {"dp": partners[number - 2]}
        return pltpu.make_async_remote_copy(
            src_ref=vecs.at[number],
            dst_ref=vec_recv.at[number],
            send_sem=v_send.at[number],
            recv_sem=v_recv.at[number],
            device_id=there,
            device_id_type=MESH,
        )

    for number in range(5):
        hop(number).start()
        advance(1 if number < 2 else 2)
        hop(number).wait_recv()
        summed = vecs[number] + vec_recv[number]
        if number < 2:
            row = lax.broadcasted_iota(jnp.int32, summed.shape, 0)
            summed = jnp.where(row < 4, summed, vecs[number])
        vecs[number + 1] = summed
    vec_out[...] = vecs[5]
    advance(2)
    outs[1].wait_recv()
    outs_far.wait_recv()
    loads[6].wait()
    loads[7].wait()
    for j in range(0, rows, 64):
        tile = slice(j, j + 64)
        layer[tile, :] = (
            attended[tile, :]
            + ffn_own[1, tile, :].astype(f32)
            + ffn_recv[1, tile, :].astype(f32)
            + ffn_far[tile, :].astype(f32)
        ).astype(bf16)
    layer_store = pltpu.make_async_copy(layer, layer_out, local.at[10])
    layer_store.start()
    results = [
        pltpu.make_async_copy(wsum.at[:, pl.ds(i * width, width)], out, local.at[12 + i])
        for i, out in enumerate((query_sum, key_sum, value_sum))
    ] + [pltpu.make_async_copy(osum, out_sum, local.at[15])]
    for item in plan:
        tick(*item)
        if item == (n - 1, 1):
            for copy in results[:-1]:
                copy.start()
    results[-1].start()
    for group in lanes:
        for lane in group:
            lane.finish()
    for copy in near + [far] + outs + [outs_far]:
        copy.wait_send()
    for number in range(5):
        hop(number).wait_send()
    for copy in results + [layer_store, input_store]:
        copy.wait()


def leave(normed, dlin, qkv, mixed, resid, datt, x, attended, ffn, small, vec, n):
    rows, model = x.shape
    size = model // n
    seq, width = mixed.shape
    shape = jax.ShapeDtypeStruct
    own = lambda kind: pltpu.VMEM((rows, model), kind)
    return pl.pallas_call(
        lambda *refs: leave_kernel(n, *refs),
        in_specs=[HBM] * 9 + [VMEM] * 2,
        out_specs=[HBM] * 6 + [VMEM],
        out_shape=[shape((rows, model), bf16), shape((rows, model), f32)]
        + [shape((size, width), f32)] * 3
        + [shape((width, size), f32), shape((8, model), f32)],
        scratch_shapes=[
            pltpu.VMEM((4, n, size // 2, 3 * width // 2), bf16),
            pltpu.VMEM((2, n, size // 2, width), bf16),
            pltpu.VMEM((seq, model), bf16),
            pltpu.VMEM((seq, 3 * width), bf16),
            pltpu.VMEM((n, size, 3 * width), bf16),
            pltpu.VMEM((n, 3 * width, size), bf16),
            pltpu.VMEM((seq, width), bf16),
            pltpu.VMEM((seq, model), bf16),
            own(f32),
            own(f32),
            own(bf16),
            own(f32),
            pltpu.VMEM((2, rows, model), bf16),
            pltpu.VMEM((2, rows, model), bf16),
            own(bf16),
            own(bf16),
            pltpu.VMEM((2, rows, model), bf16),
            pltpu.VMEM((2, rows, model), bf16),
            own(bf16),
            own(bf16),
            own(bf16),
            pltpu.VMEM((2, 16, model), f32),
            own(f32),
            pltpu.VMEM((size, 3 * width), f32),
            pltpu.VMEM((width, size), f32),
            pltpu.VMEM((6, 8, model), f32),
            pltpu.VMEM((5, 8, model), f32),
            DMA((6, n - 1)),
            DMA((6, n - 1)),
            DMA((6,)),
            DMA((6,)),
            DMA((5,)),
            DMA((5,)),
            DMA((16,)),
        ],
        compiler_params=pltpu.CompilerParams(collective_id=4, has_side_effects=True, vmem_limit_bytes=62 << 20),
        cost_estimate=pl.CostEstimate(flops=14 * seq * model * width, bytes_accessed=40 << 20, transcendentals=0),
        name="leave",
    )(normed, dlin, qkv.reshape(n, size, 3 * width), mixed, resid, datt, x, attended, ffn.reshape(4, rows, model), small, vec)

def finish_kernel(
    n,
    layer, input_grad, query_sum, key_sum, value_sum, out_sum, gate_sum, up_sum, down_sum, vec,
    layer_out, input_out, gain_one, shift_one, query_out, key_out, value_out, bias_q, bias_k, bias_v, out_out, gain_two, shift_two,
    gate_out, up_out, down_out,
    out_in, down_in, down_turned, held_input, held_layer, held, small_held, sems,
):
    loads = [
        pltpu.make_async_copy(src, dst, sems.at[i])
        for i, (src, dst) in enumerate(
            (
                (down_sum, down_in),
                (out_sum, out_in),
                (input_grad, held_input),
                (layer, held_layer),
                (gate_sum, held.at[0]),
                (up_sum, held.at[1]),
                (query_sum, small_held.at[0]),
                (key_sum, small_held.at[1]),
                (value_sum, small_held.at[2]),
            )
        )
    ]
    for load in loads:
        load.start()
    me, t = lax.axis_index("dp"), lax.axis_index("tensor")
    each = gain_one.shape[1]
    at = me * 4 + t
    fit = 128 // each
    for r, out in enumerate((gain_one, shift_one, gain_two, shift_two)):
        wide = vec[r : r + 1, pl.ds(pl.multiple_of(lax.div(at, fit) * 128, 128), 128)]
        value = wide[:, 0:each]
        for i in range(1, fit):
            value = jnp.where(lax.rem(at, fit) == i, wide[:, i * each : (i + 1) * each], value)
        out[...] = value
    heads, per = bias_q.shape
    row = vec[4:5, :]
    for part, out in ((0, bias_q), (2, bias_v)):
        base = part * heads * HD
        own = jnp.concatenate([row[:, base + h * HD : base + (h + 1) * HD] for h in range(heads)], axis=0)
        value = own[:, 0:per]
        for d in range(1, n):
            value = jnp.where(me == d, own[:, d * per : (d + 1) * per], value)
        out[...] = value
    base = heads * HD
    bias_k[...] = jnp.concatenate([row[:, base + h * HD : base + h * HD + ROT] for h in range(heads)], axis=0)
    stores = []

    def store(src, dst):
        stores.append(pltpu.make_async_copy(src, dst, sems.at[9 + len(stores)]))
        stores[-1].start()

    loads[0].wait()
    down_turned[...] = down_in[...].T
    store(down_turned, down_out)
    loads[1].wait()
    store(out_in, out_out)
    for load, src, dst in zip(
        loads[2:],
        (held_input, held_layer, held.at[0], held.at[1], small_held.at[0], small_held.at[1], small_held.at[2]),
        (input_out, layer_out, gate_out, up_out, query_out, key_out, value_out),
    ):
        load.wait()
        store(src, dst)
    for copy in stores:
        copy.wait()


def finish(layer, input_grad, query_sum, key_sum, value_sum, out_sum, gate_sum, up_sum, down_sum, vec, n):
    shape = jax.ShapeDtypeStruct
    size, width = query_sum.shape
    heads, model = width // HD, vec.shape[1]
    each = shape((1, model // (4 * n)), f32)
    bias = shape((heads, HD // n), f32)
    like = lambda value: shape(value.shape, value.dtype)
    results = pl.pallas_call(
        lambda *refs: finish_kernel(n, *refs),
        in_specs=[HBM] * 9 + [VMEM],
        out_specs=[HBM, HBM, VMEM, VMEM, HBM, HBM, HBM, VMEM, VMEM, VMEM, HBM, VMEM, VMEM, HBM, HBM, HBM],
        out_shape=[
            like(layer), like(input_grad), each, each, like(query_sum), like(key_sum), like(value_sum),
            bias, shape((heads, ROT), f32), bias, like(out_sum), each, each,
            like(gate_sum), like(up_sum), shape(down_sum.shape[::-1], f32),
        ],
        scratch_shapes=[
            pltpu.VMEM(out_sum.shape, f32),
            pltpu.VMEM(down_sum.shape, f32),
            pltpu.VMEM(down_sum.shape[::-1], f32),
            pltpu.VMEM(input_grad.shape, f32),
            pltpu.VMEM(layer.shape, bf16),
            pltpu.VMEM((2,) + gate_sum.shape, f32),
            pltpu.VMEM((3,) + query_sum.shape, f32),
            DMA((18,)),
        ],
        compiler_params=pltpu.CompilerParams(vmem_limit_bytes=62 << 20),
        name="finish",
    )(layer, input_grad, query_sum, key_sum, value_sum, out_sum, gate_sum, up_sum, down_sum, vec)
    return tuple(r.reshape(-1) if r.shape[0] == 1 else r for r in results)


def norm_forward(rows):
    center = rows - jnp.mean(rows, axis=-1, keepdims=True)
    rstd = lax.rsqrt(jnp.mean(center * center, axis=-1, keepdims=True) + EPS)
    return center * rstd, rstd


def norm_backward(grad_out, normal, rstd, gain):
    scaled = grad_out * gain
    return rstd * (
        scaled
        - jnp.mean(scaled, axis=-1, keepdims=True)
        - normal * jnp.mean(scaled * normal, axis=-1, keepdims=True)
    )


def local(
    layer_input,
    segments,
    positions,
    first_gain,
    first_shift,
    query_weight,
    key_weight,
    value_weight,
    query_bias,
    key_bias,
    value_bias,
    out_weight,
    second_gain,
    second_shift,
    gate_weight,
    up_weight,
    down_weight,
    out_grad,
):
    ring = Ring()
    n = ring.n
    width = query_weight.shape[1]
    heads = width // HD
    model = layer_input.shape[1]

    per = HD // n
    if ring.ring:
        normed, g_full, qkv, out_t, lin, small = enter(
            layer_input, out_grad, query_weight, key_weight, value_weight, out_weight,
            (first_gain, first_shift, second_gain, second_shift), (query_bias, value_bias), n
        )
        g_full = g_full.reshape(-1, model)
        qkv = qkv.reshape(model, -1)
        out_t = out_t.reshape(model, -1)
    else:
        gather = lambda vector: lax.all_gather(vector, "dp", axis=0, tiled=True).astype(f32)
        gain_one, shift_one, gain_two, shift_two = map(gather, (first_gain, first_shift, second_gain, second_shift))
        bias_query, bias_value = (gather(b.T).T.reshape(-1) for b in (query_bias, value_bias))
        bias_key = jnp.pad(key_bias.astype(f32), ((0, 0), (0, HD - ROT))).reshape(-1)
        bias_lin = jnp.concatenate([bias_query, bias_key, bias_value])
        x_full = tensor_gather(layer_input)
        g_full = tensor_gather(out_grad, after=x_full)
        qkv, _ = ring.gather(jnp.concatenate([query_weight, key_weight, value_weight], axis=1))
        out_t, _ = ring.gather(out_weight.T)
        gate, _ = ring.gather(gate_weight)
        up, _ = ring.gather(up_weight)
        down_t, _ = ring.gather(down_weight.T)
        hat_full, _ = norm_forward(x_full.astype(f32))
        normed = (hat_full * gain_one + shift_one).astype(bf16)
        lin = dot(qkv, normed, ((0,), (1,)))

    freqs = jnp.exp(-(2.0 / ROT) * jnp.arange(HALF).astype(f32) * math.log(10000.0))
    angles = freqs[:, None] * positions.astype(f32)[None, :]
    cosine, sine = jnp.cos(angles), jnp.sin(angles)
    rows = layer_input.astype(f32)
    if ring.ring:
        q_rot, k_rot, v_heads, logs, mixed, attended, second, gate, up, hidden, ffn, grad_gate, grad_up = middle(
            lin, key_bias, cosine, sine, segments, layer_input, out_t, small, gate_weight, up_weight, down_weight, g_full, n
        )
        second, gate, up = second.reshape(-1, model), gate.reshape(model, -1), up.reshape(model, -1)
        hidden, ffn = hidden.reshape(second.shape[0], -1), ffn.reshape(-1, model)
        grad_gate, grad_up = grad_gate.reshape(hidden.shape), grad_up.reshape(hidden.shape)
    else:
        index = jnp.arange(segments.shape[0], dtype=jnp.int32)
        allowed = (index[:, None] <= index[None, :]) & (segments[:, None] == segments[None, :])
        bias = jnp.where(allowed, 0.0, NEG).astype(f32)
        mixed, q_rot, k_rot, v_heads, logs = attend_forward(lin + bias_lin[:, None], cosine, sine, bias)
        attended = rows + tensor_scatter(dot(mixed, out_t, ((1,), (1,))))

        hat_two, rstd_two = norm_forward(attended)
        second = tensor_gather((hat_two * gain_two + shift_two).astype(bf16))
        gate_lin = dot(second, gate, ((1,), (0,)))
        up_lin = dot(second, up, ((1,), (0,)))
        sigma = jax.nn.sigmoid(gate_lin)
        activated = gate_lin * sigma
        hidden = (activated * up_lin).astype(bf16)
        ffn = dot(hidden, down_t, ((1,), (1,)))
        grad_hidden = dot(g_full, down_t, ((1,), (0,)))
        grad_gate = (grad_hidden * up_lin * sigma * (1.0 + gate_lin * (1.0 - sigma))).astype(bf16)
        grad_up = (grad_hidden * activated).astype(bf16)
    if ring.ring:
        down_sum, gate_sum, up_sum, grad_attended, residual, grad_lin, vec = back(
            grad_gate, grad_up, hidden, second, g_full, gate, up, attended, small, out_t,
            q_rot, k_rot, v_heads, logs, cosine, sine, segments, n
        )
        layer_output, input_grad, query_sum, key_sum, value_sum, out_sum, vec = leave(
            normed, grad_lin, qkv, mixed, residual.reshape(-1, model), grad_attended, layer_input, attended, ffn, small, vec, n
        )
        return finish(
            layer_output, input_grad, query_sum, key_sum, value_sum, out_sum, gate_sum, up_sum, down_sum, vec, n
        )
    else:
        down_grad = dot(g_full, hidden, ((0,), (0,)))
        grad_second = tensor_scatter(dot(grad_gate, gate, ((1,), (1,))) + dot(grad_up, up, ((1,), (1,))))
        gate_grad = dot(second, grad_gate, ((0,), (0,)))
        up_grad = dot(second, grad_up, ((0,), (0,)))
        down_sum = ring.scatter(down_grad).T
        gate_sum = ring.scatter(gate_grad)
        up_sum = ring.scatter(up_grad)
        grad_attended = out_grad.astype(f32) + norm_backward(grad_second, hat_two, rstd_two, gain_two)
        residual = tensor_gather(grad_attended.astype(bf16))
        grad_mixed = dot(out_t, residual, ((0,), (1,))).astype(bf16)
        dq, dk, dv, sums = attend_backward(q_rot, k_rot, v_heads, grad_mixed, logs, cosine, sine, bias)
        grad_lin = jnp.concatenate([dq, dk, dv], axis=0)
        sums = sums.reshape(width, 128)[:, :3]
        out_sum = ring.scatter(dot(residual, mixed, ((0,), (0,)))).T
        qkv_sum = ring.scatter(dot(normed, grad_lin, ((0,), (1,))))
        query_sum, key_sum, value_sum = (qkv_sum[:, i * width : (i + 1) * width] for i in range(3))
        grad_first = tensor_scatter(dot(grad_lin, qkv, ((0,), (1,))))
        hat_one, rstd_one = norm_forward(rows)
        input_grad = grad_attended + norm_backward(grad_first, hat_one, rstd_one, gain_one)
        layer_output = (attended + tensor_scatter(ffn.astype(f32))).astype(bf16)
        vectors = jnp.stack(
            [
                jnp.sum(grad_first * hat_one, axis=0),
                jnp.sum(grad_first, axis=0),
                jnp.sum(grad_second * hat_two, axis=0),
                jnp.sum(grad_second, axis=0),
            ]
        )
        packed = sum_all(jnp.concatenate([sum_all(vectors, ["tensor"]).reshape(-1), sums.T.reshape(-1)]), ["dp"])
        vectors, sums = packed[: 4 * model].reshape(4, model), packed[4 * model :].reshape(3, width)

    each = model // (n * lax.axis_size("tensor"))
    at = ring.me * lax.axis_size("tensor") + lax.axis_index("tensor")
    vectors = lax.dynamic_slice(vectors.reshape(4, -1, each), (0, at, 0), (4, 1, each))[:, 0]
    sums = sums.reshape(3, heads, n, per)
    mine = lax.dynamic_slice(sums, (0, 0, ring.me, 0), (3, heads, 1, per))[:, :, 0]
    key_bias_sum = sums[1].reshape(heads, HD)[:, :ROT]

    return (
        layer_output,
        input_grad,
        vectors[0],
        vectors[1],
        query_sum,
        key_sum,
        value_sum,
        mine[0],
        key_bias_sum,
        mine[2],
        out_sum,
        vectors[2],
        vectors[3],
        gate_sum,
        up_sum,
        down_sum,
    )


def solution(mesh):
    both = ("dp", "tensor")
    return jax.shard_map(
        local,
        mesh=mesh,
        in_specs=(
            P(both, None),
            P("dp"),
            P("dp"),
            P("dp"),
            P("dp"),
            P("dp", "tensor"),
            P("dp", "tensor"),
            P("dp", "tensor"),
            P("tensor", "dp"),
            P("tensor", None),
            P("tensor", "dp"),
            P("tensor", "dp"),
            P("dp"),
            P("dp"),
            P("dp", "tensor"),
            P("dp", "tensor"),
            P("tensor", "dp"),
            P(both, None),
        ),
        out_specs=(
            P(both, None),
            P(both, None),
            P(both),
            P(both),
            P("dp", "tensor"),
            P("dp", "tensor"),
            P("dp", "tensor"),
            P("tensor", "dp"),
            P("tensor", None),
            P("tensor", "dp"),
            P("tensor", "dp"),
            P(both),
            P(both),
            P("dp", "tensor"),
            P("dp", "tensor"),
            P("tensor", "dp"),
        ),
        check_vma=False,
    )
```

```python
import math

import jax
import jax.numpy as jnp
from jax import lax
from jax.experimental import pallas as pl
from jax.experimental.pallas import tpu as pltpu
from jax.sharding import PartitionSpec as P

HD = 64
ROT = 16
SEQ = 1024
HALF = ROT // 2
SCALE = HD ** (-0.5)

EPS = 1e-05
NEG = -1e30
QB = 256
f32 = jnp.float32
bf16 = jnp.bfloat16


def barrier(value, after):
    return lax.optimization_barrier((value, after))[0]


class Ring:
    def __init__(self):
        self.n = lax.axis_size("dp")
        self.ring = self.n == 8 and lax.axis_size("tensor") == 4
        order = list(range(0, self.n, 2)) + list(range(self.n - 1, 0, -2))
        self.up = [(order[i], order[(i + 1) % self.n]) for i in range(self.n)]
        self.down = [(b, a) for a, b in self.up]
        me = lax.axis_index("dp")
        self.me = me
        self.pos = jnp.where(me % 2 == 0, me // 2, self.n - 1 - (me - 1) // 2)

    def owner(self, offset):
        p = (self.pos + offset + 2 * self.n) % self.n
        return jnp.where(p < self.n // 2, 2 * p, 2 * (self.n - 1 - p) + 1)

    def gather(self, shard, pieces=1, after=None):
        n = self.n
        rows, cols = shard.shape
        if not self.ring:
            return lax.all_gather(shard, "dp", axis=0, tiled=True), [shard] * n
        if after is not None:
            shard = barrier(shard, after)
        full = jnp.zeros((n, rows, cols), shard.dtype)
        full = lax.dynamic_update_slice(full, shard[None], (self.me, 0, 0))
        size = rows // (2 * pieces)
        lanes = []
        for k in range(2 * pieces):
            lanes.append([k % 2, k * size, shard[k * size : (k + 1) * size]])
        marks = []
        for step in range(1, n):
            for lane in lanes:
                way, base, block = lane
                block = lax.ppermute(block, "dp", self.down if way else self.up)
                lane[2] = block
                whose = self.owner(step if way else -step)
                full = lax.dynamic_update_slice(full, block[None], (whose, base, 0))
            marks.append(lanes[-1][2])
        return full.reshape(n * rows, cols), marks

    def scatter(self, partial, pieces=1, after=None):
        n = self.n
        if not self.ring:
            return lax.psum_scatter(partial.astype(bf16), "dp", scatter_dimension=0, tiled=True).astype(f32)
        cols = partial.shape[1]
        rows = partial.shape[0] // n
        partial = partial.reshape(n, rows, cols)
        size = rows // (2 * pieces)
        done = []
        for k in range(2 * pieces):
            way = k % 2

            def block(step):
                whose = self.owner(1 + step if way else -1 - step)
                return lax.dynamic_slice(partial, (whose, k * size, 0), (1, size, cols))[0].astype(f32)

            moving = block(0)
            for step in range(1, n):
                got = lax.ppermute(moving.astype(bf16), "dp", self.down if way else self.up)
                moving = got.astype(f32) + block(step)
            done.append(moving)
        return jnp.concatenate(done, axis=0)


CORE = [(0, 1), (1, 0), (2, 3), (3, 2)]
CHIP = [(0, 2), (2, 0), (1, 3), (3, 1)]


def tensor_gather(rows, after=None):
    if lax.axis_size("tensor") != 4:
        return lax.all_gather(rows, "tensor", axis=0, tiled=True)
    if after is not None:
        rows = barrier(rows, after)
    t = lax.axis_index("tensor")
    far = lax.ppermute(rows, "tensor", CHIP)
    near = lax.ppermute(rows, "tensor", CORE)
    last = lax.ppermute(far, "tensor", CORE)
    full = jnp.zeros((4,) + rows.shape, rows.dtype)
    for flip, block in ((0, rows), (1, near), (2, far), (3, last)):
        full = lax.dynamic_update_slice(full, block[None], (t ^ flip, 0, 0))
    return full.reshape(4 * rows.shape[0], rows.shape[1])


def tensor_scatter(partial):
    if lax.axis_size("tensor") != 4:
        return lax.psum_scatter(partial.astype(bf16), "tensor", scatter_dimension=0, tiled=True).astype(f32)
    t = lax.axis_index("tensor")
    rows = partial.shape[0] // 4
    blocks = partial.reshape(4, rows, partial.shape[1])

    def block(flip):
        return lax.dynamic_slice(blocks, (t ^ flip, 0, 0), (1,) + blocks.shape[1:])[0]

    other = lax.ppermute(block(3).astype(bf16), "tensor", CORE)
    own = lax.ppermute(block(1).astype(bf16), "tensor", CORE)
    far = lax.ppermute((block(2) + other.astype(f32)).astype(bf16), "tensor", CHIP)
    return block(0) + own.astype(f32) + far.astype(f32)


def sum_all(vector, axes):
    for axis in axes:
        n = lax.axis_size(axis)
        if n & (n - 1):
            vector = lax.psum(vector, axis)
            continue
        step = 1
        while step < n:
            vector = vector + lax.ppermute(vector, axis, [(i, i ^ step) for i in range(n)])
            step *= 2
    return vector


def rotate(rows, cosine, sine, direction):
    first, second = rows[:HALF], rows[HALF:ROT]
    return jnp.concatenate(
        [first * cosine - direction * second * sine, second * cosine + direction * first * sine, rows[ROT:]], axis=0
    )


def dot(a, b, dims):
    return lax.dot_general(a, b, ((dims[0], dims[1]), ((), ())), preferred_element_type=f32)


def forward_kernel(q_ref, k_ref, v_ref, cos_ref, sin_ref, bias_ref, mixed_ref, q_out, k_out, v_out, log_ref):
    seq = q_ref.shape[1]
    cosine, sine = cos_ref[...], sin_ref[...]
    v_all = v_ref[...].astype(bf16)
    v_out[...] = v_all
    parts = []
    for head in range(q_ref.shape[0] // HD):
        rows = slice(head * HD, (head + 1) * HD)
        q = rotate(q_ref[rows, :], cosine, sine, 1.0).astype(bf16)
        k = rotate(k_ref[rows, :], cosine, sine, 1.0).astype(bf16)
        q_out[rows, :] = q
        k_out[rows, :] = k
        keys = k.T
        values = v_all[rows, :]
        q = q * jnp.asarray(SCALE, bf16)
        cols = []
        for start in range(0, seq, QB):
            end = start + QB
            scores = dot(keys[:end], q[:, start:end], ((1,), (0,))) + bias_ref[:end, start:end]
            top = jnp.max(scores, axis=0, keepdims=True)
            expo = jnp.exp(scores - top)
            total = jnp.sum(expo, axis=0, keepdims=True)
            probs = (expo * (1.0 / total)).astype(bf16)
            cols.append(dot(values[:, :end], probs, ((1,), (0,))).astype(bf16))
            log_ref[0, head : head + 1, start:end] = top + jnp.log(total)
        parts.append(jnp.concatenate(cols, axis=1))
    mixed_ref[...] = jnp.concatenate(parts, axis=0).T


def attend_forward(lin, cosine, sine, bias):
    width, seq = lin.shape[0] // 3, lin.shape[1]
    pair = 2 * HD
    count = width // pair
    outs = []
    block = lambda base: pl.BlockSpec((pair, seq), lambda i: (base * count + i, 0))
    whole = lambda shape: pl.BlockSpec(shape, lambda i: (0, 0))
    return pl.pallas_call(
        forward_kernel,
        grid=(count,),
        in_specs=[block(0), block(1), block(2), whole(cosine.shape), whole(sine.shape), whole(bias.shape)],
        out_specs=[
            pl.BlockSpec((seq, pair), lambda i: (0, i)),
            pl.BlockSpec((pair, seq), lambda i: (i, 0)),
            pl.BlockSpec((pair, seq), lambda i: (i, 0)),
            pl.BlockSpec((pair, seq), lambda i: (i, 0)),
            pl.BlockSpec((1, 2, seq), lambda i: (i, 0, 0)),
        ],
        out_shape=[
            jax.ShapeDtypeStruct((seq, width), bf16),
            jax.ShapeDtypeStruct((width, seq), bf16),
            jax.ShapeDtypeStruct((width, seq), bf16),
            jax.ShapeDtypeStruct((width, seq), bf16),
            jax.ShapeDtypeStruct((count, 2, seq), f32),
        ],
        compiler_params=pltpu.CompilerParams(vmem_limit_bytes=48 << 20),
        cost_estimate=pl.CostEstimate(
            flops=4 * width * seq * seq, bytes_accessed=30 << 20, transcendentals=width // HD * seq * seq
        ),
        name="attend_forward",
    )(lin, lin, lin, cosine, sine, bias)


def backward_kernel(q_ref, k_ref, v_ref, d_ref, log_ref, cos_ref, sin_ref, bias_ref, dq_out, dk_out, dv_out, sums_ref, dk_acc, dv_acc):
    seq = q_ref.shape[1]
    cosine, sine = cos_ref[...], sin_ref[...]
    for head in range(q_ref.shape[0] // HD):
        rows = slice(head * HD, (head + 1) * HD)
        q, k, v, d = q_ref[rows, :], k_ref[rows, :], v_ref[rows, :], d_ref[rows, :]
        keys, values = k.T, v.T
        q_small = q * jnp.asarray(SCALE, bf16)
        dk_acc[...] = jnp.zeros_like(dk_acc)
        dv_acc[...] = jnp.zeros_like(dv_acc)
        cols = []
        for start in range(0, seq, QB):
            end = start + QB
            here = slice(start, end)
            scores = dot(keys[:end], q_small[:, here], ((1,), (0,))) + bias_ref[:end, here]
            probs = jnp.exp(scores - log_ref[0, head : head + 1, here])
            grad = dot(values[:end], d[:, here], ((1,), (0,)))
            both = probs * grad
            inner = jnp.sum(both, axis=0, keepdims=True)
            grad = ((both - probs * inner) * SCALE).astype(bf16)
            probs = probs.astype(bf16)
            cols.append(dot(k[:, :end], grad, ((1,), (0,))))
            dk_acc[:, :end] += dot(q[:, here], grad, ((1,), (1,)))
            dv_acc[:, :end] += dot(d[:, here], probs, ((1,), (1,)))
        dq = rotate(jnp.concatenate(cols, axis=1), cosine, sine, -1.0)
        dk = rotate(dk_acc[...], cosine, sine, -1.0)
        dv = dv_acc[...]
        for part, (out, value) in enumerate(((dq_out, dq), (dk_out, dk), (dv_out, dv))):
            out[rows, :] = value.astype(bf16)
            sums_ref[0, rows, part : part + 1] = jnp.sum(value, axis=1, keepdims=True)


def attend_backward(q, k, v, d, logs, cosine, sine, bias):
    width, seq = q.shape
    pair = 2 * HD
    count = width // pair
    block = pl.BlockSpec((pair, seq), lambda i: (i, 0))
    whole = lambda shape: pl.BlockSpec(shape, lambda i: (0, 0))
    return pl.pallas_call(
        backward_kernel,
        grid=(count,),
        in_specs=[block] * 4
        + [pl.BlockSpec((1, 2, seq), lambda i: (i, 0, 0)), whole(cosine.shape), whole(sine.shape), whole(bias.shape)],
        out_specs=[block] * 3 + [pl.BlockSpec((1, pair, 128), lambda i: (i, 0, 0))],
        out_shape=[jax.ShapeDtypeStruct((width, seq), bf16)] * 3 + [jax.ShapeDtypeStruct((count, pair, 128), f32)],
        scratch_shapes=[pltpu.VMEM((HD, seq), f32), pltpu.VMEM((HD, seq), f32)],
        compiler_params=pltpu.CompilerParams(vmem_limit_bytes=48 << 20),
        cost_estimate=pl.CostEstimate(
            flops=10 * width * seq * seq, bytes_accessed=30 << 20, transcendentals=width // HD * seq * seq
        ),
        name="attend_backward",
    )(q, k, v, d, logs, cosine, sine, bias)


MESH = pl.DeviceIdType.MESH
HBM = pl.BlockSpec(memory_space=pl.ANY)
VMEM = pl.BlockSpec(memory_space=pltpu.VMEM)
DMA = pltpu.SemaphoreType.DMA


class Place:
    def __init__(self, n):
        self.n = n
        self.me = lax.axis_index("dp")
        self.t = lax.axis_index("tensor")
        odd = lax.rem(self.me, 2)
        half = lax.div(self.me, 2)
        self.pos = jnp.where(odd == 0, half, n - 1 - half)
        self.up = self.owner(1)
        self.down = self.owner(-1)
        self.core = self.t + 1 - 2 * lax.rem(self.t, 2)
        self.chip = lax.rem(self.t + 2, 4)
        self.cross = lax.rem(self.core + 2, 4)

    def owner(self, offset):
        p = lax.rem(self.pos + (offset + 2 * self.n), self.n)
        return jnp.where(p < self.n // 2, 2 * p, 2 * (self.n - 1 - p) + 1)

    def barrier(self, dp, tensor):
        sem = pltpu.get_barrier_semaphore()
        for there in dp:
            pl.semaphore_signal(sem, inc=1, device_id={"dp": there}, device_id_type=MESH)
        for there in tensor:
            pl.semaphore_signal(sem, inc=1, device_id={"tensor": there}, device_id_type=MESH)
        pl.semaphore_wait(sem, len(dp) + len(tensor))


class Lane:
    def __init__(self, place, full, base, size, way, send, recv):
        self.place, self.full, self.base, self.size, self.way = place, full, base, size, way
        self.send, self.recv = send, recv

    def whose(self, step):
        return self.place.owner(step if self.way else -step)

    def copy(self, step, whose):
        piece = self.full.at[whose, pl.ds(self.base, self.size)]
        return pltpu.make_async_remote_copy(
            src_ref=piece,
            dst_ref=piece,
            send_sem=self.send.at[step - 1],
            recv_sem=self.recv.at[step - 1],
            device_id={"dp": self.place.down if self.way else self.place.up},
            device_id_type=MESH,
        )

    def start(self, step):
        self.copy(step, self.whose(step - 1)).start()

    def arrive(self, step):
        self.copy(step, self.whose(step)).wait_recv()

    def finish(self):
        for step in range(1, self.place.n):
            self.copy(step, self.whose(step - 1)).wait_send()


class Exchange:
    def __init__(self, send, recv):
        self.send, self.recv = send, recv

    def copy(self, number, src, dst, there):
        return pltpu.make_async_remote_copy(
            src_ref=src,
            dst_ref=dst,
            send_sem=self.send.at[number],
            recv_sem=self.recv.at[number],
            device_id={"tensor": there},
            device_id_type=MESH,
        )


def row_norm(value, gain, shift):
    center = value - jnp.mean(value, axis=1, keepdims=True)
    rstd = lax.rsqrt(jnp.mean(center * center, axis=1, keepdims=True) + EPS)
    return center * rstd * gain + shift


def lane_vector(full, first, count):
    pieces = [full[d, r : r + 1, :] for d in range(full.shape[0]) for r in range(first, first + count)]
    return jnp.concatenate(pieces, axis=1)


def enter_kernel(
    n,
    x_ref, g_ref, wq, wk, wv, wo, gain_one, shift_one, gain_two, shift_two, bias_q, bias_v,
    normed_out, g_out, qkv_out, out_out, lin_out, small_full,
    x_full, normed, left, right, outs, lin, small_ref,
    small_send, small_recv, send, recv, x_send, x_recv, local, stored, lin_stored,
):
    place = Place(n)
    rows = x_ref.shape[0]
    size = wq.shape[0]
    width = wq.shape[1]
    half = width // 2
    me, t = place.me, place.t
    loads = [
        pltpu.make_async_copy(wq, left.at[me, :, pl.ds(0, width)], local.at[0]),
        pltpu.make_async_copy(wk.at[:, pl.ds(0, half)], left.at[me, :, pl.ds(width, half)], local.at[1]),
        pltpu.make_async_copy(wk.at[:, pl.ds(half, half)], right.at[me, :, pl.ds(0, half)], local.at[2]),
        pltpu.make_async_copy(wv, right.at[me, :, pl.ds(half, width)], local.at[3]),
        pltpu.make_async_copy(x_ref, x_full.at[t], local.at[4]),
        pltpu.make_async_copy(g_ref, g_out.at[t], local.at[5]),
    ]
    for load in loads:
        load.start()
    outs[me] = wo[...].T
    count = small_ref.shape[1]
    each = size // count
    small_ref[...] = jnp.zeros_like(small_ref)
    for i, vector in enumerate((gain_one, shift_one, gain_two, shift_two)):
        for r in range(each):
            small_ref[i * each + r, :] = vector[r * count : (r + 1) * count].astype(f32)
    heads, per = bias_q.shape
    small_ref[4 * each : 4 * each + heads, 0:per] = bias_q[...].astype(f32)
    small_ref[4 * each : 4 * each + heads, per : 2 * per] = bias_v[...].astype(f32)
    small_full[me] = small_ref[...]
    place.barrier([place.owner(k) for k in range(1, n)], [place.core, place.chip])

    smalls = []
    for k in range(1, n):
        smalls.append(
            pltpu.make_async_remote_copy(
                src_ref=small_ref,
                dst_ref=small_full.at[me],
                send_sem=small_send.at[k - 1],
                recv_sem=small_recv.at[k - 1],
                device_id={"dp": place.owner(k)},
                device_id_type=MESH,
            )
        )
        smalls[-1].start()

    swap = Exchange(x_send, x_recv)
    to_chip = swap.copy(0, x_ref, x_full.at[t], place.chip)
    to_core = swap.copy(1, x_ref, x_full.at[t], place.core)
    relay = swap.copy(2, x_full.at[place.chip], x_full.at[place.chip], place.core)
    g_chip = swap.copy(3, g_ref, g_out.at[t], place.chip)
    g_core = swap.copy(4, g_ref, g_out.at[t], place.core)
    g_relay = swap.copy(5, g_out.at[place.chip], g_out.at[place.chip], place.core)
    to_chip.start()
    to_core.start()
    for load in loads[:4]:
        load.wait()
    lanes = []
    for number, (full, base, count, way) in enumerate(
        (
            (left, 0, size // 2, 0),
            (right, 0, size // 2, 1),
            (left, size // 2, size // 2, 0),
            (right, size // 2, size // 2, 1),
            (outs, 0, size // 2, 0),
            (outs, size // 2, size // 2, 1),
        )
    ):
        lanes.append(Lane(place, full, base, count, way, send.at[number], recv.at[number]))

    def store(step):
        whose, other = place.owner(-step), place.owner(step)
        if step == n:
            return []
        return [
            pltpu.make_async_copy(left.at[whose], qkv_out.at[whose, :, pl.ds(0, width + half)], stored.at[0, step]),
            pltpu.make_async_copy(right.at[other], qkv_out.at[other, :, pl.ds(width + half, width + half)], stored.at[1, step]),
            pltpu.make_async_copy(outs.at[whose, pl.ds(0, size // 2)], out_out.at[whose, pl.ds(0, size // 2)], stored.at[2, step]),
            pltpu.make_async_copy(
                outs.at[other, pl.ds(size // 2, size // 2)], out_out.at[other, pl.ds(size // 2, size // 2)], stored.at[3, step]
            ),
        ]

    writes = []

    def tick(step):
        for lane in lanes:
            if step > 1:
                lane.arrive(step - 1)
            if step < n:
                lane.start(step)
        for write in store(step - 1):
            write.start()
            writes.append(write)

    gain = shift = None

    def norm(block):
        @pl.loop(0, rows // 16)
        def _(i):
            here = pl.ds(pl.multiple_of(i * 16, 16), 16)
            there = pl.ds(pl.multiple_of(block * rows + i * 16, 16), 16)
            normed[there, :] = row_norm(x_full[block, here, :].astype(f32), gain, shift).astype(bf16)

    def project(step):
        for full, whose, base in ((left, place.owner(-step), 0), (right, place.owner(step), width + half)):
            xs = normed[:, pl.ds(pl.multiple_of(whose * size, size), size)]
            for j in range(0, width + half, 256):
                part = dot(full[whose, :, j : j + 256].T, xs, ((1,), (1,)))
                where = slice(base + j, base + j + 256)
                if step == 0:
                    lin[where, :] = part
                else:
                    lin[where, :] += part
                if step == n - 1:
                    lin_store(base + j).start()

    def lin_store(first):
        at = pl.ds(first, 256)
        return pltpu.make_async_copy(lin.at[at], lin_out.at[at], lin_stored.at[first // 256])

    tick(1)
    loads[4].wait()
    for small in smalls:
        small.wait_recv()
    gain = lane_vector(small_full, 0, each)
    shift = lane_vector(small_full, each, each)
    norm(t)
    to_core.wait_recv()
    norm(place.core)
    tick(2)
    tick(3)
    to_chip.wait_recv()
    relay.start()
    g_chip.start()
    g_core.start()
    norm(place.chip)
    tick(4)
    relay.wait_recv()
    norm(place.cross)
    normed_store = pltpu.make_async_copy(normed, normed_out, local.at[6])
    normed_store.start()
    project(0)
    done = 1
    for step in range(5, n):
        tick(step)
        while done < min(step - 1, 2 * (step - 4) + 1):
            project(done)
            done += 1
    g_chip.wait_recv()
    g_relay.start()
    while done < n - 1:
        project(done)
        done += 1
    tick(n)
    project(n - 1)
    for copy in (to_chip, to_core, relay, g_chip, g_core, g_relay):
        copy.wait_send()
    g_core.wait_recv()
    g_relay.wait_recv()
    for small in smalls:
        small.wait_send()
    for lane in lanes:
        lane.finish()
    loads[5].wait()
    for write in writes:
        write.wait()
    normed_store.wait()
    for first in range(0, 3 * width, 256):
        lin_store(first).wait()


def enter(x, g, wq, wk, wv, wo, vectors, biases, n):
    rows, model = x.shape
    size, width = wq.shape
    big = 3 * width // 2
    kernel = lambda *refs: enter_kernel(n, *refs)
    return pl.pallas_call(
        kernel,
        in_specs=[HBM] * 5 + [VMEM] * 7,
        out_specs=[HBM, HBM, HBM, HBM, HBM, VMEM],
        out_shape=[
            jax.ShapeDtypeStruct((4 * rows, model), bf16),
            jax.ShapeDtypeStruct((4, rows, model), bf16),
            jax.ShapeDtypeStruct((n, size, 3 * width), bf16),
            jax.ShapeDtypeStruct((n, size, width), bf16),
            jax.ShapeDtypeStruct((3 * width, 4 * rows), f32),
            jax.ShapeDtypeStruct((n, 16, 128), f32),
        ],
        scratch_shapes=[
            pltpu.VMEM((4, rows, model), bf16),
            pltpu.VMEM((4 * rows, model), bf16),
            pltpu.VMEM((n, size, big), bf16),
            pltpu.VMEM((n, size, big), bf16),
            pltpu.VMEM((n, size, width), bf16),
            pltpu.VMEM((3 * width, 4 * rows), f32),
            pltpu.VMEM((16, 128), f32),
            DMA((n - 1,)),
            DMA((n - 1,)),
            DMA((6, n - 1)),
            DMA((6, n - 1)),
            DMA((6,)),
            DMA((6,)),
            DMA((7,)),
            DMA((4, n)),
            DMA((3 * width // 256,)),
        ],
        compiler_params=pltpu.CompilerParams(collective_id=1, has_side_effects=True, vmem_limit_bytes=56 << 20),
        cost_estimate=pl.CostEstimate(flops=6 * width * rows * 4 * model, bytes_accessed=40 << 20, transcendentals=0),
        name="enter",
    )(x, g, wq, wk, wv, wo, *vectors, *biases)

def attend_pair(pair, lin, bias_ref, cosine, sine, mask, q_all, k_all, v_all, logs, flat, mixed):
    width, seq = q_all.shape

    @pl.loop(0, 2)
    def _(j):
        head = pair * 2 + j
        first = pl.multiple_of(head * HD, HD)
        rows = pl.ds(first, HD)

        def load(part):
            at = pl.ds(pl.multiple_of(part * width + first, HD), HD)
            return lin[at, :] + bias_ref[at, :]

        q = rotate(load(0), cosine, sine, 1.0).astype(bf16)
        k = rotate(load(1), cosine, sine, 1.0).astype(bf16)
        values = load(2).astype(bf16)
        q_all[rows, :] = q
        k_all[rows, :] = k
        v_all[rows, :] = values
        keys = k.T
        q = q * jnp.asarray(SCALE, bf16)
        mine = pl.ds(pl.multiple_of(j * HD, HD), HD)
        for start in range(0, seq, QB):
            end = start + QB
            scores = dot(keys[:end], q[:, start:end], ((1,), (0,))) + mask[:end, start:end]
            top = jnp.max(scores, axis=0, keepdims=True)
            expo = jnp.exp(scores - top)
            total = jnp.sum(expo, axis=0, keepdims=True)
            probs = (expo * (1.0 / total)).astype(bf16)
            flat[mine, start:end] = dot(values[:, :end], probs, ((1,), (0,))).astype(bf16)
            logs[pl.ds(head, 1), start:end] = top + jnp.log(total)

    mixed[:, pair * 2 * HD : (pair + 1) * 2 * HD] = flat[...].T


def build_mask(mask, column, seg_row):
    seq = mask.shape[0]
    segments = seg_row[...].astype(f32)
    column[...] = jnp.broadcast_to(segments, (128, seq)).T

    @pl.loop(0, seq // 32)
    def _(i):
        here = pl.ds(pl.multiple_of(i * 32, 32), 32)
        key = lax.broadcasted_iota(jnp.int32, (32, seq), 0) + i * 32
        query = lax.broadcasted_iota(jnp.int32, (32, seq), 1)
        allowed = (key <= query) & (column[here, 0:1] == segments)
        mask[here, :] = jnp.where(allowed, 0.0, NEG).astype(f32)


def middle_kernel(
    n,
    lin_ref, key_bias, cos_ref, sin_ref, seg_row, x_ref, out_ref, small, gate_w, up_w, down_w, g_ref,
    q_out, k_out, v_out, logs, mixed_out, att_out, second_out, gate_out, up_out, hidden_out, ffn_out, dgate_out, dup_out,
    gate, up, down, second, near_send, near_recv, far_send, far_recv, attended,
    send, recv, x_send, x_recv, local, stored, staged,
):
    place = Place(n)
    t = place.t
    rows, model = x_ref.shape
    size, cols = gate_w.shape
    seq = 4 * rows
    width = out_ref.shape[1]
    loads = [
        pltpu.make_async_copy(gate_w, gate.at[place.me], local.at[0]),
        pltpu.make_async_copy(up_w, up.at[place.me], local.at[1]),
    ]
    for load in loads:
        load.start()
    down[place.me] = down_w[...].T
    place.barrier([place.up, place.down], [place.core, place.chip])
    for load in loads:
        load.wait()

    half, quarter = size // 2, size // 4
    lanes = [
        [Lane(place, full, half * sub, half, way, send.at[2 * way + sub], recv.at[2 * way + sub]) for way, full in ((0, gate), (1, up))]
        for sub in range(2)
    ]
    downs = [
        [
            Lane(place, down, half * way + quarter * sub, quarter, way, send.at[4 + 2 * way + sub], recv.at[4 + 2 * way + sub])
            for way in range(2)
        ]
        for sub in range(2)
    ]

    def write(step):
        gated, upped = place.owner(-step), place.owner(step)
        return [
            pltpu.make_async_copy(gate.at[gated], gate_out.at[gated], stored.at[0, step]),
            pltpu.make_async_copy(up.at[upped], up_out.at[upped], stored.at[1, step]),
        ]

    def tick(kind, step, sub):
        for lane in (downs if kind else lanes)[sub]:
            if step > 1:
                lane.arrive(step - 1)
            if step < n:
                lane.start(step)
        if sub == 1 and not kind:
            for copy in write(step - 1):
                copy.start()

    plan = [(0, step, sub) for step in range(1, n) for sub in range(2)]
    plan += [(1, 1, 0), (1, 1, 1), (0, n, 0), (0, n, 1)]
    plan += [(1, step, sub) for step in range(2, n + 1) for sub in range(2)]
    plan = iter(plan)

    def advance(count=1):
        for _ in range(count):
            tick(*next(plan))

    swap = Exchange(x_send, x_recv)
    near = [swap.copy(i, near_send.at[i], near_recv.at[i], place.core) for i in range(2)]
    far = swap.copy(2, far_send, far_recv, place.chip)
    to_chip = swap.copy(3, second.at[t], second.at[t], place.chip)
    to_core = swap.copy(4, second.at[t], second.at[t], place.core)
    relay = swap.copy(5, second.at[place.chip], second.at[place.chip], place.core)
    copies = near + [far, to_chip, to_core, relay]

    advance(2)

    def attention(lin, mask, q_all, k_all, v_all, flat, mixed, out_t, bias_ref, column):
        pairs = width // (2 * HD)
        fetch = []
        for part in range(3):
            for pair in range(pairs):
                at = pl.ds(part * width + pair * 2 * HD, 2 * HD)
                fetch.append(pltpu.make_async_copy(lin_ref.at[at], lin.at[at], local.at[2 + part * pairs + pair]))
        for pair in range(pairs):
            for part in range(3):
                fetch[part * pairs + pair].start()
        weights = pltpu.make_async_copy(out_ref, out_t, local.at[2 + 3 * pairs])
        weights.start()
        build_mask(mask, column, seg_row)
        heads, per = width // HD, HD // n
        first = small.shape[1] - heads
        turned = [small[d, first:, :].T for d in range(n)]
        keys = key_bias[...].astype(f32).T
        for head in range(heads):
            for part in range(3):
                if part == 1:
                    rest = jnp.zeros((HD - ROT, 1), f32)
                    piece = jnp.concatenate([keys[:, head : head + 1], rest], axis=0)
                else:
                    at = part // 2 * per
                    piece = jnp.concatenate([turned[d][at : at + per, head : head + 1] for d in range(n)], axis=0)
                where = part * width + head * HD
                bias_ref[where : where + HD, :] = piece
        cosine, sine = cos_ref[...], sin_ref[...]
        for pair in range(pairs):
            for part in range(3):
                fetch[part * pairs + pair].wait()
            attend_pair(pair, lin, bias_ref, cosine, sine, mask, q_all, k_all, v_all, logs, flat, mixed)
            advance()
        keep = [
            pltpu.make_async_copy(src, dst, local.at[3 + 3 * pairs + i])
            for i, (src, dst) in enumerate(((q_all, q_out), (k_all, k_out), (v_all, v_out), (mixed, mixed_out)))
        ]
        for copy in keep:
            copy.start()
        weights.wait()

        def project(block, j):
            at = pl.ds(pl.multiple_of(block * rows, rows), rows)
            return dot(mixed[at, :], out_t[j : j + 512, :], ((1,), (1,)))

        for i, block in enumerate((place.cross, place.core)):
            for j in range(0, model, 512):
                near_send[i, :, j : j + 512] = project(block, j).astype(bf16)
            near[i].start()
        near[0].wait_recv()
        for j in range(0, model, 512):
            tile = slice(j, j + 512)
            far_send[:, tile] = (project(place.chip, j) + near_recv[0, :, tile].astype(f32)).astype(bf16)
        far.start()
        own = pltpu.make_async_copy(x_ref, far_copy, local.at[7 + 3 * pairs])
        own.start()
        advance()
        near[1].wait_recv()
        own.wait()
        for j in range(0, model, 512):
            tile = slice(j, j + 512)
            attended[:, tile] = far_copy[:, tile].astype(f32) + project(t, j) + near_recv[1, :, tile].astype(f32)
        for copy in keep:
            copy.wait()

    far_copy = second.at[t]
    pl.run_scoped(
        attention,
        pltpu.VMEM((3 * width, seq), f32),
        pltpu.VMEM((seq, seq), f32),
        pltpu.VMEM((width, seq), bf16),
        pltpu.VMEM((width, seq), bf16),
        pltpu.VMEM((width, seq), bf16),
        pltpu.VMEM((2 * HD, seq), bf16),
        pltpu.VMEM((seq, width), bf16),
        pltpu.VMEM((model, width), bf16),
        pltpu.VMEM((3 * width, 1), f32),
        pltpu.VMEM((seq, 128), f32),
    )
    last = 7 + 3 * (width // (2 * HD))

    def feed(gate_lin, up_lin, grad, hidden, g, stage):
        g_load = pltpu.make_async_copy(g_ref, g, local.at[last + 1])
        g_load.start()
        gate_lin[...] = jnp.zeros_like(gate_lin)
        up_lin[...] = jnp.zeros_like(up_lin)
        grad[...] = jnp.zeros_like(grad)
        count = small.shape[2]
        gain = lane_vector(small, 2 * size // count, size // count)
        shift = lane_vector(small, 3 * size // count, size // count)
        advance(2)
        far.wait_recv()

        @pl.loop(0, rows // 16)
        def _(i):
            here = pl.ds(pl.multiple_of(i * 16, 16), 16)
            value = attended[here, :] + far_recv[here, :].astype(f32)
            attended[here, :] = value
            second[t, here, :] = row_norm(value, gain, shift).astype(bf16)

        to_chip.start()
        to_core.start()
        att_store = pltpu.make_async_copy(attended, att_out, local.at[last + 2])
        att_store.start()

        def add(block, low, high):
            @pl.loop(low, high)
            def _(step):
                for full, total, whose in ((gate, gate_lin, place.owner(-step)), (up, up_lin, place.owner(step))):
                    xs = second[block, :, pl.ds(pl.multiple_of(whose * size, size), size)]
                    total[block] += dot(xs, full[whose], ((1,), (0,)))

        advance()
        ready = 5
        add(t, 0, ready)
        to_core.wait_recv()
        advance()
        add(place.core, 0, ready)
        advance()
        to_chip.wait_recv()
        relay.start()
        add(place.chip, 0, ready)
        relay.wait_recv()
        second_store = pltpu.make_async_copy(second, second_out, local.at[last + 3])
        second_store.start()
        advance()
        add(place.cross, 0, ready)
        every = lambda low, high: pl.loop(0, 4)(lambda block: add(block, low, high))
        every(ready, n - 2)
        advance(2)
        advance()
        every(n - 2, n - 1)
        advance(2)
        every(n - 1, n)

        @pl.loop(0, 4 * rows // 16)
        def _(i):
            block = lax.div(i, rows // 16)
            here = pl.ds(pl.multiple_of(lax.rem(i, rows // 16) * 16, 16), 16)
            value = gate_lin[block, here, :]
            sigma = jax.nn.sigmoid(value)
            activated = value * sigma
            upward = up_lin[block, here, :]
            hidden[block, here, :] = (activated * upward).astype(bf16)
            gate_lin[block, here, :] = activated
            up_lin[block, here, :] = upward * sigma * (1.0 + value * (1.0 - sigma))

        hidden_store = pltpu.make_async_copy(hidden, hidden_out, local.at[last + 4])
        hidden_store.start()
        g_load.wait()
        stages = []

        def output(whose, base, count):
            number = len(stages)
            slot = number % 2
            if number >= 2:
                stages[number - 2].wait()

            right = down[whose, base : base + count].T
            for block in range(4):
                tile = dot(hidden[block], right, ((1,), (0,)))
                stage[slot, block, :, 0:count] = tile.astype(bf16)

            at = pl.ds(pl.multiple_of(whose * size + base, count), count)
            stages.append(pltpu.make_async_copy(stage.at[slot, :, :, pl.ds(0, count)], ffn_out.at[:, :, at], staged.at[number]))
            stages[-1].start()

        def collect(whose, base, count):
            at = pl.ds(pl.multiple_of(whose * size + base, count), count)

            @pl.loop(0, 4)
            def _(block):
                grad[block] += dot(g[block, :, at], down[whose, base : base + count], ((1,), (0,)))

        def use(whose, base=0, count=size):
            collect(whose, base, count)
            output(whose, base, count)

        after, before = place.owner(n - 1), place.owner(1 - n)
        use(place.me)
        for step in range(2, n):
            advance(2)
            if step - 1 == n // 2:
                use(place.owner(n // 2))
                use(after, 0, half)
                use(before, half, half)
            elif step - 1 > n // 2:
                one, other = place.owner(step - 1), place.owner(1 - step)
                first_at, other_at = (pl.ds(pl.multiple_of(whose * size, size), size) for whose in (one, other))

                @pl.loop(0, 4)
                def _(block):
                    both = dot(g[block, :, first_at], down[one], ((1,), (0,)))
                    both = both + dot(g[block, :, other_at], down[other], ((1,), (0,)))
                    grad[block] += both

                output(one, 0, size)
                output(other, 0, size)
        for lane in lanes[0] + lanes[1]:
            lane.finish()
        for step in range(n):
            for copy in write(step):
                copy.wait()
        advance(2)
        collect(before, 0, half)
        collect(after, half, half)
        final = []
        for block in range(4):

            @pl.loop(0, rows // 16)
            def _(i):
                here = pl.ds(pl.multiple_of(i * 16, 16), 16)
                incoming = grad[block, here, :]
                gate[block, here, :] = (incoming * up_lin[block, here, :]).astype(bf16)
                gate[4 + block, here, :] = (incoming * gate_lin[block, here, :]).astype(bf16)

            for first, out in ((0, dgate_out), (4, dup_out)):
                final.append(pltpu.make_async_copy(gate.at[first + block], out.at[block], local.at[last + 5 + len(final)]))
                final[-1].start()
        output(before, 0, half)
        output(after, half, half)
        for lane in downs[0] + downs[1]:
            lane.finish()
        for copy in final + stages[-2:] + [hidden_store, second_store, att_store]:
            copy.wait()

    pl.run_scoped(
        feed,
        pltpu.VMEM((4, rows, cols), f32),
        pltpu.VMEM((4, rows, cols), f32),
        pltpu.VMEM((4, rows, cols), f32),
        pltpu.VMEM((4, rows, cols), bf16),
        pltpu.VMEM((4, rows, model), bf16),
        pltpu.VMEM((2, 4, rows, size), bf16),
    )
    for copy in copies:
        copy.wait_send()


def middle(lin, key_bias, cosine, sine, segments, x, out_t, small, gate, up, down, g, n):
    rows, model = x.shape
    size, cols = gate.shape
    seq = 4 * rows
    width = out_t.shape[1]
    heads = width // HD
    shape = jax.ShapeDtypeStruct
    return pl.pallas_call(
        lambda *refs: middle_kernel(n, *refs),
        in_specs=[HBM] + [VMEM] * 4 + [HBM, HBM, VMEM, HBM, HBM, VMEM, HBM],
        out_specs=[HBM, HBM, HBM, VMEM] + [HBM] * 9,
        out_shape=[
            shape((width, seq), bf16),
            shape((width, seq), bf16),
            shape((width, seq), bf16),
            shape((heads, seq), f32),
            shape((seq, width), bf16),
            shape((rows, model), f32),
            shape((4, rows, model), bf16),
            shape((n, size, cols), bf16),
            shape((n, size, cols), bf16),
            shape((4, rows, cols), bf16),
            shape((4, rows, model), bf16),
            shape((4, rows, cols), bf16),
            shape((4, rows, cols), bf16),
        ],
        scratch_shapes=[
            pltpu.VMEM((n, size, cols), bf16),
            pltpu.VMEM((n, size, cols), bf16),
            pltpu.VMEM((n, size, cols), bf16),
            pltpu.VMEM((4, rows, model), bf16),
            pltpu.VMEM((2, rows, model), bf16),
            pltpu.VMEM((2, rows, model), bf16),
            pltpu.VMEM((rows, model), bf16),
            pltpu.VMEM((rows, model), bf16),
            pltpu.VMEM((rows, model), f32),
            DMA((8, n - 1)),
            DMA((8, n - 1)),
            DMA((6,)),
            DMA((6,)),
            DMA((20 + 3 * width // (2 * HD),)),
            DMA((2, n)),
            DMA((2 * n,)),
        ],
        compiler_params=pltpu.CompilerParams(collective_id=2, has_side_effects=True, vmem_limit_bytes=62 << 20),
        cost_estimate=pl.CostEstimate(
            flops=10 * seq * model * cols, bytes_accessed=60 << 20, transcendentals=heads * seq * seq
        ),
        name="middle",
    )(
        lin, key_bias, cosine, sine, segments[None, :],
        x, out_t, small, gate, up, down, g.reshape(4, rows, model),
    )

class Sum:
    def __init__(self, place, slots, way, send, recv):
        self.place, self.slots, self.way, self.send, self.recv = place, slots, way, send, recv

    def whose(self, step):
        return self.place.owner(1 + step if self.way else -1 - step)

    def copy(self, step):
        return pltpu.make_async_remote_copy(
            src_ref=self.slots.at[step - 1],
            dst_ref=self.slots.at[step],
            send_sem=self.send.at[step - 1],
            recv_sem=self.recv.at[step - 1],
            device_id={"dp": self.place.down if self.way else self.place.up},
            device_id_type=MESH,
        )

    def tick(self, step, product, final):
        if step > 0:
            self.copy(step).wait_recv()
        cols = self.slots.shape[2]
        for low in range(0, cols, 512):
            tile = slice(low, min(low + 512, cols))
            part = product(tile)
            if step > 0:
                part = part + self.slots[step, :, tile].astype(f32)
            if step == self.place.n - 1:
                final(tile, part)
            else:
                self.slots[step, :, tile] = part.astype(bf16)
        if step < self.place.n - 1:
            self.copy(step + 1).start()

    def finish(self):
        for step in range(1, self.place.n):
            self.copy(step).wait_send()


def columns_of(left, whose, size, way):
    half = size // 2
    return left[:, pl.ds(pl.multiple_of(whose * size + way * half, half), half)].T


def retreat_pair(pair, q_all, k_all, v_all, d_all, logs, cosine, sine, mask, dk_acc, dv_acc, tmp, vec):
    width, seq = q_all.shape

    @pl.loop(0, 2)
    def _(j):
        head = pair * 2 + j
        rows = pl.ds(pl.multiple_of(head * HD, HD), HD)
        q, k, v, d = q_all[rows, :], k_all[rows, :], v_all[rows, :], d_all[rows, :]
        keys, values = k.T, v.T
        q_small = q * jnp.asarray(SCALE, bf16)
        dk_acc[...] = jnp.zeros_like(dk_acc)
        dv_acc[...] = jnp.zeros_like(dv_acc)
        cols = []
        for start in range(0, seq, QB):
            end = start + QB
            here = slice(start, end)
            scores = dot(keys[:end], q_small[:, here], ((1,), (0,))) + mask[:end, here]
            probs = jnp.exp(scores - logs[pl.ds(head, 1), here])
            grad = dot(values[:end], d[:, here], ((1,), (0,)))
            both = probs * grad
            inner = jnp.sum(both, axis=0, keepdims=True)
            grad = ((both - probs * inner) * SCALE).astype(bf16)
            probs = probs.astype(bf16)
            cols.append(dot(k[:, :end], grad, ((1,), (0,))))
            dk_acc[:, :end] += dot(q[:, here], grad, ((1,), (1,)))
            dv_acc[:, :end] += dot(d[:, here], probs, ((1,), (1,)))
        dq = rotate(jnp.concatenate(cols, axis=1), cosine, sine, -1.0)
        dk = rotate(dk_acc[...], cosine, sine, -1.0)
        dv = dv_acc[...]
        mine = pl.ds(pl.multiple_of(j * HD, HD), HD)
        for part, (out, value) in enumerate(((q_all, dq), (k_all, dk), (v_all, dv))):
            out[rows, :] = value.astype(bf16)
            lanes = value[:, :128]
            for i in range(128, seq, 128):
                lanes = lanes + value[:, i : i + 128]
            tmp[part, mine, :] = lanes

    for part in range(3):
        at = part * width + pair * 2 * HD
        vec[4:5, at : at + 2 * HD] = jnp.sum(tmp[part].T, axis=0, keepdims=True)


def back_kernel(
    n,
    dgate_ref, dup_ref, hidden_ref, second_ref, g_ref, gate_ref, up_ref, att_ref, small, out_ref,
    q_ref, k_ref, v_ref, logs, cos_ref, sin_ref, seg_row,
    down_sum, gate_sum, up_sum, datt_out, resid_out, dlin_out, vec,
    slots, g, second, hidden, dgate, dup, near_send, near_recv, far_send, far_recv, datt, acc,
    send, recv, x_send, x_recv, local,
):
    place = Place(n)
    t = place.t
    rows, model = att_ref.shape
    size, cols = gate_ref.shape[1:]
    seq, width = 4 * rows, out_ref.shape[1]
    loads = [
        pltpu.make_async_copy(src, dst, local.at[i])
        for i, (src, dst) in enumerate(
            ((g_ref, g), (hidden_ref, hidden), (second_ref, second), (dgate_ref, dgate), (dup_ref, dup))
        )
    ]
    for load in loads[:2]:
        load.start()
    place.barrier([place.up, place.down], [place.core, place.chip])

    lanes = [[Sum(place, slots.at[2 * i + way], way, send.at[2 * i + way], recv.at[2 * i + way]) for way in range(2)] for i in range(3)]
    sources = ((g, hidden), (second, dgate), (second, dup))
    sums = (down_sum, gate_sum, up_sum)

    def stored(i):
        return pltpu.make_async_copy(datt.at[:, pl.ds(0, cols)], sums[i], local.at[6 + i])

    def tick(step, i):
        left, right = sources[i]
        if step == n - 1:
            (stored(i - 1) if i else datt_copy()).wait()
        for lane in lanes[i]:

            def final(tile, total):
                datt[lane.way * size // 2 : (lane.way + 1) * size // 2, tile] = total

            block = columns_of(left, lane.whose(step), size, lane.way)
            lane.tick(step, lambda tile: dot(block, right[:, tile], ((1,), (0,))), final)
        if step == n - 1:
            stored(i).start()

    plan = iter([(step, i) for step in range(n) for i in range(3)])

    def advance(count=1):
        for _ in range(count):
            tick(*next(plan))

    def datt_copy():
        return pltpu.make_async_copy(datt, datt_out, local.at[9])

    swap = Exchange(x_send, x_recv)
    near = [swap.copy(i, near_send.at[i], near_recv.at[i], place.core) for i in range(2)]
    far = swap.copy(2, far_send, far_recv, place.chip)
    to_chip = swap.copy(3, far_send, resid_out.at[t], place.chip)
    to_core = swap.copy(4, far_send, resid_out.at[t], place.core)
    relay = swap.copy(5, resid_out.at[place.chip], resid_out.at[place.chip], place.core)
    keep = pltpu.make_async_copy(far_send, resid_out.at[t], local.at[10])
    own = pl.ds(pl.multiple_of(t * rows, rows), rows)

    def feed(gate, up):
        weights = [
            pltpu.make_async_copy(gate_ref, gate, local.at[11]),
            pltpu.make_async_copy(up_ref, up, local.at[12]),
        ]
        loads[0].wait()
        loads[1].wait()
        for load in loads[2:]:
            load.start()
        advance()
        loads[2].wait()
        loads[3].wait()
        for copy in weights:
            copy.start()
        advance()
        loads[4].wait()
        advance()
        for copy in weights:
            copy.wait()

        def product(block, j):
            at = pl.ds(pl.multiple_of(block * rows, rows), rows)
            return dot(dgate[at, :], gate[j], ((1,), (1,))) + dot(dup[at, :], up[j], ((1,), (1,)))

        for i, block in enumerate((place.cross, place.core)):
            for j in range(n):
                near_send[i, :, j * size : (j + 1) * size] = product(block, j).astype(bf16)
            near[i].start()
            advance()
        near[0].wait_recv()
        for j in range(n):
            tile = slice(j * size, (j + 1) * size)
            far_send[:, tile] = (product(place.chip, j) + near_recv[0, :, tile].astype(f32)).astype(bf16)
        far.start()
        advance()
        near[1].wait_recv()
        for j in range(n):
            tile = slice(j * size, (j + 1) * size)
            datt[:, tile] = product(t, j) + near_recv[1, :, tile].astype(f32)
        advance()

    pl.run_scoped(feed, pltpu.VMEM((n, size, cols), bf16), pltpu.VMEM((n, size, cols), bf16))

    def attention(attended, mask, q_all, k_all, v_all, d_all, out_t, dk_acc, dv_acc, tmp, column):
        load_attended = pltpu.make_async_copy(att_ref, attended, local.at[5])
        load_attended.start()
        fetch = [
            pltpu.make_async_copy(src, dst, local.at[13 + i])
            for i, (src, dst) in enumerate(((out_ref, out_t), (q_ref, q_all), (k_ref, k_all), (v_ref, v_all)))
        ]
        for copy in fetch:
            copy.start()
        build_mask(mask, column, seg_row)
        count = small.shape[2]
        gain = lane_vector(small, 2 * size // count, size // count)
        acc[...] = jnp.zeros_like(acc)
        advance(1)
        far.wait_recv()
        far.wait_send()
        load_attended.wait()

        @pl.loop(0, rows // 16)
        def _(i):
            here = pl.ds(pl.multiple_of(i * 16, 16), 16)
            value = attended[here, :]
            center = value - jnp.mean(value, axis=1, keepdims=True)
            rstd = lax.rsqrt(jnp.mean(center * center, axis=1, keepdims=True) + EPS)
            hat = center * rstd
            incoming = datt[here, :] + far_recv[here, :].astype(f32)
            acc[0] += incoming * hat
            acc[1] += incoming
            scaled = incoming * gain
            back = rstd * (
                scaled - jnp.mean(scaled, axis=1, keepdims=True) - hat * jnp.mean(scaled * hat, axis=1, keepdims=True)
            )
            whole = g[pl.ds(pl.multiple_of(t * rows + i * 16, 16), 16), :].astype(f32) + back
            datt[here, :] = whole
            far_send[here, :] = whole.astype(bf16)

        to_chip.start()
        to_core.start()
        keep.start()
        datt_copy().start()
        vec[...] = jnp.zeros_like(vec)
        vec[2:3, :] = jnp.sum(acc[0], axis=0, keepdims=True)
        vec[3:4, :] = jnp.sum(acc[1], axis=0, keepdims=True)
        for copy in near:
            copy.wait_send()
        fetch[0].wait()

        def mix(block, source):
            value = dot(source[...], out_t[...], ((1,), (0,))).astype(bf16)
            d_all[:, pl.ds(pl.multiple_of(block * rows, rows), rows)] = value.T

        def bring(block, slot, number):
            return pltpu.make_async_copy(resid_out.at[block], near_send.at[slot], local.at[number])

        mix(t, far_send)
        advance()
        to_core.wait_recv()
        first = bring(place.core, 0, 17)
        first.start()
        first.wait()
        mix(place.core, near_send.at[0])
        advance(2)
        to_chip.wait_recv()
        relay.start()
        second_block = bring(place.chip, 1, 18)
        second_block.start()
        second_block.wait()
        mix(place.chip, near_send.at[1])
        relay.wait_recv()
        third = bring(place.cross, 0, 19)
        third.start()
        third.wait()
        mix(place.cross, near_send.at[0])
        for copy in fetch[1:]:
            copy.wait()
        cosine, sine = cos_ref[...], sin_ref[...]
        for pair in range(width // (2 * HD)):
            advance()
            retreat_pair(pair, q_all, k_all, v_all, d_all, logs, cosine, sine, mask, dk_acc, dv_acc, tmp, vec)
            here = slice(pair * 2 * HD, (pair + 1) * 2 * HD)
            out_t[0:seq, here] = q_all[here, :].T
            out_t[seq : 2 * seq, here] = k_all[here, :].T
            turned = v_all[here, :].T
            for block in range(4):
                at = block * width + pair * 2 * HD
                near_recv[0, :, at : at + 2 * HD] = turned[block * rows : (block + 1) * rows]
        final = [
            pltpu.make_async_copy(out_t.at[pl.ds(i * seq, seq)], dlin_out.at[:, pl.ds(i * width, width)], local.at[20 + i])
            for i in range(2)
        ] + [
            pltpu.make_async_copy(
                near_recv.at[0, :, pl.ds(block * width, width)],
                dlin_out.at[pl.ds(block * rows, rows), pl.ds(2 * width, width)],
                local.at[22 + block],
            )
            for block in range(4)
        ]
        for copy in final:
            copy.start()
        advance(2)
        for copy in final:
            copy.wait()

    pl.run_scoped(
        attention,
        pltpu.VMEM((rows, model), f32),
        pltpu.VMEM((seq, seq), f32),
        pltpu.VMEM((width, seq), bf16),
        pltpu.VMEM((width, seq), bf16),
        pltpu.VMEM((width, seq), bf16),
        pltpu.VMEM((width, seq), bf16),
        pltpu.VMEM((model, width), bf16),
        pltpu.VMEM((HD, seq), f32),
        pltpu.VMEM((HD, seq), f32),
        pltpu.VMEM((3, 2 * HD, 128), f32),
        pltpu.VMEM((seq, 128), f32),
    )
    for step in plan:
        tick(*step)
    for pair in lanes:
        for lane in pair:
            lane.finish()
    for copy in (to_chip, to_core, relay):
        copy.wait_send()
    keep.wait()
    stored(2).wait()


def back(dgate, dup, hidden, second, g, gate, up, attended, small, out_t, q, k, v, logs, cosine, sine, segments, n):
    rows, model = attended.shape
    size, cols = model // n, hidden.shape[1]
    seq, width = 4 * rows, out_t.shape[1]
    shape = jax.ShapeDtypeStruct
    return pl.pallas_call(
        lambda *refs: back_kernel(n, *refs),
        in_specs=[HBM] * 8 + [VMEM] + [HBM] * 4 + [VMEM] * 4,
        out_specs=[HBM] * 6 + [VMEM],
        out_shape=[
            shape((size, cols), f32),
            shape((size, cols), f32),
            shape((size, cols), f32),
            shape((rows, model), f32),
            shape((4, rows, model), bf16),
            shape((seq, 3 * width), bf16),
            shape((8, model), f32),
        ],
        scratch_shapes=[
            pltpu.VMEM((6, n, size // 2, cols), bf16),
            pltpu.VMEM((seq, model), bf16),
            pltpu.VMEM((seq, model), bf16),
            pltpu.VMEM((seq, cols), bf16),
            pltpu.VMEM((seq, cols), bf16),
            pltpu.VMEM((seq, cols), bf16),
            pltpu.VMEM((2, rows, model), bf16),
            pltpu.VMEM((2, rows, model), bf16),
            pltpu.VMEM((rows, model), bf16),
            pltpu.VMEM((rows, model), bf16),
            pltpu.VMEM((rows, model), f32),
            pltpu.VMEM((2, 16, model), f32),
            DMA((6, n - 1)),
            DMA((6, n - 1)),
            DMA((6,)),
            DMA((6,)),
            DMA((26,)),
        ],
        compiler_params=pltpu.CompilerParams(collective_id=3, has_side_effects=True, vmem_limit_bytes=62 << 20),
        cost_estimate=pl.CostEstimate(
            flops=14 * seq * model * cols, bytes_accessed=60 << 20, transcendentals=width // HD * seq * seq
        ),
        name="back",
    )(
        dgate, dup, hidden, second, g, gate.reshape(n, size, cols), up.reshape(n, size, cols), attended, small, out_t,
        q, k, v, logs, cosine, sine, segments[None, :],
    )

def leave_kernel(
    n,
    normed_ref, dlin_ref, qkv_ref, mixed_ref, resid_ref, datt_ref, x_ref, att_ref, ffn_ref, small, vec_ref,
    layer_out, input_out, query_sum, key_sum, value_sum, out_sum, vec_out,
    wide, narrow, normed, dlin, qkv, turned, mixed, resid, datt, attended, x, first, near_send, near_recv, far_send, far_recv,
    ffn_own, ffn_recv, ffn_send, ffn_far, layer, acc, totals, wsum, osum, vecs, vec_recv,
    send, recv, x_send, x_recv, v_send, v_recv, local, blocks,
):
    place = Place(n)
    t, me = place.t, place.me
    rows, model = att_ref.shape
    size = model // n
    total_cols = dlin_ref.shape[1]
    width = total_cols // 3
    part = total_cols // 2
    loads = [
        pltpu.make_async_copy(src, dst, local.at[i])
        for i, (src, dst) in enumerate(
            (
                (dlin_ref.at[:, pl.ds(0, part)], dlin.at[:, pl.ds(0, part)]),
                (dlin_ref.at[:, pl.ds(part, part)], dlin.at[:, pl.ds(part, part)]),
                (mixed_ref, mixed),
                (qkv_ref, qkv),
                (ffn_ref.at[place.chip], ffn_own.at[0]),
                (ffn_ref.at[t], ffn_own.at[1]),
                (att_ref, attended),
                (x_ref, x),
                (datt_ref, datt),
            )
        )
    ]
    hops = [1, 2, 4]
    partners = [me + hop - 2 * hop * lax.rem(lax.div(me, hop), 2) for hop in hops]

    lanes = [
        [Sum(place, wide.at[2 * i + way], way, send.at[2 * i + way], recv.at[2 * i + way]) for way in range(2)] for i in range(2)
    ] + [[Sum(place, narrow.at[way], way, send.at[4 + way], recv.at[4 + way]) for way in range(2)]]

    swap = Exchange(x_send, x_recv)
    near = [swap.copy(i, near_send.at[i], near_recv.at[i], place.core) for i in range(2)]
    far = swap.copy(2, far_send, far_recv, place.chip)
    outs = [swap.copy(3 + i, ffn_ref.at[block], ffn_recv.at[i], place.core) for i, block in enumerate((place.cross, place.core))]
    outs_far = swap.copy(5, ffn_send, ffn_far, place.chip)

    def block_of(step, way, i):
        lane = lanes[0][way]
        at = pl.ds(pl.multiple_of(lane.whose(step) * size + way * (size // 2), size // 2), size // 2)
        src, dst = ((normed_ref, normed), (resid_ref, resid))[i]
        return pltpu.make_async_copy(src.at[:, at], dst.at[:, at], blocks.at[i, way, step])

    def fetch(steps, i):
        for step in steps:
            for way in range(2):
                block_of(step, way, i).start()

    fetch(range(1), 0)
    loads[0].start()
    loads[1].start()
    fetch(range(1), 1)
    loads[2].start()
    fetch(range(1, 3), 0)
    fetch(range(1, 3), 1)
    place.barrier([place.up, place.down] + partners, [place.core, place.chip])

    def tick(step, i):
        if i != 1:
            for way in range(2):
                block_of(step, way, i // 2).wait()
        for lane in lanes[i]:
            half = slice(lane.way * size // 2, (lane.way + 1) * size // 2)
            if i == 2:

                def product(left, tile):
                    return dot(left, mixed[:, tile], ((1,), (0,)))

                def final(tile, total):
                    osum[tile, half] = total.T

            else:

                def product(left, tile):
                    return dot(left, dlin[:, part * i + tile.start : part * i + tile.stop], ((1,), (0,)))

                def final(tile, total):
                    wsum[half, part * i + tile.start : part * i + tile.stop] = total

            left = columns_of(resid if i == 2 else normed, lane.whose(step), size, lane.way)
            lane.tick(step, lambda tile: product(left, tile), final)

    plan = iter([(step, i) for step in range(n) for i in range(3)])

    def advance(count=1):
        for _ in range(count):
            tick(*next(plan))

    loads[0].wait()
    advance()
    loads[1].wait()
    loads[3].start()
    advance()
    for load in loads[4:]:
        load.start()
    fetch(range(3, n), 0)
    fetch(range(3, n), 1)
    loads[2].wait()
    advance()
    loads[3].wait()

    def lines(block):
        return dlin[pl.ds(pl.multiple_of(block * rows, rows), rows), :]

    def product(block, use):
        for j in range(n):
            use(slice(j * size, (j + 1) * size), dot(lines(block), turned[j], ((1,), (0,))))

    for j in range(n):
        turned[j] = qkv[j].T
    for i, block in enumerate((place.cross, place.core)):

        def use_near(tile, value):
            near_send[i, :, tile] = value.astype(bf16)

        product(block, use_near)
        near[i].start()
        advance()
    near[0].wait_recv()

    def use_far(tile, value):
        far_send[:, tile] = (value + near_recv[0, :, tile].astype(f32)).astype(bf16)

    product(place.chip, use_far)
    far.start()
    advance()

    def use_own(tile, value):
        first[:, tile] = value

    product(t, use_own)
    near[1].wait_recv()
    advance()
    for copy in outs:
        copy.start()
    advance()
    outs[0].wait_recv()
    loads[4].wait()
    for j in range(0, rows, 64):
        tile = slice(j, j + 64)
        ffn_send[tile, :] = (ffn_own[0, tile, :].astype(f32) + ffn_recv[0, tile, :].astype(f32)).astype(bf16)
    outs_far.start()

    count = small.shape[2]
    gain = lane_vector(small, 0, size // count)
    acc[...] = jnp.zeros_like(acc)
    loads[7].wait()
    loads[8].wait()
    advance(4)
    far.wait_recv()

    @pl.loop(0, rows // 16)
    def _(i):
        here = pl.ds(pl.multiple_of(i * 16, 16), 16)
        value = x[here, :].astype(f32)
        center = value - jnp.mean(value, axis=1, keepdims=True)
        rstd = lax.rsqrt(jnp.mean(center * center, axis=1, keepdims=True) + EPS)
        hat = center * rstd
        incoming = first[here, :] + near_recv[1, here, :].astype(f32) + far_recv[here, :].astype(f32)
        acc[0] += incoming * hat
        acc[1] += incoming
        scaled = incoming * gain
        back_rows = rstd * (
            scaled - jnp.mean(scaled, axis=1, keepdims=True) - hat * jnp.mean(scaled * hat, axis=1, keepdims=True)
        )
        totals[here, :] = datt[here, :] + back_rows

    input_store = pltpu.make_async_copy(totals, input_out, local.at[11])
    input_store.start()
    vecs[0] = vec_ref[...]
    vecs[0, 0:1, :] = jnp.sum(acc[0], axis=0, keepdims=True)
    vecs[0, 1:2, :] = jnp.sum(acc[1], axis=0, keepdims=True)

    def hop(number):
        there = {"tensor": (place.core, place.chip)[number]} if number < 2 else {"dp": partners[number - 2]}
        return pltpu.make_async_remote_copy(
            src_ref=vecs.at[number],
            dst_ref=vec_recv.at[number],
            send_sem=v_send.at[number],
            recv_sem=v_recv.at[number],
            device_id=there,
            device_id_type=MESH,
        )

    for number in range(5):
        hop(number).start()
        advance(1 if number < 2 else 2)
        hop(number).wait_recv()
        summed = vecs[number] + vec_recv[number]
        if number < 2:
            row = lax.broadcasted_iota(jnp.int32, summed.shape, 0)
            summed = jnp.where(row < 4, summed, vecs[number])
        vecs[number + 1] = summed
    vec_out[...] = vecs[5]
    advance(2)
    outs[1].wait_recv()
    outs_far.wait_recv()
    loads[5].wait()
    loads[6].wait()
    for j in range(0, rows, 64):
        tile = slice(j, j + 64)
        layer[tile, :] = (
            attended[tile, :]
            + ffn_own[1, tile, :].astype(f32)
            + ffn_recv[1, tile, :].astype(f32)
            + ffn_far[tile, :].astype(f32)
        ).astype(bf16)
    layer_store = pltpu.make_async_copy(layer, layer_out, local.at[10])
    layer_store.start()
    results = [
        pltpu.make_async_copy(wsum.at[:, pl.ds(i * width, width)], out, local.at[12 + i])
        for i, out in enumerate((query_sum, key_sum, value_sum))
    ] + [pltpu.make_async_copy(osum, out_sum, local.at[15])]
    for item in plan:
        tick(*item)
        if item == (n - 1, 1):
            for copy in results[:-1]:
                copy.start()
    results[-1].start()
    for group in lanes:
        for lane in group:
            lane.finish()
    for copy in near + [far] + outs + [outs_far]:
        copy.wait_send()
    for number in range(5):
        hop(number).wait_send()
    for copy in results + [layer_store, input_store]:
        copy.wait()


def leave(normed, dlin, qkv, mixed, resid, datt, x, attended, ffn, small, vec, n):
    rows, model = x.shape
    size = model // n
    seq, width = mixed.shape
    shape = jax.ShapeDtypeStruct
    own = lambda kind: pltpu.VMEM((rows, model), kind)
    return pl.pallas_call(
        lambda *refs: leave_kernel(n, *refs),
        in_specs=[HBM] * 9 + [VMEM] * 2,
        out_specs=[HBM] * 6 + [VMEM],
        out_shape=[shape((rows, model), bf16), shape((rows, model), f32)]
        + [shape((size, width), f32)] * 3
        + [shape((width, size), f32), shape((8, model), f32)],
        scratch_shapes=[
            pltpu.VMEM((4, n, size // 2, 3 * width // 2), bf16),
            pltpu.VMEM((2, n, size // 2, width), bf16),
            pltpu.VMEM((seq, model), bf16),
            pltpu.VMEM((seq, 3 * width), bf16),
            pltpu.VMEM((n, size, 3 * width), bf16),
            pltpu.VMEM((n, 3 * width, size), bf16),
            pltpu.VMEM((seq, width), bf16),
            pltpu.VMEM((seq, model), bf16),
            own(f32),
            own(f32),
            own(bf16),
            own(f32),
            pltpu.VMEM((2, rows, model), bf16),
            pltpu.VMEM((2, rows, model), bf16),
            own(bf16),
            own(bf16),
            pltpu.VMEM((2, rows, model), bf16),
            pltpu.VMEM((2, rows, model), bf16),
            own(bf16),
            own(bf16),
            own(bf16),
            pltpu.VMEM((2, 16, model), f32),
            own(f32),
            pltpu.VMEM((size, 3 * width), f32),
            pltpu.VMEM((width, size), f32),
            pltpu.VMEM((6, 8, model), f32),
            pltpu.VMEM((5, 8, model), f32),
            DMA((6, n - 1)),
            DMA((6, n - 1)),
            DMA((6,)),
            DMA((6,)),
            DMA((5,)),
            DMA((5,)),
            DMA((16,)),
            DMA((2, 2, n)),
        ],
        compiler_params=pltpu.CompilerParams(collective_id=4, has_side_effects=True, vmem_limit_bytes=62 << 20),
        cost_estimate=pl.CostEstimate(flops=14 * seq * model * width, bytes_accessed=40 << 20, transcendentals=0),
        name="leave",
    )(normed, dlin, qkv.reshape(n, size, 3 * width), mixed, resid, datt, x, attended, ffn.reshape(4, rows, model), small, vec)

def finish_kernel(
    n,
    layer, input_grad, query_sum, key_sum, value_sum, out_sum, gate_sum, up_sum, down_sum, vec,
    layer_out, input_out, gain_one, shift_one, query_out, key_out, value_out, bias_q, bias_k, bias_v, out_out, gain_two, shift_two,
    gate_out, up_out, down_out,
    out_in, down_in, down_turned, held_input, held_layer, held, small_held, sems,
):
    loads = [
        pltpu.make_async_copy(src, dst, sems.at[i])
        for i, (src, dst) in enumerate(
            (
                (down_sum, down_in),
                (out_sum, out_in),
                (input_grad, held_input),
                (layer, held_layer),
                (gate_sum, held.at[0]),
                (up_sum, held.at[1]),
                (query_sum, small_held.at[0]),
                (key_sum, small_held.at[1]),
                (value_sum, small_held.at[2]),
            )
        )
    ]
    for load in loads:
        load.start()
    me, t = lax.axis_index("dp"), lax.axis_index("tensor")
    each = gain_one.shape[1]
    at = me * 4 + t
    fit = 128 // each
    for r, out in enumerate((gain_one, shift_one, gain_two, shift_two)):
        wide = vec[r : r + 1, pl.ds(pl.multiple_of(lax.div(at, fit) * 128, 128), 128)]
        value = wide[:, 0:each]
        for i in range(1, fit):
            value = jnp.where(lax.rem(at, fit) == i, wide[:, i * each : (i + 1) * each], value)
        out[...] = value
    heads, per = bias_q.shape
    row = vec[4:5, :]
    for part, out in ((0, bias_q), (2, bias_v)):
        base = part * heads * HD
        own = jnp.concatenate([row[:, base + h * HD : base + (h + 1) * HD] for h in range(heads)], axis=0)
        value = own[:, 0:per]
        for d in range(1, n):
            value = jnp.where(me == d, own[:, d * per : (d + 1) * per], value)
        out[...] = value
    base = heads * HD
    bias_k[...] = jnp.concatenate([row[:, base + h * HD : base + h * HD + ROT] for h in range(heads)], axis=0)
    stores = []

    def store(src, dst):
        stores.append(pltpu.make_async_copy(src, dst, sems.at[9 + len(stores)]))
        stores[-1].start()

    loads[0].wait()
    down_turned[...] = down_in[...].T
    store(down_turned, down_out)
    loads[1].wait()
    store(out_in, out_out)
    for load, src, dst in zip(
        loads[2:],
        (held_input, held_layer, held.at[0], held.at[1], small_held.at[0], small_held.at[1], small_held.at[2]),
        (input_out, layer_out, gate_out, up_out, query_out, key_out, value_out),
    ):
        load.wait()
        store(src, dst)
    for copy in stores:
        copy.wait()


def finish(layer, input_grad, query_sum, key_sum, value_sum, out_sum, gate_sum, up_sum, down_sum, vec, n):
    shape = jax.ShapeDtypeStruct
    size, width = query_sum.shape
    heads, model = width // HD, vec.shape[1]
    each = shape((1, model // (4 * n)), f32)
    bias = shape((heads, HD // n), f32)
    like = lambda value: shape(value.shape, value.dtype)
    results = pl.pallas_call(
        lambda *refs: finish_kernel(n, *refs),
        in_specs=[HBM] * 9 + [VMEM],
        out_specs=[HBM, HBM, VMEM, VMEM, HBM, HBM, HBM, VMEM, VMEM, VMEM, HBM, VMEM, VMEM, HBM, HBM, HBM],
        out_shape=[
            like(layer), like(input_grad), each, each, like(query_sum), like(key_sum), like(value_sum),
            bias, shape((heads, ROT), f32), bias, like(out_sum), each, each,
            like(gate_sum), like(up_sum), shape(down_sum.shape[::-1], f32),
        ],
        scratch_shapes=[
            pltpu.VMEM(out_sum.shape, f32),
            pltpu.VMEM(down_sum.shape, f32),
            pltpu.VMEM(down_sum.shape[::-1], f32),
            pltpu.VMEM(input_grad.shape, f32),
            pltpu.VMEM(layer.shape, bf16),
            pltpu.VMEM((2,) + gate_sum.shape, f32),
            pltpu.VMEM((3,) + query_sum.shape, f32),
            DMA((18,)),
        ],
        compiler_params=pltpu.CompilerParams(vmem_limit_bytes=62 << 20),
        name="finish",
    )(layer, input_grad, query_sum, key_sum, value_sum, out_sum, gate_sum, up_sum, down_sum, vec)
    return tuple(r.reshape(-1) if r.shape[0] == 1 else r for r in results)


def norm_forward(rows):
    center = rows - jnp.mean(rows, axis=-1, keepdims=True)
    rstd = lax.rsqrt(jnp.mean(center * center, axis=-1, keepdims=True) + EPS)
    return center * rstd, rstd


def norm_backward(grad_out, normal, rstd, gain):
    scaled = grad_out * gain
    return rstd * (
        scaled
        - jnp.mean(scaled, axis=-1, keepdims=True)
        - normal * jnp.mean(scaled * normal, axis=-1, keepdims=True)
    )


def local(
    layer_input,
    segments,
    positions,
    first_gain,
    first_shift,
    query_weight,
    key_weight,
    value_weight,
    query_bias,
    key_bias,
    value_bias,
    out_weight,
    second_gain,
    second_shift,
    gate_weight,
    up_weight,
    down_weight,
    out_grad,
):
    ring = Ring()
    n = ring.n
    width = query_weight.shape[1]
    heads = width // HD
    model = layer_input.shape[1]

    per = HD // n
    if ring.ring:
        normed, g_full, qkv, out_t, lin, small = enter(
            layer_input, out_grad, query_weight, key_weight, value_weight, out_weight,
            (first_gain, first_shift, second_gain, second_shift), (query_bias, value_bias), n
        )
        g_full = g_full.reshape(-1, model)
        qkv = qkv.reshape(model, -1)
        out_t = out_t.reshape(model, -1)
    else:
        gather = lambda vector: lax.all_gather(vector, "dp", axis=0, tiled=True).astype(f32)
        gain_one, shift_one, gain_two, shift_two = map(gather, (first_gain, first_shift, second_gain, second_shift))
        bias_query, bias_value = (gather(b.T).T.reshape(-1) for b in (query_bias, value_bias))
        bias_key = jnp.pad(key_bias.astype(f32), ((0, 0), (0, HD - ROT))).reshape(-1)
        bias_lin = jnp.concatenate([bias_query, bias_key, bias_value])
        x_full = tensor_gather(layer_input)
        g_full = tensor_gather(out_grad, after=x_full)
        qkv, _ = ring.gather(jnp.concatenate([query_weight, key_weight, value_weight], axis=1))
        out_t, _ = ring.gather(out_weight.T)
        gate, _ = ring.gather(gate_weight)
        up, _ = ring.gather(up_weight)
        down_t, _ = ring.gather(down_weight.T)
        hat_full, _ = norm_forward(x_full.astype(f32))
        normed = (hat_full * gain_one + shift_one).astype(bf16)
        lin = dot(qkv, normed, ((0,), (1,)))

    freqs = jnp.exp(-(2.0 / ROT) * jnp.arange(HALF).astype(f32) * math.log(10000.0))
    angles = freqs[:, None] * positions.astype(f32)[None, :]
    cosine, sine = jnp.cos(angles), jnp.sin(angles)
    rows = layer_input.astype(f32)
    if ring.ring:
        q_rot, k_rot, v_heads, logs, mixed, attended, second, gate, up, hidden, ffn, grad_gate, grad_up = middle(
            lin, key_bias, cosine, sine, segments, layer_input, out_t, small, gate_weight, up_weight, down_weight, g_full, n
        )
        second, gate, up = second.reshape(-1, model), gate.reshape(model, -1), up.reshape(model, -1)
        hidden, ffn = hidden.reshape(second.shape[0], -1), ffn.reshape(-1, model)
        grad_gate, grad_up = grad_gate.reshape(hidden.shape), grad_up.reshape(hidden.shape)
    else:
        index = jnp.arange(segments.shape[0], dtype=jnp.int32)
        allowed = (index[:, None] <= index[None, :]) & (segments[:, None] == segments[None, :])
        bias = jnp.where(allowed, 0.0, NEG).astype(f32)
        mixed, q_rot, k_rot, v_heads, logs = attend_forward(lin + bias_lin[:, None], cosine, sine, bias)
        attended = rows + tensor_scatter(dot(mixed, out_t, ((1,), (1,))))

        hat_two, rstd_two = norm_forward(attended)
        second = tensor_gather((hat_two * gain_two + shift_two).astype(bf16))
        gate_lin = dot(second, gate, ((1,), (0,)))
        up_lin = dot(second, up, ((1,), (0,)))
        sigma = jax.nn.sigmoid(gate_lin)
        activated = gate_lin * sigma
        hidden = (activated * up_lin).astype(bf16)
        ffn = dot(hidden, down_t, ((1,), (1,)))
        grad_hidden = dot(g_full, down_t, ((1,), (0,)))
        grad_gate = (grad_hidden * up_lin * sigma * (1.0 + gate_lin * (1.0 - sigma))).astype(bf16)
        grad_up = (grad_hidden * activated).astype(bf16)
    if ring.ring:
        down_sum, gate_sum, up_sum, grad_attended, residual, grad_lin, vec = back(
            grad_gate, grad_up, hidden, second, g_full, gate, up, attended, small, out_t,
            q_rot, k_rot, v_heads, logs, cosine, sine, segments, n
        )
        layer_output, input_grad, query_sum, key_sum, value_sum, out_sum, vec = leave(
            normed, grad_lin, qkv, mixed, residual.reshape(-1, model), grad_attended, layer_input, attended, ffn, small, vec, n
        )
        return finish(
            layer_output, input_grad, query_sum, key_sum, value_sum, out_sum, gate_sum, up_sum, down_sum, vec, n
        )
    else:
        down_grad = dot(g_full, hidden, ((0,), (0,)))
        grad_second = tensor_scatter(dot(grad_gate, gate, ((1,), (1,))) + dot(grad_up, up, ((1,), (1,))))
        gate_grad = dot(second, grad_gate, ((0,), (0,)))
        up_grad = dot(second, grad_up, ((0,), (0,)))
        down_sum = ring.scatter(down_grad).T
        gate_sum = ring.scatter(gate_grad)
        up_sum = ring.scatter(up_grad)
        grad_attended = out_grad.astype(f32) + norm_backward(grad_second, hat_two, rstd_two, gain_two)
        residual = tensor_gather(grad_attended.astype(bf16))
        grad_mixed = dot(out_t, residual, ((0,), (1,))).astype(bf16)
        dq, dk, dv, sums = attend_backward(q_rot, k_rot, v_heads, grad_mixed, logs, cosine, sine, bias)
        grad_lin = jnp.concatenate([dq, dk, dv], axis=0)
        sums = sums.reshape(width, 128)[:, :3]
        out_sum = ring.scatter(dot(residual, mixed, ((0,), (0,)))).T
        qkv_sum = ring.scatter(dot(normed, grad_lin, ((0,), (1,))))
        query_sum, key_sum, value_sum = (qkv_sum[:, i * width : (i + 1) * width] for i in range(3))
        grad_first = tensor_scatter(dot(grad_lin, qkv, ((0,), (1,))))
        hat_one, rstd_one = norm_forward(rows)
        input_grad = grad_attended + norm_backward(grad_first, hat_one, rstd_one, gain_one)
        layer_output = (attended + tensor_scatter(ffn.astype(f32))).astype(bf16)
        vectors = jnp.stack(
            [
                jnp.sum(grad_first * hat_one, axis=0),
                jnp.sum(grad_first, axis=0),
                jnp.sum(grad_second * hat_two, axis=0),
                jnp.sum(grad_second, axis=0),
            ]
        )
        packed = sum_all(jnp.concatenate([sum_all(vectors, ["tensor"]).reshape(-1), sums.T.reshape(-1)]), ["dp"])
        vectors, sums = packed[: 4 * model].reshape(4, model), packed[4 * model :].reshape(3, width)

    each = model // (n * lax.axis_size("tensor"))
    at = ring.me * lax.axis_size("tensor") + lax.axis_index("tensor")
    vectors = lax.dynamic_slice(vectors.reshape(4, -1, each), (0, at, 0), (4, 1, each))[:, 0]
    sums = sums.reshape(3, heads, n, per)
    mine = lax.dynamic_slice(sums, (0, 0, ring.me, 0), (3, heads, 1, per))[:, :, 0]
    key_bias_sum = sums[1].reshape(heads, HD)[:, :ROT]

    return (
        layer_output,
        input_grad,
        vectors[0],
        vectors[1],
        query_sum,
        key_sum,
        value_sum,
        mine[0],
        key_bias_sum,
        mine[2],
        out_sum,
        vectors[2],
        vectors[3],
        gate_sum,
        up_sum,
        down_sum,
    )


def solution(mesh):
    both = ("dp", "tensor")
    return jax.shard_map(
        local,
        mesh=mesh,
        in_specs=(
            P(both, None),
            P("dp"),
            P("dp"),
            P("dp"),
            P("dp"),
            P("dp", "tensor"),
            P("dp", "tensor"),
            P("dp", "tensor"),
            P("tensor", "dp"),
            P("tensor", None),
            P("tensor", "dp"),
            P("tensor", "dp"),
            P("dp"),
            P("dp"),
            P("dp", "tensor"),
            P("dp", "tensor"),
            P("tensor", "dp"),
            P(both, None),
        ),
        out_specs=(
            P(both, None),
            P(both, None),
            P(both),
            P(both),
            P("dp", "tensor"),
            P("dp", "tensor"),
            P("dp", "tensor"),
            P("tensor", "dp"),
            P("tensor", None),
            P("tensor", "dp"),
            P("tensor", "dp"),
            P(both),
            P(both),
            P("dp", "tensor"),
            P("dp", "tensor"),
            P("tensor", "dp"),
        ),
        check_vma=False,
    )
```

```python
import math

import jax
import jax.numpy as jnp
from jax import lax
from jax.experimental import pallas as pl
from jax.experimental.pallas import tpu as pltpu
from jax.sharding import PartitionSpec as P

HD = 64
ROT = 16
SEQ = 1024
HALF = ROT // 2
SCALE = HD ** (-0.5)

EPS = 1e-05
NEG = -1e30
QB = 256
f32 = jnp.float32
bf16 = jnp.bfloat16


def barrier(value, after):
    return lax.optimization_barrier((value, after))[0]


class Ring:
    def __init__(self):
        self.n = lax.axis_size("dp")
        self.ring = self.n == 8 and lax.axis_size("tensor") == 4
        order = list(range(0, self.n, 2)) + list(range(self.n - 1, 0, -2))
        self.up = [(order[i], order[(i + 1) % self.n]) for i in range(self.n)]
        self.down = [(b, a) for a, b in self.up]
        me = lax.axis_index("dp")
        self.me = me
        self.pos = jnp.where(me % 2 == 0, me // 2, self.n - 1 - (me - 1) // 2)

    def owner(self, offset):
        p = (self.pos + offset + 2 * self.n) % self.n
        return jnp.where(p < self.n // 2, 2 * p, 2 * (self.n - 1 - p) + 1)

    def gather(self, shard, pieces=1, after=None):
        n = self.n
        rows, cols = shard.shape
        if not self.ring:
            return lax.all_gather(shard, "dp", axis=0, tiled=True), [shard] * n
        if after is not None:
            shard = barrier(shard, after)
        full = jnp.zeros((n, rows, cols), shard.dtype)
        full = lax.dynamic_update_slice(full, shard[None], (self.me, 0, 0))
        size = rows // (2 * pieces)
        lanes = []
        for k in range(2 * pieces):
            lanes.append([k % 2, k * size, shard[k * size : (k + 1) * size]])
        marks = []
        for step in range(1, n):
            for lane in lanes:
                way, base, block = lane
                block = lax.ppermute(block, "dp", self.down if way else self.up)
                lane[2] = block
                whose = self.owner(step if way else -step)
                full = lax.dynamic_update_slice(full, block[None], (whose, base, 0))
            marks.append(lanes[-1][2])
        return full.reshape(n * rows, cols), marks

    def scatter(self, partial, pieces=1, after=None):
        n = self.n
        if not self.ring:
            return lax.psum_scatter(partial.astype(bf16), "dp", scatter_dimension=0, tiled=True).astype(f32)
        cols = partial.shape[1]
        rows = partial.shape[0] // n
        partial = partial.reshape(n, rows, cols)
        size = rows // (2 * pieces)
        done = []
        for k in range(2 * pieces):
            way = k % 2

            def block(step):
                whose = self.owner(1 + step if way else -1 - step)
                return lax.dynamic_slice(partial, (whose, k * size, 0), (1, size, cols))[0].astype(f32)

            moving = block(0)
            for step in range(1, n):
                got = lax.ppermute(moving.astype(bf16), "dp", self.down if way else self.up)
                moving = got.astype(f32) + block(step)
            done.append(moving)
        return jnp.concatenate(done, axis=0)


CORE = [(0, 1), (1, 0), (2, 3), (3, 2)]
CHIP = [(0, 2), (2, 0), (1, 3), (3, 1)]


def tensor_gather(rows, after=None):
    if lax.axis_size("tensor") != 4:
        return lax.all_gather(rows, "tensor", axis=0, tiled=True)
    if after is not None:
        rows = barrier(rows, after)
    t = lax.axis_index("tensor")
    far = lax.ppermute(rows, "tensor", CHIP)
    near = lax.ppermute(rows, "tensor", CORE)
    last = lax.ppermute(far, "tensor", CORE)
    full = jnp.zeros((4,) + rows.shape, rows.dtype)
    for flip, block in ((0, rows), (1, near), (2, far), (3, last)):
        full = lax.dynamic_update_slice(full, block[None], (t ^ flip, 0, 0))
    return full.reshape(4 * rows.shape[0], rows.shape[1])


def tensor_scatter(partial):
    if lax.axis_size("tensor") != 4:
        return lax.psum_scatter(partial.astype(bf16), "tensor", scatter_dimension=0, tiled=True).astype(f32)
    t = lax.axis_index("tensor")
    rows = partial.shape[0] // 4
    blocks = partial.reshape(4, rows, partial.shape[1])

    def block(flip):
        return lax.dynamic_slice(blocks, (t ^ flip, 0, 0), (1,) + blocks.shape[1:])[0]

    other = lax.ppermute(block(3).astype(bf16), "tensor", CORE)
    own = lax.ppermute(block(1).astype(bf16), "tensor", CORE)
    far = lax.ppermute((block(2) + other.astype(f32)).astype(bf16), "tensor", CHIP)
    return block(0) + own.astype(f32) + far.astype(f32)


def sum_all(vector, axes):
    for axis in axes:
        n = lax.axis_size(axis)
        if n & (n - 1):
            vector = lax.psum(vector, axis)
            continue
        step = 1
        while step < n:
            vector = vector + lax.ppermute(vector, axis, [(i, i ^ step) for i in range(n)])
            step *= 2
    return vector


def rotate(rows, cosine, sine, direction):
    first, second = rows[:HALF], rows[HALF:ROT]
    return jnp.concatenate(
        [first * cosine - direction * second * sine, second * cosine + direction * first * sine, rows[ROT:]], axis=0
    )


def dot(a, b, dims):
    return lax.dot_general(a, b, ((dims[0], dims[1]), ((), ())), preferred_element_type=f32)


def forward_kernel(q_ref, k_ref, v_ref, cos_ref, sin_ref, bias_ref, mixed_ref, q_out, k_out, v_out, log_ref):
    seq = q_ref.shape[1]
    cosine, sine = cos_ref[...], sin_ref[...]
    v_all = v_ref[...].astype(bf16)
    v_out[...] = v_all
    parts = []
    for head in range(q_ref.shape[0] // HD):
        rows = slice(head * HD, (head + 1) * HD)
        q = rotate(q_ref[rows, :], cosine, sine, 1.0).astype(bf16)
        k = rotate(k_ref[rows, :], cosine, sine, 1.0).astype(bf16)
        q_out[rows, :] = q
        k_out[rows, :] = k
        keys = k.T
        values = v_all[rows, :]
        q = q * jnp.asarray(SCALE, bf16)
        cols = []
        for start in range(0, seq, QB):
            end = start + QB
            scores = dot(keys[:end], q[:, start:end], ((1,), (0,))) + bias_ref[:end, start:end]
            top = jnp.max(scores, axis=0, keepdims=True)
            expo = jnp.exp(scores - top)
            total = jnp.sum(expo, axis=0, keepdims=True)
            probs = (expo * (1.0 / total)).astype(bf16)
            cols.append(dot(values[:, :end], probs, ((1,), (0,))).astype(bf16))
            log_ref[0, head : head + 1, start:end] = top + jnp.log(total)
        parts.append(jnp.concatenate(cols, axis=1))
    mixed_ref[...] = jnp.concatenate(parts, axis=0).T


def attend_forward(lin, cosine, sine, bias):
    width, seq = lin.shape[0] // 3, lin.shape[1]
    pair = 2 * HD
    count = width // pair
    outs = []
    block = lambda base: pl.BlockSpec((pair, seq), lambda i: (base * count + i, 0))
    whole = lambda shape: pl.BlockSpec(shape, lambda i: (0, 0))
    return pl.pallas_call(
        forward_kernel,
        grid=(count,),
        in_specs=[block(0), block(1), block(2), whole(cosine.shape), whole(sine.shape), whole(bias.shape)],
        out_specs=[
            pl.BlockSpec((seq, pair), lambda i: (0, i)),
            pl.BlockSpec((pair, seq), lambda i: (i, 0)),
            pl.BlockSpec((pair, seq), lambda i: (i, 0)),
            pl.BlockSpec((pair, seq), lambda i: (i, 0)),
            pl.BlockSpec((1, 2, seq), lambda i: (i, 0, 0)),
        ],
        out_shape=[
            jax.ShapeDtypeStruct((seq, width), bf16),
            jax.ShapeDtypeStruct((width, seq), bf16),
            jax.ShapeDtypeStruct((width, seq), bf16),
            jax.ShapeDtypeStruct((width, seq), bf16),
            jax.ShapeDtypeStruct((count, 2, seq), f32),
        ],
        compiler_params=pltpu.CompilerParams(vmem_limit_bytes=48 << 20),
        cost_estimate=pl.CostEstimate(
            flops=4 * width * seq * seq, bytes_accessed=30 << 20, transcendentals=width // HD * seq * seq
        ),
        name="attend_forward",
    )(lin, lin, lin, cosine, sine, bias)


def backward_kernel(q_ref, k_ref, v_ref, d_ref, log_ref, cos_ref, sin_ref, bias_ref, dq_out, dk_out, dv_out, sums_ref, dk_acc, dv_acc):
    seq = q_ref.shape[1]
    cosine, sine = cos_ref[...], sin_ref[...]
    for head in range(q_ref.shape[0] // HD):
        rows = slice(head * HD, (head + 1) * HD)
        q, k, v, d = q_ref[rows, :], k_ref[rows, :], v_ref[rows, :], d_ref[rows, :]
        keys, values = k.T, v.T
        q_small = q * jnp.asarray(SCALE, bf16)
        dk_acc[...] = jnp.zeros_like(dk_acc)
        dv_acc[...] = jnp.zeros_like(dv_acc)
        cols = []
        for start in range(0, seq, QB):
            end = start + QB
            here = slice(start, end)
            scores = dot(keys[:end], q_small[:, here], ((1,), (0,))) + bias_ref[:end, here]
            probs = jnp.exp(scores - log_ref[0, head : head + 1, here])
            grad = dot(values[:end], d[:, here], ((1,), (0,)))
            both = probs * grad
            inner = jnp.sum(both, axis=0, keepdims=True)
            grad = ((both - probs * inner) * SCALE).astype(bf16)
            probs = probs.astype(bf16)
            cols.append(dot(k[:, :end], grad, ((1,), (0,))))
            dk_acc[:, :end] += dot(q[:, here], grad, ((1,), (1,)))
            dv_acc[:, :end] += dot(d[:, here], probs, ((1,), (1,)))
        dq = rotate(jnp.concatenate(cols, axis=1), cosine, sine, -1.0)
        dk = rotate(dk_acc[...], cosine, sine, -1.0)
        dv = dv_acc[...]
        for part, (out, value) in enumerate(((dq_out, dq), (dk_out, dk), (dv_out, dv))):
            out[rows, :] = value.astype(bf16)
            sums_ref[0, rows, part : part + 1] = jnp.sum(value, axis=1, keepdims=True)


def attend_backward(q, k, v, d, logs, cosine, sine, bias):
    width, seq = q.shape
    pair = 2 * HD
    count = width // pair
    block = pl.BlockSpec((pair, seq), lambda i: (i, 0))
    whole = lambda shape: pl.BlockSpec(shape, lambda i: (0, 0))
    return pl.pallas_call(
        backward_kernel,
        grid=(count,),
        in_specs=[block] * 4
        + [pl.BlockSpec((1, 2, seq), lambda i: (i, 0, 0)), whole(cosine.shape), whole(sine.shape), whole(bias.shape)],
        out_specs=[block] * 3 + [pl.BlockSpec((1, pair, 128), lambda i: (i, 0, 0))],
        out_shape=[jax.ShapeDtypeStruct((width, seq), bf16)] * 3 + [jax.ShapeDtypeStruct((count, pair, 128), f32)],
        scratch_shapes=[pltpu.VMEM((HD, seq), f32), pltpu.VMEM((HD, seq), f32)],
        compiler_params=pltpu.CompilerParams(vmem_limit_bytes=48 << 20),
        cost_estimate=pl.CostEstimate(
            flops=10 * width * seq * seq, bytes_accessed=30 << 20, transcendentals=width // HD * seq * seq
        ),
        name="attend_backward",
    )(q, k, v, d, logs, cosine, sine, bias)


MESH = pl.DeviceIdType.MESH
HBM = pl.BlockSpec(memory_space=pl.ANY)
VMEM = pl.BlockSpec(memory_space=pltpu.VMEM)
DMA = pltpu.SemaphoreType.DMA


class Place:
    def __init__(self, n):
        self.n = n
        self.me = lax.axis_index("dp")
        self.t = lax.axis_index("tensor")
        odd = lax.rem(self.me, 2)
        half = lax.div(self.me, 2)
        self.pos = jnp.where(odd == 0, half, n - 1 - half)
        self.up = self.owner(1)
        self.down = self.owner(-1)
        self.core = self.t + 1 - 2 * lax.rem(self.t, 2)
        self.chip = lax.rem(self.t + 2, 4)
        self.cross = lax.rem(self.core + 2, 4)

    def owner(self, offset):
        p = lax.rem(self.pos + (offset + 2 * self.n), self.n)
        return jnp.where(p < self.n // 2, 2 * p, 2 * (self.n - 1 - p) + 1)

    def barrier(self, dp, tensor):
        sem = pltpu.get_barrier_semaphore()
        for there in dp:
            pl.semaphore_signal(sem, inc=1, device_id={"dp": there}, device_id_type=MESH)
        for there in tensor:
            pl.semaphore_signal(sem, inc=1, device_id={"tensor": there}, device_id_type=MESH)
        pl.semaphore_wait(sem, len(dp) + len(tensor))


class Lane:
    def __init__(self, place, full, base, size, way, send, recv):
        self.place, self.full, self.base, self.size, self.way = place, full, base, size, way
        self.send, self.recv = send, recv

    def whose(self, step):
        return self.place.owner(step if self.way else -step)

    def copy(self, step, whose):
        piece = self.full.at[whose, pl.ds(self.base, self.size)]
        return pltpu.make_async_remote_copy(
            src_ref=piece,
            dst_ref=piece,
            send_sem=self.send.at[step - 1],
            recv_sem=self.recv.at[step - 1],
            device_id={"dp": self.place.down if self.way else self.place.up},
            device_id_type=MESH,
        )

    def start(self, step):
        self.copy(step, self.whose(step - 1)).start()

    def arrive(self, step):
        self.copy(step, self.whose(step)).wait_recv()

    def finish(self):
        for step in range(1, self.place.n):
            self.copy(step, self.whose(step - 1)).wait_send()


class Exchange:
    def __init__(self, send, recv):
        self.send, self.recv = send, recv

    def copy(self, number, src, dst, there):
        return pltpu.make_async_remote_copy(
            src_ref=src,
            dst_ref=dst,
            send_sem=self.send.at[number],
            recv_sem=self.recv.at[number],
            device_id={"tensor": there},
            device_id_type=MESH,
        )


def row_norm(value, gain, shift):
    center = value - jnp.mean(value, axis=1, keepdims=True)
    rstd = lax.rsqrt(jnp.mean(center * center, axis=1, keepdims=True) + EPS)
    return center * rstd * gain + shift


def lane_vector(full, first, count):
    pieces = [full[d, r : r + 1, :] for d in range(full.shape[0]) for r in range(first, first + count)]
    return jnp.concatenate(pieces, axis=1)


def enter_kernel(
    n,
    x_ref, g_ref, wq, wk, wv, wo, gain_one, shift_one, gain_two, shift_two, bias_q, bias_v,
    normed_out, g_out, qkv_out, out_out, lin_out, small_full,
    x_full, normed, left, right, outs, lin, small_ref,
    small_send, small_recv, send, recv, x_send, x_recv, local, stored, lin_stored,
):
    place = Place(n)
    rows = x_ref.shape[0]
    size = wq.shape[0]
    width = wq.shape[1]
    half = width // 2
    me, t = place.me, place.t
    loads = [
        pltpu.make_async_copy(wq, left.at[me, :, pl.ds(0, width)], local.at[0]),
        pltpu.make_async_copy(wk.at[:, pl.ds(0, half)], left.at[me, :, pl.ds(width, half)], local.at[1]),
        pltpu.make_async_copy(wk.at[:, pl.ds(half, half)], right.at[me, :, pl.ds(0, half)], local.at[2]),
        pltpu.make_async_copy(wv, right.at[me, :, pl.ds(half, width)], local.at[3]),
        pltpu.make_async_copy(x_ref, x_full.at[t], local.at[4]),
        pltpu.make_async_copy(g_ref, g_out.at[t], local.at[5]),
    ]
    for load in loads:
        load.start()
    outs[me] = wo[...].T
    count = small_ref.shape[1]
    each = size // count
    small_ref[...] = jnp.zeros_like(small_ref)
    for i, vector in enumerate((gain_one, shift_one, gain_two, shift_two)):
        for r in range(each):
            small_ref[i * each + r, :] = vector[r * count : (r + 1) * count].astype(f32)
    heads, per = bias_q.shape
    small_ref[4 * each : 4 * each + heads, 0:per] = bias_q[...].astype(f32)
    small_ref[4 * each : 4 * each + heads, per : 2 * per] = bias_v[...].astype(f32)
    small_full[me] = small_ref[...]
    place.barrier([place.owner(k) for k in range(1, n)], [place.core, place.chip])

    smalls = []
    for k in range(1, n):
        smalls.append(
            pltpu.make_async_remote_copy(
                src_ref=small_ref,
                dst_ref=small_full.at[me],
                send_sem=small_send.at[k - 1],
                recv_sem=small_recv.at[k - 1],
                device_id={"dp": place.owner(k)},
                device_id_type=MESH,
            )
        )
        smalls[-1].start()

    swap = Exchange(x_send, x_recv)
    to_chip = swap.copy(0, x_ref, x_full.at[t], place.chip)
    to_core = swap.copy(1, x_ref, x_full.at[t], place.core)
    relay = swap.copy(2, x_full.at[place.chip], x_full.at[place.chip], place.core)
    g_chip = swap.copy(3, g_ref, g_out.at[t], place.chip)
    g_core = swap.copy(4, g_ref, g_out.at[t], place.core)
    g_relay = swap.copy(5, g_out.at[place.chip], g_out.at[place.chip], place.core)
    to_chip.start()
    to_core.start()
    for load in loads[:4]:
        load.wait()
    lanes = []
    for number, (full, base, count, way) in enumerate(
        (
            (left, 0, size // 2, 0),
            (right, 0, size // 2, 1),
            (left, size // 2, size // 2, 0),
            (right, size // 2, size // 2, 1),
            (outs, 0, size // 2, 0),
            (outs, size // 2, size // 2, 1),
        )
    ):
        lanes.append(Lane(place, full, base, count, way, send.at[number], recv.at[number]))

    def store(step):
        whose, other = place.owner(-step), place.owner(step)
        if step == n:
            return []
        return [
            pltpu.make_async_copy(left.at[whose], qkv_out.at[whose, :, pl.ds(0, width + half)], stored.at[0, step]),
            pltpu.make_async_copy(right.at[other], qkv_out.at[other, :, pl.ds(width + half, width + half)], stored.at[1, step]),
            pltpu.make_async_copy(outs.at[whose, pl.ds(0, size // 2)], out_out.at[whose, pl.ds(0, size // 2)], stored.at[2, step]),
            pltpu.make_async_copy(
                outs.at[other, pl.ds(size // 2, size // 2)], out_out.at[other, pl.ds(size // 2, size // 2)], stored.at[3, step]
            ),
        ]

    writes = []

    def tick(step):
        for lane in lanes:
            if step > 1:
                lane.arrive(step - 1)
            if step < n:
                lane.start(step)
        for write in store(step - 1):
            write.start()
            writes.append(write)

    gain = shift = None

    def norm(block):
        @pl.loop(0, rows // 16)
        def _(i):
            here = pl.ds(pl.multiple_of(i * 16, 16), 16)
            there = pl.ds(pl.multiple_of(block * rows + i * 16, 16), 16)
            normed[there, :] = row_norm(x_full[block, here, :].astype(f32), gain, shift).astype(bf16)

    def project(step):
        for full, whose, base in ((left, place.owner(-step), 0), (right, place.owner(step), width + half)):
            xs = normed[:, pl.ds(pl.multiple_of(whose * size, size), size)]
            for j in range(0, width + half, 256):
                part = dot(full[whose, :, j : j + 256].T, xs, ((1,), (1,)))
                where = slice(base + j, base + j + 256)
                if step == 0:
                    lin[where, :] = part
                else:
                    lin[where, :] += part
                if step == n - 1:
                    lin_store(base + j).start()

    def lin_store(first):
        at = pl.ds(first, 256)
        return pltpu.make_async_copy(lin.at[at], lin_out.at[at], lin_stored.at[first // 256])

    tick(1)
    loads[4].wait()
    for small in smalls:
        small.wait_recv()
    gain = lane_vector(small_full, 0, each)
    shift = lane_vector(small_full, each, each)
    norm(t)
    to_core.wait_recv()
    norm(place.core)
    tick(2)
    tick(3)
    to_chip.wait_recv()
    relay.start()
    g_chip.start()
    g_core.start()
    norm(place.chip)
    tick(4)
    relay.wait_recv()
    norm(place.cross)
    normed_store = pltpu.make_async_copy(normed, normed_out, local.at[6])
    normed_store.start()
    project(0)
    done = 1
    for step in range(5, n):
        tick(step)
        while done < min(step - 1, 2 * (step - 4) + 1):
            project(done)
            done += 1
    g_chip.wait_recv()
    g_relay.start()
    while done < n - 1:
        project(done)
        done += 1
    tick(n)
    project(n - 1)
    for copy in (to_chip, to_core, relay, g_chip, g_core, g_relay):
        copy.wait_send()
    g_core.wait_recv()
    g_relay.wait_recv()
    for small in smalls:
        small.wait_send()
    for lane in lanes:
        lane.finish()
    loads[5].wait()
    for write in writes:
        write.wait()
    normed_store.wait()
    for first in range(0, 3 * width, 256):
        lin_store(first).wait()


def enter(x, g, wq, wk, wv, wo, vectors, biases, n):
    rows, model = x.shape
    size, width = wq.shape
    big = 3 * width // 2
    kernel = lambda *refs: enter_kernel(n, *refs)
    return pl.pallas_call(
        kernel,
        in_specs=[HBM] * 5 + [VMEM] * 7,
        out_specs=[HBM, HBM, HBM, HBM, HBM, VMEM],
        out_shape=[
            jax.ShapeDtypeStruct((4 * rows, model), bf16),
            jax.ShapeDtypeStruct((4, rows, model), bf16),
            jax.ShapeDtypeStruct((n, size, 3 * width), bf16),
            jax.ShapeDtypeStruct((n, size, width), bf16),
            jax.ShapeDtypeStruct((3 * width, 4 * rows), f32),
            jax.ShapeDtypeStruct((n, 16, 128), f32),
        ],
        scratch_shapes=[
            pltpu.VMEM((4, rows, model), bf16),
            pltpu.VMEM((4 * rows, model), bf16),
            pltpu.VMEM((n, size, big), bf16),
            pltpu.VMEM((n, size, big), bf16),
            pltpu.VMEM((n, size, width), bf16),
            pltpu.VMEM((3 * width, 4 * rows), f32),
            pltpu.VMEM((16, 128), f32),
            DMA((n - 1,)),
            DMA((n - 1,)),
            DMA((6, n - 1)),
            DMA((6, n - 1)),
            DMA((6,)),
            DMA((6,)),
            DMA((7,)),
            DMA((4, n)),
            DMA((3 * width // 256,)),
        ],
        compiler_params=pltpu.CompilerParams(collective_id=1, has_side_effects=True, vmem_limit_bytes=56 << 20),
        cost_estimate=pl.CostEstimate(flops=6 * width * rows * 4 * model, bytes_accessed=40 << 20, transcendentals=0),
        name="enter",
    )(x, g, wq, wk, wv, wo, *vectors, *biases)

def attend_pair(pair, lin, bias_ref, cosine, sine, mask, q_all, k_all, v_all, logs, flat, mixed):
    width, seq = q_all.shape

    @pl.loop(0, 2)
    def _(j):
        head = pair * 2 + j
        first = pl.multiple_of(head * HD, HD)
        rows = pl.ds(first, HD)

        def load(part):
            at = pl.ds(pl.multiple_of(part * width + first, HD), HD)
            return lin[at, :] + bias_ref[at, :]

        q = rotate(load(0), cosine, sine, 1.0).astype(bf16)
        k = rotate(load(1), cosine, sine, 1.0).astype(bf16)
        values = load(2).astype(bf16)
        q_all[rows, :] = q
        k_all[rows, :] = k
        v_all[rows, :] = values
        keys = k.T
        q = q * jnp.asarray(SCALE, bf16)
        mine = pl.ds(pl.multiple_of(j * HD, HD), HD)
        for start in range(0, seq, QB):
            end = start + QB
            scores = dot(keys[:end], q[:, start:end], ((1,), (0,))) + mask[:end, start:end]
            top = jnp.max(scores, axis=0, keepdims=True)
            expo = jnp.exp(scores - top)
            total = jnp.sum(expo, axis=0, keepdims=True)
            probs = (expo * (1.0 / total)).astype(bf16)
            flat[mine, start:end] = dot(values[:, :end], probs, ((1,), (0,))).astype(bf16)
            logs[pl.ds(head, 1), start:end] = top + jnp.log(total)

    mixed[:, pair * 2 * HD : (pair + 1) * 2 * HD] = flat[...].T


def build_mask(mask, column, seg_row):
    seq = mask.shape[0]
    segments = seg_row[...].astype(f32)
    column[...] = jnp.broadcast_to(segments, (128, seq)).T

    @pl.loop(0, seq // 32)
    def _(i):
        here = pl.ds(pl.multiple_of(i * 32, 32), 32)
        key = lax.broadcasted_iota(jnp.int32, (32, seq), 0) + i * 32
        query = lax.broadcasted_iota(jnp.int32, (32, seq), 1)
        allowed = (key <= query) & (column[here, 0:1] == segments)
        mask[here, :] = jnp.where(allowed, 0.0, NEG).astype(f32)


def middle_kernel(
    n,
    lin_ref, key_bias, cos_ref, sin_ref, seg_row, x_ref, out_ref, small, gate_w, up_w, down_w, g_ref,
    q_out, k_out, v_out, logs, mixed_out, att_out, second_out, gate_out, up_out, hidden_out, ffn_out, dgate_out, dup_out,
    gate, up, down, second, near_send, near_recv, far_send, far_recv, attended,
    send, recv, x_send, x_recv, local, stored, staged,
):
    place = Place(n)
    t = place.t
    rows, model = x_ref.shape
    size, cols = gate_w.shape
    seq = 4 * rows
    width = out_ref.shape[1]
    loads = [
        pltpu.make_async_copy(gate_w, gate.at[place.me], local.at[0]),
        pltpu.make_async_copy(up_w, up.at[place.me], local.at[1]),
    ]
    for load in loads:
        load.start()
    down[place.me] = down_w[...].T
    place.barrier([place.up, place.down], [place.core, place.chip])
    for load in loads:
        load.wait()

    half, quarter = size // 2, size // 4
    lanes = [
        [Lane(place, full, half * sub, half, way, send.at[2 * way + sub], recv.at[2 * way + sub]) for way, full in ((0, gate), (1, up))]
        for sub in range(2)
    ]
    downs = [
        [
            Lane(place, down, half * way + quarter * sub, quarter, way, send.at[4 + 2 * way + sub], recv.at[4 + 2 * way + sub])
            for way in range(2)
        ]
        for sub in range(2)
    ]

    def write(step):
        gated, upped = place.owner(-step), place.owner(step)
        return [
            pltpu.make_async_copy(gate.at[gated], gate_out.at[gated], stored.at[0, step]),
            pltpu.make_async_copy(up.at[upped], up_out.at[upped], stored.at[1, step]),
        ]

    def tick(kind, step, sub):
        for lane in (downs if kind else lanes)[sub]:
            if step > 1:
                lane.arrive(step - 1)
            if step < n:
                lane.start(step)
        if sub == 1 and not kind:
            for copy in write(step - 1):
                copy.start()

    plan = [(0, step, sub) for step in range(1, n) for sub in range(2)]
    plan += [(1, 1, 0), (1, 1, 1), (0, n, 0), (0, n, 1)]
    plan += [(1, step, sub) for step in range(2, n + 1) for sub in range(2)]
    plan = iter(plan)

    def advance(count=1):
        for _ in range(count):
            tick(*next(plan))

    swap = Exchange(x_send, x_recv)
    near = [swap.copy(i, near_send.at[i], near_recv.at[i], place.core) for i in range(2)]
    far = swap.copy(2, far_send, far_recv, place.chip)
    to_chip = swap.copy(3, second.at[t], second.at[t], place.chip)
    to_core = swap.copy(4, second.at[t], second.at[t], place.core)
    relay = swap.copy(5, second.at[place.chip], second.at[place.chip], place.core)
    copies = near + [far, to_chip, to_core, relay]

    advance(2)

    def attention(lin, mask, q_all, k_all, v_all, flat, mixed, out_t, bias_ref, column):
        pairs = width // (2 * HD)
        fetch = []
        for part in range(3):
            for pair in range(pairs):
                at = pl.ds(part * width + pair * 2 * HD, 2 * HD)
                fetch.append(pltpu.make_async_copy(lin_ref.at[at], lin.at[at], local.at[2 + part * pairs + pair]))
        for pair in range(pairs):
            for part in range(3):
                fetch[part * pairs + pair].start()
        weights = pltpu.make_async_copy(out_ref, out_t, local.at[2 + 3 * pairs])
        weights.start()
        build_mask(mask, column, seg_row)
        heads, per = width // HD, HD // n
        first = small.shape[1] - heads
        turned = [small[d, first:, :].T for d in range(n)]
        keys = key_bias[...].astype(f32).T
        for head in range(heads):
            for part in range(3):
                if part == 1:
                    rest = jnp.zeros((HD - ROT, 1), f32)
                    piece = jnp.concatenate([keys[:, head : head + 1], rest], axis=0)
                else:
                    at = part // 2 * per
                    piece = jnp.concatenate([turned[d][at : at + per, head : head + 1] for d in range(n)], axis=0)
                where = part * width + head * HD
                bias_ref[where : where + HD, :] = piece
        cosine, sine = cos_ref[...], sin_ref[...]
        for pair in range(pairs):
            for part in range(3):
                fetch[part * pairs + pair].wait()
            attend_pair(pair, lin, bias_ref, cosine, sine, mask, q_all, k_all, v_all, logs, flat, mixed)
            advance()
        keep = [
            pltpu.make_async_copy(src, dst, local.at[3 + 3 * pairs + i])
            for i, (src, dst) in enumerate(((q_all, q_out), (k_all, k_out), (v_all, v_out), (mixed, mixed_out)))
        ]
        for copy in keep:
            copy.start()
        weights.wait()

        def project(block, j):
            at = pl.ds(pl.multiple_of(block * rows, rows), rows)
            return dot(mixed[at, :], out_t[j : j + 512, :], ((1,), (1,)))

        for i, block in enumerate((place.cross, place.core)):
            for j in range(0, model, 512):
                near_send[i, :, j : j + 512] = project(block, j).astype(bf16)
            near[i].start()
        near[0].wait_recv()
        for j in range(0, model, 512):
            tile = slice(j, j + 512)
            far_send[:, tile] = (project(place.chip, j) + near_recv[0, :, tile].astype(f32)).astype(bf16)
        far.start()
        own = pltpu.make_async_copy(x_ref, far_copy, local.at[7 + 3 * pairs])
        own.start()
        advance()
        near[1].wait_recv()
        own.wait()
        for j in range(0, model, 512):
            tile = slice(j, j + 512)
            attended[:, tile] = far_copy[:, tile].astype(f32) + project(t, j) + near_recv[1, :, tile].astype(f32)
        for copy in keep:
            copy.wait()

    far_copy = second.at[t]
    pl.run_scoped(
        attention,
        pltpu.VMEM((3 * width, seq), f32),
        pltpu.VMEM((seq, seq), f32),
        pltpu.VMEM((width, seq), bf16),
        pltpu.VMEM((width, seq), bf16),
        pltpu.VMEM((width, seq), bf16),
        pltpu.VMEM((2 * HD, seq), bf16),
        pltpu.VMEM((seq, width), bf16),
        pltpu.VMEM((model, width), bf16),
        pltpu.VMEM((3 * width, 1), f32),
        pltpu.VMEM((seq, 128), f32),
    )
    last = 7 + 3 * (width // (2 * HD))

    def feed(gate_lin, up_lin, grad, hidden, g, stage):
        g_load = pltpu.make_async_copy(g_ref, g, local.at[last + 1])
        g_load.start()
        gate_lin[...] = jnp.zeros_like(gate_lin)
        up_lin[...] = jnp.zeros_like(up_lin)
        grad[...] = jnp.zeros_like(grad)
        count = small.shape[2]
        gain = lane_vector(small, 2 * size // count, size // count)
        shift = lane_vector(small, 3 * size // count, size // count)
        advance(2)
        far.wait_recv()

        @pl.loop(0, rows // 16)
        def _(i):
            here = pl.ds(pl.multiple_of(i * 16, 16), 16)
            value = attended[here, :] + far_recv[here, :].astype(f32)
            attended[here, :] = value
            second[t, here, :] = row_norm(value, gain, shift).astype(bf16)

        to_chip.start()
        to_core.start()
        att_store = pltpu.make_async_copy(attended, att_out, local.at[last + 2])
        att_store.start()

        def add(block, low, high):
            @pl.loop(low, high)
            def _(step):
                for full, total, whose in ((gate, gate_lin, place.owner(-step)), (up, up_lin, place.owner(step))):
                    xs = second[block, :, pl.ds(pl.multiple_of(whose * size, size), size)]
                    total[block] += dot(xs, full[whose], ((1,), (0,)))

        advance()
        ready = 5
        add(t, 0, ready)
        to_core.wait_recv()
        advance()
        add(place.core, 0, ready)
        advance()
        to_chip.wait_recv()
        relay.start()
        add(place.chip, 0, ready)
        relay.wait_recv()
        second_store = pltpu.make_async_copy(second, second_out, local.at[last + 3])
        second_store.start()
        advance()
        add(place.cross, 0, ready)
        every = lambda low, high: pl.loop(0, 4)(lambda block: add(block, low, high))
        every(ready, n - 2)
        advance(2)
        advance()
        every(n - 2, n - 1)
        advance(2)
        every(n - 1, n)

        @pl.loop(0, 4 * rows // 16)
        def _(i):
            block = lax.div(i, rows // 16)
            here = pl.ds(pl.multiple_of(lax.rem(i, rows // 16) * 16, 16), 16)
            value = gate_lin[block, here, :]
            sigma = jax.nn.sigmoid(value)
            activated = value * sigma
            upward = up_lin[block, here, :]
            hidden[block, here, :] = (activated * upward).astype(bf16)
            gate_lin[block, here, :] = activated
            up_lin[block, here, :] = upward * sigma * (1.0 + value * (1.0 - sigma))

        hidden_store = pltpu.make_async_copy(hidden, hidden_out, local.at[last + 4])
        hidden_store.start()
        g_load.wait()
        stages = []

        def output(whose, base, count):
            number = len(stages)
            slot = number % 2
            if number >= 2:
                stages[number - 2].wait()

            right = down[whose, base : base + count].T
            for block in range(4):
                tile = dot(hidden[block], right, ((1,), (0,)))
                stage[slot, block, :, 0:count] = tile.astype(bf16)

            at = pl.ds(pl.multiple_of(whose * size + base, count), count)
            stages.append(pltpu.make_async_copy(stage.at[slot, :, :, pl.ds(0, count)], ffn_out.at[:, :, at], staged.at[number]))
            stages[-1].start()

        def collect(whose, base, count):
            at = pl.ds(pl.multiple_of(whose * size + base, count), count)

            @pl.loop(0, 4)
            def _(block):
                grad[block] += dot(g[block, :, at], down[whose, base : base + count], ((1,), (0,)))

        def use(whose, base=0, count=size):
            collect(whose, base, count)
            output(whose, base, count)

        after, before = place.owner(n - 1), place.owner(1 - n)
        use(place.me)
        for step in range(2, n):
            advance(2)
            if step - 1 == n // 2:
                use(place.owner(n // 2))
                use(after, 0, half)
                use(before, half, half)
            elif step - 1 > n // 2:
                one, other = place.owner(step - 1), place.owner(1 - step)
                first_at, other_at = (pl.ds(pl.multiple_of(whose * size, size), size) for whose in (one, other))

                @pl.loop(0, 4)
                def _(block):
                    both = dot(g[block, :, first_at], down[one], ((1,), (0,)))
                    both = both + dot(g[block, :, other_at], down[other], ((1,), (0,)))
                    grad[block] += both

                output(one, 0, size)
                output(other, 0, size)
        for lane in lanes[0] + lanes[1]:
            lane.finish()
        for step in range(n):
            for copy in write(step):
                copy.wait()
        advance(2)
        low_at = pl.ds(pl.multiple_of(before * size, half), half)
        high_at = pl.ds(pl.multiple_of(after * size + half, half), half)

        def leaving(block):
            return [
                pltpu.make_async_copy(gate.at[first + block], out.at[block], local.at[last + 5 + i * 4 + block])
                for i, (first, out) in enumerate(((0, dgate_out), (4, dup_out)))
            ]

        @pl.loop(0, 4)
        def _(block):
            for low in range(0, cols, 512):
                tile = slice(low, min(low + 512, cols))
                total = dot(g[block, :, low_at], down[before, 0:half, tile], ((1,), (0,)))
                total = total + dot(g[block, :, high_at], down[after, half:, tile], ((1,), (0,)))
                total = total + grad[block, :, tile]
                gate[block, :, tile] = (total * up_lin[block, :, tile]).astype(bf16)
                gate[4 + block, :, tile] = (total * gate_lin[block, :, tile]).astype(bf16)
            for copy in leaving(block):
                copy.start()

        output(before, 0, half)
        output(after, half, half)
        for lane in downs[0] + downs[1]:
            lane.finish()
        final = [copy for block in range(4) for copy in leaving(block)]
        for copy in final + stages[-2:] + [hidden_store, second_store, att_store]:
            copy.wait()

    pl.run_scoped(
        feed,
        pltpu.VMEM((4, rows, cols), f32),
        pltpu.VMEM((4, rows, cols), f32),
        pltpu.VMEM((4, rows, cols), f32),
        pltpu.VMEM((4, rows, cols), bf16),
        pltpu.VMEM((4, rows, model), bf16),
        pltpu.VMEM((2, 4, rows, size), bf16),
    )
    for copy in copies:
        copy.wait_send()


def middle(lin, key_bias, cosine, sine, segments, x, out_t, small, gate, up, down, g, n):
    rows, model = x.shape
    size, cols = gate.shape
    seq = 4 * rows
    width = out_t.shape[1]
    heads = width // HD
    shape = jax.ShapeDtypeStruct
    return pl.pallas_call(
        lambda *refs: middle_kernel(n, *refs),
        in_specs=[HBM] + [VMEM] * 4 + [HBM, HBM, VMEM, HBM, HBM, VMEM, HBM],
        out_specs=[HBM, HBM, HBM, VMEM] + [HBM] * 9,
        out_shape=[
            shape((width, seq), bf16),
            shape((width, seq), bf16),
            shape((width, seq), bf16),
            shape((heads, seq), f32),
            shape((seq, width), bf16),
            shape((rows, model), f32),
            shape((4, rows, model), bf16),
            shape((n, size, cols), bf16),
            shape((n, size, cols), bf16),
            shape((4, rows, cols), bf16),
            shape((4, rows, model), bf16),
            shape((4, rows, cols), bf16),
            shape((4, rows, cols), bf16),
        ],
        scratch_shapes=[
            pltpu.VMEM((n, size, cols), bf16),
            pltpu.VMEM((n, size, cols), bf16),
            pltpu.VMEM((n, size, cols), bf16),
            pltpu.VMEM((4, rows, model), bf16),
            pltpu.VMEM((2, rows, model), bf16),
            pltpu.VMEM((2, rows, model), bf16),
            pltpu.VMEM((rows, model), bf16),
            pltpu.VMEM((rows, model), bf16),
            pltpu.VMEM((rows, model), f32),
            DMA((8, n - 1)),
            DMA((8, n - 1)),
            DMA((6,)),
            DMA((6,)),
            DMA((20 + 3 * width // (2 * HD),)),
            DMA((2, n)),
            DMA((2 * n,)),
        ],
        compiler_params=pltpu.CompilerParams(collective_id=2, has_side_effects=True, vmem_limit_bytes=62 << 20),
        cost_estimate=pl.CostEstimate(
            flops=10 * seq * model * cols, bytes_accessed=60 << 20, transcendentals=heads * seq * seq
        ),
        name="middle",
    )(
        lin, key_bias, cosine, sine, segments[None, :],
        x, out_t, small, gate, up, down, g.reshape(4, rows, model),
    )

class Sum:
    def __init__(self, place, slots, way, send, recv):
        self.place, self.slots, self.way, self.send, self.recv = place, slots, way, send, recv

    def whose(self, step):
        return self.place.owner(1 + step if self.way else -1 - step)

    def copy(self, step):
        return pltpu.make_async_remote_copy(
            src_ref=self.slots.at[step - 1],
            dst_ref=self.slots.at[step],
            send_sem=self.send.at[step - 1],
            recv_sem=self.recv.at[step - 1],
            device_id={"dp": self.place.down if self.way else self.place.up},
            device_id_type=MESH,
        )

    def tick(self, step, product, final):
        if step > 0:
            self.copy(step).wait_recv()
        cols = self.slots.shape[2]
        for low in range(0, cols, 512):
            tile = slice(low, min(low + 512, cols))
            part = product(tile)
            if step > 0:
                part = part + self.slots[step, :, tile].astype(f32)
            if step == self.place.n - 1:
                final(tile, part)
            else:
                self.slots[step, :, tile] = part.astype(bf16)
        if step < self.place.n - 1:
            self.copy(step + 1).start()

    def finish(self):
        for step in range(1, self.place.n):
            self.copy(step).wait_send()


def columns_of(left, whose, size, way):
    half = size // 2
    return left[:, pl.ds(pl.multiple_of(whose * size + way * half, half), half)].T


def retreat_pair(pair, q_all, k_all, v_all, d_all, logs, cosine, sine, mask, dk_acc, dv_acc, tmp, vec):
    width, seq = q_all.shape

    @pl.loop(0, 2)
    def _(j):
        head = pair * 2 + j
        rows = pl.ds(pl.multiple_of(head * HD, HD), HD)
        q, k, v, d = q_all[rows, :], k_all[rows, :], v_all[rows, :], d_all[rows, :]
        keys, values = k.T, v.T
        q_small = q * jnp.asarray(SCALE, bf16)
        dk_acc[...] = jnp.zeros_like(dk_acc)
        dv_acc[...] = jnp.zeros_like(dv_acc)
        cols = []
        for start in range(0, seq, QB):
            end = start + QB
            here = slice(start, end)
            scores = dot(keys[:end], q_small[:, here], ((1,), (0,))) + mask[:end, here]
            probs = jnp.exp(scores - logs[pl.ds(head, 1), here])
            grad = dot(values[:end], d[:, here], ((1,), (0,)))
            both = probs * grad
            inner = jnp.sum(both, axis=0, keepdims=True)
            grad = ((both - probs * inner) * SCALE).astype(bf16)
            probs = probs.astype(bf16)
            cols.append(dot(k[:, :end], grad, ((1,), (0,))))
            dk_acc[:, :end] += dot(q[:, here], grad, ((1,), (1,)))
            dv_acc[:, :end] += dot(d[:, here], probs, ((1,), (1,)))
        dq = rotate(jnp.concatenate(cols, axis=1), cosine, sine, -1.0)
        dk = rotate(dk_acc[...], cosine, sine, -1.0)
        dv = dv_acc[...]
        mine = pl.ds(pl.multiple_of(j * HD, HD), HD)
        for part, (out, value) in enumerate(((q_all, dq), (k_all, dk), (v_all, dv))):
            out[rows, :] = value.astype(bf16)
            lanes = value[:, :128]
            for i in range(128, seq, 128):
                lanes = lanes + value[:, i : i + 128]
            tmp[part, mine, :] = lanes

    for part in range(3):
        at = part * width + pair * 2 * HD
        vec[4:5, at : at + 2 * HD] = jnp.sum(tmp[part].T, axis=0, keepdims=True)


def back_kernel(
    n,
    dgate_ref, dup_ref, hidden_ref, second_ref, g_ref, gate_ref, up_ref, att_ref, small, out_ref,
    q_ref, k_ref, v_ref, logs, cos_ref, sin_ref, seg_row,
    down_sum, gate_sum, up_sum, datt_out, resid_out, dlin_out, vec,
    slots, g, second, hidden, dgate, dup, near_send, near_recv, far_send, far_recv, datt, acc,
    send, recv, x_send, x_recv, local,
):
    place = Place(n)
    t = place.t
    rows, model = att_ref.shape
    size, cols = gate_ref.shape[1:]
    seq, width = 4 * rows, out_ref.shape[1]
    loads = [
        pltpu.make_async_copy(src, dst, local.at[i])
        for i, (src, dst) in enumerate(
            ((g_ref, g), (hidden_ref, hidden), (second_ref, second), (dgate_ref, dgate), (dup_ref, dup))
        )
    ]
    for load in loads[:2]:
        load.start()
    place.barrier([place.up, place.down], [place.core, place.chip])

    lanes = [[Sum(place, slots.at[2 * i + way], way, send.at[2 * i + way], recv.at[2 * i + way]) for way in range(2)] for i in range(3)]
    sources = ((g, hidden), (second, dgate), (second, dup))
    sums = (down_sum, gate_sum, up_sum)

    def stored(i):
        return pltpu.make_async_copy(datt.at[:, pl.ds(0, cols)], sums[i], local.at[6 + i])

    def tick(step, i):
        left, right = sources[i]
        if step == n - 1:
            (stored(i - 1) if i else datt_copy()).wait()
        for lane in lanes[i]:

            def final(tile, total):
                datt[lane.way * size // 2 : (lane.way + 1) * size // 2, tile] = total

            block = columns_of(left, lane.whose(step), size, lane.way)
            lane.tick(step, lambda tile: dot(block, right[:, tile], ((1,), (0,))), final)
        if step == n - 1:
            stored(i).start()

    plan = iter([(step, i) for step in range(n) for i in range(3)])

    def advance(count=1):
        for _ in range(count):
            tick(*next(plan))

    def datt_copy():
        return pltpu.make_async_copy(datt, datt_out, local.at[9])

    swap = Exchange(x_send, x_recv)
    near = [swap.copy(i, near_send.at[i], near_recv.at[i], place.core) for i in range(2)]
    far = swap.copy(2, far_send, far_recv, place.chip)
    to_chip = swap.copy(3, far_send, resid_out.at[t], place.chip)
    to_core = swap.copy(4, far_send, resid_out.at[t], place.core)
    relay = swap.copy(5, resid_out.at[place.chip], resid_out.at[place.chip], place.core)
    keep = pltpu.make_async_copy(far_send, resid_out.at[t], local.at[10])
    own = pl.ds(pl.multiple_of(t * rows, rows), rows)

    def feed(gate, up):
        weights = [
            pltpu.make_async_copy(gate_ref, gate, local.at[11]),
            pltpu.make_async_copy(up_ref, up, local.at[12]),
        ]
        loads[0].wait()
        loads[1].wait()
        for load in loads[2:]:
            load.start()
        advance()
        loads[2].wait()
        loads[3].wait()
        for copy in weights:
            copy.start()
        advance()
        loads[4].wait()
        advance()
        for copy in weights:
            copy.wait()

        def product(block, j):
            at = pl.ds(pl.multiple_of(block * rows, rows), rows)
            return dot(dgate[at, :], gate[j], ((1,), (1,))) + dot(dup[at, :], up[j], ((1,), (1,)))

        for i, block in enumerate((place.cross, place.core)):
            for j in range(n):
                near_send[i, :, j * size : (j + 1) * size] = product(block, j).astype(bf16)
            near[i].start()
            advance()
        near[0].wait_recv()
        for j in range(n):
            tile = slice(j * size, (j + 1) * size)
            far_send[:, tile] = (product(place.chip, j) + near_recv[0, :, tile].astype(f32)).astype(bf16)
        far.start()
        advance()
        near[1].wait_recv()
        for j in range(n):
            tile = slice(j * size, (j + 1) * size)
            datt[:, tile] = product(t, j) + near_recv[1, :, tile].astype(f32)
        advance()

    pl.run_scoped(feed, pltpu.VMEM((n, size, cols), bf16), pltpu.VMEM((n, size, cols), bf16))

    def attention(attended, mask, q_all, k_all, v_all, d_all, out_t, dk_acc, dv_acc, tmp, column):
        load_attended = pltpu.make_async_copy(att_ref, attended, local.at[5])
        load_attended.start()
        fetch = [
            pltpu.make_async_copy(src, dst, local.at[13 + i])
            for i, (src, dst) in enumerate(((out_ref, out_t), (q_ref, q_all), (k_ref, k_all), (v_ref, v_all)))
        ]
        for copy in fetch:
            copy.start()
        build_mask(mask, column, seg_row)
        count = small.shape[2]
        gain = lane_vector(small, 2 * size // count, size // count)
        acc[...] = jnp.zeros_like(acc)
        advance(1)
        far.wait_recv()
        far.wait_send()
        load_attended.wait()

        @pl.loop(0, rows // 16)
        def _(i):
            here = pl.ds(pl.multiple_of(i * 16, 16), 16)
            value = attended[here, :]
            center = value - jnp.mean(value, axis=1, keepdims=True)
            rstd = lax.rsqrt(jnp.mean(center * center, axis=1, keepdims=True) + EPS)
            hat = center * rstd
            incoming = datt[here, :] + far_recv[here, :].astype(f32)
            acc[0] += incoming * hat
            acc[1] += incoming
            scaled = incoming * gain
            back = rstd * (
                scaled - jnp.mean(scaled, axis=1, keepdims=True) - hat * jnp.mean(scaled * hat, axis=1, keepdims=True)
            )
            whole = g[pl.ds(pl.multiple_of(t * rows + i * 16, 16), 16), :].astype(f32) + back
            datt[here, :] = whole
            far_send[here, :] = whole.astype(bf16)

        to_chip.start()
        to_core.start()
        keep.start()
        datt_copy().start()
        vec[...] = jnp.zeros_like(vec)
        vec[2:3, :] = jnp.sum(acc[0], axis=0, keepdims=True)
        vec[3:4, :] = jnp.sum(acc[1], axis=0, keepdims=True)
        for copy in near:
            copy.wait_send()
        fetch[0].wait()

        def mix(block, source):
            value = dot(source[...], out_t[...], ((1,), (0,))).astype(bf16)
            d_all[:, pl.ds(pl.multiple_of(block * rows, rows), rows)] = value.T

        def bring(block, slot, number):
            return pltpu.make_async_copy(resid_out.at[block], near_send.at[slot], local.at[number])

        mix(t, far_send)
        advance()
        to_core.wait_recv()
        first = bring(place.core, 0, 17)
        first.start()
        first.wait()
        mix(place.core, near_send.at[0])
        advance(2)
        to_chip.wait_recv()
        relay.start()
        second_block = bring(place.chip, 1, 18)
        second_block.start()
        second_block.wait()
        mix(place.chip, near_send.at[1])
        relay.wait_recv()
        third = bring(place.cross, 0, 19)
        third.start()
        third.wait()
        mix(place.cross, near_send.at[0])
        for copy in fetch[1:]:
            copy.wait()
        cosine, sine = cos_ref[...], sin_ref[...]
        for pair in range(width // (2 * HD)):
            advance()
            retreat_pair(pair, q_all, k_all, v_all, d_all, logs, cosine, sine, mask, dk_acc, dv_acc, tmp, vec)
            here = slice(pair * 2 * HD, (pair + 1) * 2 * HD)
            out_t[0:seq, here] = q_all[here, :].T
            out_t[seq : 2 * seq, here] = k_all[here, :].T
            turned = v_all[here, :].T
            for block in range(4):
                at = block * width + pair * 2 * HD
                near_recv[0, :, at : at + 2 * HD] = turned[block * rows : (block + 1) * rows]
        final = [
            pltpu.make_async_copy(out_t.at[pl.ds(i * seq, seq)], dlin_out.at[:, pl.ds(i * width, width)], local.at[20 + i])
            for i in range(2)
        ] + [
            pltpu.make_async_copy(
                near_recv.at[0, :, pl.ds(block * width, width)],
                dlin_out.at[pl.ds(block * rows, rows), pl.ds(2 * width, width)],
                local.at[22 + block],
            )
            for block in range(4)
        ]
        for copy in final:
            copy.start()
        advance(2)
        for copy in final:
            copy.wait()

    pl.run_scoped(
        attention,
        pltpu.VMEM((rows, model), f32),
        pltpu.VMEM((seq, seq), f32),
        pltpu.VMEM((width, seq), bf16),
        pltpu.VMEM((width, seq), bf16),
        pltpu.VMEM((width, seq), bf16),
        pltpu.VMEM((width, seq), bf16),
        pltpu.VMEM((model, width), bf16),
        pltpu.VMEM((HD, seq), f32),
        pltpu.VMEM((HD, seq), f32),
        pltpu.VMEM((3, 2 * HD, 128), f32),
        pltpu.VMEM((seq, 128), f32),
    )
    for step in plan:
        tick(*step)
    for pair in lanes:
        for lane in pair:
            lane.finish()
    for copy in (to_chip, to_core, relay):
        copy.wait_send()
    keep.wait()
    stored(2).wait()


def back(dgate, dup, hidden, second, g, gate, up, attended, small, out_t, q, k, v, logs, cosine, sine, segments, n):
    rows, model = attended.shape
    size, cols = model // n, hidden.shape[1]
    seq, width = 4 * rows, out_t.shape[1]
    shape = jax.ShapeDtypeStruct
    return pl.pallas_call(
        lambda *refs: back_kernel(n, *refs),
        in_specs=[HBM] * 8 + [VMEM] + [HBM] * 4 + [VMEM] * 4,
        out_specs=[HBM] * 6 + [VMEM],
        out_shape=[
            shape((size, cols), f32),
            shape((size, cols), f32),
            shape((size, cols), f32),
            shape((rows, model), f32),
            shape((4, rows, model), bf16),
            shape((seq, 3 * width), bf16),
            shape((8, model), f32),
        ],
        scratch_shapes=[
            pltpu.VMEM((6, n, size // 2, cols), bf16),
            pltpu.VMEM((seq, model), bf16),
            pltpu.VMEM((seq, model), bf16),
            pltpu.VMEM((seq, cols), bf16),
            pltpu.VMEM((seq, cols), bf16),
            pltpu.VMEM((seq, cols), bf16),
            pltpu.VMEM((2, rows, model), bf16),
            pltpu.VMEM((2, rows, model), bf16),
            pltpu.VMEM((rows, model), bf16),
            pltpu.VMEM((rows, model), bf16),
            pltpu.VMEM((rows, model), f32),
            pltpu.VMEM((2, 16, model), f32),
            DMA((6, n - 1)),
            DMA((6, n - 1)),
            DMA((6,)),
            DMA((6,)),
            DMA((26,)),
        ],
        compiler_params=pltpu.CompilerParams(collective_id=3, has_side_effects=True, vmem_limit_bytes=62 << 20),
        cost_estimate=pl.CostEstimate(
            flops=14 * seq * model * cols, bytes_accessed=60 << 20, transcendentals=width // HD * seq * seq
        ),
        name="back",
    )(
        dgate, dup, hidden, second, g, gate.reshape(n, size, cols), up.reshape(n, size, cols), attended, small, out_t,
        q, k, v, logs, cosine, sine, segments[None, :],
    )

def leave_kernel(
    n,
    normed_ref, dlin_ref, qkv_ref, mixed_ref, resid_ref, datt_ref, x_ref, att_ref, ffn_ref, small, vec_ref,
    layer_out, input_out, query_sum, key_sum, value_sum, out_sum, vec_out,
    wide, narrow, normed, dlin, qkv, turned, mixed, resid, datt, attended, x, first, near_send, near_recv, far_send, far_recv,
    ffn_own, ffn_recv, ffn_send, ffn_far, layer, acc, totals, wsum, osum, vecs, vec_recv,
    send, recv, x_send, x_recv, v_send, v_recv, local, blocks,
):
    place = Place(n)
    t, me = place.t, place.me
    rows, model = att_ref.shape
    size = model // n
    total_cols = dlin_ref.shape[1]
    width = total_cols // 3
    part = total_cols // 2
    loads = [
        pltpu.make_async_copy(src, dst, local.at[i])
        for i, (src, dst) in enumerate(
            (
                (dlin_ref.at[:, pl.ds(0, part)], dlin.at[:, pl.ds(0, part)]),
                (dlin_ref.at[:, pl.ds(part, part)], dlin.at[:, pl.ds(part, part)]),
                (mixed_ref, mixed),
                (qkv_ref, qkv),
                (ffn_ref.at[place.chip], ffn_own.at[0]),
                (ffn_ref.at[t], ffn_own.at[1]),
                (att_ref, attended),
                (x_ref, x),
                (datt_ref, datt),
            )
        )
    ]
    hops = [1, 2, 4]
    partners = [me + hop - 2 * hop * lax.rem(lax.div(me, hop), 2) for hop in hops]

    lanes = [
        [Sum(place, wide.at[2 * i + way], way, send.at[2 * i + way], recv.at[2 * i + way]) for way in range(2)] for i in range(2)
    ] + [[Sum(place, narrow.at[way], way, send.at[4 + way], recv.at[4 + way]) for way in range(2)]]

    swap = Exchange(x_send, x_recv)
    near = [swap.copy(i, near_send.at[i], near_recv.at[i], place.core) for i in range(2)]
    far = swap.copy(2, far_send, far_recv, place.chip)
    outs = [swap.copy(3 + i, ffn_ref.at[block], ffn_recv.at[i], place.core) for i, block in enumerate((place.cross, place.core))]
    outs_far = swap.copy(5, ffn_send, ffn_far, place.chip)

    def block_of(step, way, i):
        lane = lanes[0][way]
        at = pl.ds(pl.multiple_of(lane.whose(step) * size + way * (size // 2), size // 2), size // 2)
        src, dst = ((normed_ref, normed), (resid_ref, resid))[i]
        return pltpu.make_async_copy(src.at[:, at], dst.at[:, at], blocks.at[i, way, step])

    def fetch(steps, i):
        for step in steps:
            for way in range(2):
                block_of(step, way, i).start()

    fetch(range(1), 0)
    loads[0].start()
    loads[1].start()
    fetch(range(1), 1)
    loads[2].start()
    fetch(range(1, 3), 0)
    fetch(range(1, 3), 1)
    place.barrier([place.up, place.down] + partners, [place.core, place.chip])

    def tick(step, i):
        if i != 1:
            for way in range(2):
                block_of(step, way, i // 2).wait()
        for lane in lanes[i]:
            half = slice(lane.way * size // 2, (lane.way + 1) * size // 2)
            if i == 2:

                def product(left, tile):
                    return dot(left, mixed[:, tile], ((1,), (0,)))

                def final(tile, total):
                    osum[tile, half] = total.T

            else:

                def product(left, tile):
                    return dot(left, dlin[:, part * i + tile.start : part * i + tile.stop], ((1,), (0,)))

                def final(tile, total):
                    wsum[half, part * i + tile.start : part * i + tile.stop] = total

            left = columns_of(resid if i == 2 else normed, lane.whose(step), size, lane.way)
            lane.tick(step, lambda tile: product(left, tile), final)

    plan = iter([(step, i) for step in range(n) for i in range(3)])

    def advance(count=1):
        for _ in range(count):
            tick(*next(plan))

    loads[0].wait()
    advance()
    loads[1].wait()
    loads[3].start()
    advance()
    for load in loads[4:]:
        load.start()
    fetch(range(3, n), 0)
    fetch(range(3, n), 1)
    loads[2].wait()
    advance()
    loads[3].wait()

    def lines(block):
        return dlin[pl.ds(pl.multiple_of(block * rows, rows), rows), :]

    def product(block, use):
        for j in range(n):
            use(slice(j * size, (j + 1) * size), dot(lines(block), turned[j], ((1,), (0,))))

    for j in range(n):
        turned[j] = qkv[j].T
    for i, block in enumerate((place.cross, place.core)):

        def use_near(tile, value):
            near_send[i, :, tile] = value.astype(bf16)

        product(block, use_near)
        near[i].start()
        advance()
    near[0].wait_recv()

    def use_far(tile, value):
        far_send[:, tile] = (value + near_recv[0, :, tile].astype(f32)).astype(bf16)

    product(place.chip, use_far)
    far.start()
    advance()

    def use_own(tile, value):
        first[:, tile] = value

    product(t, use_own)
    near[1].wait_recv()
    advance()
    for copy in outs:
        copy.start()
    advance()
    outs[0].wait_recv()
    loads[4].wait()
    for j in range(0, rows, 64):
        tile = slice(j, j + 64)
        ffn_send[tile, :] = (ffn_own[0, tile, :].astype(f32) + ffn_recv[0, tile, :].astype(f32)).astype(bf16)
    outs_far.start()

    count = small.shape[2]
    gain = lane_vector(small, 0, size // count)
    acc[...] = jnp.zeros_like(acc)
    loads[7].wait()
    loads[8].wait()
    advance(4)
    far.wait_recv()

    @pl.loop(0, rows // 16)
    def _(i):
        here = pl.ds(pl.multiple_of(i * 16, 16), 16)
        value = x[here, :].astype(f32)
        center = value - jnp.mean(value, axis=1, keepdims=True)
        rstd = lax.rsqrt(jnp.mean(center * center, axis=1, keepdims=True) + EPS)
        hat = center * rstd
        incoming = first[here, :] + near_recv[1, here, :].astype(f32) + far_recv[here, :].astype(f32)
        acc[0] += incoming * hat
        acc[1] += incoming
        scaled = incoming * gain
        back_rows = rstd * (
            scaled - jnp.mean(scaled, axis=1, keepdims=True) - hat * jnp.mean(scaled * hat, axis=1, keepdims=True)
        )
        totals[here, :] = datt[here, :] + back_rows

    input_store = pltpu.make_async_copy(totals, input_out, local.at[11])
    input_store.start()
    vecs[0] = vec_ref[...]
    vecs[0, 0:1, :] = jnp.sum(acc[0], axis=0, keepdims=True)
    vecs[0, 1:2, :] = jnp.sum(acc[1], axis=0, keepdims=True)

    def hop(number):
        there = {"tensor": (place.core, place.chip)[number]} if number < 2 else {"dp": partners[number - 2]}
        return pltpu.make_async_remote_copy(
            src_ref=vecs.at[number],
            dst_ref=vec_recv.at[number],
            send_sem=v_send.at[number],
            recv_sem=v_recv.at[number],
            device_id=there,
            device_id_type=MESH,
        )

    for number in range(5):
        hop(number).start()
        advance(1 if number < 2 else 2)
        hop(number).wait_recv()
        summed = vecs[number] + vec_recv[number]
        if number < 2:
            row = lax.broadcasted_iota(jnp.int32, summed.shape, 0)
            summed = jnp.where(row < 4, summed, vecs[number])
        vecs[number + 1] = summed
    vec_out[...] = vecs[5]
    advance(2)
    outs[1].wait_recv()
    outs_far.wait_recv()
    loads[5].wait()
    loads[6].wait()
    for j in range(0, rows, 64):
        tile = slice(j, j + 64)
        layer[tile, :] = (
            attended[tile, :]
            + ffn_own[1, tile, :].astype(f32)
            + ffn_recv[1, tile, :].astype(f32)
            + ffn_far[tile, :].astype(f32)
        ).astype(bf16)
    layer_store = pltpu.make_async_copy(layer, layer_out, local.at[10])
    layer_store.start()
    results = [
        pltpu.make_async_copy(wsum.at[:, pl.ds(i * width, width)], out, local.at[12 + i])
        for i, out in enumerate((query_sum, key_sum, value_sum))
    ] + [pltpu.make_async_copy(osum, out_sum, local.at[15])]
    for item in plan:
        tick(*item)
        if item == (n - 1, 1):
            for copy in results[:-1]:
                copy.start()
    results[-1].start()
    for group in lanes:
        for lane in group:
            lane.finish()
    for copy in near + [far] + outs + [outs_far]:
        copy.wait_send()
    for number in range(5):
        hop(number).wait_send()
    for copy in results + [layer_store, input_store]:
        copy.wait()


def leave(normed, dlin, qkv, mixed, resid, datt, x, attended, ffn, small, vec, n):
    rows, model = x.shape
    size = model // n
    seq, width = mixed.shape
    shape = jax.ShapeDtypeStruct
    own = lambda kind: pltpu.VMEM((rows, model), kind)
    return pl.pallas_call(
        lambda *refs: leave_kernel(n, *refs),
        in_specs=[HBM] * 9 + [VMEM] * 2,
        out_specs=[HBM] * 6 + [VMEM],
        out_shape=[shape((rows, model), bf16), shape((rows, model), f32)]
        + [shape((size, width), f32)] * 3
        + [shape((width, size), f32), shape((8, model), f32)],
        scratch_shapes=[
            pltpu.VMEM((4, n, size // 2, 3 * width // 2), bf16),
            pltpu.VMEM((2, n, size // 2, width), bf16),
            pltpu.VMEM((seq, model), bf16),
            pltpu.VMEM((seq, 3 * width), bf16),
            pltpu.VMEM((n, size, 3 * width), bf16),
            pltpu.VMEM((n, 3 * width, size), bf16),
            pltpu.VMEM((seq, width), bf16),
            pltpu.VMEM((seq, model), bf16),
            own(f32),
            own(f32),
            own(bf16),
            own(f32),
            pltpu.VMEM((2, rows, model), bf16),
            pltpu.VMEM((2, rows, model), bf16),
            own(bf16),
            own(bf16),
            pltpu.VMEM((2, rows, model), bf16),
            pltpu.VMEM((2, rows, model), bf16),
            own(bf16),
            own(bf16),
            own(bf16),
            pltpu.VMEM((2, 16, model), f32),
            own(f32),
            pltpu.VMEM((size, 3 * width), f32),
            pltpu.VMEM((width, size), f32),
            pltpu.VMEM((6, 8, model), f32),
            pltpu.VMEM((5, 8, model), f32),
            DMA((6, n - 1)),
            DMA((6, n - 1)),
            DMA((6,)),
            DMA((6,)),
            DMA((5,)),
            DMA((5,)),
            DMA((16,)),
            DMA((2, 2, n)),
        ],
        compiler_params=pltpu.CompilerParams(collective_id=4, has_side_effects=True, vmem_limit_bytes=62 << 20),
        cost_estimate=pl.CostEstimate(flops=14 * seq * model * width, bytes_accessed=40 << 20, transcendentals=0),
        name="leave",
    )(normed, dlin, qkv.reshape(n, size, 3 * width), mixed, resid, datt, x, attended, ffn.reshape(4, rows, model), small, vec)

def finish_kernel(
    n,
    layer, input_grad, query_sum, key_sum, value_sum, out_sum, gate_sum, up_sum, down_sum, vec,
    layer_out, input_out, gain_one, shift_one, query_out, key_out, value_out, bias_q, bias_k, bias_v, out_out, gain_two, shift_two,
    gate_out, up_out, down_out,
    out_in, down_in, down_turned, held_input, held_layer, held, small_held, sems,
):
    loads = [
        pltpu.make_async_copy(src, dst, sems.at[i])
        for i, (src, dst) in enumerate(
            (
                (down_sum, down_in),
                (out_sum, out_in),
                (input_grad, held_input),
                (layer, held_layer),
                (gate_sum, held.at[0]),
                (up_sum, held.at[1]),
                (query_sum, small_held.at[0]),
                (key_sum, small_held.at[1]),
                (value_sum, small_held.at[2]),
            )
        )
    ]
    for load in loads:
        load.start()
    me, t = lax.axis_index("dp"), lax.axis_index("tensor")
    each = gain_one.shape[1]
    at = me * 4 + t
    fit = 128 // each
    for r, out in enumerate((gain_one, shift_one, gain_two, shift_two)):
        wide = vec[r : r + 1, pl.ds(pl.multiple_of(lax.div(at, fit) * 128, 128), 128)]
        value = wide[:, 0:each]
        for i in range(1, fit):
            value = jnp.where(lax.rem(at, fit) == i, wide[:, i * each : (i + 1) * each], value)
        out[...] = value
    heads, per = bias_q.shape
    row = vec[4:5, :]
    for part, out in ((0, bias_q), (2, bias_v)):
        base = part * heads * HD
        own = jnp.concatenate([row[:, base + h * HD : base + (h + 1) * HD] for h in range(heads)], axis=0)
        value = own[:, 0:per]
        for d in range(1, n):
            value = jnp.where(me == d, own[:, d * per : (d + 1) * per], value)
        out[...] = value
    base = heads * HD
    bias_k[...] = jnp.concatenate([row[:, base + h * HD : base + h * HD + ROT] for h in range(heads)], axis=0)
    stores = []

    def store(src, dst):
        stores.append(pltpu.make_async_copy(src, dst, sems.at[9 + len(stores)]))
        stores[-1].start()

    loads[0].wait()
    down_turned[...] = down_in[...].T
    store(down_turned, down_out)
    loads[1].wait()
    store(out_in, out_out)
    for load, src, dst in zip(
        loads[2:],
        (held_input, held_layer, held.at[0], held.at[1], small_held.at[0], small_held.at[1], small_held.at[2]),
        (input_out, layer_out, gate_out, up_out, query_out, key_out, value_out),
    ):
        load.wait()
        store(src, dst)
    for copy in stores:
        copy.wait()


def finish(layer, input_grad, query_sum, key_sum, value_sum, out_sum, gate_sum, up_sum, down_sum, vec, n):
    shape = jax.ShapeDtypeStruct
    size, width = query_sum.shape
    heads, model = width // HD, vec.shape[1]
    each = shape((1, model // (4 * n)), f32)
    bias = shape((heads, HD // n), f32)
    like = lambda value: shape(value.shape, value.dtype)
    results = pl.pallas_call(
        lambda *refs: finish_kernel(n, *refs),
        in_specs=[HBM] * 9 + [VMEM],
        out_specs=[HBM, HBM, VMEM, VMEM, HBM, HBM, HBM, VMEM, VMEM, VMEM, HBM, VMEM, VMEM, HBM, HBM, HBM],
        out_shape=[
            like(layer), like(input_grad), each, each, like(query_sum), like(key_sum), like(value_sum),
            bias, shape((heads, ROT), f32), bias, like(out_sum), each, each,
            like(gate_sum), like(up_sum), shape(down_sum.shape[::-1], f32),
        ],
        scratch_shapes=[
            pltpu.VMEM(out_sum.shape, f32),
            pltpu.VMEM(down_sum.shape, f32),
            pltpu.VMEM(down_sum.shape[::-1], f32),
            pltpu.VMEM(input_grad.shape, f32),
            pltpu.VMEM(layer.shape, bf16),
            pltpu.VMEM((2,) + gate_sum.shape, f32),
            pltpu.VMEM((3,) + query_sum.shape, f32),
            DMA((18,)),
        ],
        compiler_params=pltpu.CompilerParams(vmem_limit_bytes=62 << 20),
        name="finish",
    )(layer, input_grad, query_sum, key_sum, value_sum, out_sum, gate_sum, up_sum, down_sum, vec)
    return tuple(r.reshape(-1) if r.shape[0] == 1 else r for r in results)


def norm_forward(rows):
    center = rows - jnp.mean(rows, axis=-1, keepdims=True)
    rstd = lax.rsqrt(jnp.mean(center * center, axis=-1, keepdims=True) + EPS)
    return center * rstd, rstd


def norm_backward(grad_out, normal, rstd, gain):
    scaled = grad_out * gain
    return rstd * (
        scaled
        - jnp.mean(scaled, axis=-1, keepdims=True)
        - normal * jnp.mean(scaled * normal, axis=-1, keepdims=True)
    )


def local(
    layer_input,
    segments,
    positions,
    first_gain,
    first_shift,
    query_weight,
    key_weight,
    value_weight,
    query_bias,
    key_bias,
    value_bias,
    out_weight,
    second_gain,
    second_shift,
    gate_weight,
    up_weight,
    down_weight,
    out_grad,
):
    ring = Ring()
    n = ring.n
    width = query_weight.shape[1]
    heads = width // HD
    model = layer_input.shape[1]

    per = HD // n
    if ring.ring:
        normed, g_full, qkv, out_t, lin, small = enter(
            layer_input, out_grad, query_weight, key_weight, value_weight, out_weight,
            (first_gain, first_shift, second_gain, second_shift), (query_bias, value_bias), n
        )
        g_full = g_full.reshape(-1, model)
        qkv = qkv.reshape(model, -1)
        out_t = out_t.reshape(model, -1)
    else:
        gather = lambda vector: lax.all_gather(vector, "dp", axis=0, tiled=True).astype(f32)
        gain_one, shift_one, gain_two, shift_two = map(gather, (first_gain, first_shift, second_gain, second_shift))
        bias_query, bias_value = (gather(b.T).T.reshape(-1) for b in (query_bias, value_bias))
        bias_key = jnp.pad(key_bias.astype(f32), ((0, 0), (0, HD - ROT))).reshape(-1)
        bias_lin = jnp.concatenate([bias_query, bias_key, bias_value])
        x_full = tensor_gather(layer_input)
        g_full = tensor_gather(out_grad, after=x_full)
        qkv, _ = ring.gather(jnp.concatenate([query_weight, key_weight, value_weight], axis=1))
        out_t, _ = ring.gather(out_weight.T)
        gate, _ = ring.gather(gate_weight)
        up, _ = ring.gather(up_weight)
        down_t, _ = ring.gather(down_weight.T)
        hat_full, _ = norm_forward(x_full.astype(f32))
        normed = (hat_full * gain_one + shift_one).astype(bf16)
        lin = dot(qkv, normed, ((0,), (1,)))

    freqs = jnp.exp(-(2.0 / ROT) * jnp.arange(HALF).astype(f32) * math.log(10000.0))
    angles = freqs[:, None] * positions.astype(f32)[None, :]
    cosine, sine = jnp.cos(angles), jnp.sin(angles)
    rows = layer_input.astype(f32)
    if ring.ring:
        q_rot, k_rot, v_heads, logs, mixed, attended, second, gate, up, hidden, ffn, grad_gate, grad_up = middle(
            lin, key_bias, cosine, sine, segments, layer_input, out_t, small, gate_weight, up_weight, down_weight, g_full, n
        )
        second, gate, up = second.reshape(-1, model), gate.reshape(model, -1), up.reshape(model, -1)
        hidden, ffn = hidden.reshape(second.shape[0], -1), ffn.reshape(-1, model)
        grad_gate, grad_up = grad_gate.reshape(hidden.shape), grad_up.reshape(hidden.shape)
    else:
        index = jnp.arange(segments.shape[0], dtype=jnp.int32)
        allowed = (index[:, None] <= index[None, :]) & (segments[:, None] == segments[None, :])
        bias = jnp.where(allowed, 0.0, NEG).astype(f32)
        mixed, q_rot, k_rot, v_heads, logs = attend_forward(lin + bias_lin[:, None], cosine, sine, bias)
        attended = rows + tensor_scatter(dot(mixed, out_t, ((1,), (1,))))

        hat_two, rstd_two = norm_forward(attended)
        second = tensor_gather((hat_two * gain_two + shift_two).astype(bf16))
        gate_lin = dot(second, gate, ((1,), (0,)))
        up_lin = dot(second, up, ((1,), (0,)))
        sigma = jax.nn.sigmoid(gate_lin)
        activated = gate_lin * sigma
        hidden = (activated * up_lin).astype(bf16)
        ffn = dot(hidden, down_t, ((1,), (1,)))
        grad_hidden = dot(g_full, down_t, ((1,), (0,)))
        grad_gate = (grad_hidden * up_lin * sigma * (1.0 + gate_lin * (1.0 - sigma))).astype(bf16)
        grad_up = (grad_hidden * activated).astype(bf16)
    if ring.ring:
        down_sum, gate_sum, up_sum, grad_attended, residual, grad_lin, vec = back(
            grad_gate, grad_up, hidden, second, g_full, gate, up, attended, small, out_t,
            q_rot, k_rot, v_heads, logs, cosine, sine, segments, n
        )
        layer_output, input_grad, query_sum, key_sum, value_sum, out_sum, vec = leave(
            normed, grad_lin, qkv, mixed, residual.reshape(-1, model), grad_attended, layer_input, attended, ffn, small, vec, n
        )
        return finish(
            layer_output, input_grad, query_sum, key_sum, value_sum, out_sum, gate_sum, up_sum, down_sum, vec, n
        )
    else:
        down_grad = dot(g_full, hidden, ((0,), (0,)))
        grad_second = tensor_scatter(dot(grad_gate, gate, ((1,), (1,))) + dot(grad_up, up, ((1,), (1,))))
        gate_grad = dot(second, grad_gate, ((0,), (0,)))
        up_grad = dot(second, grad_up, ((0,), (0,)))
        down_sum = ring.scatter(down_grad).T
        gate_sum = ring.scatter(gate_grad)
        up_sum = ring.scatter(up_grad)
        grad_attended = out_grad.astype(f32) + norm_backward(grad_second, hat_two, rstd_two, gain_two)
        residual = tensor_gather(grad_attended.astype(bf16))
        grad_mixed = dot(out_t, residual, ((0,), (1,))).astype(bf16)
        dq, dk, dv, sums = attend_backward(q_rot, k_rot, v_heads, grad_mixed, logs, cosine, sine, bias)
        grad_lin = jnp.concatenate([dq, dk, dv], axis=0)
        sums = sums.reshape(width, 128)[:, :3]
        out_sum = ring.scatter(dot(residual, mixed, ((0,), (0,)))).T
        qkv_sum = ring.scatter(dot(normed, grad_lin, ((0,), (1,))))
        query_sum, key_sum, value_sum = (qkv_sum[:, i * width : (i + 1) * width] for i in range(3))
        grad_first = tensor_scatter(dot(grad_lin, qkv, ((0,), (1,))))
        hat_one, rstd_one = norm_forward(rows)
        input_grad = grad_attended + norm_backward(grad_first, hat_one, rstd_one, gain_one)
        layer_output = (attended + tensor_scatter(ffn.astype(f32))).astype(bf16)
        vectors = jnp.stack(
            [
                jnp.sum(grad_first * hat_one, axis=0),
                jnp.sum(grad_first, axis=0),
                jnp.sum(grad_second * hat_two, axis=0),
                jnp.sum(grad_second, axis=0),
            ]
        )
        packed = sum_all(jnp.concatenate([sum_all(vectors, ["tensor"]).reshape(-1), sums.T.reshape(-1)]), ["dp"])
        vectors, sums = packed[: 4 * model].reshape(4, model), packed[4 * model :].reshape(3, width)

    each = model // (n * lax.axis_size("tensor"))
    at = ring.me * lax.axis_size("tensor") + lax.axis_index("tensor")
    vectors = lax.dynamic_slice(vectors.reshape(4, -1, each), (0, at, 0), (4, 1, each))[:, 0]
    sums = sums.reshape(3, heads, n, per)
    mine = lax.dynamic_slice(sums, (0, 0, ring.me, 0), (3, heads, 1, per))[:, :, 0]
    key_bias_sum = sums[1].reshape(heads, HD)[:, :ROT]

    return (
        layer_output,
        input_grad,
        vectors[0],
        vectors[1],
        query_sum,
        key_sum,
        value_sum,
        mine[0],
        key_bias_sum,
        mine[2],
        out_sum,
        vectors[2],
        vectors[3],
        gate_sum,
        up_sum,
        down_sum,
    )


def solution(mesh):
    both = ("dp", "tensor")
    return jax.shard_map(
        local,
        mesh=mesh,
        in_specs=(
            P(both, None),
            P("dp"),
            P("dp"),
            P("dp"),
            P("dp"),
            P("dp", "tensor"),
            P("dp", "tensor"),
            P("dp", "tensor"),
            P("tensor", "dp"),
            P("tensor", None),
            P("tensor", "dp"),
            P("tensor", "dp"),
            P("dp"),
            P("dp"),
            P("dp", "tensor"),
            P("dp", "tensor"),
            P("tensor", "dp"),
            P(both, None),
        ),
        out_specs=(
            P(both, None),
            P(both, None),
            P(both),
            P(both),
            P("dp", "tensor"),
            P("dp", "tensor"),
            P("dp", "tensor"),
            P("tensor", "dp"),
            P("tensor", None),
            P("tensor", "dp"),
            P("tensor", "dp"),
            P(both),
            P(both),
            P("dp", "tensor"),
            P("dp", "tensor"),
            P("tensor", "dp"),
        ),
        check_vma=False,
    )
```
